32 devices in a mesh: wide: 8 (over z, x), narrow: 4 (over y, core).
Axes of the slice: x: 2, y: 2, z: 4, core: 2. Of those that a mesh axis runs over, the one named last changes fastest.
Arguments:
- query_states: bfloat16 [4096, 8192], P('wide', 'narrow'), may hold values from -8 to 8
- key_states: bfloat16 [4096, 8192], P('wide', 'narrow'), may hold values from -8 to 8
- value_states: bfloat16 [4096, 8192], P('wide', 'narrow'), may hold values from -6 to 6
- cache_keys: bfloat16 [4096, 1024], P('wide'), may hold values from -8 to 8
- cache_values: bfloat16 [4096, 1024], P('wide'), may hold values from -6 to 6
- gate_fast: bfloat16 [8, 512, 512], P('narrow'), may hold values from -0.25 to 0.25
- lift_fast: bfloat16 [8, 512, 512], P('narrow'), may hold values from -0.25 to 0.25
- down_fast: bfloat16 [8, 512, 512], P('narrow'), may hold values from -0.25 to 0.25
- token_rates: float32 [8, 8192], replicated, may hold values from 0.05 to 1
Outputs:
- attended: bfloat16 [4096, 8192], P('wide', 'narrow')
- recalled: bfloat16 [4096, 8192], P('wide', 'narrow')
The draws below stay inside these ranges and needn't reach their ends.
All inputs are finite; a program needn't handle non-finite values.
Results may differ from the reference program's by a relative error of at most 0.0094.
Values may be sent and summed in bfloat16 or wider, within the bound.
No kernel may reach another device: no remote copies, remote signals or barrier semaphores. Data moves between devices by JAX's collectives and lax.ppermute only.
A program may use at most 128 MiB of HBM per device.

```python
import math
import jax
import jax.numpy as jnp
from jax import lax

FAST_HEADS = 8
FD = 512
FH = 512
D = 4096
HEAD_SIZE = 128
HEADS = 32
WINDOW = 1024
TOKENS = 8192
NS_ITERS = 2


def background(key):
    drawn = jnp.clip(1.5 * jax.random.normal(key, (D, TOKENS), jnp.float32), -8.0, 8.0)
    return drawn


def draw_query_states(key, part):
    drawn = background(jax.random.fold_in(key, 11))
    return drawn.astype(jnp.bfloat16)


def draw_key_states(key, part):
    drawn = background(jax.random.fold_in(key, 13))
    return drawn.astype(jnp.bfloat16)


def block_levels(rng, shape, shards, smallest, top_value):
    def one(dim, parts):
        draws = jax.random.uniform(jax.random.fold_in(jax.random.fold_in(rng, 6), dim), (parts,), jnp.float32, smallest / len(shards), top_value / len(shards))
        return jnp.repeat(jnp.exp(draws), shape[dim] // parts).reshape((-1,) + (1,) * (len(shape) - dim - 1))

    gain = one(*shards[0])
    for cut in shards[1:]:
        gain = gain * one(*cut)
    return gain


def scatter_about(key, shape, spread, limit, split=(), kind=jnp.bfloat16):
    entries = spread * jax.random.normal(key, shape, jnp.float32)
    if split:
        entries = entries * block_levels(key, shape, split, -0.22, 0.18)
    return jnp.clip(entries, -limit, limit).astype(kind)


def setup_inputs(seed: int = 0) -> dict:
    key_list = jax.random.split(jax.random.key(seed), 10)
    query_states = draw_query_states(jax.random.fold_in(key_list[9], 71), 0)
    key_states = draw_key_states(jax.random.fold_in(key_list[9], 71), 0)
    value_states = scatter_about(key_list[2], (D, TOKENS), 1.0, 6.0, ((0, 8), (1, 4)))
    cache_keys = scatter_about(key_list[3], (D, WINDOW), 1.5, 8.0, ((0, 8),))
    cache_values = scatter_about(key_list[4], (D, WINDOW), 1.0, 6.0, ((0, 8),))
    gate_fast = scatter_about(key_list[5], (FAST_HEADS, FH, FD), FD ** -0.5, 0.25, ((0, 4),))
    lift_fast = scatter_about(key_list[6], (FAST_HEADS, FH, FD), FD ** -0.5, 0.25, ((0, 4),))
    down_fast = scatter_about(key_list[7], (FAST_HEADS, FD, FH), FH ** -0.5, 0.25, ((0, 4),))
    token_rates = jnp.clip(jnp.exp(jax.random.uniform(key_list[8], (FAST_HEADS, TOKENS), jnp.float32, math.log(0.05), math.log(1.0))), 0.05, 1.0)
    return {"query_states": query_states, "key_states": key_states, "value_states": value_states, "cache_keys": cache_keys, "cache_values": cache_values, "gate_fast": gate_fast, "lift_fast": lift_fast, "down_fast": down_fast, "token_rates": token_rates}


EPS = 1e-06
COEF_A = 3.4445
COEF_B = -4.775
COEF_C = 2.0315

def stored(value):
    return lax.optimization_barrier(value.astype(jnp.bfloat16))

def attend_head(head_queries, head_keys, head_values):
    block_rows = min(512, TOKENS)
    block_count = TOKENS // block_rows
    key_span = WINDOW + block_rows
    scaling = 1.0 / math.sqrt(HEAD_SIZE)
    rows_at = jnp.arange(block_rows, dtype=jnp.int32)[:, None]
    cols_at = jnp.arange(key_span, dtype=jnp.int32)[None, :]
    visible = (cols_at > rows_at) & (cols_at <= rows_at + WINDOW)

    def one_block(block_index):
        offset = block_index * block_rows
        query_part = lax.dynamic_slice_in_dim(head_queries, offset, block_rows, 1)
        key_part = lax.dynamic_slice_in_dim(head_keys, offset, key_span, 1)
        value_part = lax.dynamic_slice_in_dim(head_values, offset, key_span, 1)
        scores = jnp.dot(query_part.T, key_part, preferred_element_type=jnp.float32) * scaling
        scores = jnp.where(visible, scores, -jnp.inf)
        highest = lax.optimization_barrier(jnp.max(scores, axis=1, keepdims=True))
        raised = jnp.exp(scores - highest)
        weights = (raised / lax.optimization_barrier(jnp.sum(raised, axis=1, keepdims=True))).astype(jnp.bfloat16)
        return jnp.dot(value_part, weights.T, preferred_element_type=jnp.float32).astype(jnp.bfloat16)
    blocks_out = lax.map(one_block, jnp.arange(block_count, dtype=jnp.int32))
    return jnp.transpose(blocks_out, (1, 0, 2)).reshape(HEAD_SIZE, TOKENS)

def orthogonal(gradient):
    rounded = stored(gradient)
    widened = rounded.astype(jnp.float32)
    norm_val = jnp.sqrt(jnp.sum(jnp.square(widened)) + EPS)
    current = stored(widened / norm_val)
    for sweep_index in range(NS_ITERS):
        gram_mat = jnp.dot(current.T, current, preferred_element_type=jnp.float32).astype(jnp.bfloat16)
        lifted = stored(jnp.dot(current, gram_mat, preferred_element_type=jnp.float32))
        current = stored(COEF_A * current.astype(jnp.float32) + COEF_B * lifted.astype(jnp.float32) + COEF_C * jnp.dot(lifted, gram_mat, preferred_element_type=jnp.float32))
    return current

def refreshed(weight, ortho):
    initial = weight.astype(jnp.float32)
    moved_rows = initial - ortho.astype(jnp.float32)
    wanted = jnp.sqrt(lax.optimization_barrier(jnp.mean(jnp.square(initial), axis=-1, keepdims=True)) + EPS)
    present = jnp.sqrt(lax.optimization_barrier(jnp.mean(jnp.square(moved_rows), axis=-1, keepdims=True)) + EPS)
    return (moved_rows * (wanted / present)).astype(jnp.bfloat16)

def reference(query_states, key_states, value_states, cache_keys, cache_values, gate_fast, lift_fast, down_fast, token_rates):
    ext_keys = jnp.concatenate([cache_keys, key_states], axis=1)
    ext_values = jnp.concatenate([cache_values, value_states], axis=1)

    def per_head(head_index):
        first_row = head_index * HEAD_SIZE
        return attend_head(lax.dynamic_slice_in_dim(query_states, first_row, HEAD_SIZE, 0), lax.dynamic_slice_in_dim(ext_keys, first_row, HEAD_SIZE, 0), lax.dynamic_slice_in_dim(ext_values, first_row, HEAD_SIZE, 0))
    attended = lax.map(per_head, jnp.arange(HEADS, dtype=jnp.int32)).reshape(D, TOKENS)

    def per_fast(head_index):
        first_row = head_index * FD
        query_fast = lax.dynamic_slice_in_dim(query_states, first_row, FD, 0)
        key_fast = lax.dynamic_slice_in_dim(key_states, first_row, FD, 0)
        value_fast = lax.dynamic_slice_in_dim(value_states, first_row, FD, 0)
        gate_weight = gate_fast[head_index]
        lift_weight = lift_fast[head_index]
        down_weight = down_fast[head_index]
        rates_row = token_rates[head_index]
        pre_gate = jnp.dot(gate_weight, key_fast, preferred_element_type=jnp.float32)
        pre_lift = jnp.dot(lift_weight, key_fast, preferred_element_type=jnp.float32)
        sigmoid_gate = jax.nn.sigmoid(pre_gate)
        silu_gate = pre_gate * sigmoid_gate
        hidden = (silu_gate * pre_lift).astype(jnp.bfloat16)
        target = (-(value_fast.astype(jnp.float32) * rates_row[None, :])).astype(jnp.bfloat16)
        grad_down = jnp.dot(target, hidden.T, preferred_element_type=jnp.float32)
        back_hidden = jnp.dot(down_weight.T, target, preferred_element_type=jnp.float32)
        back_lift = (back_hidden * silu_gate).astype(jnp.bfloat16)
        back_gate = (back_hidden * pre_lift * sigmoid_gate * (1.0 + pre_gate * (1.0 - sigmoid_gate))).astype(jnp.bfloat16)
        grad_gate = jnp.dot(back_gate, key_fast.T, preferred_element_type=jnp.float32)
        grad_lift = jnp.dot(back_lift, key_fast.T, preferred_element_type=jnp.float32)
        fresh_gate = refreshed(gate_weight, orthogonal(grad_gate))
        fresh_lift = refreshed(lift_weight, orthogonal(grad_lift))
        fresh_down = refreshed(down_weight, orthogonal(grad_down))
        query_gate = jnp.dot(fresh_gate, query_fast, preferred_element_type=jnp.float32)
        query_lift = jnp.dot(fresh_lift, query_fast, preferred_element_type=jnp.float32)
        query_hidden = (jax.nn.silu(query_gate) * query_lift).astype(jnp.bfloat16)
        return jnp.dot(fresh_down, query_hidden, preferred_element_type=jnp.float32).astype(jnp.bfloat16)
    recalled = lax.map(per_fast, jnp.arange(FAST_HEADS, dtype=jnp.int32)).reshape(D, TOKENS)
    return (attended, recalled)
```

```python
import functools
import math

import jax
import jax.numpy as jnp
from jax import lax
from jax.experimental import pallas as pl
from jax.experimental.pallas import tpu as pltpu
from jax.sharding import PartitionSpec as P

FD = 512
HEAD_SIZE = 128
WINDOW = 1024
NS_ITERS = 2


EPS = 1e-06
COEF_A = 3.4445
COEF_B = -4.775
COEF_C = 2.0315
LOG2E = math.log2(math.e)


def swapped(array, axis, distance):
    return lax.ppermute(array, axis, [(i, i ^ 1 << distance) for i in range(lax.axis_size(axis))])


def shortened(array):

    def short(part):
        return part.astype(jnp.bfloat16) if part.dtype == jnp.float32 else part

    return jax.tree.map(short, array)


def from_behind(value, axis, steps):
    count = lax.axis_size(axis)
    initial, last = (max(0, -steps), min(count, count - steps))
    return lax.ppermute(value, axis, [(source, source + steps) for source in range(initial, last)])


def stored(value):
    return lax.optimization_barrier(value.astype(jnp.bfloat16))


def attend_local(query_states, ext_keys, ext_values, key_start):
    features, tok_count = query_states.shape
    head_count = features // HEAD_SIZE
    block_rows = min(512, tok_count)
    block_count = tok_count // block_rows
    key_span = WINDOW + block_rows
    scaling = 1.0 / math.sqrt(HEAD_SIZE)
    rows_at = lax.broadcasted_iota(jnp.int32, (block_rows, key_span), 0)
    cols_at = lax.broadcasted_iota(jnp.int32, (block_rows, key_span), 1)
    visible = (cols_at > rows_at) & (cols_at <= rows_at + WINDOW)

    def one_block(block_index):
        offset = block_index * block_rows
        query_part = lax.dynamic_slice_in_dim(query_states, offset, block_rows, 1).reshape(
            head_count, HEAD_SIZE, block_rows
        )
        key_part = lax.dynamic_slice_in_dim(ext_keys, key_start + offset, key_span, 1).reshape(
            head_count, HEAD_SIZE, key_span
        )
        value_part = lax.dynamic_slice_in_dim(ext_values, key_start + offset, key_span, 1).reshape(
            head_count, HEAD_SIZE, key_span
        )
        scores = (
            jnp.einsum("hdq,hdk->hqk", query_part, key_part, preferred_element_type=jnp.float32)
            * scaling
        )
        scores = jnp.where(visible[None], scores, -jnp.inf)
        highest = jnp.max(scores, axis=2, keepdims=True)
        raised = jnp.exp(scores - highest)
        weights = (raised / jnp.sum(raised, axis=2, keepdims=True)).astype(jnp.bfloat16)
        blended = jnp.einsum(
            "hdk,hqk->hdq", value_part, weights, preferred_element_type=jnp.float32
        )
        return blended.astype(jnp.bfloat16).reshape(features, block_rows)

    blocks_out = lax.map(one_block, jnp.arange(block_count, dtype=jnp.int32))
    return jnp.transpose(blocks_out, (1, 0, 2)).reshape(features, tok_count)


def attend_paired(query_states, ext_keys, ext_values):
    features, tok_count = query_states.shape
    half_rows = tok_count // 2
    lower = lax.axis_index("wide") % 2 == 0
    query_send = jnp.where(lower, query_states[:, half_rows:], query_states[:, :half_rows])
    query_keep = jnp.where(lower, query_states[:, :half_rows], query_states[:, half_rows:])
    other_keys, other_values, other_queries = swapped((ext_keys, ext_values, query_send), "wide", 0)
    full_keys = jnp.where(
        lower,
        jnp.concatenate([ext_keys, other_keys], axis=0),
        jnp.concatenate([other_keys, ext_keys], axis=0),
    )
    full_values = jnp.where(
        lower,
        jnp.concatenate([ext_values, other_values], axis=0),
        jnp.concatenate([other_values, ext_values], axis=0),
    )
    full_queries = jnp.where(
        lower,
        jnp.concatenate([query_keep, other_queries], axis=0),
        jnp.concatenate([other_queries, query_keep], axis=0),
    )
    key_start = jnp.where(lower, 0, half_rows).astype(jnp.int32)
    head_out = attend_local(full_queries, full_keys, full_values, key_start)
    out_keep = jnp.where(lower, head_out[:features], head_out[features:])
    out_send = jnp.where(lower, head_out[features:], head_out[:features])
    out_other = swapped(shortened(out_send), "wide", 0).astype(out_send.dtype)
    return jnp.where(
        lower,
        jnp.concatenate([out_keep, out_other], axis=1),
        jnp.concatenate([out_other, out_keep], axis=1),
    )


def fast_terms(gate_weight, lift_weight, down_weight, key_heads, value_heads, rates_here):
    pre_gate = jnp.einsum(
        "hcf,hft->hct", gate_weight, key_heads, preferred_element_type=jnp.float32
    )
    pre_lift = jnp.einsum(
        "hcf,hft->hct", lift_weight, key_heads, preferred_element_type=jnp.float32
    )
    sigmoid_gate = jax.nn.sigmoid(pre_gate)
    silu_gate = pre_gate * sigmoid_gate
    hidden = (silu_gate * pre_lift).astype(jnp.bfloat16)
    target = (-(value_heads.astype(jnp.float32) * rates_here[:, None, :])).astype(jnp.bfloat16)
    grad_down = jnp.einsum("hft,hct->hfc", target, hidden, preferred_element_type=jnp.float32)
    back_hidden = jnp.einsum(
        "hfc,hft->hct", down_weight, target, preferred_element_type=jnp.float32
    )
    back_lift = (back_hidden * silu_gate).astype(jnp.bfloat16)
    back_gate = (
        back_hidden * pre_lift * sigmoid_gate * (1.0 + pre_gate * (1.0 - sigmoid_gate))
    ).astype(jnp.bfloat16)
    grad_gate = jnp.einsum("hct,hft->hcf", back_gate, key_heads, preferred_element_type=jnp.float32)
    grad_lift = jnp.einsum("hct,hft->hcf", back_lift, key_heads, preferred_element_type=jnp.float32)
    return (grad_gate, grad_lift, grad_down)


def scaled_start(rounded):
    widened = rounded.astype(jnp.float32)
    norm_val = jnp.sqrt(jnp.sum(jnp.square(widened), axis=(1, 2), keepdims=True) + EPS)
    return stored(widened / norm_val)


def starting(grad_gate, grad_lift, grad_down):
    sum_gate, sum_lift, sum_down = lax.psum((grad_gate, grad_lift, grad_down), "wide")
    return (
        scaled_start(stored(sum_gate)),
        scaled_start(stored(sum_lift)),
        scaled_start(stored(sum_down)),
    )


def orthogonal(current):
    for sweep_index in range(NS_ITERS):
        gram_mat = jnp.einsum(
            "hrc,hrd->hcd", current, current, preferred_element_type=jnp.float32
        ).astype(jnp.bfloat16)
        lifted = stored(
            jnp.einsum("hrc,hcd->hrd", current, gram_mat, preferred_element_type=jnp.float32)
        )
        current = stored(
            COEF_A * current.astype(jnp.float32)
            + COEF_B * lifted.astype(jnp.float32)
            + COEF_C
            * jnp.einsum("hrc,hcd->hrd", lifted, gram_mat, preferred_element_type=jnp.float32)
        )
    return current


def refreshed(weight, ortho):
    initial = weight.astype(jnp.float32)
    moved_rows = initial - ortho.astype(jnp.float32)
    wanted = jnp.sqrt(jnp.mean(jnp.square(initial), axis=-1, keepdims=True) + EPS)
    present = jnp.sqrt(jnp.mean(jnp.square(moved_rows), axis=-1, keepdims=True) + EPS)
    return (moved_rows * (wanted / present)).astype(jnp.bfloat16)


def fast_group(
    gate_weight, lift_weight, down_weight, query_heads, key_heads, value_heads, rates_here
):
    grad_gate, grad_lift, grad_down = fast_terms(
        gate_weight, lift_weight, down_weight, key_heads, value_heads, rates_here
    )
    start_gate, start_lift, start_down = starting(grad_gate, grad_lift, grad_down)
    fresh_gate = refreshed(gate_weight, orthogonal(start_gate))
    fresh_lift = refreshed(lift_weight, orthogonal(start_lift))
    fresh_down = refreshed(down_weight, orthogonal(start_down))
    query_gate = jnp.einsum(
        "hcf,hft->hct", fresh_gate, query_heads, preferred_element_type=jnp.float32
    )
    query_lift = jnp.einsum(
        "hcf,hft->hct", fresh_lift, query_heads, preferred_element_type=jnp.float32
    )
    query_hidden = (jax.nn.silu(query_gate) * query_lift).astype(jnp.bfloat16)
    return jnp.einsum(
        "hfc,hct->hft", fresh_down, query_hidden, preferred_element_type=jnp.float32
    ).astype(jnp.bfloat16)


def attend_body(flag_ref, q_ref, kp_ref, vp_ref, kc_ref, vc_ref, *rest, block, has_cache, hd, window):
    if has_cache:
        ck_ref, cv_ref, o_prev, o_ref, kt_ref, v_ref = rest
    else:
        o_ref, kt_ref, v_ref = rest
    scale = LOG2E / math.sqrt(hd)
    def place(k, v):
        kt = k[...].T
        kt_ref[:window, :hd] = kt
        kt_ref[:window, hd:] = kt
        v_ref[:hd, :window] = v[...]
    if has_cache:
        @pl.when(flag_ref[0] == 1)
        def _(): place(ck_ref, cv_ref)
        @pl.when(flag_ref[0] != 1)
        def _(): place(kp_ref, vp_ref)
    else:
        place(kp_ref, vp_ref)
    kt = kc_ref[...].T
    kt_ref[window:, :hd] = kt
    kt_ref[window:, hd:] = kt
    v_ref[:hd, window:] = vc_ref[...]
    v_ref[hd:, :] = jnp.ones((v_ref.shape[0]-hd, 2*window), jnp.bfloat16)
    rows = lax.broadcasted_iota(jnp.int32, (block, block), 0)
    cols = lax.broadcasted_iota(jnp.int32, (block, block), 1)
    first = rows > cols
    inner = window // block
    for b in range(window // block):
        q = q_ref[:, b*block:(b+1)*block].astype(jnp.float32) * scale
        hi = q.astype(jnp.bfloat16)
        lo = (q - hi.astype(jnp.float32)).astype(jnp.bfloat16)
        q2 = jnp.concatenate([hi, lo], axis=0)
        s = []
        for j in range(inner + 1):
            lo_row = (b + j) * block
            s.append(jnp.dot(kt_ref[lo_row:lo_row+block, :], q2, preferred_element_type=jnp.float32))
        s[0] = jnp.where(first, s[0], s[inner])
        top = s[0]
        for j in range(1, inner): top = jnp.maximum(top, s[j])
        top = jnp.max(top, axis=0, keepdims=True)
        p = [jnp.exp2(s[j] - top).astype(jnp.bfloat16) for j in range(inner)]
        zero = jnp.zeros_like(p[0])
        parts = [jnp.where(first, p[0], zero)] + p[1:] + [jnp.where(first, zero, p[0])]
        w = jnp.concatenate(parts, axis=0)
        o = jnp.dot(v_ref[:, b*block:(b+inner+1)*block], w, preferred_element_type=jnp.float32)
        o_ref[:, b*block:(b+1)*block] = (o[:hd] * (1.0 / o[hd:hd+1])).astype(jnp.bfloat16)

def attend_late(q, k, v, block=256):
    f, T = q.shape
    hd, W = HEAD_SIZE, WINDOW
    heads, chunks = f//hd, T//W - 1
    cur = pl.BlockSpec((hd, W), lambda h, c: (h, c+1))
    prev = pl.BlockSpec((hd, W), lambda h, c: (h, c))
    return pl.pallas_call(
        functools.partial(attend_body, block=block, has_cache=False, hd=hd, window=W),
        out_shape=jax.ShapeDtypeStruct((f, T), jnp.bfloat16),
        grid=(heads, chunks),
        in_specs=[pl.BlockSpec(memory_space=pltpu.SMEM), cur, prev, prev, cur, cur],
        out_specs=cur,
        scratch_shapes=[pltpu.VMEM((2*W, 2*hd), jnp.bfloat16), pltpu.VMEM((hd+16, 2*W), jnp.bfloat16)],
        cost_estimate=pl.CostEstimate(flops=heads*chunks*W*W*hd*5, bytes_accessed=5*f*W*2, transcendentals=heads*chunks*W*W),
        name="attend_late",
    )(jnp.zeros((1,), jnp.int32), q, k, v, k, v)

def attend_early(flag, q, k, v, prior, ck, cv, out, block=256):
    f, T = q.shape
    hd, W = HEAD_SIZE, WINDOW
    heads = f//hd
    cur = pl.BlockSpec((hd, W), lambda h: (h, 0))
    prior_k = pl.BlockSpec((None, hd, W), lambda h: (0, h, 0))
    prior_v = pl.BlockSpec((None, hd, W), lambda h: (1, h, 0))
    return pl.pallas_call(
        functools.partial(attend_body, block=block, has_cache=True, hd=hd, window=W),
        out_shape=jax.ShapeDtypeStruct((f, T), jnp.bfloat16),
        grid=(heads,),
        in_specs=[pl.BlockSpec(memory_space=pltpu.SMEM), cur, prior_k, prior_v, cur, cur, cur, cur, pl.BlockSpec(memory_space=pl.ANY)],
        out_specs=cur,
        scratch_shapes=[pltpu.VMEM((2*W, 2*hd), jnp.bfloat16), pltpu.VMEM((hd+16, 2*W), jnp.bfloat16)],
        input_output_aliases={8: 0},
        cost_estimate=pl.CostEstimate(flops=heads*W*W*hd*5, bytes_accessed=7*f*W*2, transcendentals=heads*W*W),
        name="attend_early",
    )(flag, q, prior, prior, k, v, ck, cv, out)


def pick_weights(role, sources, target, sem):
    for place, source in enumerate(sources):

        @pl.when(role == place)
        def _(source=source):
            pltpu.sync_copy(source, target)


def terms_body(where_ref, *refs):
    sources = refs[:-12]
    (
        key_ref, value_ref, rate_ref, keep_ref, send_ref,
        w_ref, turned_ref, hidden_ref, target_ref, back_ref, sem, _,
    ) = refs[-12:]
    features, tokens = key_ref.shape
    hidden_rows = w_ref.shape[1]
    half = hidden_rows // 2
    block = min(256, tokens)
    side = where_ref[1]
    pick_weights(where_ref[0], sources, w_ref, sem)
    turned_ref[...] = w_ref[2].T
    gate_lift = w_ref[0:2].reshape(2 * hidden_rows, features)

    def step(index, carry):
        at = pl.ds(pl.multiple_of(index * block, block), block)
        keys = key_ref[:, at]
        pre = jnp.dot(gate_lift, keys, preferred_element_type=jnp.float32)
        pre_gate = pre[:hidden_rows]
        pre_lift = pre[hidden_rows:]
        rates = rate_ref[pl.ds(where_ref[2], 1), at]
        target = (-(value_ref[:, at].astype(jnp.float32) * rates)).astype(jnp.bfloat16)
        back_hidden = jnp.dot(turned_ref[...], target, preferred_element_type=jnp.float32)
        sigmoid_gate = 0.5 * jnp.tanh(0.5 * pre_gate) + 0.5
        silu_gate = pre_gate * sigmoid_gate
        hidden_ref[:, at] = (silu_gate * pre_lift).astype(jnp.bfloat16)
        target_ref[:, at] = target
        back_lift = (back_hidden * silu_gate).astype(jnp.bfloat16)
        slope = sigmoid_gate + silu_gate * (1.0 - sigmoid_gate)
        back_gate = (back_hidden * pre_lift * slope).astype(jnp.bfloat16)
        for part in range(2):
            back_ref[part, :half, at] = back_gate[part * half : (part + 1) * half]
            back_ref[part, half:, at] = back_lift[part * half : (part + 1) * half]
        return carry

    lax.fori_loop(0, tokens // block, step, 0, unroll=2)
    contract = (((1,), (1,)), ((), ()))
    for part, out_ref in ((1 - side, send_ref), (side, keep_ref)):
        sums = lax.dot_general(
            back_ref[part], key_ref[...], contract, preferred_element_type=jnp.float32
        )
        out_ref[0] = sums[:half].astype(out_ref.dtype)
        out_ref[1] = sums[half:].astype(out_ref.dtype)
        rows = pl.ds(pl.multiple_of(part * half, half), half)
        out_ref[2] = lax.dot_general(
            target_ref[rows, :], hidden_ref[...], contract, preferred_element_type=jnp.float32
        ).astype(out_ref.dtype)


def fast_sums(where, sources, keys, values, rates):
    features, tokens = keys.shape
    _, hidden_rows, _ = sources[0].shape
    half = hidden_rows // 2
    whole = lambda i, where: (0, 0)
    parts = lambda i, where: (0, 0, 0)
    return pl.pallas_call(
        terms_body,
        out_shape=(
            jax.ShapeDtypeStruct((3, half, features), jnp.float32),
            jax.ShapeDtypeStruct((3, half, features), jnp.bfloat16),
        ),
        grid_spec=pltpu.PrefetchScalarGridSpec(
            num_scalar_prefetch=1,
            grid=(1,),
            in_specs=[pl.BlockSpec(memory_space=pl.ANY)] * len(sources)
            + [
                pl.BlockSpec((features, tokens), whole),
                pl.BlockSpec((features, tokens), whole),
                pl.BlockSpec((rates.shape[0], tokens), lambda i, where: (0, where[3])),
            ],
            out_specs=(
                pl.BlockSpec((3, half, features), parts),
                pl.BlockSpec((3, half, features), parts),
            ),
            scratch_shapes=[
                pltpu.VMEM((3, hidden_rows, features), jnp.bfloat16),
                pltpu.VMEM((hidden_rows, features), jnp.bfloat16),
                pltpu.VMEM((hidden_rows, tokens), jnp.bfloat16),
                pltpu.VMEM((features, tokens), jnp.bfloat16),
                pltpu.VMEM((2, hidden_rows, tokens), jnp.bfloat16),
                pltpu.SemaphoreType.DMA(()),
                pltpu.SMEM((1,), jnp.int32),
            ],
        ),
        cost_estimate=pl.CostEstimate(
            flops=12 * hidden_rows * features * tokens,
            bytes_accessed=4 * features * tokens + 6 * hidden_rows * features,
            transcendentals=hidden_rows * tokens,
        ),
        name="fast_sums",
    )(where, *sources, keys, values, rates)


def recall_body(where_ref, *refs):
    sources = refs[:-7]
    mine_ref, other_ref, query_ref, out_ref, w_ref, fresh_ref, sem = refs[-7:]
    half = mine_ref.shape[1]

    @pl.when(pl.program_id(0) == 0)
    def _():
        side = where_ref[1]
        pick_weights(where_ref[0], sources, w_ref, sem)
        rows_mine = pl.ds(pl.multiple_of(side * half, half), half)
        rows_other = pl.ds(pl.multiple_of((1 - side) * half, half), half)
        fresh_ref[:, rows_mine, :] = mine_ref[...]
        fresh_ref[:, rows_other, :] = other_ref[...]
        current = []
        for i in range(3):
            widened = fresh_ref[i].astype(jnp.float32)
            total = jnp.sum(jnp.sum(widened * widened, axis=0, keepdims=True), axis=1, keepdims=True)
            current.append((widened / jnp.sqrt(total + EPS)).astype(jnp.bfloat16))
        for _ in range(NS_ITERS):
            gram = [
                lax.dot_general(
                    x, x, (((0,), (0,)), ((), ())), preferred_element_type=jnp.float32
                ).astype(jnp.bfloat16)
                for x in current
            ]
            lifted = [
                jnp.dot(x, g, preferred_element_type=jnp.float32).astype(jnp.bfloat16)
                for x, g in zip(current, gram)
            ]
            current = [
                (
                    COEF_A * x.astype(jnp.float32)
                    + COEF_B * y.astype(jnp.float32)
                    + COEF_C * jnp.dot(y, g, preferred_element_type=jnp.float32)
                ).astype(jnp.bfloat16)
                for x, y, g in zip(current, lifted, gram)
            ]
        for i in range(3):
            initial = w_ref[i].astype(jnp.float32)
            moved = initial - current[i].astype(jnp.float32)
            wanted = jnp.mean(jnp.square(initial), axis=-1, keepdims=True) + EPS
            present = jnp.mean(jnp.square(moved), axis=-1, keepdims=True) + EPS
            fresh_ref[i] = (moved * (jnp.sqrt(wanted) / jnp.sqrt(present))).astype(jnp.bfloat16)

    hidden_rows, features = fresh_ref.shape[1:]
    pre = jnp.dot(
        fresh_ref[0:2].reshape(2 * hidden_rows, features),
        query_ref[...],
        preferred_element_type=jnp.float32,
    )
    gate = pre[:hidden_rows]
    hidden = (gate * (0.5 * jnp.tanh(0.5 * gate) + 0.5) * pre[hidden_rows:]).astype(jnp.bfloat16)
    out_ref[...] = jnp.dot(fresh_ref[2], hidden, preferred_element_type=jnp.float32).astype(
        jnp.bfloat16
    )


def fast_recall(where, sources, mine, other, queries):
    features, tokens = queries.shape
    _, hidden_rows, _ = sources[0].shape
    block = min(512, tokens)
    half = hidden_rows // 2
    parts = lambda i, where: (0, 0, 0)
    piece = pl.BlockSpec((features, block), lambda i, where: (0, i))
    return pl.pallas_call(
        recall_body,
        out_shape=jax.ShapeDtypeStruct((features, tokens), jnp.bfloat16),
        grid_spec=pltpu.PrefetchScalarGridSpec(
            num_scalar_prefetch=1,
            grid=(tokens // block,),
            in_specs=[pl.BlockSpec(memory_space=pl.ANY)] * len(sources)
            + [
                pl.BlockSpec((3, half, features), parts),
                pl.BlockSpec((3, half, features), parts),
                piece,
            ],
            out_specs=piece,
            scratch_shapes=[
                pltpu.VMEM((3, hidden_rows, features), jnp.bfloat16),
                pltpu.VMEM((3, hidden_rows, features), jnp.bfloat16),
                pltpu.SemaphoreType.DMA(()),
            ],
        ),
        cost_estimate=pl.CostEstimate(
            flops=6 * hidden_rows * features * tokens + 36 * NS_ITERS * hidden_rows * features**2 // 2,
            bytes_accessed=4 * features * tokens + 12 * hidden_rows * features,
            transcendentals=hidden_rows * tokens,
        ),
        name="fast_recall",
    )(where, *sources, mine, other, queries)


def in_place(query_states, key_states, value_states, cache_keys, cache_values, gate_fast, *rest):
    features, tok_count = query_states.shape
    narrow_count = lax.axis_size("narrow")
    return (
        features == FD
        and gate_fast.shape[1:] == (FD, FD)
        and features % HEAD_SIZE == 0
        and tok_count % WINDOW == 0
        and tok_count >= 2 * WINDOW
        and narrow_count >= 2
        and narrow_count & (narrow_count - 1) == 0
    )


def in_place_plan(
    query_states,
    key_states,
    value_states,
    cache_keys,
    cache_values,
    gate_fast,
    lift_fast,
    down_fast,
    token_rates,
):
    tok_count = query_states.shape[1]
    wide_count = lax.axis_size("wide")
    narrow_count = lax.axis_size("narrow")
    owned = gate_fast.shape[0]
    wide_at = lax.axis_index("wide")
    narrow_at = lax.axis_index("narrow")
    role = narrow_at ^ (wide_at // owned)
    where = jnp.stack([role, narrow_at % 2, wide_at, narrow_at]).astype(jnp.int32)

    def sent(value, step):
        source = step & (step - 1)
        pairs = []
        for wide in range(wide_count):
            owner = wide // owned
            pairs.append(
                (wide * narrow_count + (owner ^ source), wide * narrow_count + (owner ^ step))
            )
        return lax.ppermute(value, ("wide", "narrow"), pairs)

    local = wide_at % owned
    sources = [
        jnp.stack(
            [
                lax.dynamic_index_in_dim(weight, local, 0, keepdims=False)
                for weight in (gate_fast, lift_fast, down_fast)
            ]
        )
    ]
    for step in range(1, narrow_count):
        sources.append(sent(sources[step & (step - 1)], step))
    edge_cols = jnp.stack(
        [key_states[:, tok_count - WINDOW :], value_states[:, tok_count - WINDOW :]]
    )
    arrived = from_behind(edge_cols, "narrow", 1)
    late = attend_late(query_states, key_states, value_states)
    keep, send = fast_sums(where, sources, key_states, value_states, token_rates)
    total = keep + swapped(send, "narrow", 0).astype(jnp.float32)
    distance = 1
    while 1 << distance < narrow_count:
        other = swapped(total.astype(jnp.bfloat16), "narrow", distance)
        total = total + other.astype(jnp.float32)
        distance += 1
    mine = stored(total)
    theirs = swapped(mine, "narrow", 0)
    leading = (narrow_at == 0).astype(jnp.int32).reshape(1)
    attended = attend_early(
        leading, query_states, key_states, value_states, arrived, cache_keys, cache_values, late
    )
    recalled = fast_recall(where, sources, mine, theirs, query_states)
    return (attended, recalled)


def spread_plan(
    query_states,
    key_states,
    value_states,
    cache_keys,
    cache_values,
    gate_fast,
    lift_fast,
    down_fast,
    token_rates,
):
    features, tok_count = query_states.shape
    edge_cols = jnp.stack(
        [key_states[:, tok_count - WINDOW :], value_states[:, tok_count - WINDOW :]]
    )
    arrived = from_behind(edge_cols, "narrow", 1)
    leading = lax.axis_index("narrow") == 0
    prior_cols = jnp.where(leading, jnp.stack([cache_keys, cache_values]), arrived)
    ext_keys = jnp.concatenate([prior_cols[0], key_states], axis=1)
    ext_values = jnp.concatenate([prior_cols[1], value_states], axis=1)
    if features % HEAD_SIZE == 0:
        attended = attend_local(query_states, ext_keys, ext_values, 0)
    else:
        attended = attend_paired(query_states, ext_keys, ext_values)
    query_fast, key_fast, value_fast = (
        lax.all_to_all(
            lax.all_to_all(query_states, "wide", split_axis=1, concat_axis=0, tiled=True),
            "narrow",
            split_axis=0,
            concat_axis=1,
            tiled=True,
        ),
        lax.all_to_all(
            lax.all_to_all(key_states, "wide", split_axis=1, concat_axis=0, tiled=True),
            "narrow",
            split_axis=0,
            concat_axis=1,
            tiled=True,
        ),
        lax.all_to_all(
            lax.all_to_all(value_states, "wide", split_axis=1, concat_axis=0, tiled=True),
            "narrow",
            split_axis=0,
            concat_axis=1,
            tiled=True,
        ),
    )
    head_count = gate_fast.shape[0]
    wide_count = lax.axis_size("wide")
    narrow_count = lax.axis_size("narrow")
    piece_rows = tok_count // wide_count
    fast_tokens = query_fast.shape[1]
    rate_blocks = token_rates.reshape(token_rates.shape[0], narrow_count, wide_count, piece_rows)
    rates_here = lax.dynamic_slice(
        rate_blocks,
        (lax.axis_index("narrow") * head_count, 0, lax.axis_index("wide"), 0),
        (head_count, narrow_count, 1, piece_rows),
    ).reshape(head_count, fast_tokens)
    query_heads = query_fast.reshape(head_count, FD, fast_tokens)
    key_heads = key_fast.reshape(head_count, FD, fast_tokens)
    value_heads = value_fast.reshape(head_count, FD, fast_tokens)
    recall = fast_group(
        gate_fast, lift_fast, down_fast, query_heads, key_heads, value_heads, rates_here
    )
    recall = recall.reshape(head_count * FD, fast_tokens)
    recalled = lax.all_to_all(
        lax.all_to_all(recall, "narrow", split_axis=1, concat_axis=0, tiled=True),
        "wide",
        split_axis=0,
        concat_axis=1,
        tiled=True,
    )
    return (attended, recalled)


def per_device(*arrays):
    if in_place(*arrays):
        return in_place_plan(*arrays)
    return spread_plan(*arrays)


def solution(mesh):
    in_specs = (
        P("wide", "narrow"),
        P("wide", "narrow"),
        P("wide", "narrow"),
        P("wide", None),
        P("wide", None),
        P("narrow", None, None),
        P("narrow", None, None),
        P("narrow", None, None),
        P(),
    )
    out_specs = (P("wide", "narrow"), P("wide", "narrow"))
    return jax.shard_map(
        per_device, mesh=mesh, in_specs=in_specs, out_specs=out_specs, check_vma=False
    )
```

```python
import functools
import math

import jax
import jax.numpy as jnp
from jax import lax
from jax.experimental import pallas as pl
from jax.experimental.pallas import tpu as pltpu
from jax.sharding import PartitionSpec as P


FD = 512
HEAD_SIZE = 128
WINDOW = 1024
NS_ITERS = 2


EPS = 1e-06
COEF_A = 3.4445
COEF_B = -4.775
COEF_C = 2.0315
LOG2E = math.log2(math.e)


def swapped(array, axis, distance):
    return lax.ppermute(array, axis, [(i, i ^ 1 << distance) for i in range(lax.axis_size(axis))])


def shortened(array):

    def short(part):
        return part.astype(jnp.bfloat16) if part.dtype == jnp.float32 else part

    return jax.tree.map(short, array)


def from_behind(value, axis, steps):
    count = lax.axis_size(axis)
    initial, last = (max(0, -steps), min(count, count - steps))
    return lax.ppermute(value, axis, [(source, source + steps) for source in range(initial, last)])


def stored(value):
    return lax.optimization_barrier(value.astype(jnp.bfloat16))


def attend_local(query_states, ext_keys, ext_values, key_start):
    features, tok_count = query_states.shape
    head_count = features // HEAD_SIZE
    block_rows = min(512, tok_count)
    block_count = tok_count // block_rows
    key_span = WINDOW + block_rows
    scaling = 1.0 / math.sqrt(HEAD_SIZE)
    rows_at = lax.broadcasted_iota(jnp.int32, (block_rows, key_span), 0)
    cols_at = lax.broadcasted_iota(jnp.int32, (block_rows, key_span), 1)
    visible = (cols_at > rows_at) & (cols_at <= rows_at + WINDOW)

    def one_block(block_index):
        offset = block_index * block_rows
        query_part = lax.dynamic_slice_in_dim(query_states, offset, block_rows, 1).reshape(
            head_count, HEAD_SIZE, block_rows
        )
        key_part = lax.dynamic_slice_in_dim(ext_keys, key_start + offset, key_span, 1).reshape(
            head_count, HEAD_SIZE, key_span
        )
        value_part = lax.dynamic_slice_in_dim(ext_values, key_start + offset, key_span, 1).reshape(
            head_count, HEAD_SIZE, key_span
        )
        scores = (
            jnp.einsum("hdq,hdk->hqk", query_part, key_part, preferred_element_type=jnp.float32)
            * scaling
        )
        scores = jnp.where(visible[None], scores, -jnp.inf)
        highest = jnp.max(scores, axis=2, keepdims=True)
        raised = jnp.exp(scores - highest)
        weights = (raised / jnp.sum(raised, axis=2, keepdims=True)).astype(jnp.bfloat16)
        blended = jnp.einsum(
            "hdk,hqk->hdq", value_part, weights, preferred_element_type=jnp.float32
        )
        return blended.astype(jnp.bfloat16).reshape(features, block_rows)

    blocks_out = lax.map(one_block, jnp.arange(block_count, dtype=jnp.int32))
    return jnp.transpose(blocks_out, (1, 0, 2)).reshape(features, tok_count)


def attend_paired(query_states, ext_keys, ext_values):
    features, tok_count = query_states.shape
    half_rows = tok_count // 2
    lower = lax.axis_index("wide") % 2 == 0
    query_send = jnp.where(lower, query_states[:, half_rows:], query_states[:, :half_rows])
    query_keep = jnp.where(lower, query_states[:, :half_rows], query_states[:, half_rows:])
    other_keys, other_values, other_queries = swapped((ext_keys, ext_values, query_send), "wide", 0)
    full_keys = jnp.where(
        lower,
        jnp.concatenate([ext_keys, other_keys], axis=0),
        jnp.concatenate([other_keys, ext_keys], axis=0),
    )
    full_values = jnp.where(
        lower,
        jnp.concatenate([ext_values, other_values], axis=0),
        jnp.concatenate([other_values, ext_values], axis=0),
    )
    full_queries = jnp.where(
        lower,
        jnp.concatenate([query_keep, other_queries], axis=0),
        jnp.concatenate([other_queries, query_keep], axis=0),
    )
    key_start = jnp.where(lower, 0, half_rows).astype(jnp.int32)
    head_out = attend_local(full_queries, full_keys, full_values, key_start)
    out_keep = jnp.where(lower, head_out[:features], head_out[features:])
    out_send = jnp.where(lower, head_out[features:], head_out[:features])
    out_other = swapped(shortened(out_send), "wide", 0).astype(out_send.dtype)
    return jnp.where(
        lower,
        jnp.concatenate([out_keep, out_other], axis=1),
        jnp.concatenate([out_other, out_keep], axis=1),
    )


def fast_terms(gate_weight, lift_weight, down_weight, key_heads, value_heads, rates_here):
    pre_gate = jnp.einsum(
        "hcf,hft->hct", gate_weight, key_heads, preferred_element_type=jnp.float32
    )
    pre_lift = jnp.einsum(
        "hcf,hft->hct", lift_weight, key_heads, preferred_element_type=jnp.float32
    )
    sigmoid_gate = jax.nn.sigmoid(pre_gate)
    silu_gate = pre_gate * sigmoid_gate
    hidden = (silu_gate * pre_lift).astype(jnp.bfloat16)
    target = (-(value_heads.astype(jnp.float32) * rates_here[:, None, :])).astype(jnp.bfloat16)
    grad_down = jnp.einsum("hft,hct->hfc", target, hidden, preferred_element_type=jnp.float32)
    back_hidden = jnp.einsum(
        "hfc,hft->hct", down_weight, target, preferred_element_type=jnp.float32
    )
    back_lift = (back_hidden * silu_gate).astype(jnp.bfloat16)
    back_gate = (
        back_hidden * pre_lift * sigmoid_gate * (1.0 + pre_gate * (1.0 - sigmoid_gate))
    ).astype(jnp.bfloat16)
    grad_gate = jnp.einsum("hct,hft->hcf", back_gate, key_heads, preferred_element_type=jnp.float32)
    grad_lift = jnp.einsum("hct,hft->hcf", back_lift, key_heads, preferred_element_type=jnp.float32)
    return (grad_gate, grad_lift, grad_down)


def scaled_start(rounded):
    widened = rounded.astype(jnp.float32)
    norm_val = jnp.sqrt(jnp.sum(jnp.square(widened), axis=(1, 2), keepdims=True) + EPS)
    return stored(widened / norm_val)


def starting(grad_gate, grad_lift, grad_down):
    sum_gate, sum_lift, sum_down = lax.psum((grad_gate, grad_lift, grad_down), "wide")
    return (
        scaled_start(stored(sum_gate)),
        scaled_start(stored(sum_lift)),
        scaled_start(stored(sum_down)),
    )


def orthogonal(current):
    for _ in range(NS_ITERS):
        gram_mat = jnp.einsum(
            "hrc,hrd->hcd", current, current, preferred_element_type=jnp.float32
        ).astype(jnp.bfloat16)
        lifted = stored(
            jnp.einsum("hrc,hcd->hrd", current, gram_mat, preferred_element_type=jnp.float32)
        )
        current = stored(
            COEF_A * current.astype(jnp.float32)
            + COEF_B * lifted.astype(jnp.float32)
            + COEF_C
            * jnp.einsum("hrc,hcd->hrd", lifted, gram_mat, preferred_element_type=jnp.float32)
        )
    return current


def refreshed(weight, ortho):
    initial = weight.astype(jnp.float32)
    moved_rows = initial - ortho.astype(jnp.float32)
    wanted = jnp.sqrt(jnp.mean(jnp.square(initial), axis=-1, keepdims=True) + EPS)
    present = jnp.sqrt(jnp.mean(jnp.square(moved_rows), axis=-1, keepdims=True) + EPS)
    return (moved_rows * (wanted / present)).astype(jnp.bfloat16)


def fast_group(
    gate_weight, lift_weight, down_weight, query_heads, key_heads, value_heads, rates_here
):
    grad_gate, grad_lift, grad_down = fast_terms(
        gate_weight, lift_weight, down_weight, key_heads, value_heads, rates_here
    )
    start_gate, start_lift, start_down = starting(grad_gate, grad_lift, grad_down)
    fresh_gate = refreshed(gate_weight, orthogonal(start_gate))
    fresh_lift = refreshed(lift_weight, orthogonal(start_lift))
    fresh_down = refreshed(down_weight, orthogonal(start_down))
    query_gate = jnp.einsum(
        "hcf,hft->hct", fresh_gate, query_heads, preferred_element_type=jnp.float32
    )
    query_lift = jnp.einsum(
        "hcf,hft->hct", fresh_lift, query_heads, preferred_element_type=jnp.float32
    )
    query_hidden = (jax.nn.silu(query_gate) * query_lift).astype(jnp.bfloat16)
    return jnp.einsum(
        "hfc,hct->hft", fresh_down, query_hidden, preferred_element_type=jnp.float32
    ).astype(jnp.bfloat16)


def attend_body(flag_ref, q_ref, kp_ref, vp_ref, kc_ref, vc_ref, *rest, block, has_cache, hd, window):
    if has_cache:
        ck_ref, cv_ref, _, o_ref, kt_ref, v_ref = rest
    else:
        o_ref, kt_ref, v_ref = rest
    scale = LOG2E / math.sqrt(hd)

    def place(k, v):
        kt = k[...].T
        kt_ref[:window, :hd] = kt
        kt_ref[:window, hd:] = kt
        v_ref[:hd, :window] = v[...]

    if has_cache:
        @pl.when(flag_ref[0] == 1)
        def _(): place(ck_ref, cv_ref)

        @pl.when(flag_ref[0] != 1)
        def _(): place(kp_ref, vp_ref)
    else:
        place(kp_ref, vp_ref)
    kt = kc_ref[...].T
    kt_ref[window:, :hd] = kt
    kt_ref[window:, hd:] = kt
    v_ref[:hd, window:] = vc_ref[...]
    v_ref[hd:, :] = jnp.ones((v_ref.shape[0]-hd, 2*window), jnp.bfloat16)
    rows = lax.broadcasted_iota(jnp.int32, (block, block), 0)
    cols = lax.broadcasted_iota(jnp.int32, (block, block), 1)
    first = rows > cols
    inner = window // block
    for b in range(window // block):
        q = q_ref[:, b*block:(b+1)*block].astype(jnp.float32) * scale
        hi = q.astype(jnp.bfloat16)
        lo = (q - hi.astype(jnp.float32)).astype(jnp.bfloat16)
        q2 = jnp.concatenate([hi, lo], axis=0)
        s = []
        for j in range(inner + 1):
            lo_row = (b + j) * block
            s.append(jnp.dot(kt_ref[lo_row:lo_row+block, :], q2, preferred_element_type=jnp.float32))
        s[0] = jnp.where(first, s[0], s[inner])
        top = s[0]
        for j in range(1, inner): top = jnp.maximum(top, s[j])
        top = jnp.max(top, axis=0, keepdims=True)
        p = [jnp.exp2(s[j] - top).astype(jnp.bfloat16) for j in range(inner)]
        zero = jnp.zeros_like(p[0])
        parts = [jnp.where(first, p[0], zero)] + p[1:] + [jnp.where(first, zero, p[0])]
        w = jnp.concatenate(parts, axis=0)
        o = jnp.dot(v_ref[:, b*block:(b+inner+1)*block], w, preferred_element_type=jnp.float32)
        o_ref[:, b*block:(b+1)*block] = (o[:hd] * (1.0 / o[hd:hd+1])).astype(jnp.bfloat16)


def attend_late(q, k, v, block=256):
    f, T = q.shape
    hd, W = HEAD_SIZE, WINDOW
    heads, chunks = f//hd, T//W - 1
    cur = pl.BlockSpec((hd, W), lambda h, c: (h, c+1))
    prev = pl.BlockSpec((hd, W), lambda h, c: (h, c))
    return pl.pallas_call(
        functools.partial(attend_body, block=block, has_cache=False, hd=hd, window=W),
        out_shape=jax.ShapeDtypeStruct((f, T), jnp.bfloat16),
        grid=(heads, chunks),
        in_specs=[pl.BlockSpec(memory_space=pltpu.SMEM), cur, prev, prev, cur, cur],
        out_specs=cur,
        scratch_shapes=[pltpu.VMEM((2*W, 2*hd), jnp.bfloat16), pltpu.VMEM((hd+16, 2*W), jnp.bfloat16)],
        cost_estimate=pl.CostEstimate(flops=heads*chunks*W*W*hd*5, bytes_accessed=5*f*W*2, transcendentals=heads*chunks*W*W),
        name="attend_late",
    )(jnp.zeros((1,), jnp.int32), q, k, v, k, v)


def attend_early(flag, q, k, v, prior, ck, cv, out, block=256):
    f, T = q.shape
    hd, W = HEAD_SIZE, WINDOW
    heads = f//hd
    cur = pl.BlockSpec((hd, W), lambda h: (h, 0))
    prior_k = pl.BlockSpec((None, hd, W), lambda h: (0, h, 0))
    prior_v = pl.BlockSpec((None, hd, W), lambda h: (1, h, 0))
    return pl.pallas_call(
        functools.partial(attend_body, block=block, has_cache=True, hd=hd, window=W),
        out_shape=jax.ShapeDtypeStruct((f, T), jnp.bfloat16),
        grid=(heads,),
        in_specs=[pl.BlockSpec(memory_space=pltpu.SMEM), cur, prior_k, prior_v, cur, cur, cur, cur, pl.BlockSpec(memory_space=pl.ANY)],
        out_specs=cur,
        scratch_shapes=[pltpu.VMEM((2*W, 2*hd), jnp.bfloat16), pltpu.VMEM((hd+16, 2*W), jnp.bfloat16)],
        input_output_aliases={8: 0},
        cost_estimate=pl.CostEstimate(flops=heads*W*W*hd*5, bytes_accessed=7*f*W*2, transcendentals=heads*W*W),
        name="attend_early",
    )(flag, q, prior, prior, k, v, ck, cv, out)


def in_hbm(array):
    return pltpu.with_memory_space_constraint(array, pltpu.HBM)


def prepare_body(where_ref, gate_ref, lift_ref, down_ref, own_ref, other_ref, w_ref, sem):
    local = where_ref[4]
    copies = [
        pltpu.make_async_copy(source.at[local], w_ref.at[place], sem.at[place])
        for place, source in enumerate((down_ref, gate_ref, lift_ref))
    ]
    for copy in copies:
        copy.start()
    half = own_ref.shape[1]
    side = where_ref[1]
    copies[0].wait()
    w_ref[0] = w_ref[0].T
    copies[1].wait()
    copies[2].wait()
    for out_ref, part in ((own_ref, side), (other_ref, 1 - side)):
        rows = pl.ds(pl.multiple_of(part * half, half), half)
        out_ref[0] = w_ref[1, rows, :]
        out_ref[1] = w_ref[2, rows, :]
        out_ref[2] = w_ref[0, rows, :]


def prepare(where, gate_fast, lift_fast, down_fast):
    _, hidden_rows, features = gate_fast.shape
    shape = (3, hidden_rows // 2, features)
    return pl.pallas_call(
        prepare_body,
        out_shape=(jax.ShapeDtypeStruct(shape, jnp.bfloat16),) * 2,
        in_specs=[pl.BlockSpec(memory_space=pltpu.SMEM)] + [pl.BlockSpec(memory_space=pl.ANY)] * 3,
        out_specs=(pl.BlockSpec(memory_space=pltpu.VMEM),) * 2,
        scratch_shapes=[
            pltpu.VMEM((3, hidden_rows, features), jnp.bfloat16),
            pltpu.SemaphoreType.DMA((3,)),
        ],
        cost_estimate=pl.CostEstimate(
            flops=0, bytes_accessed=12 * hidden_rows * features, transcendentals=0
        ),
        name="prepare",
    )(where, gate_fast, lift_fast, down_fast)


def edges_body(key_ref, value_ref, out_ref):
    out_ref[0] = key_ref[...]
    out_ref[1] = value_ref[...]


def edges(keys, values):
    features, tokens = keys.shape
    last = tokens // WINDOW - 1
    rows = HEAD_SIZE
    piece = pl.BlockSpec((rows, WINDOW), lambda i: (i, last))
    return pl.pallas_call(
        edges_body,
        out_shape=jax.ShapeDtypeStruct((2, features, WINDOW), jnp.bfloat16),
        grid=(features // rows,),
        in_specs=[piece, piece],
        out_specs=pl.BlockSpec((2, rows, WINDOW), lambda i: (0, i, 0)),
        cost_estimate=pl.CostEstimate(
            flops=0, bytes_accessed=8 * features * WINDOW, transcendentals=0
        ),
        name="edges",
    )(keys, values)


def sums_body(where_ref, *refs):
    sources = refs[:-15]
    (
        key_ref, value_ref, pair_key_ref, pair_value_ref, rate_ref,
        keep_ref, send_ref, pack_ref,
        keys_ref, values_ref, hidden_ref, target_ref, back_ref, sem, sem_in,
    ) = refs[-15:]
    features, tokens = key_ref.shape
    half = pack_ref.shape[1]
    block = min(512, tokens)
    count = tokens // block

    def moved(keys, values, index, slot):
        source = pl.ds(pl.multiple_of(index * block, block), block)
        target = pl.ds(pl.multiple_of(slot * block, block), block)
        return (
            pltpu.make_async_copy(keys.at[:, source], keys_ref.at[:, target], sem_in.at[0, slot]),
            pltpu.make_async_copy(
                values.at[:, source], values_ref.at[:, target], sem_in.at[1, slot]
            ),
        )

    for index in range(count):
        for copy in moved(key_ref, value_ref, index, index):
            copy.start()
    for place, source in enumerate(sources):

        @pl.when(where_ref[0] == place)
        def _(source=source):
            pltpu.make_async_copy(source, pack_ref, sem).start()

    for index in range(count):
        for copy in moved(pair_key_ref, pair_value_ref, index, count + index):
            copy.start()
    pltpu.make_async_copy(sources[0], pack_ref, sem).wait()
    gate_lift = pack_ref[0:2].reshape(2 * half, features)
    row = where_ref[2]

    def step(slot, carry):
        for copy in moved(key_ref, value_ref, 0, slot):
            copy.wait()
        at = pl.ds(pl.multiple_of(slot * block, block), block)
        mirrored = where_ref[3] ^ (slot // count)
        rate_at = pl.ds(pl.multiple_of(mirrored * tokens + (slot % count) * block, block), block)
        keys = keys_ref[:, at]
        pre = jnp.dot(gate_lift, keys, preferred_element_type=jnp.float32)
        pre_gate = pre[:half]
        pre_lift = pre[half:]
        rates = rate_ref[pl.ds(row, 1), rate_at]
        target = (-(values_ref[:, at].astype(jnp.float32) * rates)).astype(jnp.bfloat16)
        back_hidden = jnp.dot(pack_ref[2], target, preferred_element_type=jnp.float32)
        sigmoid_gate = 0.5 * jnp.tanh(0.5 * pre_gate) + 0.5
        silu_gate = pre_gate * sigmoid_gate
        hidden_ref[:, at] = (silu_gate * pre_lift).astype(jnp.bfloat16)
        target_ref[:, at] = target
        slope = sigmoid_gate + silu_gate * (1.0 - sigmoid_gate)
        back_ref[:half, at] = (back_hidden * pre_lift * slope).astype(jnp.bfloat16)
        back_ref[half:, at] = (back_hidden * silu_gate).astype(jnp.bfloat16)
        return carry

    lax.fori_loop(0, 2 * count, step, 0, unroll=2)
    contract = (((1,), (1,)), ((), ()))
    sums = lax.dot_general(
        back_ref[...], keys_ref[...], contract, preferred_element_type=jnp.float32
    )
    down = lax.dot_general(
        hidden_ref[...], target_ref[...], contract, preferred_element_type=jnp.float32
    )
    for place, value in enumerate((sums[:half], sums[half:], down)):
        keep_ref[place] = value
        send_ref[place] = value.astype(jnp.bfloat16)


def fast_sums(where, sources, keys, values, pair_keys, pair_values, rates):
    features, tokens = keys.shape
    shape = sources[0].shape
    half = shape[1]
    block = min(512, tokens)
    anywhere = pl.BlockSpec(memory_space=pl.ANY)
    resident = pl.BlockSpec(memory_space=pltpu.VMEM)
    return pl.pallas_call(
        sums_body,
        out_shape=(
            jax.ShapeDtypeStruct(shape, jnp.float32),
            jax.ShapeDtypeStruct(shape, jnp.bfloat16),
            jax.ShapeDtypeStruct(shape, jnp.bfloat16),
        ),
        in_specs=[pl.BlockSpec(memory_space=pltpu.SMEM)]
        + [anywhere] * (len(sources) + 4)
        + [resident],
        out_specs=(resident,) * 3,
        scratch_shapes=[
            pltpu.VMEM((features, 2 * tokens), jnp.bfloat16),
            pltpu.VMEM((features, 2 * tokens), jnp.bfloat16),
            pltpu.VMEM((half, 2 * tokens), jnp.bfloat16),
            pltpu.VMEM((features, 2 * tokens), jnp.bfloat16),
            pltpu.VMEM((2 * half, 2 * tokens), jnp.bfloat16),
            pltpu.SemaphoreType.DMA(()),
            pltpu.SemaphoreType.DMA((2, 2 * tokens // block)),
        ],
        cost_estimate=pl.CostEstimate(
            flops=24 * half * features * tokens,
            bytes_accessed=8 * features * tokens + 8 * 3 * half * features,
            transcendentals=2 * half * tokens,
        ),
        name="fast_sums",
    )(where, *sources, keys, values, pair_keys, pair_values, rates)


def recall_body(where_ref, mine_ref, other_ref, pack_ref, pair_pack_ref, query_ref, out_ref, w_ref, fresh_ref):
    half = mine_ref.shape[1]

    @pl.when(pl.program_id(0) == 0)
    def _():
        side = where_ref[1]
        rows_mine = pl.ds(pl.multiple_of(side * half, half), half)
        rows_other = pl.ds(pl.multiple_of((1 - side) * half, half), half)
        fresh_ref[:, rows_mine, :] = mine_ref[...]
        fresh_ref[:, rows_other, :] = other_ref[...]
        w_ref[:, rows_mine, :] = pack_ref[...]
        w_ref[:, rows_other, :] = pair_pack_ref[...]
        current = []
        for i in range(3):
            rounded = fresh_ref[i].T if i == 2 else fresh_ref[i]
            widened = rounded.astype(jnp.float32)
            total = jnp.sum(jnp.sum(widened * widened, axis=0, keepdims=True), axis=1, keepdims=True)
            current.append((widened / jnp.sqrt(total + EPS)).astype(jnp.bfloat16))
        for _ in range(NS_ITERS):
            gram = [
                lax.dot_general(
                    x, x, (((0,), (0,)), ((), ())), preferred_element_type=jnp.float32
                ).astype(jnp.bfloat16)
                for x in current
            ]
            lifted = [
                jnp.dot(x, g, preferred_element_type=jnp.float32).astype(jnp.bfloat16)
                for x, g in zip(current, gram)
            ]
            current = [
                (
                    COEF_A * x.astype(jnp.float32)
                    + COEF_B * y.astype(jnp.float32)
                    + COEF_C * jnp.dot(y, g, preferred_element_type=jnp.float32)
                ).astype(jnp.bfloat16)
                for x, y, g in zip(current, lifted, gram)
            ]
        for i in range(3):
            weight = w_ref[i].T if i == 2 else w_ref[i]
            initial = weight.astype(jnp.float32)
            moved = initial - current[i].astype(jnp.float32)
            wanted = jnp.mean(jnp.square(initial), axis=-1, keepdims=True) + EPS
            present = jnp.mean(jnp.square(moved), axis=-1, keepdims=True) + EPS
            fresh_ref[i] = (moved * (jnp.sqrt(wanted) / jnp.sqrt(present))).astype(jnp.bfloat16)

    hidden_rows, features = fresh_ref.shape[1:]
    pre = jnp.dot(
        fresh_ref[0:2].reshape(2 * hidden_rows, features),
        query_ref[...],
        preferred_element_type=jnp.float32,
    )
    gate = pre[:hidden_rows]
    hidden = (gate * (0.5 * jnp.tanh(0.5 * gate) + 0.5) * pre[hidden_rows:]).astype(jnp.bfloat16)
    out_ref[...] = jnp.dot(fresh_ref[2], hidden, preferred_element_type=jnp.float32).astype(
        jnp.bfloat16
    )


def fast_recall(where, mine, other, pack, pair_pack, queries):
    features, tokens = queries.shape
    half = mine.shape[1]
    hidden_rows = 2 * half
    block = min(512, tokens)
    parts = pl.BlockSpec((3, half, features), lambda i: (0, 0, 0))
    piece = pl.BlockSpec((features, block), lambda i: (0, i))
    return pl.pallas_call(
        recall_body,
        out_shape=jax.ShapeDtypeStruct((features, tokens), jnp.bfloat16),
        grid=(tokens // block,),
        in_specs=[pl.BlockSpec(memory_space=pltpu.SMEM)] + [parts] * 4 + [piece],
        out_specs=piece,
        scratch_shapes=[
            pltpu.VMEM((3, hidden_rows, features), jnp.bfloat16),
            pltpu.VMEM((3, hidden_rows, features), jnp.bfloat16),
        ],
        cost_estimate=pl.CostEstimate(
            flops=6 * hidden_rows * features * tokens + 18 * NS_ITERS * hidden_rows * features**2,
            bytes_accessed=4 * features * tokens + 12 * hidden_rows * features,
            transcendentals=hidden_rows * tokens,
        ),
        name="fast_recall",
    )(where, mine, other, pack, pair_pack, queries)


def in_place(query_states, key_states, value_states, cache_keys, cache_values, gate_fast, *rest):
    features, tok_count = query_states.shape
    narrow_count = lax.axis_size("narrow")
    return (
        features == FD
        and gate_fast.shape[1:] == (FD, FD)
        and features % HEAD_SIZE == 0
        and tok_count % WINDOW == 0
        and tok_count >= 2 * WINDOW
        and narrow_count >= 2
        and narrow_count & (narrow_count - 1) == 0
    )


def in_place_plan(
    query_states,
    key_states,
    value_states,
    cache_keys,
    cache_values,
    gate_fast,
    lift_fast,
    down_fast,
    token_rates,
):
    wide_count = lax.axis_size("wide")
    narrow_count = lax.axis_size("narrow")
    owned = gate_fast.shape[0]
    wide_at = lax.axis_index("wide")
    narrow_at = lax.axis_index("narrow")
    role = narrow_at ^ (wide_at // owned)
    where = jnp.stack([role, narrow_at % 2, wide_at, narrow_at, wide_at % owned]).astype(jnp.int32)

    def from_owner(value, step):
        pairs = []
        for wide in range(wide_count):
            start = wide * narrow_count
            owner = wide // owned
            pairs.append((start + owner, start + (owner ^ step)))
        return lax.ppermute(value, ("wide", "narrow"), pairs)

    own, other = prepare(where, gate_fast, lift_fast, down_fast)
    arrivals = {}
    for step in reversed(range(1, narrow_count)):
        arrivals[step] = from_owner((own, other)[step % 2], step)
    pair_keys = swapped(key_states, "narrow", 0)
    pair_values = swapped(value_states, "narrow", 0)
    prior = from_behind(edges(key_states, value_states), "narrow", 1)
    late = attend_late(query_states, key_states, value_states)
    sources = [own] + [arrivals[step] for step in range(1, narrow_count)]
    sources, late = lax.optimization_barrier((sources, late))
    keep, send, pack = fast_sums(
        where, sources, key_states, value_states, pair_keys, pair_values, token_rates
    )
    pair_pack = swapped(pack, "narrow", 0)
    total = keep
    rounded = send
    for distance in range(1, narrow_count.bit_length() - 1):
        if distance > 1:
            rounded = total.astype(jnp.bfloat16)
        partner = swapped(rounded, "narrow", distance)
        total = total + partner.astype(jnp.float32)
    mine = stored(total)
    theirs = swapped(mine, "narrow", 0)
    leading = (narrow_at == 0).astype(jnp.int32).reshape(1)
    attended = attend_early(
        leading, query_states, key_states, value_states, in_hbm(prior), cache_keys, cache_values, late
    )
    recalled = fast_recall(where, mine, theirs, pack, pair_pack, query_states)
    return (attended, recalled)


def spread_plan(
    query_states,
    key_states,
    value_states,
    cache_keys,
    cache_values,
    gate_fast,
    lift_fast,
    down_fast,
    token_rates,
):
    features, tok_count = query_states.shape
    edge_cols = jnp.stack(
        [key_states[:, tok_count - WINDOW :], value_states[:, tok_count - WINDOW :]]
    )
    arrived = from_behind(edge_cols, "narrow", 1)
    leading = lax.axis_index("narrow") == 0
    prior_cols = jnp.where(leading, jnp.stack([cache_keys, cache_values]), arrived)
    ext_keys = jnp.concatenate([prior_cols[0], key_states], axis=1)
    ext_values = jnp.concatenate([prior_cols[1], value_states], axis=1)
    if features % HEAD_SIZE == 0:
        attended = attend_local(query_states, ext_keys, ext_values, 0)
    else:
        attended = attend_paired(query_states, ext_keys, ext_values)
    query_fast, key_fast, value_fast = (
        lax.all_to_all(
            lax.all_to_all(query_states, "wide", split_axis=1, concat_axis=0, tiled=True),
            "narrow",
            split_axis=0,
            concat_axis=1,
            tiled=True,
        ),
        lax.all_to_all(
            lax.all_to_all(key_states, "wide", split_axis=1, concat_axis=0, tiled=True),
            "narrow",
            split_axis=0,
            concat_axis=1,
            tiled=True,
        ),
        lax.all_to_all(
            lax.all_to_all(value_states, "wide", split_axis=1, concat_axis=0, tiled=True),
            "narrow",
            split_axis=0,
            concat_axis=1,
            tiled=True,
        ),
    )
    head_count = gate_fast.shape[0]
    wide_count = lax.axis_size("wide")
    narrow_count = lax.axis_size("narrow")
    piece_rows = tok_count // wide_count
    fast_tokens = query_fast.shape[1]
    rate_blocks = token_rates.reshape(token_rates.shape[0], narrow_count, wide_count, piece_rows)
    rates_here = lax.dynamic_slice(
        rate_blocks,
        (lax.axis_index("narrow") * head_count, 0, lax.axis_index("wide"), 0),
        (head_count, narrow_count, 1, piece_rows),
    ).reshape(head_count, fast_tokens)
    query_heads = query_fast.reshape(head_count, FD, fast_tokens)
    key_heads = key_fast.reshape(head_count, FD, fast_tokens)
    value_heads = value_fast.reshape(head_count, FD, fast_tokens)
    recall = fast_group(
        gate_fast, lift_fast, down_fast, query_heads, key_heads, value_heads, rates_here
    )
    recall = recall.reshape(head_count * FD, fast_tokens)
    recalled = lax.all_to_all(
        lax.all_to_all(recall, "narrow", split_axis=1, concat_axis=0, tiled=True),
        "wide",
        split_axis=0,
        concat_axis=1,
        tiled=True,
    )
    return (attended, recalled)


def per_device(*arrays):
    if in_place(*arrays):
        return in_place_plan(*arrays)
    return spread_plan(*arrays)


def solution(mesh):
    in_specs = (
        P("wide", "narrow"),
        P("wide", "narrow"),
        P("wide", "narrow"),
        P("wide", None),
        P("wide", None),
        P("narrow", None, None),
        P("narrow", None, None),
        P("narrow", None, None),
        P(),
    )
    out_specs = (P("wide", "narrow"), P("wide", "narrow"))
    return jax.shard_map(
        per_device, mesh=mesh, in_specs=in_specs, out_specs=out_specs, check_vma=False
    )
```

```python
import functools
import math

import jax
import jax.numpy as jnp
from jax import lax
from jax.experimental import pallas as pl
from jax.experimental.pallas import tpu as pltpu
from jax.sharding import PartitionSpec as P


FD = 512
HEAD_SIZE = 128
WINDOW = 1024
NS_ITERS = 2


EPS = 1e-06
COEF_A = 3.4445
COEF_B = -4.775
COEF_C = 2.0315
LOG2E = math.log2(math.e)
VMEM_GRANT = 67043328


def swapped(array, axis, distance):
    return lax.ppermute(array, axis, [(i, i ^ 1 << distance) for i in range(lax.axis_size(axis))])


def shortened(array):

    def short(part):
        return part.astype(jnp.bfloat16) if part.dtype == jnp.float32 else part

    return jax.tree.map(short, array)


def from_behind(value, axis, steps):
    count = lax.axis_size(axis)
    initial, last = (max(0, -steps), min(count, count - steps))
    return lax.ppermute(value, axis, [(source, source + steps) for source in range(initial, last)])


def stored(value):
    return lax.optimization_barrier(value.astype(jnp.bfloat16))


def attend_local(query_states, ext_keys, ext_values, key_start):
    features, tok_count = query_states.shape
    head_count = features // HEAD_SIZE
    block_rows = min(512, tok_count)
    block_count = tok_count // block_rows
    key_span = WINDOW + block_rows
    scaling = 1.0 / math.sqrt(HEAD_SIZE)
    rows_at = lax.broadcasted_iota(jnp.int32, (block_rows, key_span), 0)
    cols_at = lax.broadcasted_iota(jnp.int32, (block_rows, key_span), 1)
    visible = (cols_at > rows_at) & (cols_at <= rows_at + WINDOW)

    def one_block(block_index):
        offset = block_index * block_rows
        query_part = lax.dynamic_slice_in_dim(query_states, offset, block_rows, 1).reshape(
            head_count, HEAD_SIZE, block_rows
        )
        key_part = lax.dynamic_slice_in_dim(ext_keys, key_start + offset, key_span, 1).reshape(
            head_count, HEAD_SIZE, key_span
        )
        value_part = lax.dynamic_slice_in_dim(ext_values, key_start + offset, key_span, 1).reshape(
            head_count, HEAD_SIZE, key_span
        )
        scores = (
            jnp.einsum("hdq,hdk->hqk", query_part, key_part, preferred_element_type=jnp.float32)
            * scaling
        )
        scores = jnp.where(visible[None], scores, -jnp.inf)
        highest = jnp.max(scores, axis=2, keepdims=True)
        raised = jnp.exp(scores - highest)
        weights = (raised / jnp.sum(raised, axis=2, keepdims=True)).astype(jnp.bfloat16)
        blended = jnp.einsum(
            "hdk,hqk->hdq", value_part, weights, preferred_element_type=jnp.float32
        )
        return blended.astype(jnp.bfloat16).reshape(features, block_rows)

    blocks_out = lax.map(one_block, jnp.arange(block_count, dtype=jnp.int32))
    return jnp.transpose(blocks_out, (1, 0, 2)).reshape(features, tok_count)


def attend_paired(query_states, ext_keys, ext_values):
    features, tok_count = query_states.shape
    half_rows = tok_count // 2
    lower = lax.axis_index("wide") % 2 == 0
    query_send = jnp.where(lower, query_states[:, half_rows:], query_states[:, :half_rows])
    query_keep = jnp.where(lower, query_states[:, :half_rows], query_states[:, half_rows:])
    other_keys, other_values, other_queries = swapped((ext_keys, ext_values, query_send), "wide", 0)
    full_keys = jnp.where(
        lower,
        jnp.concatenate([ext_keys, other_keys], axis=0),
        jnp.concatenate([other_keys, ext_keys], axis=0),
    )
    full_values = jnp.where(
        lower,
        jnp.concatenate([ext_values, other_values], axis=0),
        jnp.concatenate([other_values, ext_values], axis=0),
    )
    full_queries = jnp.where(
        lower,
        jnp.concatenate([query_keep, other_queries], axis=0),
        jnp.concatenate([other_queries, query_keep], axis=0),
    )
    key_start = jnp.where(lower, 0, half_rows).astype(jnp.int32)
    head_out = attend_local(full_queries, full_keys, full_values, key_start)
    out_keep = jnp.where(lower, head_out[:features], head_out[features:])
    out_send = jnp.where(lower, head_out[features:], head_out[:features])
    out_other = swapped(shortened(out_send), "wide", 0).astype(out_send.dtype)
    return jnp.where(
        lower,
        jnp.concatenate([out_keep, out_other], axis=1),
        jnp.concatenate([out_other, out_keep], axis=1),
    )


def fast_terms(gate_weight, lift_weight, down_weight, key_heads, value_heads, rates_here):
    pre_gate = jnp.einsum(
        "hcf,hft->hct", gate_weight, key_heads, preferred_element_type=jnp.float32
    )
    pre_lift = jnp.einsum(
        "hcf,hft->hct", lift_weight, key_heads, preferred_element_type=jnp.float32
    )
    sigmoid_gate = jax.nn.sigmoid(pre_gate)
    silu_gate = pre_gate * sigmoid_gate
    hidden = (silu_gate * pre_lift).astype(jnp.bfloat16)
    target = (-(value_heads.astype(jnp.float32) * rates_here[:, None, :])).astype(jnp.bfloat16)
    grad_down = jnp.einsum("hft,hct->hfc", target, hidden, preferred_element_type=jnp.float32)
    back_hidden = jnp.einsum(
        "hfc,hft->hct", down_weight, target, preferred_element_type=jnp.float32
    )
    back_lift = (back_hidden * silu_gate).astype(jnp.bfloat16)
    back_gate = (
        back_hidden * pre_lift * sigmoid_gate * (1.0 + pre_gate * (1.0 - sigmoid_gate))
    ).astype(jnp.bfloat16)
    grad_gate = jnp.einsum("hct,hft->hcf", back_gate, key_heads, preferred_element_type=jnp.float32)
    grad_lift = jnp.einsum("hct,hft->hcf", back_lift, key_heads, preferred_element_type=jnp.float32)
    return (grad_gate, grad_lift, grad_down)


def scaled_start(rounded):
    widened = rounded.astype(jnp.float32)
    norm_val = jnp.sqrt(jnp.sum(jnp.square(widened), axis=(1, 2), keepdims=True) + EPS)
    return stored(widened / norm_val)


def starting(grad_gate, grad_lift, grad_down):
    sum_gate, sum_lift, sum_down = lax.psum((grad_gate, grad_lift, grad_down), "wide")
    return (
        scaled_start(stored(sum_gate)),
        scaled_start(stored(sum_lift)),
        scaled_start(stored(sum_down)),
    )


def orthogonal(current):
    for _ in range(NS_ITERS):
        gram_mat = jnp.einsum(
            "hrc,hrd->hcd", current, current, preferred_element_type=jnp.float32
        ).astype(jnp.bfloat16)
        lifted = stored(
            jnp.einsum("hrc,hcd->hrd", current, gram_mat, preferred_element_type=jnp.float32)
        )
        current = stored(
            COEF_A * current.astype(jnp.float32)
            + COEF_B * lifted.astype(jnp.float32)
            + COEF_C
            * jnp.einsum("hrc,hcd->hrd", lifted, gram_mat, preferred_element_type=jnp.float32)
        )
    return current


def refreshed(weight, ortho):
    initial = weight.astype(jnp.float32)
    moved_rows = initial - ortho.astype(jnp.float32)
    wanted = jnp.sqrt(jnp.mean(jnp.square(initial), axis=-1, keepdims=True) + EPS)
    present = jnp.sqrt(jnp.mean(jnp.square(moved_rows), axis=-1, keepdims=True) + EPS)
    return (moved_rows * (wanted / present)).astype(jnp.bfloat16)


def fast_group(
    gate_weight, lift_weight, down_weight, query_heads, key_heads, value_heads, rates_here
):
    grad_gate, grad_lift, grad_down = fast_terms(
        gate_weight, lift_weight, down_weight, key_heads, value_heads, rates_here
    )
    start_gate, start_lift, start_down = starting(grad_gate, grad_lift, grad_down)
    fresh_gate = refreshed(gate_weight, orthogonal(start_gate))
    fresh_lift = refreshed(lift_weight, orthogonal(start_lift))
    fresh_down = refreshed(down_weight, orthogonal(start_down))
    query_gate = jnp.einsum(
        "hcf,hft->hct", fresh_gate, query_heads, preferred_element_type=jnp.float32
    )
    query_lift = jnp.einsum(
        "hcf,hft->hct", fresh_lift, query_heads, preferred_element_type=jnp.float32
    )
    query_hidden = (jax.nn.silu(query_gate) * query_lift).astype(jnp.bfloat16)
    return jnp.einsum(
        "hfc,hct->hft", fresh_down, query_hidden, preferred_element_type=jnp.float32
    ).astype(jnp.bfloat16)


def attend_body(q_ref, kp_ref, vp_ref, kc_ref, vc_ref, *rest, block, window):
    cached = len(rest) > 3
    o_ref, kt_ref, v_ref = rest[-3:]
    hd = q_ref.shape[0]
    scale = LOG2E / math.sqrt(hd)

    def place(k, v, at):
        turned = k[...].T
        kt_ref[at : at + window, :hd] = turned
        kt_ref[at : at + window, hd:] = turned
        v_ref[:hd, at : at + window] = v[...]

    if cached:
        leading = lax.axis_index("narrow") == 0

        @pl.when(leading)
        def _():
            place(*rest[:2], 0)

        @pl.when(jnp.logical_not(leading))
        def _():
            place(kp_ref, vp_ref, 0)

    else:
        place(kp_ref, vp_ref, 0)
    place(kc_ref, vc_ref, window)
    v_ref[hd:, :] = jnp.ones((v_ref.shape[0] - hd, 2 * window), jnp.bfloat16)
    rows = lax.broadcasted_iota(jnp.int32, (block, block), 0)
    cols = lax.broadcasted_iota(jnp.int32, (block, block), 1)
    first = rows > cols
    inner = window // block

    def scores(b):
        q = q_ref[:, b * block : (b + 1) * block].astype(jnp.float32) * scale
        high = q.astype(jnp.bfloat16)
        low = (q - high.astype(jnp.float32)).astype(jnp.bfloat16)
        pair = jnp.concatenate([high, low], axis=0)
        parts = [
            jnp.dot(
                kt_ref[(b + j) * block : (b + j + 1) * block, :],
                pair,
                preferred_element_type=jnp.float32,
            )
            for j in range(inner + 1)
        ]
        return [jnp.where(first, parts[0], parts[inner])] + parts[1:inner]

    def blend(b, parts):
        top = functools.reduce(jnp.maximum, parts)
        top = jnp.max(top, axis=0, keepdims=True)
        raised = [jnp.exp2(part - top).astype(jnp.bfloat16) for part in parts]
        zero = jnp.zeros_like(raised[0])
        ends = jnp.where(first, raised[0], zero), jnp.where(first, zero, raised[0])
        weights = jnp.concatenate([ends[0]] + raised[1:] + [ends[1]], axis=0)
        span = v_ref[:, b * block : (b + inner + 1) * block]
        out = jnp.dot(span, weights, preferred_element_type=jnp.float32)
        o_ref[:, b * block : (b + 1) * block] = (out[:hd] * (1.0 / out[hd : hd + 1])).astype(
            jnp.bfloat16
        )

    ready = scores(0)
    for b in range(1, inner):
        following = scores(b)
        blend(b - 1, ready)
        ready = following
    blend(inner - 1, ready)


def attend_scratch():
    return [
        pltpu.VMEM((2 * WINDOW, 2 * HEAD_SIZE), jnp.bfloat16),
        pltpu.VMEM((HEAD_SIZE + 16, 2 * WINDOW), jnp.bfloat16),
    ]


def attend_late(queries, keys, values):
    features, tokens = queries.shape
    heads, chunks = features // HEAD_SIZE, tokens // WINDOW - 1
    here = pl.BlockSpec((HEAD_SIZE, WINDOW), lambda h, c: (h, c + 1))
    before = pl.BlockSpec((HEAD_SIZE, WINDOW), lambda h, c: (h, c))
    return pl.pallas_call(
        functools.partial(attend_body, block=min(256, WINDOW), window=WINDOW),
        out_shape=jax.ShapeDtypeStruct((features, tokens), jnp.bfloat16),
        grid=(heads, chunks),
        in_specs=[here, before, before, here, here],
        out_specs=here,
        scratch_shapes=attend_scratch(),
        cost_estimate=pl.CostEstimate(
            flops=5 * features * chunks * WINDOW**2,
            bytes_accessed=10 * features * chunks * WINDOW,
            transcendentals=heads * chunks * WINDOW**2,
        ),
        name="attend_late",
    )(queries, keys, values, keys, values)


def attend_early(queries, keys, values, prior, cache_keys, cache_values, late):
    features, tokens = queries.shape
    heads = features // HEAD_SIZE
    here = pl.BlockSpec((HEAD_SIZE, WINDOW), lambda h: (h, 0))
    prior_keys = pl.BlockSpec((None, HEAD_SIZE, WINDOW), lambda h: (0, h, 0))
    prior_values = pl.BlockSpec((None, HEAD_SIZE, WINDOW), lambda h: (1, h, 0))
    body = functools.partial(attend_body, block=min(256, WINDOW), window=WINDOW)

    def early_body(*refs):
        body(*refs[:7], *refs[8:])

    return pl.pallas_call(
        early_body,
        out_shape=jax.ShapeDtypeStruct((features, tokens), jnp.bfloat16),
        grid=(heads,),
        in_specs=[here, prior_keys, prior_values, here, here, here, here]
        + [pl.BlockSpec(memory_space=pl.ANY)],
        out_specs=here,
        scratch_shapes=attend_scratch(),
        input_output_aliases={7: 0},
        cost_estimate=pl.CostEstimate(
            flops=5 * features * WINDOW**2,
            bytes_accessed=14 * features * WINDOW,
            transcendentals=heads * WINDOW**2,
        ),
        name="attend_early",
        compiler_params=pltpu.CompilerParams(vmem_limit_bytes=VMEM_GRANT),
    )(queries, prior, prior, keys, values, cache_keys, cache_values, late)


def anywhere(count):
    return [pl.BlockSpec(memory_space=pl.ANY)] * count


def half_rows(part, half):
    return pl.ds(pl.multiple_of(part * half, half), half)


def prepare_body(gate_ref, lift_ref, down_ref, own_ref, other_ref, w_ref, out_ref, sem):
    owned = gate_ref.shape[0]
    local = lax.axis_index("wide") % owned
    side = lax.axis_index("narrow") % 2
    half = own_ref.shape[1]
    copies = [
        pltpu.make_async_copy(source.at[local], w_ref.at[place], sem.at[0, place])
        for place, source in enumerate((down_ref, gate_ref, lift_ref))
    ]
    for copy in copies:
        copy.start()
    leaving = []
    copies[0].wait()
    out_ref[...] = w_ref[0].T
    for order, (place, source) in enumerate(((2, out_ref), (0, w_ref.at[1]), (1, w_ref.at[2]))):
        if order:
            copies[order].wait()
        for turn, (target, part) in enumerate(((own_ref, side), (other_ref, 1 - side))):
            leaving.append(
                pltpu.make_async_copy(
                    source.at[half_rows(part, half)], target.at[place], sem.at[1 + turn, place]
                )
            )
            leaving[-1].start()
    for copy in leaving:
        copy.wait()


def prepare(gate_fast, lift_fast, down_fast):
    _, hidden_rows, features = gate_fast.shape
    shape = (3, hidden_rows // 2, features)
    return pl.pallas_call(
        prepare_body,
        out_shape=(jax.ShapeDtypeStruct(shape, jnp.bfloat16),) * 2,
        in_specs=anywhere(3),
        out_specs=tuple(anywhere(2)),
        scratch_shapes=[
            pltpu.VMEM((3, hidden_rows, features), jnp.bfloat16),
            pltpu.VMEM((hidden_rows, features), jnp.bfloat16),
            pltpu.SemaphoreType.DMA((3, 3)),
        ],
        cost_estimate=pl.CostEstimate(
            flops=0, bytes_accessed=12 * hidden_rows * features, transcendentals=0
        ),
        name="prepare",
    )(gate_fast, lift_fast, down_fast)


def edges_body(key_ref, value_ref, out_ref, held_ref, sem):
    features, tokens = key_ref.shape
    rows = min(HEAD_SIZE, features)
    window = out_ref.shape[2]
    moves = []
    for place, source in enumerate((key_ref, value_ref)):
        for part in range(features // rows):
            at = slice(part * rows, (part + 1) * rows)
            arriving = pltpu.make_async_copy(
                source.at[at, tokens - window :], held_ref.at[place, at], sem.at[0, place, part]
            )
            leaving = pltpu.make_async_copy(
                held_ref.at[place, at], out_ref.at[place, at], sem.at[1, place, part]
            )
            arriving.start()
            moves.append((arriving, leaving))
    for arriving, leaving in moves:
        arriving.wait()
        leaving.start()
    for _, leaving in moves:
        leaving.wait()


def edges(keys, values):
    features = keys.shape[0]
    shape = (2, features, WINDOW)
    return pl.pallas_call(
        edges_body,
        out_shape=jax.ShapeDtypeStruct(shape, jnp.bfloat16),
        in_specs=anywhere(2),
        out_specs=pl.BlockSpec(memory_space=pl.ANY),
        scratch_shapes=[
            pltpu.VMEM(shape, jnp.bfloat16),
            pltpu.SemaphoreType.DMA((2, 2, features // min(HEAD_SIZE, features))),
        ],
        cost_estimate=pl.CostEstimate(
            flops=0, bytes_accessed=8 * features * WINDOW, transcendentals=0
        ),
        name="edges",
    )(keys, values)


def sums_body(*refs, owned):
    sources = refs[:-14]
    (
        key_ref, value_ref, pair_key_ref, pair_value_ref, rate_ref,
        send_ref, pack_ref,
        keys_ref, values_ref, hidden_ref, target_ref, back_ref, sem, sem_in,
    ) = refs[-14:]
    _, tokens = key_ref.shape
    half = pack_ref.shape[1]
    block = min(1024, tokens)
    count = tokens // block
    wide_at = lax.axis_index("wide")
    narrow_at = lax.axis_index("narrow")
    role = narrow_at ^ (wide_at // owned)

    def moved(keys, values, index, slot):
        source = slice(index * block, (index + 1) * block)
        target = slice(slot * block, (slot + 1) * block)
        return (
            pltpu.make_async_copy(keys.at[:, source], keys_ref.at[:, target], sem_in.at[0, slot]),
            pltpu.make_async_copy(
                values.at[:, source], values_ref.at[:, target], sem_in.at[1, slot]
            ),
        )

    for place, source in enumerate(sources):

        @pl.when(role == place)
        def _(source=source):
            pltpu.make_async_copy(source, pack_ref, sem).start()

    arrivals = [moved(key_ref, value_ref, index, index) for index in range(count)]
    arrivals += [moved(pair_key_ref, pair_value_ref, index, count + index) for index in range(count)]
    for copies in arrivals:
        for copy in copies:
            copy.start()
    pltpu.make_async_copy(sources[0], pack_ref, sem).wait()
    gate_lift = jnp.concatenate([pack_ref[0] * jnp.bfloat16(0.5), pack_ref[1]], axis=0)
    down = pack_ref[2]
    for slot, copies in enumerate(arrivals):
        for copy in copies:
            copy.wait()
        at = slice(slot * block, (slot + 1) * block)
        begin = (narrow_at ^ (slot // count)) * tokens + (slot % count) * block
        rates = rate_ref[pl.ds(wide_at, 1), pl.ds(pl.multiple_of(begin, block), block)]
        pre = jnp.dot(gate_lift, keys_ref[:, at], preferred_element_type=jnp.float32)
        target = (values_ref[:, at].astype(jnp.float32) * -rates).astype(jnp.bfloat16)
        target_ref[:, at] = target
        back_hidden = jnp.dot(down, target, preferred_element_type=jnp.float32)
        half_gate = pre[:half]
        pre_lift = pre[half:]
        twice = jnp.tanh(half_gate) + 1.0
        silu_gate = half_gate * twice
        hidden_ref[:, at] = (silu_gate * pre_lift).astype(jnp.bfloat16)
        slope = twice + silu_gate * (2.0 - twice)
        back_ref[:half, at] = (back_hidden * pre_lift * slope).astype(jnp.bfloat16)
        back_ref[half:, at] = (back_hidden * silu_gate).astype(jnp.bfloat16)
    contract = (((1,), (1,)), ((), ()))
    sums = lax.dot_general(
        back_ref[...], keys_ref[...], contract, preferred_element_type=jnp.float32
    )
    down_sums = lax.dot_general(
        hidden_ref[...], target_ref[...], contract, preferred_element_type=jnp.float32
    )
    for place, value in enumerate((sums[:half] * 0.5, sums[half:], down_sums)):
        send_ref[place] = value.astype(jnp.bfloat16)


def fast_sums(sources, keys, values, pair_keys, pair_values, rates, owned):
    features, tokens = keys.shape
    shape = sources[0].shape
    half = shape[1]
    block = min(1024, tokens)
    resident = pl.BlockSpec(memory_space=pltpu.VMEM)
    return pl.pallas_call(
        functools.partial(sums_body, owned=owned),
        out_shape=(jax.ShapeDtypeStruct(shape, jnp.bfloat16),) * 2,
        in_specs=anywhere(len(sources) + 4) + [resident],
        out_specs=(resident,) * 2,
        scratch_shapes=[
            pltpu.VMEM((features, 2 * tokens), jnp.bfloat16),
            pltpu.VMEM((features, 2 * tokens), jnp.bfloat16),
            pltpu.VMEM((half, 2 * tokens), jnp.bfloat16),
            pltpu.VMEM((features, 2 * tokens), jnp.bfloat16),
            pltpu.VMEM((2 * half, 2 * tokens), jnp.bfloat16),
            pltpu.SemaphoreType.DMA(()),
            pltpu.SemaphoreType.DMA((2, 2 * tokens // block)),
        ],
        cost_estimate=pl.CostEstimate(
            flops=24 * half * features * tokens,
            bytes_accessed=8 * features * tokens + 6 * 3 * half * features,
            transcendentals=2 * half * tokens,
        ),
        name="fast_sums",
        compiler_params=pltpu.CompilerParams(vmem_limit_bytes=VMEM_GRANT),
    )(*sources, keys, values, pair_keys, pair_values, rates)


def recall_body(mine_ref, other_ref, pack_ref, pair_pack_ref, query_ref, out_ref, w_ref, fresh_ref, turned_ref, sem):
    half = mine_ref.shape[1]
    nt = (((1,), (1,)), ((), ()))

    @pl.when(pl.program_id(0) == 0)
    def _():
        side = lax.axis_index("narrow") % 2
        copies = [
            pltpu.make_async_copy(
                source, target.at[:, half_rows(part, half)], sem.at[place]
            )
            for place, (source, target, part) in enumerate(
                (
                    (mine_ref, fresh_ref, side),
                    (other_ref, fresh_ref, 1 - side),
                    (pack_ref, w_ref, side),
                    (pair_pack_ref, w_ref, 1 - side),
                )
            )
        ]
        for copy in copies:
            copy.start()
        copies[0].wait()
        copies[1].wait()
        current = []
        for i in range(3):
            widened = fresh_ref[i].astype(jnp.float32)
            total = jnp.sum(jnp.sum(widened * widened, axis=0, keepdims=True), axis=1, keepdims=True)
            current.append((widened * lax.rsqrt(total + EPS)).astype(jnp.bfloat16))
        for _ in range(NS_ITERS):
            gram = [
                lax.dot_general(x, x, nt, preferred_element_type=jnp.float32).astype(jnp.bfloat16)
                for x in current
            ]
            lifted = [
                jnp.dot(g, x, preferred_element_type=jnp.float32).astype(jnp.bfloat16)
                for x, g in zip(current, gram)
            ]
            current = [
                (
                    COEF_A * x.astype(jnp.float32)
                    + COEF_B * y.astype(jnp.float32)
                    + COEF_C * jnp.dot(g, y, preferred_element_type=jnp.float32)
                ).astype(jnp.bfloat16)
                for x, y, g in zip(current, lifted, gram)
            ]
        copies[2].wait()
        copies[3].wait()
        for i in range(3):
            axis = 0 if i == 2 else 1
            initial = w_ref[i].astype(jnp.float32)
            moved = initial - current[i].astype(jnp.float32)
            wanted = jnp.mean(jnp.square(initial), axis=axis, keepdims=True) + EPS
            present = jnp.mean(jnp.square(moved), axis=axis, keepdims=True) + EPS
            fresh = (moved * (wanted * lax.rsqrt(wanted * present))).astype(jnp.bfloat16)
            if i == 2:
                turned_ref[...] = fresh.T
            else:
                fresh_ref[i] = fresh

    hidden_rows, features = fresh_ref.shape[1:]
    pre = jnp.dot(
        fresh_ref[0:2].reshape(2 * hidden_rows, features),
        query_ref[...],
        preferred_element_type=jnp.float32,
    )
    gate = 0.5 * pre[:hidden_rows]
    hidden = (gate * (jnp.tanh(gate) + 1.0) * pre[hidden_rows:]).astype(jnp.bfloat16)
    out_ref[...] = jnp.dot(turned_ref[...], hidden, preferred_element_type=jnp.float32).astype(
        jnp.bfloat16
    )


def fast_recall(mine, other, pack, pair_pack, queries):
    features, tokens = queries.shape
    half = mine.shape[1]
    hidden_rows = 2 * half
    block = min(512, tokens)
    piece = pl.BlockSpec((features, block), lambda i: (0, i))
    return pl.pallas_call(
        recall_body,
        out_shape=jax.ShapeDtypeStruct((features, tokens), jnp.bfloat16),
        grid=(tokens // block,),
        in_specs=anywhere(4) + [piece],
        out_specs=piece,
        scratch_shapes=[
            pltpu.VMEM((3, hidden_rows, features), jnp.bfloat16),
            pltpu.VMEM((3, hidden_rows, features), jnp.bfloat16),
            pltpu.VMEM((features, hidden_rows), jnp.bfloat16),
            pltpu.SemaphoreType.DMA((4,)),
        ],
        cost_estimate=pl.CostEstimate(
            flops=6 * hidden_rows * features * tokens + 18 * NS_ITERS * hidden_rows * features**2,
            bytes_accessed=4 * features * tokens + 12 * hidden_rows * features,
            transcendentals=hidden_rows * tokens,
        ),
        name="fast_recall",
        compiler_params=pltpu.CompilerParams(vmem_limit_bytes=VMEM_GRANT),
    )(mine, other, pack, pair_pack, queries)


def in_place(query_states, key_states, value_states, cache_keys, cache_values, gate_fast, *rest):
    features, tok_count = query_states.shape
    narrow_count = lax.axis_size("narrow")
    return (
        features == FD
        and gate_fast.shape[1:] == (FD, FD)
        and features % HEAD_SIZE == 0
        and tok_count % WINDOW == 0
        and tok_count >= 2 * WINDOW
        and narrow_count >= 2
        and narrow_count & (narrow_count - 1) == 0
    )


def in_place_plan(
    query_states,
    key_states,
    value_states,
    cache_keys,
    cache_values,
    gate_fast,
    lift_fast,
    down_fast,
    token_rates,
):
    wide_count = lax.axis_size("wide")
    narrow_count = lax.axis_size("narrow")
    owned = gate_fast.shape[0]

    def from_owner(value, step):
        pairs = []
        for wide in range(wide_count):
            start = wide * narrow_count
            owner = wide // owned
            pairs.append((start + owner, start + (owner ^ step)))
        return lax.ppermute(value, ("wide", "narrow"), pairs)

    own, other = prepare(gate_fast, lift_fast, down_fast)
    arrivals = {}
    for step in reversed(range(1, narrow_count)):
        arrivals[step] = from_owner((own, other)[step % 2], step)
    pair_keys = swapped(key_states, "narrow", 0)
    pair_values = swapped(value_states, "narrow", 0)
    ends = edges(key_states, value_states)
    late = attend_late(query_states, key_states, value_states)
    sources = [own] + [arrivals[step] for step in range(1, narrow_count)]
    sources, late, ends = lax.optimization_barrier((sources, late, ends))
    prior = from_behind(ends, "narrow", 1)
    total, pack = fast_sums(
        sources, key_states, value_states, pair_keys, pair_values, token_rates, owned
    )
    pair_pack = swapped(pack, "narrow", 0)
    for distance in range(1, narrow_count.bit_length() - 1):
        partner = swapped(total, "narrow", distance)
        total = stored(total.astype(jnp.float32) + partner.astype(jnp.float32))
    theirs = swapped(total, "narrow", 0)
    attended = attend_early(
        query_states, key_states, value_states, prior, cache_keys, cache_values, late
    )
    recalled = fast_recall(total, theirs, pack, pair_pack, query_states)
    return (attended, recalled)


def spread_plan(
    query_states,
    key_states,
    value_states,
    cache_keys,
    cache_values,
    gate_fast,
    lift_fast,
    down_fast,
    token_rates,
):
    features, tok_count = query_states.shape
    edge_cols = jnp.stack(
        [key_states[:, tok_count - WINDOW :], value_states[:, tok_count - WINDOW :]]
    )
    arrived = from_behind(edge_cols, "narrow", 1)
    leading = lax.axis_index("narrow") == 0
    prior_cols = jnp.where(leading, jnp.stack([cache_keys, cache_values]), arrived)
    ext_keys = jnp.concatenate([prior_cols[0], key_states], axis=1)
    ext_values = jnp.concatenate([prior_cols[1], value_states], axis=1)
    if features % HEAD_SIZE == 0:
        attended = attend_local(query_states, ext_keys, ext_values, 0)
    else:
        attended = attend_paired(query_states, ext_keys, ext_values)
    query_fast, key_fast, value_fast = (
        lax.all_to_all(
            lax.all_to_all(query_states, "wide", split_axis=1, concat_axis=0, tiled=True),
            "narrow",
            split_axis=0,
            concat_axis=1,
            tiled=True,
        ),
        lax.all_to_all(
            lax.all_to_all(key_states, "wide", split_axis=1, concat_axis=0, tiled=True),
            "narrow",
            split_axis=0,
            concat_axis=1,
            tiled=True,
        ),
        lax.all_to_all(
            lax.all_to_all(value_states, "wide", split_axis=1, concat_axis=0, tiled=True),
            "narrow",
            split_axis=0,
            concat_axis=1,
            tiled=True,
        ),
    )
    head_count = gate_fast.shape[0]
    wide_count = lax.axis_size("wide")
    narrow_count = lax.axis_size("narrow")
    piece_rows = tok_count // wide_count
    fast_tokens = query_fast.shape[1]
    rate_blocks = token_rates.reshape(token_rates.shape[0], narrow_count, wide_count, piece_rows)
    rates_here = lax.dynamic_slice(
        rate_blocks,
        (lax.axis_index("narrow") * head_count, 0, lax.axis_index("wide"), 0),
        (head_count, narrow_count, 1, piece_rows),
    ).reshape(head_count, fast_tokens)
    query_heads = query_fast.reshape(head_count, FD, fast_tokens)
    key_heads = key_fast.reshape(head_count, FD, fast_tokens)
    value_heads = value_fast.reshape(head_count, FD, fast_tokens)
    recall = fast_group(
        gate_fast, lift_fast, down_fast, query_heads, key_heads, value_heads, rates_here
    )
    recall = recall.reshape(head_count * FD, fast_tokens)
    recalled = lax.all_to_all(
        lax.all_to_all(recall, "narrow", split_axis=1, concat_axis=0, tiled=True),
        "wide",
        split_axis=0,
        concat_axis=1,
        tiled=True,
    )
    return (attended, recalled)


def per_device(*arrays):
    if in_place(*arrays):
        return in_place_plan(*arrays)
    return spread_plan(*arrays)


def solution(mesh):
    in_specs = (
        P("wide", "narrow"),
        P("wide", "narrow"),
        P("wide", "narrow"),
        P("wide", None),
        P("wide", None),
        P("narrow", None, None),
        P("narrow", None, None),
        P("narrow", None, None),
        P(),
    )
    out_specs = (P("wide", "narrow"), P("wide", "narrow"))
    return jax.shard_map(
        per_device, mesh=mesh, in_specs=in_specs, out_specs=out_specs, check_vma=False
    )
```

```python
import functools
import math

import jax
import jax.numpy as jnp
from jax import lax
from jax.experimental import pallas as pl
from jax.experimental.pallas import tpu as pltpu
from jax.sharding import PartitionSpec as P


FD = 512
HEAD_SIZE = 128
WINDOW = 1024
NS_ITERS = 2


EPS = 1e-06
COEF_A = 3.4445
COEF_B = -4.775
COEF_C = 2.0315
LOG2E = math.log2(math.e)
VMEM_GRANT = 67043328


def swapped(array, axis, distance):
    return lax.ppermute(array, axis, [(i, i ^ 1 << distance) for i in range(lax.axis_size(axis))])


def shortened(array):

    def short(part):
        return part.astype(jnp.bfloat16) if part.dtype == jnp.float32 else part

    return jax.tree.map(short, array)


def from_behind(value, axis, steps):
    count = lax.axis_size(axis)
    initial, last = (max(0, -steps), min(count, count - steps))
    return lax.ppermute(value, axis, [(source, source + steps) for source in range(initial, last)])


def stored(value):
    return lax.optimization_barrier(value.astype(jnp.bfloat16))


def attend_local(query_states, ext_keys, ext_values, key_start):
    features, tok_count = query_states.shape
    head_count = features // HEAD_SIZE
    block_rows = min(512, tok_count)
    block_count = tok_count // block_rows
    key_span = WINDOW + block_rows
    scaling = 1.0 / math.sqrt(HEAD_SIZE)
    rows_at = lax.broadcasted_iota(jnp.int32, (block_rows, key_span), 0)
    cols_at = lax.broadcasted_iota(jnp.int32, (block_rows, key_span), 1)
    visible = (cols_at > rows_at) & (cols_at <= rows_at + WINDOW)

    def one_block(block_index):
        offset = block_index * block_rows
        query_part = lax.dynamic_slice_in_dim(query_states, offset, block_rows, 1).reshape(
            head_count, HEAD_SIZE, block_rows
        )
        key_part = lax.dynamic_slice_in_dim(ext_keys, key_start + offset, key_span, 1).reshape(
            head_count, HEAD_SIZE, key_span
        )
        value_part = lax.dynamic_slice_in_dim(ext_values, key_start + offset, key_span, 1).reshape(
            head_count, HEAD_SIZE, key_span
        )
        scores = (
            jnp.einsum("hdq,hdk->hqk", query_part, key_part, preferred_element_type=jnp.float32)
            * scaling
        )
        scores = jnp.where(visible[None], scores, -jnp.inf)
        highest = jnp.max(scores, axis=2, keepdims=True)
        raised = jnp.exp(scores - highest)
        weights = (raised / jnp.sum(raised, axis=2, keepdims=True)).astype(jnp.bfloat16)
        blended = jnp.einsum(
            "hdk,hqk->hdq", value_part, weights, preferred_element_type=jnp.float32
        )
        return blended.astype(jnp.bfloat16).reshape(features, block_rows)

    blocks_out = lax.map(one_block, jnp.arange(block_count, dtype=jnp.int32))
    return jnp.transpose(blocks_out, (1, 0, 2)).reshape(features, tok_count)


def attend_paired(query_states, ext_keys, ext_values):
    features, tok_count = query_states.shape
    half_rows = tok_count // 2
    lower = lax.axis_index("wide") % 2 == 0
    query_send = jnp.where(lower, query_states[:, half_rows:], query_states[:, :half_rows])
    query_keep = jnp.where(lower, query_states[:, :half_rows], query_states[:, half_rows:])
    other_keys, other_values, other_queries = swapped((ext_keys, ext_values, query_send), "wide", 0)
    full_keys = jnp.where(
        lower,
        jnp.concatenate([ext_keys, other_keys], axis=0),
        jnp.concatenate([other_keys, ext_keys], axis=0),
    )
    full_values = jnp.where(
        lower,
        jnp.concatenate([ext_values, other_values], axis=0),
        jnp.concatenate([other_values, ext_values], axis=0),
    )
    full_queries = jnp.where(
        lower,
        jnp.concatenate([query_keep, other_queries], axis=0),
        jnp.concatenate([other_queries, query_keep], axis=0),
    )
    key_start = jnp.where(lower, 0, half_rows).astype(jnp.int32)
    head_out = attend_local(full_queries, full_keys, full_values, key_start)
    out_keep = jnp.where(lower, head_out[:features], head_out[features:])
    out_send = jnp.where(lower, head_out[features:], head_out[:features])
    out_other = swapped(shortened(out_send), "wide", 0).astype(out_send.dtype)
    return jnp.where(
        lower,
        jnp.concatenate([out_keep, out_other], axis=1),
        jnp.concatenate([out_other, out_keep], axis=1),
    )


def fast_terms(gate_weight, lift_weight, down_weight, key_heads, value_heads, rates_here):
    pre_gate = jnp.einsum(
        "hcf,hft->hct", gate_weight, key_heads, preferred_element_type=jnp.float32
    )
    pre_lift = jnp.einsum(
        "hcf,hft->hct", lift_weight, key_heads, preferred_element_type=jnp.float32
    )
    sigmoid_gate = jax.nn.sigmoid(pre_gate)
    silu_gate = pre_gate * sigmoid_gate
    hidden = (silu_gate * pre_lift).astype(jnp.bfloat16)
    target = (-(value_heads.astype(jnp.float32) * rates_here[:, None, :])).astype(jnp.bfloat16)
    grad_down = jnp.einsum("hft,hct->hfc", target, hidden, preferred_element_type=jnp.float32)
    back_hidden = jnp.einsum(
        "hfc,hft->hct", down_weight, target, preferred_element_type=jnp.float32
    )
    back_lift = (back_hidden * silu_gate).astype(jnp.bfloat16)
    back_gate = (
        back_hidden * pre_lift * sigmoid_gate * (1.0 + pre_gate * (1.0 - sigmoid_gate))
    ).astype(jnp.bfloat16)
    grad_gate = jnp.einsum("hct,hft->hcf", back_gate, key_heads, preferred_element_type=jnp.float32)
    grad_lift = jnp.einsum("hct,hft->hcf", back_lift, key_heads, preferred_element_type=jnp.float32)
    return (grad_gate, grad_lift, grad_down)


def scaled_start(rounded):
    widened = rounded.astype(jnp.float32)
    norm_val = jnp.sqrt(jnp.sum(jnp.square(widened), axis=(1, 2), keepdims=True) + EPS)
    return stored(widened / norm_val)


def starting(grad_gate, grad_lift, grad_down):
    sum_gate, sum_lift, sum_down = lax.psum((grad_gate, grad_lift, grad_down), "wide")
    return (
        scaled_start(stored(sum_gate)),
        scaled_start(stored(sum_lift)),
        scaled_start(stored(sum_down)),
    )


def orthogonal(current):
    for _ in range(NS_ITERS):
        gram_mat = jnp.einsum(
            "hrc,hrd->hcd", current, current, preferred_element_type=jnp.float32
        ).astype(jnp.bfloat16)
        lifted = stored(
            jnp.einsum("hrc,hcd->hrd", current, gram_mat, preferred_element_type=jnp.float32)
        )
        current = stored(
            COEF_A * current.astype(jnp.float32)
            + COEF_B * lifted.astype(jnp.float32)
            + COEF_C
            * jnp.einsum("hrc,hcd->hrd", lifted, gram_mat, preferred_element_type=jnp.float32)
        )
    return current


def refreshed(weight, ortho):
    initial = weight.astype(jnp.float32)
    moved_rows = initial - ortho.astype(jnp.float32)
    wanted = jnp.sqrt(jnp.mean(jnp.square(initial), axis=-1, keepdims=True) + EPS)
    present = jnp.sqrt(jnp.mean(jnp.square(moved_rows), axis=-1, keepdims=True) + EPS)
    return (moved_rows * (wanted / present)).astype(jnp.bfloat16)


def fast_group(
    gate_weight, lift_weight, down_weight, query_heads, key_heads, value_heads, rates_here
):
    grad_gate, grad_lift, grad_down = fast_terms(
        gate_weight, lift_weight, down_weight, key_heads, value_heads, rates_here
    )
    start_gate, start_lift, start_down = starting(grad_gate, grad_lift, grad_down)
    fresh_gate = refreshed(gate_weight, orthogonal(start_gate))
    fresh_lift = refreshed(lift_weight, orthogonal(start_lift))
    fresh_down = refreshed(down_weight, orthogonal(start_down))
    query_gate = jnp.einsum(
        "hcf,hft->hct", fresh_gate, query_heads, preferred_element_type=jnp.float32
    )
    query_lift = jnp.einsum(
        "hcf,hft->hct", fresh_lift, query_heads, preferred_element_type=jnp.float32
    )
    query_hidden = (jax.nn.silu(query_gate) * query_lift).astype(jnp.bfloat16)
    return jnp.einsum(
        "hfc,hct->hft", fresh_down, query_hidden, preferred_element_type=jnp.float32
    ).astype(jnp.bfloat16)


def attend_body(q_ref, kp_ref, vp_ref, kc_ref, vc_ref, *rest, block, window):
    cached = len(rest) > 3
    o_ref, kt_ref, v_ref = rest[-3:]
    hd = q_ref.shape[0]
    scale = LOG2E / math.sqrt(hd)

    def place(k, v, at):
        turned = k[...].T
        kt_ref[at : at + window, :hd] = turned
        kt_ref[at : at + window, hd:] = turned
        v_ref[:hd, at : at + window] = v[...]

    if cached:
        leading = lax.axis_index("narrow") == 0

        @pl.when(leading)
        def _():
            place(*rest[:2], 0)

        @pl.when(jnp.logical_not(leading))
        def _():
            place(kp_ref, vp_ref, 0)

    else:
        place(kp_ref, vp_ref, 0)
    place(kc_ref, vc_ref, window)
    v_ref[hd:, :] = jnp.ones((v_ref.shape[0] - hd, 2 * window), jnp.bfloat16)
    rows = lax.broadcasted_iota(jnp.int32, (block, block), 0)
    cols = lax.broadcasted_iota(jnp.int32, (block, block), 1)
    first = rows > cols
    inner = window // block

    def scores(b):
        q = q_ref[:, b * block : (b + 1) * block].astype(jnp.float32) * scale
        high = q.astype(jnp.bfloat16)
        low = (q - high.astype(jnp.float32)).astype(jnp.bfloat16)
        pair = jnp.concatenate([high, low], axis=0)
        parts = [
            jnp.dot(
                kt_ref[(b + j) * block : (b + j + 1) * block, :],
                pair,
                preferred_element_type=jnp.float32,
            )
            for j in range(inner + 1)
        ]
        return [jnp.where(first, parts[0], parts[inner])] + parts[1:inner]

    def blend(b, parts):
        top = functools.reduce(jnp.maximum, parts)
        top = jnp.max(top, axis=0, keepdims=True)
        raised = [jnp.exp2(part - top).astype(jnp.bfloat16) for part in parts]
        zero = jnp.zeros_like(raised[0])
        ends = jnp.where(first, raised[0], zero), jnp.where(first, zero, raised[0])
        weights = jnp.concatenate([ends[0]] + raised[1:] + [ends[1]], axis=0)
        span = v_ref[:, b * block : (b + inner + 1) * block]
        out = jnp.dot(span, weights, preferred_element_type=jnp.float32)
        o_ref[:, b * block : (b + 1) * block] = (out[:hd] * (1.0 / out[hd : hd + 1])).astype(
            jnp.bfloat16
        )

    ready = scores(0)
    for b in range(1, inner):
        following = scores(b)
        blend(b - 1, ready)
        ready = following
    blend(inner - 1, ready)


def attend_scratch():
    return [
        pltpu.VMEM((2 * WINDOW, 2 * HEAD_SIZE), jnp.bfloat16),
        pltpu.VMEM((HEAD_SIZE + 16, 2 * WINDOW), jnp.bfloat16),
    ]


def attend_late(queries, keys, values):
    features, tokens = queries.shape
    heads, chunks = features // HEAD_SIZE, tokens // WINDOW - 1
    here = pl.BlockSpec((HEAD_SIZE, WINDOW), lambda h, c: (h, c + 1))
    before = pl.BlockSpec((HEAD_SIZE, WINDOW), lambda h, c: (h, c))
    return pl.pallas_call(
        functools.partial(attend_body, block=min(256, WINDOW), window=WINDOW),
        out_shape=jax.ShapeDtypeStruct((features, tokens), jnp.bfloat16),
        grid=(heads, chunks),
        in_specs=[here, before, before, here, here],
        out_specs=here,
        scratch_shapes=attend_scratch(),
        cost_estimate=pl.CostEstimate(
            flops=5 * features * chunks * WINDOW**2,
            bytes_accessed=10 * features * chunks * WINDOW,
            transcendentals=heads * chunks * WINDOW**2,
        ),
        name="attend_late",
    )(queries, keys, values, keys, values)


def attend_early(queries, keys, values, prior, cache_keys, cache_values, late, part):
    features, tokens = queries.shape
    heads = prior.shape[1] // HEAD_SIZE
    here = pl.BlockSpec((HEAD_SIZE, WINDOW), lambda h: (h + part * heads, 0))
    prior_keys = pl.BlockSpec((None, HEAD_SIZE, WINDOW), lambda h: (0, h, 0))
    prior_values = pl.BlockSpec((None, HEAD_SIZE, WINDOW), lambda h: (1, h, 0))
    body = functools.partial(attend_body, block=min(256, WINDOW), window=WINDOW)

    def early_body(*refs):
        body(*refs[:7], *refs[8:])

    return pl.pallas_call(
        early_body,
        out_shape=jax.ShapeDtypeStruct((features, tokens), jnp.bfloat16),
        grid=(heads,),
        in_specs=[here, prior_keys, prior_values, here, here, here, here]
        + [pl.BlockSpec(memory_space=pl.ANY)],
        out_specs=here,
        scratch_shapes=attend_scratch(),
        input_output_aliases={7: 0},
        cost_estimate=pl.CostEstimate(
            flops=5 * heads * HEAD_SIZE * WINDOW**2,
            bytes_accessed=14 * heads * HEAD_SIZE * WINDOW,
            transcendentals=heads * WINDOW**2,
        ),
        name="attend_early",
        compiler_params=pltpu.CompilerParams(vmem_limit_bytes=VMEM_GRANT),
    )(queries, prior, prior, keys, values, cache_keys, cache_values, late)


def anywhere(count):
    return [pl.BlockSpec(memory_space=pl.ANY)] * count


def half_rows(part, half):
    return pl.ds(pl.multiple_of(part * half, half), half)


def prepare_body(gate_ref, lift_ref, down_ref, own_ref, other_ref, w_ref, out_ref, sem):
    owned = gate_ref.shape[0]
    local = lax.axis_index("wide") % owned
    side = lax.axis_index("narrow") % 2
    half = own_ref.shape[1]
    copies = [
        pltpu.make_async_copy(source.at[local], w_ref.at[place], sem.at[0, place])
        for place, source in enumerate((down_ref, gate_ref, lift_ref))
    ]
    for copy in copies:
        copy.start()
    leaving = []
    copies[0].wait()
    out_ref[...] = w_ref[0].T
    for order, (place, source) in enumerate(((2, out_ref), (0, w_ref.at[1]), (1, w_ref.at[2]))):
        if order:
            copies[order].wait()
        for turn, (target, part) in enumerate(((own_ref, side), (other_ref, 1 - side))):
            leaving.append(
                pltpu.make_async_copy(
                    source.at[half_rows(part, half)], target.at[place], sem.at[1 + turn, place]
                )
            )
            leaving[-1].start()
    for copy in leaving:
        copy.wait()


def prepare(gate_fast, lift_fast, down_fast):
    _, hidden_rows, features = gate_fast.shape
    shape = (3, hidden_rows // 2, features)
    return pl.pallas_call(
        prepare_body,
        out_shape=(jax.ShapeDtypeStruct(shape, jnp.bfloat16),) * 2,
        in_specs=anywhere(3),
        out_specs=tuple(anywhere(2)),
        scratch_shapes=[
            pltpu.VMEM((3, hidden_rows, features), jnp.bfloat16),
            pltpu.VMEM((hidden_rows, features), jnp.bfloat16),
            pltpu.SemaphoreType.DMA((3, 3)),
        ],
        cost_estimate=pl.CostEstimate(
            flops=0, bytes_accessed=12 * hidden_rows * features, transcendentals=0
        ),
        name="prepare",
    )(gate_fast, lift_fast, down_fast)


def edges_body(key_ref, value_ref, *refs):
    out_refs, (held_ref, sem) = refs[:-2], refs[-2:]
    _, tokens = key_ref.shape
    rows, window = out_refs[0].shape[1:]
    moves = []
    for part, out_ref in enumerate(out_refs):
        at = slice(part * rows, (part + 1) * rows)
        for place, source in enumerate((key_ref, value_ref)):
            arriving = pltpu.make_async_copy(
                source.at[at, tokens - window :], held_ref.at[place, at], sem.at[0, place, part]
            )
            leaving = pltpu.make_async_copy(
                held_ref.at[place, at], out_ref.at[place], sem.at[1, place, part]
            )
            arriving.start()
            moves.append((arriving, leaving))
    for arriving, leaving in moves:
        arriving.wait()
        leaving.start()
    for _, leaving in moves:
        leaving.wait()


def edges(keys, values, parts):
    features = keys.shape[0]
    return pl.pallas_call(
        edges_body,
        out_shape=(jax.ShapeDtypeStruct((2, features // parts, WINDOW), jnp.bfloat16),) * parts,
        in_specs=anywhere(2),
        out_specs=tuple(anywhere(parts)),
        scratch_shapes=[
            pltpu.VMEM((2, features, WINDOW), jnp.bfloat16),
            pltpu.SemaphoreType.DMA((2, 2, parts)),
        ],
        cost_estimate=pl.CostEstimate(
            flops=0, bytes_accessed=8 * features * WINDOW, transcendentals=0
        ),
        name="edges",
    )(keys, values)


def sums_body(*refs, owned):
    sources = refs[:-14]
    (
        key_ref, value_ref, pair_key_ref, pair_value_ref, rate_ref,
        send_ref, pack_ref,
        keys_ref, values_ref, hidden_ref, target_ref, back_ref, sem, sem_in,
    ) = refs[-14:]
    _, tokens = key_ref.shape
    half = pack_ref.shape[1]
    block = min(1024, tokens)
    count = tokens // block
    wide_at = lax.axis_index("wide")
    narrow_at = lax.axis_index("narrow")
    role = narrow_at ^ (wide_at // owned)

    def moved(keys, values, index, slot):
        source = slice(index * block, (index + 1) * block)
        target = slice(slot * block, (slot + 1) * block)
        return (
            pltpu.make_async_copy(keys.at[:, source], keys_ref.at[:, target], sem_in.at[0, slot]),
            pltpu.make_async_copy(
                values.at[:, source], values_ref.at[:, target], sem_in.at[1, slot]
            ),
        )

    for place, source in enumerate(sources):

        @pl.when(role == place)
        def _(source=source):
            pltpu.make_async_copy(source, pack_ref, sem).start()

    arrivals = [moved(key_ref, value_ref, index, index) for index in range(count)]
    arrivals += [moved(pair_key_ref, pair_value_ref, index, count + index) for index in range(count)]
    for copies in arrivals:
        for copy in copies:
            copy.start()
    pltpu.make_async_copy(sources[0], pack_ref, sem).wait()
    gate_lift = jnp.concatenate([pack_ref[0] * jnp.bfloat16(0.5), pack_ref[1]], axis=0)
    down = pack_ref[2]
    for slot, copies in enumerate(arrivals):
        for copy in copies:
            copy.wait()
        at = slice(slot * block, (slot + 1) * block)
        begin = (narrow_at ^ (slot // count)) * tokens + (slot % count) * block
        rates = rate_ref[pl.ds(wide_at, 1), pl.ds(pl.multiple_of(begin, block), block)]
        pre = jnp.dot(gate_lift, keys_ref[:, at], preferred_element_type=jnp.float32)
        target = (values_ref[:, at].astype(jnp.float32) * -rates).astype(jnp.bfloat16)
        target_ref[:, at] = target
        back_hidden = jnp.dot(down, target, preferred_element_type=jnp.float32)
        half_gate = pre[:half]
        pre_lift = pre[half:]
        twice = jnp.tanh(half_gate) + 1.0
        silu_gate = half_gate * twice
        hidden_ref[:, at] = (silu_gate * pre_lift).astype(jnp.bfloat16)
        slope = twice + silu_gate * (2.0 - twice)
        back_ref[:half, at] = (back_hidden * pre_lift * slope).astype(jnp.bfloat16)
        back_ref[half:, at] = (back_hidden * silu_gate).astype(jnp.bfloat16)
    contract = (((1,), (1,)), ((), ()))
    sums = lax.dot_general(
        back_ref[...], keys_ref[...], contract, preferred_element_type=jnp.float32
    )
    down_sums = lax.dot_general(
        hidden_ref[...], target_ref[...], contract, preferred_element_type=jnp.float32
    )
    for place, value in enumerate((sums[:half] * 0.5, sums[half:], down_sums)):
        send_ref[place] = value.astype(jnp.bfloat16)


def fast_sums(sources, keys, values, pair_keys, pair_values, rates, owned):
    features, tokens = keys.shape
    shape = sources[0].shape
    half = shape[1]
    block = min(1024, tokens)
    resident = pl.BlockSpec(memory_space=pltpu.VMEM)
    return pl.pallas_call(
        functools.partial(sums_body, owned=owned),
        out_shape=(jax.ShapeDtypeStruct(shape, jnp.bfloat16),) * 2,
        in_specs=anywhere(len(sources) + 4) + [resident],
        out_specs=(resident,) * 2,
        scratch_shapes=[
            pltpu.VMEM((features, 2 * tokens), jnp.bfloat16),
            pltpu.VMEM((features, 2 * tokens), jnp.bfloat16),
            pltpu.VMEM((half, 2 * tokens), jnp.bfloat16),
            pltpu.VMEM((features, 2 * tokens), jnp.bfloat16),
            pltpu.VMEM((2 * half, 2 * tokens), jnp.bfloat16),
            pltpu.SemaphoreType.DMA(()),
            pltpu.SemaphoreType.DMA((2, 2 * tokens // block)),
        ],
        cost_estimate=pl.CostEstimate(
            flops=24 * half * features * tokens,
            bytes_accessed=8 * features * tokens + 6 * 3 * half * features,
            transcendentals=2 * half * tokens,
        ),
        name="fast_sums",
        compiler_params=pltpu.CompilerParams(vmem_limit_bytes=VMEM_GRANT),
    )(*sources, keys, values, pair_keys, pair_values, rates)


def recall_body(
    mine_ref, other_ref, far_ref, other_far_ref, pack_ref, pair_pack_ref, query_ref, out_ref,
    w_ref, fresh_ref, far_sums_ref, turned_ref, sem,
):
    half = mine_ref.shape[1]
    nt = (((1,), (1,)), ((), ()))

    @pl.when(pl.program_id(0) == 0)
    def _():
        side = lax.axis_index("narrow") % 2
        copies = [
            pltpu.make_async_copy(
                source, target.at[:, half_rows(part, half)], sem.at[place]
            )
            for place, (source, target, part) in enumerate(
                (
                    (mine_ref, fresh_ref, side),
                    (other_ref, fresh_ref, 1 - side),
                    (far_ref, far_sums_ref, side),
                    (other_far_ref, far_sums_ref, 1 - side),
                    (pack_ref, w_ref, side),
                    (pair_pack_ref, w_ref, 1 - side),
                )
            )
        ]
        for copy in copies:
            copy.start()
        for copy in copies[:4]:
            copy.wait()
        current = []
        for i in range(3):
            summed = fresh_ref[i].astype(jnp.float32) + far_sums_ref[i].astype(jnp.float32)
            widened = summed.astype(jnp.bfloat16).astype(jnp.float32)
            total = jnp.sum(jnp.sum(widened * widened, axis=0, keepdims=True), axis=1, keepdims=True)
            current.append((widened * lax.rsqrt(total + EPS)).astype(jnp.bfloat16))
        for _ in range(NS_ITERS):
            gram = [
                lax.dot_general(x, x, nt, preferred_element_type=jnp.float32).astype(jnp.bfloat16)
                for x in current
            ]
            lifted = [
                jnp.dot(g, x, preferred_element_type=jnp.float32).astype(jnp.bfloat16)
                for x, g in zip(current, gram)
            ]
            current = [
                (
                    COEF_A * x.astype(jnp.float32)
                    + COEF_B * y.astype(jnp.float32)
                    + COEF_C * jnp.dot(g, y, preferred_element_type=jnp.float32)
                ).astype(jnp.bfloat16)
                for x, y, g in zip(current, lifted, gram)
            ]
        for copy in copies[4:]:
            copy.wait()
        for i in range(3):
            axis = 0 if i == 2 else 1
            initial = w_ref[i].astype(jnp.float32)
            moved = initial - current[i].astype(jnp.float32)
            wanted = jnp.mean(jnp.square(initial), axis=axis, keepdims=True) + EPS
            present = jnp.mean(jnp.square(moved), axis=axis, keepdims=True) + EPS
            fresh = (moved * (wanted * lax.rsqrt(wanted * present))).astype(jnp.bfloat16)
            if i == 2:
                turned_ref[...] = fresh.T
            else:
                fresh_ref[i] = fresh

    hidden_rows, features = fresh_ref.shape[1:]
    pre = jnp.dot(
        fresh_ref[0:2].reshape(2 * hidden_rows, features),
        query_ref[...],
        preferred_element_type=jnp.float32,
    )
    gate = 0.5 * pre[:hidden_rows]
    hidden = (gate * (jnp.tanh(gate) + 1.0) * pre[hidden_rows:]).astype(jnp.bfloat16)
    out_ref[...] = jnp.dot(turned_ref[...], hidden, preferred_element_type=jnp.float32).astype(
        jnp.bfloat16
    )


def fast_recall(sums, packs, queries):
    features, tokens = queries.shape
    half = packs[0].shape[1]
    hidden_rows = 2 * half
    block = min(512, tokens)
    piece = pl.BlockSpec((features, block), lambda i: (0, i))
    return pl.pallas_call(
        recall_body,
        out_shape=jax.ShapeDtypeStruct((features, tokens), jnp.bfloat16),
        grid=(tokens // block,),
        in_specs=anywhere(6) + [piece],
        out_specs=piece,
        scratch_shapes=[
            pltpu.VMEM((3, hidden_rows, features), jnp.bfloat16),
            pltpu.VMEM((3, hidden_rows, features), jnp.bfloat16),
            pltpu.VMEM((3, hidden_rows, features), jnp.bfloat16),
            pltpu.VMEM((features, hidden_rows), jnp.bfloat16),
            pltpu.SemaphoreType.DMA((6,)),
        ],
        cost_estimate=pl.CostEstimate(
            flops=6 * hidden_rows * features * tokens + 18 * NS_ITERS * hidden_rows * features**2,
            bytes_accessed=4 * features * tokens + 12 * hidden_rows * features,
            transcendentals=hidden_rows * tokens,
        ),
        name="fast_recall",
        compiler_params=pltpu.CompilerParams(vmem_limit_bytes=VMEM_GRANT),
    )(*sums, *packs, queries)


def in_place(query_states, key_states, value_states, cache_keys, cache_values, gate_fast, *rest):
    features, tok_count = query_states.shape
    narrow_count = lax.axis_size("narrow")
    return (
        features == FD
        and gate_fast.shape[1:] == (FD, FD)
        and features % HEAD_SIZE == 0
        and tok_count % WINDOW == 0
        and tok_count >= 2 * WINDOW
        and narrow_count >= 4
        and narrow_count & (narrow_count - 1) == 0
    )


def in_place_plan(
    query_states,
    key_states,
    value_states,
    cache_keys,
    cache_values,
    gate_fast,
    lift_fast,
    down_fast,
    token_rates,
):
    wide_count = lax.axis_size("wide")
    narrow_count = lax.axis_size("narrow")
    owned = gate_fast.shape[0]

    def from_owner(value, step):
        pairs = []
        for wide in range(wide_count):
            start = wide * narrow_count
            owner = wide // owned
            pairs.append((start + owner, start + (owner ^ step)))
        return lax.ppermute(value, ("wide", "narrow"), pairs)

    own, other = prepare(gate_fast, lift_fast, down_fast)
    arrivals = {}
    for step in reversed(range(1, narrow_count)):
        arrivals[step] = from_owner((own, other)[step % 2], step)
    pair_keys = swapped(key_states, "narrow", 0)
    pair_values = swapped(value_states, "narrow", 0)
    parts = 2
    ends = edges(key_states, value_states, parts)
    attended = attend_late(query_states, key_states, value_states)
    sources = [own] + [arrivals[step] for step in range(1, narrow_count)]
    sources, attended, ends = lax.optimization_barrier((sources, attended, ends))
    prior = []
    for end in ends:
        prior.append(from_behind(end, "narrow", 1))
    near, pack = fast_sums(
        sources, key_states, value_states, pair_keys, pair_values, token_rates, owned
    )
    distances = range(1, narrow_count.bit_length() - 1)
    for distance in distances:
        far = swapped(near, "narrow", distance)
        if distance != distances[-1]:
            near = stored(near.astype(jnp.float32) + far.astype(jnp.float32))
    pair_pack = swapped(pack, "narrow", 0)
    pair_near = swapped(near, "narrow", 0)
    pair_far = swapped(far, "narrow", 0)
    for part, before in enumerate(prior):
        attended = attend_early(
            query_states, key_states, value_states, before, cache_keys, cache_values, attended, part
        )
    recalled = fast_recall((near, pair_near, far, pair_far), (pack, pair_pack), query_states)
    return (attended, recalled)


def spread_plan(
    query_states,
    key_states,
    value_states,
    cache_keys,
    cache_values,
    gate_fast,
    lift_fast,
    down_fast,
    token_rates,
):
    features, tok_count = query_states.shape
    edge_cols = jnp.stack(
        [key_states[:, tok_count - WINDOW :], value_states[:, tok_count - WINDOW :]]
    )
    arrived = from_behind(edge_cols, "narrow", 1)
    leading = lax.axis_index("narrow") == 0
    prior_cols = jnp.where(leading, jnp.stack([cache_keys, cache_values]), arrived)
    ext_keys = jnp.concatenate([prior_cols[0], key_states], axis=1)
    ext_values = jnp.concatenate([prior_cols[1], value_states], axis=1)
    if features % HEAD_SIZE == 0:
        attended = attend_local(query_states, ext_keys, ext_values, 0)
    else:
        attended = attend_paired(query_states, ext_keys, ext_values)
    query_fast, key_fast, value_fast = (
        lax.all_to_all(
            lax.all_to_all(query_states, "wide", split_axis=1, concat_axis=0, tiled=True),
            "narrow",
            split_axis=0,
            concat_axis=1,
            tiled=True,
        ),
        lax.all_to_all(
            lax.all_to_all(key_states, "wide", split_axis=1, concat_axis=0, tiled=True),
            "narrow",
            split_axis=0,
            concat_axis=1,
            tiled=True,
        ),
        lax.all_to_all(
            lax.all_to_all(value_states, "wide", split_axis=1, concat_axis=0, tiled=True),
            "narrow",
            split_axis=0,
            concat_axis=1,
            tiled=True,
        ),
    )
    head_count = gate_fast.shape[0]
    wide_count = lax.axis_size("wide")
    narrow_count = lax.axis_size("narrow")
    piece_rows = tok_count // wide_count
    fast_tokens = query_fast.shape[1]
    rate_blocks = token_rates.reshape(token_rates.shape[0], narrow_count, wide_count, piece_rows)
    rates_here = lax.dynamic_slice(
        rate_blocks,
        (lax.axis_index("narrow") * head_count, 0, lax.axis_index("wide"), 0),
        (head_count, narrow_count, 1, piece_rows),
    ).reshape(head_count, fast_tokens)
    query_heads = query_fast.reshape(head_count, FD, fast_tokens)
    key_heads = key_fast.reshape(head_count, FD, fast_tokens)
    value_heads = value_fast.reshape(head_count, FD, fast_tokens)
    recall = fast_group(
        gate_fast, lift_fast, down_fast, query_heads, key_heads, value_heads, rates_here
    )
    recall = recall.reshape(head_count * FD, fast_tokens)
    recalled = lax.all_to_all(
        lax.all_to_all(recall, "narrow", split_axis=1, concat_axis=0, tiled=True),
        "wide",
        split_axis=0,
        concat_axis=1,
        tiled=True,
    )
    return (attended, recalled)


def per_device(*arrays):
    if in_place(*arrays):
        return in_place_plan(*arrays)
    return spread_plan(*arrays)


def solution(mesh):
    in_specs = (
        P("wide", "narrow"),
        P("wide", "narrow"),
        P("wide", "narrow"),
        P("wide", None),
        P("wide", None),
        P("narrow", None, None),
        P("narrow", None, None),
        P("narrow", None, None),
        P(),
    )
    out_specs = (P("wide", "narrow"), P("wide", "narrow"))
    return jax.shard_map(
        per_device, mesh=mesh, in_specs=in_specs, out_specs=out_specs, check_vma=False
    )
```

```python
import functools
import math

import jax
import jax.numpy as jnp
from jax import lax
from jax.experimental import pallas as pl
from jax.experimental.pallas import tpu as pltpu
from jax.sharding import PartitionSpec as P


FD = 512
HEAD_SIZE = 128
WINDOW = 1024
NS_ITERS = 2


EPS = 1e-06
COEF_A = 3.4445
COEF_B = -4.775
COEF_C = 2.0315
LOG2E = math.log2(math.e)
VMEM_GRANT = 67043328


def swapped(array, axis, distance):
    return lax.ppermute(array, axis, [(i, i ^ 1 << distance) for i in range(lax.axis_size(axis))])


def shortened(array):

    def short(part):
        return part.astype(jnp.bfloat16) if part.dtype == jnp.float32 else part

    return jax.tree.map(short, array)


def from_behind(value, axis, steps):
    count = lax.axis_size(axis)
    initial, last = (max(0, -steps), min(count, count - steps))
    return lax.ppermute(value, axis, [(source, source + steps) for source in range(initial, last)])


def stored(value):
    return lax.optimization_barrier(value.astype(jnp.bfloat16))


def attend_local(query_states, ext_keys, ext_values, key_start):
    features, tok_count = query_states.shape
    head_count = features // HEAD_SIZE
    block_rows = min(512, tok_count)
    block_count = tok_count // block_rows
    key_span = WINDOW + block_rows
    scaling = 1.0 / math.sqrt(HEAD_SIZE)
    rows_at = lax.broadcasted_iota(jnp.int32, (block_rows, key_span), 0)
    cols_at = lax.broadcasted_iota(jnp.int32, (block_rows, key_span), 1)
    visible = (cols_at > rows_at) & (cols_at <= rows_at + WINDOW)

    def one_block(block_index):
        offset = block_index * block_rows
        query_part = lax.dynamic_slice_in_dim(query_states, offset, block_rows, 1).reshape(
            head_count, HEAD_SIZE, block_rows
        )
        key_part = lax.dynamic_slice_in_dim(ext_keys, key_start + offset, key_span, 1).reshape(
            head_count, HEAD_SIZE, key_span
        )
        value_part = lax.dynamic_slice_in_dim(ext_values, key_start + offset, key_span, 1).reshape(
            head_count, HEAD_SIZE, key_span
        )
        scores = (
            jnp.einsum("hdq,hdk->hqk", query_part, key_part, preferred_element_type=jnp.float32)
            * scaling
        )
        scores = jnp.where(visible[None], scores, -jnp.inf)
        highest = jnp.max(scores, axis=2, keepdims=True)
        raised = jnp.exp(scores - highest)
        weights = (raised / jnp.sum(raised, axis=2, keepdims=True)).astype(jnp.bfloat16)
        blended = jnp.einsum(
            "hdk,hqk->hdq", value_part, weights, preferred_element_type=jnp.float32
        )
        return blended.astype(jnp.bfloat16).reshape(features, block_rows)

    blocks_out = lax.map(one_block, jnp.arange(block_count, dtype=jnp.int32))
    return jnp.transpose(blocks_out, (1, 0, 2)).reshape(features, tok_count)


def attend_paired(query_states, ext_keys, ext_values):
    features, tok_count = query_states.shape
    half_rows = tok_count // 2
    lower = lax.axis_index("wide") % 2 == 0
    query_send = jnp.where(lower, query_states[:, half_rows:], query_states[:, :half_rows])
    query_keep = jnp.where(lower, query_states[:, :half_rows], query_states[:, half_rows:])
    other_keys, other_values, other_queries = swapped((ext_keys, ext_values, query_send), "wide", 0)
    full_keys = jnp.where(
        lower,
        jnp.concatenate([ext_keys, other_keys], axis=0),
        jnp.concatenate([other_keys, ext_keys], axis=0),
    )
    full_values = jnp.where(
        lower,
        jnp.concatenate([ext_values, other_values], axis=0),
        jnp.concatenate([other_values, ext_values], axis=0),
    )
    full_queries = jnp.where(
        lower,
        jnp.concatenate([query_keep, other_queries], axis=0),
        jnp.concatenate([other_queries, query_keep], axis=0),
    )
    key_start = jnp.where(lower, 0, half_rows).astype(jnp.int32)
    head_out = attend_local(full_queries, full_keys, full_values, key_start)
    out_keep = jnp.where(lower, head_out[:features], head_out[features:])
    out_send = jnp.where(lower, head_out[features:], head_out[:features])
    out_other = swapped(shortened(out_send), "wide", 0).astype(out_send.dtype)
    return jnp.where(
        lower,
        jnp.concatenate([out_keep, out_other], axis=1),
        jnp.concatenate([out_other, out_keep], axis=1),
    )


def fast_terms(gate_weight, lift_weight, down_weight, key_heads, value_heads, rates_here):
    pre_gate = jnp.einsum(
        "hcf,hft->hct", gate_weight, key_heads, preferred_element_type=jnp.float32
    )
    pre_lift = jnp.einsum(
        "hcf,hft->hct", lift_weight, key_heads, preferred_element_type=jnp.float32
    )
    sigmoid_gate = jax.nn.sigmoid(pre_gate)
    silu_gate = pre_gate * sigmoid_gate
    hidden = (silu_gate * pre_lift).astype(jnp.bfloat16)
    target = (-(value_heads.astype(jnp.float32) * rates_here[:, None, :])).astype(jnp.bfloat16)
    grad_down = jnp.einsum("hft,hct->hfc", target, hidden, preferred_element_type=jnp.float32)
    back_hidden = jnp.einsum(
        "hfc,hft->hct", down_weight, target, preferred_element_type=jnp.float32
    )
    back_lift = (back_hidden * silu_gate).astype(jnp.bfloat16)
    back_gate = (
        back_hidden * pre_lift * sigmoid_gate * (1.0 + pre_gate * (1.0 - sigmoid_gate))
    ).astype(jnp.bfloat16)
    grad_gate = jnp.einsum("hct,hft->hcf", back_gate, key_heads, preferred_element_type=jnp.float32)
    grad_lift = jnp.einsum("hct,hft->hcf", back_lift, key_heads, preferred_element_type=jnp.float32)
    return (grad_gate, grad_lift, grad_down)


def scaled_start(rounded):
    widened = rounded.astype(jnp.float32)
    norm_val = jnp.sqrt(jnp.sum(jnp.square(widened), axis=(1, 2), keepdims=True) + EPS)
    return stored(widened / norm_val)


def starting(grad_gate, grad_lift, grad_down):
    sum_gate, sum_lift, sum_down = lax.psum((grad_gate, grad_lift, grad_down), "wide")
    return (
        scaled_start(stored(sum_gate)),
        scaled_start(stored(sum_lift)),
        scaled_start(stored(sum_down)),
    )


def orthogonal(current):
    for _ in range(NS_ITERS):
        gram_mat = jnp.einsum(
            "hrc,hrd->hcd", current, current, preferred_element_type=jnp.float32
        ).astype(jnp.bfloat16)
        lifted = stored(
            jnp.einsum("hrc,hcd->hrd", current, gram_mat, preferred_element_type=jnp.float32)
        )
        current = stored(
            COEF_A * current.astype(jnp.float32)
            + COEF_B * lifted.astype(jnp.float32)
            + COEF_C
            * jnp.einsum("hrc,hcd->hrd", lifted, gram_mat, preferred_element_type=jnp.float32)
        )
    return current


def refreshed(weight, ortho):
    initial = weight.astype(jnp.float32)
    moved_rows = initial - ortho.astype(jnp.float32)
    wanted = jnp.sqrt(jnp.mean(jnp.square(initial), axis=-1, keepdims=True) + EPS)
    present = jnp.sqrt(jnp.mean(jnp.square(moved_rows), axis=-1, keepdims=True) + EPS)
    return (moved_rows * (wanted / present)).astype(jnp.bfloat16)


def fast_group(
    gate_weight, lift_weight, down_weight, query_heads, key_heads, value_heads, rates_here
):
    grad_gate, grad_lift, grad_down = fast_terms(
        gate_weight, lift_weight, down_weight, key_heads, value_heads, rates_here
    )
    start_gate, start_lift, start_down = starting(grad_gate, grad_lift, grad_down)
    fresh_gate = refreshed(gate_weight, orthogonal(start_gate))
    fresh_lift = refreshed(lift_weight, orthogonal(start_lift))
    fresh_down = refreshed(down_weight, orthogonal(start_down))
    query_gate = jnp.einsum(
        "hcf,hft->hct", fresh_gate, query_heads, preferred_element_type=jnp.float32
    )
    query_lift = jnp.einsum(
        "hcf,hft->hct", fresh_lift, query_heads, preferred_element_type=jnp.float32
    )
    query_hidden = (jax.nn.silu(query_gate) * query_lift).astype(jnp.bfloat16)
    return jnp.einsum(
        "hfc,hct->hft", fresh_down, query_hidden, preferred_element_type=jnp.float32
    ).astype(jnp.bfloat16)


def attend_body(q_ref, kp_ref, vp_ref, kc_ref, vc_ref, *rest, block, window):
    cached = len(rest) > 3
    o_ref, kt_ref, v_ref = rest[-3:]
    hd = q_ref.shape[0]
    scale = LOG2E / math.sqrt(hd)

    def place(k, v, at):
        turned = k[...].T
        kt_ref[at : at + window, :hd] = turned
        kt_ref[at : at + window, hd:] = turned
        v_ref[:hd, at : at + window] = v[...]

    if cached:
        leading = lax.axis_index("narrow") == 0

        @pl.when(leading)
        def _():
            place(*rest[:2], 0)

        @pl.when(jnp.logical_not(leading))
        def _():
            place(kp_ref, vp_ref, 0)

    else:
        place(kp_ref, vp_ref, 0)
    place(kc_ref, vc_ref, window)
    v_ref[hd:, :] = jnp.ones((v_ref.shape[0] - hd, 2 * window), jnp.bfloat16)
    rows = lax.broadcasted_iota(jnp.int32, (block, block), 0)
    cols = lax.broadcasted_iota(jnp.int32, (block, block), 1)
    first = rows > cols
    inner = window // block

    def scores(b):
        q = q_ref[:, b * block : (b + 1) * block].astype(jnp.float32) * scale
        high = q.astype(jnp.bfloat16)
        low = (q - high.astype(jnp.float32)).astype(jnp.bfloat16)
        pair = jnp.concatenate([high, low], axis=0)
        parts = [
            jnp.dot(
                kt_ref[(b + j) * block : (b + j + 1) * block, :],
                pair,
                preferred_element_type=jnp.float32,
            )
            for j in range(inner + 1)
        ]
        return [jnp.where(first, parts[0], parts[inner])] + parts[1:inner]

    def blend(b, parts):
        top = functools.reduce(jnp.maximum, parts)
        top = jnp.max(top, axis=0, keepdims=True)
        raised = [jnp.exp2(part - top).astype(jnp.bfloat16) for part in parts]
        zero = jnp.zeros_like(raised[0])
        ends = jnp.where(first, raised[0], zero), jnp.where(first, zero, raised[0])
        weights = jnp.concatenate([ends[0]] + raised[1:] + [ends[1]], axis=0)
        span = v_ref[:, b * block : (b + inner + 1) * block]
        out = jnp.dot(span, weights, preferred_element_type=jnp.float32)
        o_ref[:, b * block : (b + 1) * block] = (out[:hd] * (1.0 / out[hd : hd + 1])).astype(
            jnp.bfloat16
        )

    ready = scores(0)
    for b in range(1, inner):
        following = scores(b)
        blend(b - 1, ready)
        ready = following
    blend(inner - 1, ready)


def attend_scratch():
    return [
        pltpu.VMEM((2 * WINDOW, 2 * HEAD_SIZE), jnp.bfloat16),
        pltpu.VMEM((HEAD_SIZE + 16, 2 * WINDOW), jnp.bfloat16),
    ]


def attend_late(queries, keys, values):
    features, tokens = queries.shape
    heads, chunks = features // HEAD_SIZE, tokens // WINDOW - 1
    here = pl.BlockSpec((HEAD_SIZE, WINDOW), lambda h, c: (h, c + 1))
    before = pl.BlockSpec((HEAD_SIZE, WINDOW), lambda h, c: (h, c))
    return pl.pallas_call(
        functools.partial(attend_body, block=min(256, WINDOW), window=WINDOW),
        out_shape=jax.ShapeDtypeStruct((features, tokens), jnp.bfloat16),
        grid=(heads, chunks),
        in_specs=[here, before, before, here, here],
        out_specs=here,
        scratch_shapes=attend_scratch(),
        cost_estimate=pl.CostEstimate(
            flops=5 * features * chunks * WINDOW**2,
            bytes_accessed=10 * features * chunks * WINDOW,
            transcendentals=heads * chunks * WINDOW**2,
        ),
        name="attend_late",
        compiler_params=pltpu.CompilerParams(vmem_limit_bytes=VMEM_GRANT),
    )(queries, keys, values, keys, values)


def attend_early(queries, keys, values, prior, cache_keys, cache_values, late, part):
    features, tokens = queries.shape
    heads = prior.shape[1] // HEAD_SIZE
    here = pl.BlockSpec((HEAD_SIZE, WINDOW), lambda h: (h + part * heads, 0))
    prior_keys = pl.BlockSpec((None, HEAD_SIZE, WINDOW), lambda h: (0, h, 0))
    prior_values = pl.BlockSpec((None, HEAD_SIZE, WINDOW), lambda h: (1, h, 0))
    body = functools.partial(attend_body, block=min(256, WINDOW), window=WINDOW)

    def early_body(*refs):
        body(*refs[:7], *refs[8:])

    return pl.pallas_call(
        early_body,
        out_shape=jax.ShapeDtypeStruct((features, tokens), jnp.bfloat16),
        grid=(heads,),
        in_specs=[here, prior_keys, prior_values, here, here, here, here]
        + [pl.BlockSpec(memory_space=pl.ANY)],
        out_specs=here,
        scratch_shapes=attend_scratch(),
        input_output_aliases={7: 0},
        cost_estimate=pl.CostEstimate(
            flops=5 * heads * HEAD_SIZE * WINDOW**2,
            bytes_accessed=14 * heads * HEAD_SIZE * WINDOW,
            transcendentals=heads * WINDOW**2,
        ),
        name="attend_early",
        compiler_params=pltpu.CompilerParams(vmem_limit_bytes=VMEM_GRANT),
    )(queries, prior, prior, keys, values, cache_keys, cache_values, late)


def anywhere(count):
    return [pl.BlockSpec(memory_space=pl.ANY)] * count


def half_rows(part, half):
    return pl.ds(pl.multiple_of(part * half, half), half)


def prepare_body(gate_ref, lift_ref, down_ref, own_ref, other_ref, w_ref, out_ref, sem):
    owned = gate_ref.shape[0]
    local = lax.axis_index("wide") % owned
    side = lax.axis_index("narrow") % 2
    half = own_ref.shape[1]
    copies = [
        pltpu.make_async_copy(source.at[local], w_ref.at[place], sem.at[0, place])
        for place, source in enumerate((down_ref, gate_ref, lift_ref))
    ]
    for copy in copies:
        copy.start()
    leaving = []
    copies[0].wait()
    out_ref[...] = w_ref[0].T
    for order, (place, source) in enumerate(((2, out_ref), (0, w_ref.at[1]), (1, w_ref.at[2]))):
        if order:
            copies[order].wait()
        for turn, (target, part) in enumerate(((own_ref, side), (other_ref, 1 - side))):
            leaving.append(
                pltpu.make_async_copy(
                    source.at[half_rows(part, half)], target.at[place], sem.at[1 + turn, place]
                )
            )
            leaving[-1].start()
    for copy in leaving:
        copy.wait()


def prepare(gate_fast, lift_fast, down_fast):
    _, hidden_rows, features = gate_fast.shape
    shape = (3, hidden_rows // 2, features)
    return pl.pallas_call(
        prepare_body,
        out_shape=(jax.ShapeDtypeStruct(shape, jnp.bfloat16),) * 2,
        in_specs=anywhere(3),
        out_specs=tuple(anywhere(2)),
        scratch_shapes=[
            pltpu.VMEM((3, hidden_rows, features), jnp.bfloat16),
            pltpu.VMEM((hidden_rows, features), jnp.bfloat16),
            pltpu.SemaphoreType.DMA((3, 3)),
        ],
        cost_estimate=pl.CostEstimate(
            flops=0, bytes_accessed=12 * hidden_rows * features, transcendentals=0
        ),
        name="prepare",
        compiler_params=pltpu.CompilerParams(vmem_limit_bytes=VMEM_GRANT),
    )(gate_fast, lift_fast, down_fast)


def stage_body(key_ref, value_ref, rate_ref, target_ref, *refs):
    end_refs, (held_ref, values_ref, made_ref, sem, sem_end) = refs[:-5], refs[-5:]
    features, tokens = key_ref.shape
    rows, window = end_refs[0].shape[1:]
    step = HEAD_SIZE
    last = slice(tokens - window, tokens)
    begin = pl.multiple_of(lax.axis_index("narrow") * tokens, tokens)
    rates = -rate_ref[pl.ds(lax.axis_index("wide"), 1), pl.ds(begin, tokens)]
    values = [
        pltpu.make_async_copy(
            value_ref.at[at : at + step], values_ref.at[at : at + step], sem.at[0, at // step]
        )
        for at in range(0, features, step)
    ]
    keys = [
        pltpu.make_async_copy(
            key_ref.at[part * rows : (part + 1) * rows, last], held_ref.at[part], sem_end.at[0, part]
        )
        for part in range(len(end_refs))
    ]
    for copy in values + keys:
        copy.start()
    leaving = []

    def leave(source, target, mark):
        leaving.append(pltpu.make_async_copy(source, target, mark))
        leaving[-1].start()

    for place, copy in enumerate(values):
        at = slice(place * step, (place + 1) * step)
        copy.wait()
        made_ref[at] = (values_ref[at].astype(jnp.float32) * rates).astype(jnp.bfloat16)
        leave(made_ref.at[at], target_ref.at[at], sem.at[1, place])
    for part, end_ref in enumerate(end_refs):
        leave(
            values_ref.at[part * rows : (part + 1) * rows, last], end_ref.at[1], sem_end.at[1, part]
        )
        keys[part].wait()
        leave(held_ref.at[part], end_ref.at[0], sem_end.at[2, part])
    for copy in leaving:
        copy.wait()


def stage(keys, values, rates, parts):
    features, tokens = keys.shape
    rows = features // parts
    return pl.pallas_call(
        stage_body,
        out_shape=(jax.ShapeDtypeStruct((features, tokens), jnp.bfloat16),)
        + (jax.ShapeDtypeStruct((2, rows, WINDOW), jnp.bfloat16),) * parts,
        in_specs=anywhere(2) + [pl.BlockSpec(memory_space=pltpu.VMEM)],
        out_specs=tuple(anywhere(1 + parts)),
        scratch_shapes=[
            pltpu.VMEM((parts, rows, WINDOW), jnp.bfloat16),
            pltpu.VMEM((features, tokens), jnp.bfloat16),
            pltpu.VMEM((features, tokens), jnp.bfloat16),
            pltpu.SemaphoreType.DMA((2, features // HEAD_SIZE)),
            pltpu.SemaphoreType.DMA((3, parts)),
        ],
        cost_estimate=pl.CostEstimate(
            flops=features * tokens,
            bytes_accessed=4 * features * tokens + 8 * features * WINDOW,
            transcendentals=0,
        ),
        name="stage",
        compiler_params=pltpu.CompilerParams(vmem_limit_bytes=VMEM_GRANT),
    )(keys, values, rates)


def sums_body(*refs, owned, block):
    sources = refs[:-12]
    (
        key_ref, target_ref, pair_key_ref, pair_target_ref,
        send_ref, pack_ref,
        keys_ref, targets_ref, hidden_ref, back_ref, sem, sem_in,
    ) = refs[-12:]
    _, tokens = key_ref.shape
    half = pack_ref.shape[1]
    count = tokens // block
    role = lax.axis_index("narrow") ^ (lax.axis_index("wide") // owned)

    def moved(keys, targets, index, slot):
        source = slice(index * block, (index + 1) * block)
        place = slice(slot * block, (slot + 1) * block)
        return (
            pltpu.make_async_copy(keys.at[:, source], keys_ref.at[:, place], sem_in.at[0, slot]),
            pltpu.make_async_copy(
                targets.at[:, source], targets_ref.at[:, place], sem_in.at[1, slot]
            ),
        )

    for place, source in enumerate(sources):

        @pl.when(role == place)
        def _(source=source):
            pltpu.make_async_copy(source, pack_ref, sem).start()

    arrivals = [moved(key_ref, target_ref, index, index) for index in range(count)]
    arrivals += [moved(pair_key_ref, pair_target_ref, index, count + index) for index in range(count)]
    for copies in arrivals:
        for copy in copies:
            copy.start()
    pltpu.make_async_copy(sources[0], pack_ref, sem).wait()
    gate_lift = jnp.concatenate([pack_ref[0] * jnp.bfloat16(0.5), pack_ref[1]], axis=0)
    down = pack_ref[2]

    def multiply(slot):
        for copy in arrivals[slot]:
            copy.wait()
        at = slice(slot * block, (slot + 1) * block)
        pre = jnp.dot(gate_lift, keys_ref[:, at], preferred_element_type=jnp.float32)
        back_hidden = jnp.dot(down, targets_ref[:, at], preferred_element_type=jnp.float32)
        return pre, back_hidden

    def combine(slot, pre, back_hidden):
        at = slice(slot * block, (slot + 1) * block)
        half_gate = pre[:half]
        pre_lift = pre[half:]
        twice = jnp.tanh(half_gate) + 1.0
        silu_gate = half_gate * twice
        hidden_ref[:, at] = (silu_gate * pre_lift).astype(jnp.bfloat16)
        slope = twice + silu_gate * (2.0 - twice)
        back_ref[:half, at] = (back_hidden * pre_lift * slope).astype(jnp.bfloat16)
        back_ref[half:, at] = (back_hidden * silu_gate).astype(jnp.bfloat16)

    for slot in range(2 * count):
        combine(slot, *multiply(slot))
    contract = (((1,), (1,)), ((), ()))
    sums = lax.dot_general(
        back_ref[...], keys_ref[...], contract, preferred_element_type=jnp.float32
    )
    down_sums = lax.dot_general(
        hidden_ref[...], targets_ref[...], contract, preferred_element_type=jnp.float32
    )
    for place, value in enumerate((sums[:half] * 0.5, sums[half:], down_sums)):
        send_ref[place] = value.astype(jnp.bfloat16)


def fast_sums(sources, keys, targets, pair_keys, pair_targets, owned):
    features, tokens = keys.shape
    shape = sources[0].shape
    half = shape[1]
    block = tokens
    resident = pl.BlockSpec(memory_space=pltpu.VMEM)
    return pl.pallas_call(
        functools.partial(sums_body, owned=owned, block=block),
        out_shape=(jax.ShapeDtypeStruct(shape, jnp.bfloat16),) * 2,
        in_specs=anywhere(len(sources) + 4),
        out_specs=(resident,) * 2,
        scratch_shapes=[
            pltpu.VMEM((features, 2 * tokens), jnp.bfloat16),
            pltpu.VMEM((features, 2 * tokens), jnp.bfloat16),
            pltpu.VMEM((half, 2 * tokens), jnp.bfloat16),
            pltpu.VMEM((2 * half, 2 * tokens), jnp.bfloat16),
            pltpu.SemaphoreType.DMA(()),
            pltpu.SemaphoreType.DMA((2, 2 * tokens // block)),
        ],
        cost_estimate=pl.CostEstimate(
            flops=24 * half * features * tokens,
            bytes_accessed=8 * features * tokens + 6 * 3 * half * features,
            transcendentals=2 * half * tokens,
        ),
        name="fast_sums",
        compiler_params=pltpu.CompilerParams(vmem_limit_bytes=VMEM_GRANT),
    )(*sources, keys, targets, pair_keys, pair_targets)


def recall_body(
    mine_ref, other_ref, far_ref, other_far_ref, pack_ref, pair_pack_ref, query_ref, out_ref,
    w_ref, near_sums_ref, far_sums_ref, fresh_ref, turned_ref, sem,
):
    half = mine_ref.shape[1]
    hidden_rows, features = fresh_ref.shape[1:]
    nt = (((1,), (1,)), ((), ()))

    @pl.when(pl.program_id(0) == 0)
    def _():
        side = lax.axis_index("narrow") % 2

        def arriving(matrix):
            moves = (
                (mine_ref, near_sums_ref, side),
                (other_ref, near_sums_ref, 1 - side),
                (far_ref, far_sums_ref, side),
                (other_far_ref, far_sums_ref, 1 - side),
            )
            return [
                pltpu.make_async_copy(
                    source.at[matrix],
                    target.at[matrix, half_rows(part, half)],
                    sem.at[place, matrix],
                )
                for place, (source, target, part) in enumerate(moves)
            ]

        sums = [arriving(matrix) for matrix in range(3)]
        weights = [
            pltpu.make_async_copy(source, w_ref.at[:, half_rows(part, half)], sem.at[4, place])
            for place, (source, part) in enumerate(((pack_ref, side), (pair_pack_ref, 1 - side)))
        ]
        for copies in sums + [weights]:
            for copy in copies:
                copy.start()
        rows = lax.broadcasted_iota(jnp.int32, (hidden_rows, features), 0)
        cols = lax.broadcasted_iota(jnp.int32, (hidden_rows, features), 1)
        diagonal = rows == cols
        rounded, gram, scale = [], [], []
        for matrix, copies in enumerate(sums):
            for copy in copies:
                copy.wait()
            summed = near_sums_ref[matrix].astype(jnp.float32) + far_sums_ref[matrix].astype(
                jnp.float32
            )
            x = summed.astype(jnp.bfloat16)
            product = lax.dot_general(x, x, nt, preferred_element_type=jnp.float32)
            trace = jnp.sum(jnp.where(diagonal, product, 0.0), axis=0, keepdims=True)
            scale.append(lax.rsqrt(jnp.sum(trace, axis=1, keepdims=True) + EPS))
            rounded.append(x)
            gram.append((product * (scale[-1] * scale[-1])).astype(jnp.bfloat16))
        current = rounded
        for sweep_index in range(NS_ITERS):
            if sweep_index:
                scale = [1.0] * 3
                gram = [
                    lax.dot_general(x, x, nt, preferred_element_type=jnp.float32).astype(
                        jnp.bfloat16
                    )
                    for x in current
                ]
            lifted = [
                jnp.dot(g, x, preferred_element_type=jnp.float32).astype(jnp.bfloat16)
                for x, g in zip(current, gram)
            ]
            current = [
                (
                    (COEF_A * r) * x.astype(jnp.float32)
                    + (COEF_B * r) * y.astype(jnp.float32)
                    + (COEF_C * r) * jnp.dot(g, y, preferred_element_type=jnp.float32)
                ).astype(jnp.bfloat16)
                for x, y, g, r in zip(current, lifted, gram, scale)
            ]
        for copy in weights:
            copy.wait()
        for i in range(3):
            axis = 0 if i == 2 else 1
            initial = w_ref[i].astype(jnp.float32)
            moved = initial - current[i].astype(jnp.float32)
            wanted = jnp.mean(jnp.square(initial), axis=axis, keepdims=True) + EPS
            present = jnp.mean(jnp.square(moved), axis=axis, keepdims=True) + EPS
            fresh = (moved * (wanted * lax.rsqrt(wanted * present))).astype(jnp.bfloat16)
            if i == 2:
                turned_ref[...] = fresh.T
            else:
                fresh_ref[i] = fresh

    pre = jnp.dot(
        fresh_ref[...].reshape(2 * hidden_rows, features),
        query_ref[...],
        preferred_element_type=jnp.float32,
    )
    gate = 0.5 * pre[:hidden_rows]
    hidden = (gate * (jnp.tanh(gate) + 1.0) * pre[hidden_rows:]).astype(jnp.bfloat16)
    out_ref[...] = jnp.dot(turned_ref[...], hidden, preferred_element_type=jnp.float32).astype(
        jnp.bfloat16
    )


def fast_recall(sums, packs, queries):
    features, tokens = queries.shape
    half = packs[0].shape[1]
    hidden_rows = 2 * half
    block = min(1024, tokens)
    piece = pl.BlockSpec((features, block), lambda i: (0, i))
    return pl.pallas_call(
        recall_body,
        out_shape=jax.ShapeDtypeStruct((features, tokens), jnp.bfloat16),
        grid=(tokens // block,),
        in_specs=anywhere(6) + [piece],
        out_specs=piece,
        scratch_shapes=[
            pltpu.VMEM((3, hidden_rows, features), jnp.bfloat16),
            pltpu.VMEM((3, hidden_rows, features), jnp.bfloat16),
            pltpu.VMEM((3, hidden_rows, features), jnp.bfloat16),
            pltpu.VMEM((2, hidden_rows, features), jnp.bfloat16),
            pltpu.VMEM((features, hidden_rows), jnp.bfloat16),
            pltpu.SemaphoreType.DMA((5, 3)),
        ],
        cost_estimate=pl.CostEstimate(
            flops=6 * hidden_rows * features * tokens + 18 * NS_ITERS * hidden_rows * features**2,
            bytes_accessed=4 * features * tokens + 12 * hidden_rows * features,
            transcendentals=hidden_rows * tokens,
        ),
        name="fast_recall",
        compiler_params=pltpu.CompilerParams(vmem_limit_bytes=VMEM_GRANT),
    )(*sums, *packs, queries)


def in_place(query_states, key_states, value_states, cache_keys, cache_values, gate_fast, *rest):
    features, tok_count = query_states.shape
    narrow_count = lax.axis_size("narrow")
    return (
        features == FD
        and gate_fast.shape[1:] == (FD, FD)
        and features % HEAD_SIZE == 0
        and tok_count % WINDOW == 0
        and tok_count >= 2 * WINDOW
        and narrow_count >= 4
        and narrow_count & (narrow_count - 1) == 0
    )


def in_place_plan(
    query_states,
    key_states,
    value_states,
    cache_keys,
    cache_values,
    gate_fast,
    lift_fast,
    down_fast,
    token_rates,
):
    wide_count = lax.axis_size("wide")
    narrow_count = lax.axis_size("narrow")
    owned = gate_fast.shape[0]

    def from_owner(value, step):
        pairs = []
        for wide in range(wide_count):
            start = wide * narrow_count
            owner = wide // owned
            pairs.append((start + owner, start + (owner ^ step)))
        return lax.ppermute(value, ("wide", "narrow"), pairs)

    own, other = prepare(gate_fast, lift_fast, down_fast)
    arrivals = {}
    for step in sorted(range(1, narrow_count), key=lambda step: step < 2):
        arrivals[step] = from_owner((own, other)[step % 2], step)
    pair_keys = swapped(key_states, "narrow", 0)
    parts = 2
    targets, *ends = stage(key_states, value_states, token_rates, parts)
    pair_targets = swapped(targets, "narrow", 0)
    attended = attend_late(query_states, key_states, value_states)
    sources = [own] + [arrivals[step] for step in range(1, narrow_count)]
    sources, attended, ends = lax.optimization_barrier((sources, attended, ends))
    prior = []
    for end in ends:
        prior.append(from_behind(end, "narrow", 1))
    near, pack = fast_sums(sources, key_states, targets, pair_keys, pair_targets, owned)
    distances = range(1, narrow_count.bit_length() - 1)
    for distance in distances:
        far = swapped(near, "narrow", distance)
        if distance != distances[-1]:
            near = stored(near.astype(jnp.float32) + far.astype(jnp.float32))
    pair_pack = swapped(pack, "narrow", 0)
    pair_near = swapped(near, "narrow", 0)
    pair_far = swapped(far, "narrow", 0)
    for part, before in enumerate(prior):
        attended = attend_early(
            query_states, key_states, value_states, before, cache_keys, cache_values, attended, part
        )
    recalled = fast_recall((near, pair_near, far, pair_far), (pack, pair_pack), query_states)
    return (attended, recalled)


def spread_plan(
    query_states,
    key_states,
    value_states,
    cache_keys,
    cache_values,
    gate_fast,
    lift_fast,
    down_fast,
    token_rates,
):
    features, tok_count = query_states.shape
    edge_cols = jnp.stack(
        [key_states[:, tok_count - WINDOW :], value_states[:, tok_count - WINDOW :]]
    )
    arrived = from_behind(edge_cols, "narrow", 1)
    leading = lax.axis_index("narrow") == 0
    prior_cols = jnp.where(leading, jnp.stack([cache_keys, cache_values]), arrived)
    ext_keys = jnp.concatenate([prior_cols[0], key_states], axis=1)
    ext_values = jnp.concatenate([prior_cols[1], value_states], axis=1)
    if features % HEAD_SIZE == 0:
        attended = attend_local(query_states, ext_keys, ext_values, 0)
    else:
        attended = attend_paired(query_states, ext_keys, ext_values)
    query_fast, key_fast, value_fast = (
        lax.all_to_all(
            lax.all_to_all(query_states, "wide", split_axis=1, concat_axis=0, tiled=True),
            "narrow",
            split_axis=0,
            concat_axis=1,
            tiled=True,
        ),
        lax.all_to_all(
            lax.all_to_all(key_states, "wide", split_axis=1, concat_axis=0, tiled=True),
            "narrow",
            split_axis=0,
            concat_axis=1,
            tiled=True,
        ),
        lax.all_to_all(
            lax.all_to_all(value_states, "wide", split_axis=1, concat_axis=0, tiled=True),
            "narrow",
            split_axis=0,
            concat_axis=1,
            tiled=True,
        ),
    )
    head_count = gate_fast.shape[0]
    wide_count = lax.axis_size("wide")
    narrow_count = lax.axis_size("narrow")
    piece_rows = tok_count // wide_count
    fast_tokens = query_fast.shape[1]
    rate_blocks = token_rates.reshape(token_rates.shape[0], narrow_count, wide_count, piece_rows)
    rates_here = lax.dynamic_slice(
        rate_blocks,
        (lax.axis_index("narrow") * head_count, 0, lax.axis_index("wide"), 0),
        (head_count, narrow_count, 1, piece_rows),
    ).reshape(head_count, fast_tokens)
    query_heads = query_fast.reshape(head_count, FD, fast_tokens)
    key_heads = key_fast.reshape(head_count, FD, fast_tokens)
    value_heads = value_fast.reshape(head_count, FD, fast_tokens)
    recall = fast_group(
        gate_fast, lift_fast, down_fast, query_heads, key_heads, value_heads, rates_here
    )
    recall = recall.reshape(head_count * FD, fast_tokens)
    recalled = lax.all_to_all(
        lax.all_to_all(recall, "narrow", split_axis=1, concat_axis=0, tiled=True),
        "wide",
        split_axis=0,
        concat_axis=1,
        tiled=True,
    )
    return (attended, recalled)


def per_device(*arrays):
    if in_place(*arrays):
        return in_place_plan(*arrays)
    return spread_plan(*arrays)


def solution(mesh):
    in_specs = (
        P("wide", "narrow"),
        P("wide", "narrow"),
        P("wide", "narrow"),
        P("wide", None),
        P("wide", None),
        P("narrow", None, None),
        P("narrow", None, None),
        P("narrow", None, None),
        P(),
    )
    out_specs = (P("wide", "narrow"), P("wide", "narrow"))
    return jax.shard_map(
        per_device, mesh=mesh, in_specs=in_specs, out_specs=out_specs, check_vma=False
    )
```

```python
import functools
import math

import jax
import jax.numpy as jnp
from jax import lax
from jax.experimental import pallas as pl
from jax.experimental.pallas import tpu as pltpu
from jax.sharding import PartitionSpec as P


FD = 512
HEAD_SIZE = 128
WINDOW = 1024
NS_ITERS = 2


EPS = 1e-06
COEF_A = 3.4445
COEF_B = -4.775
COEF_C = 2.0315
LOG2E = math.log2(math.e)
VMEM_GRANT = 67043328


def swapped(array, axis, distance):
    return lax.ppermute(array, axis, [(i, i ^ 1 << distance) for i in range(lax.axis_size(axis))])


def shortened(array):

    def short(part):
        return part.astype(jnp.bfloat16) if part.dtype == jnp.float32 else part

    return jax.tree.map(short, array)


def from_behind(value, axis, steps):
    count = lax.axis_size(axis)
    initial, last = (max(0, -steps), min(count, count - steps))
    return lax.ppermute(value, axis, [(source, source + steps) for source in range(initial, last)])


def stored(value):
    return lax.optimization_barrier(value.astype(jnp.bfloat16))


def attend_local(query_states, ext_keys, ext_values, key_start):
    features, tok_count = query_states.shape
    head_count = features // HEAD_SIZE
    block_rows = min(512, tok_count)
    block_count = tok_count // block_rows
    key_span = WINDOW + block_rows
    scaling = 1.0 / math.sqrt(HEAD_SIZE)
    rows_at = lax.broadcasted_iota(jnp.int32, (block_rows, key_span), 0)
    cols_at = lax.broadcasted_iota(jnp.int32, (block_rows, key_span), 1)
    visible = (cols_at > rows_at) & (cols_at <= rows_at + WINDOW)

    def one_block(block_index):
        offset = block_index * block_rows
        query_part = lax.dynamic_slice_in_dim(query_states, offset, block_rows, 1).reshape(
            head_count, HEAD_SIZE, block_rows
        )
        key_part = lax.dynamic_slice_in_dim(ext_keys, key_start + offset, key_span, 1).reshape(
            head_count, HEAD_SIZE, key_span
        )
        value_part = lax.dynamic_slice_in_dim(ext_values, key_start + offset, key_span, 1).reshape(
            head_count, HEAD_SIZE, key_span
        )
        scores = (
            jnp.einsum("hdq,hdk->hqk", query_part, key_part, preferred_element_type=jnp.float32)
            * scaling
        )
        scores = jnp.where(visible[None], scores, -jnp.inf)
        highest = jnp.max(scores, axis=2, keepdims=True)
        raised = jnp.exp(scores - highest)
        weights = (raised / jnp.sum(raised, axis=2, keepdims=True)).astype(jnp.bfloat16)
        blended = jnp.einsum(
            "hdk,hqk->hdq", value_part, weights, preferred_element_type=jnp.float32
        )
        return blended.astype(jnp.bfloat16).reshape(features, block_rows)

    blocks_out = lax.map(one_block, jnp.arange(block_count, dtype=jnp.int32))
    return jnp.transpose(blocks_out, (1, 0, 2)).reshape(features, tok_count)


def attend_paired(query_states, ext_keys, ext_values):
    features, tok_count = query_states.shape
    half_rows = tok_count // 2
    lower = lax.axis_index("wide") % 2 == 0
    query_send = jnp.where(lower, query_states[:, half_rows:], query_states[:, :half_rows])
    query_keep = jnp.where(lower, query_states[:, :half_rows], query_states[:, half_rows:])
    other_keys, other_values, other_queries = swapped((ext_keys, ext_values, query_send), "wide", 0)
    full_keys = jnp.where(
        lower,
        jnp.concatenate([ext_keys, other_keys], axis=0),
        jnp.concatenate([other_keys, ext_keys], axis=0),
    )
    full_values = jnp.where(
        lower,
        jnp.concatenate([ext_values, other_values], axis=0),
        jnp.concatenate([other_values, ext_values], axis=0),
    )
    full_queries = jnp.where(
        lower,
        jnp.concatenate([query_keep, other_queries], axis=0),
        jnp.concatenate([other_queries, query_keep], axis=0),
    )
    key_start = jnp.where(lower, 0, half_rows).astype(jnp.int32)
    head_out = attend_local(full_queries, full_keys, full_values, key_start)
    out_keep = jnp.where(lower, head_out[:features], head_out[features:])
    out_send = jnp.where(lower, head_out[features:], head_out[:features])
    out_other = swapped(shortened(out_send), "wide", 0).astype(out_send.dtype)
    return jnp.where(
        lower,
        jnp.concatenate([out_keep, out_other], axis=1),
        jnp.concatenate([out_other, out_keep], axis=1),
    )


def fast_terms(gate_weight, lift_weight, down_weight, key_heads, value_heads, rates_here):
    pre_gate = jnp.einsum(
        "hcf,hft->hct", gate_weight, key_heads, preferred_element_type=jnp.float32
    )
    pre_lift = jnp.einsum(
        "hcf,hft->hct", lift_weight, key_heads, preferred_element_type=jnp.float32
    )
    sigmoid_gate = jax.nn.sigmoid(pre_gate)
    silu_gate = pre_gate * sigmoid_gate
    hidden = (silu_gate * pre_lift).astype(jnp.bfloat16)
    target = (-(value_heads.astype(jnp.float32) * rates_here[:, None, :])).astype(jnp.bfloat16)
    grad_down = jnp.einsum("hft,hct->hfc", target, hidden, preferred_element_type=jnp.float32)
    back_hidden = jnp.einsum(
        "hfc,hft->hct", down_weight, target, preferred_element_type=jnp.float32
    )
    back_lift = (back_hidden * silu_gate).astype(jnp.bfloat16)
    back_gate = (
        back_hidden * pre_lift * sigmoid_gate * (1.0 + pre_gate * (1.0 - sigmoid_gate))
    ).astype(jnp.bfloat16)
    grad_gate = jnp.einsum("hct,hft->hcf", back_gate, key_heads, preferred_element_type=jnp.float32)
    grad_lift = jnp.einsum("hct,hft->hcf", back_lift, key_heads, preferred_element_type=jnp.float32)
    return (grad_gate, grad_lift, grad_down)


def scaled_start(rounded):
    widened = rounded.astype(jnp.float32)
    norm_val = jnp.sqrt(jnp.sum(jnp.square(widened), axis=(1, 2), keepdims=True) + EPS)
    return stored(widened / norm_val)


def starting(grad_gate, grad_lift, grad_down):
    sum_gate, sum_lift, sum_down = lax.psum((grad_gate, grad_lift, grad_down), "wide")
    return (
        scaled_start(stored(sum_gate)),
        scaled_start(stored(sum_lift)),
        scaled_start(stored(sum_down)),
    )


def orthogonal(current):
    for _ in range(NS_ITERS):
        gram_mat = jnp.einsum(
            "hrc,hrd->hcd", current, current, preferred_element_type=jnp.float32
        ).astype(jnp.bfloat16)
        lifted = stored(
            jnp.einsum("hrc,hcd->hrd", current, gram_mat, preferred_element_type=jnp.float32)
        )
        current = stored(
            COEF_A * current.astype(jnp.float32)
            + COEF_B * lifted.astype(jnp.float32)
            + COEF_C
            * jnp.einsum("hrc,hcd->hrd", lifted, gram_mat, preferred_element_type=jnp.float32)
        )
    return current


def refreshed(weight, ortho):
    initial = weight.astype(jnp.float32)
    moved_rows = initial - ortho.astype(jnp.float32)
    wanted = jnp.sqrt(jnp.mean(jnp.square(initial), axis=-1, keepdims=True) + EPS)
    present = jnp.sqrt(jnp.mean(jnp.square(moved_rows), axis=-1, keepdims=True) + EPS)
    return (moved_rows * (wanted / present)).astype(jnp.bfloat16)


def fast_group(
    gate_weight, lift_weight, down_weight, query_heads, key_heads, value_heads, rates_here
):
    grad_gate, grad_lift, grad_down = fast_terms(
        gate_weight, lift_weight, down_weight, key_heads, value_heads, rates_here
    )
    start_gate, start_lift, start_down = starting(grad_gate, grad_lift, grad_down)
    fresh_gate = refreshed(gate_weight, orthogonal(start_gate))
    fresh_lift = refreshed(lift_weight, orthogonal(start_lift))
    fresh_down = refreshed(down_weight, orthogonal(start_down))
    query_gate = jnp.einsum(
        "hcf,hft->hct", fresh_gate, query_heads, preferred_element_type=jnp.float32
    )
    query_lift = jnp.einsum(
        "hcf,hft->hct", fresh_lift, query_heads, preferred_element_type=jnp.float32
    )
    query_hidden = (jax.nn.silu(query_gate) * query_lift).astype(jnp.bfloat16)
    return jnp.einsum(
        "hfc,hct->hft", fresh_down, query_hidden, preferred_element_type=jnp.float32
    ).astype(jnp.bfloat16)


def attend_body(q_ref, kp_ref, vp_ref, kc_ref, vc_ref, *rest, block, window):
    cached = len(rest) > 3
    o_ref, kt_ref, v_ref = rest[-3:]
    hd = q_ref.shape[0]
    scale = LOG2E / math.sqrt(hd)

    def place(k, v, at):
        turned = k[...].T
        kt_ref[at : at + window, :hd] = turned
        kt_ref[at : at + window, hd:] = turned
        v_ref[:hd, at : at + window] = v[...]

    if cached:
        leading = lax.axis_index("narrow") == 0

        @pl.when(leading)
        def _():
            place(*rest[:2], 0)

        @pl.when(jnp.logical_not(leading))
        def _():
            place(kp_ref, vp_ref, 0)

    else:
        place(kp_ref, vp_ref, 0)
    place(kc_ref, vc_ref, window)
    v_ref[hd:, :] = jnp.ones((v_ref.shape[0] - hd, 2 * window), jnp.bfloat16)
    rows = lax.broadcasted_iota(jnp.int32, (block, block), 0)
    cols = lax.broadcasted_iota(jnp.int32, (block, block), 1)
    first = rows > cols
    inner = window // block

    def scores(b):
        q = q_ref[:, b * block : (b + 1) * block].astype(jnp.float32) * scale
        high = q.astype(jnp.bfloat16)
        low = (q - high.astype(jnp.float32)).astype(jnp.bfloat16)
        pair = jnp.concatenate([high, low], axis=0)
        parts = [
            jnp.dot(
                kt_ref[(b + j) * block : (b + j + 1) * block, :],
                pair,
                preferred_element_type=jnp.float32,
            )
            for j in range(inner + 1)
        ]
        return [jnp.where(first, parts[0], parts[inner])] + parts[1:inner]

    def blend(b, parts):
        top = functools.reduce(jnp.maximum, parts)
        top = jnp.max(top, axis=0, keepdims=True)
        raised = [jnp.exp2(part - top).astype(jnp.bfloat16) for part in parts]
        zero = jnp.zeros_like(raised[0])
        ends = jnp.where(first, raised[0], zero), jnp.where(first, zero, raised[0])
        weights = jnp.concatenate([ends[0]] + raised[1:] + [ends[1]], axis=0)
        span = v_ref[:, b * block : (b + inner + 1) * block]
        out = jnp.dot(span, weights, preferred_element_type=jnp.float32)
        o_ref[:, b * block : (b + 1) * block] = (out[:hd] * (1.0 / out[hd : hd + 1])).astype(
            jnp.bfloat16
        )

    ready = scores(0)
    for b in range(1, inner):
        following = scores(b)
        blend(b - 1, ready)
        ready = following
    blend(inner - 1, ready)


def attend_scratch():
    return [
        pltpu.VMEM((2 * WINDOW, 2 * HEAD_SIZE), jnp.bfloat16),
        pltpu.VMEM((HEAD_SIZE + 16, 2 * WINDOW), jnp.bfloat16),
    ]


def attend_late(queries, keys, values):
    features, tokens = queries.shape
    heads, chunks = features // HEAD_SIZE, tokens // WINDOW - 1
    here = pl.BlockSpec((HEAD_SIZE, WINDOW), lambda h, c: (h, c + 1))
    before = pl.BlockSpec((HEAD_SIZE, WINDOW), lambda h, c: (h, c))
    return pl.pallas_call(
        functools.partial(attend_body, block=min(256, WINDOW), window=WINDOW),
        out_shape=jax.ShapeDtypeStruct((features, tokens), jnp.bfloat16),
        grid=(heads, chunks),
        in_specs=[here, before, before, here, here],
        out_specs=here,
        scratch_shapes=attend_scratch(),
        cost_estimate=pl.CostEstimate(
            flops=5 * features * chunks * WINDOW**2,
            bytes_accessed=10 * features * chunks * WINDOW,
            transcendentals=heads * chunks * WINDOW**2,
        ),
        name="attend_late",
        compiler_params=pltpu.CompilerParams(vmem_limit_bytes=VMEM_GRANT),
    )(queries, keys, values, keys, values)


def attend_early(queries, keys, values, prior, cache_keys, cache_values, late, part):
    features, tokens = queries.shape
    heads = prior.shape[1] // HEAD_SIZE
    here = pl.BlockSpec((HEAD_SIZE, WINDOW), lambda h: (h + part * heads, 0))
    prior_keys = pl.BlockSpec((None, HEAD_SIZE, WINDOW), lambda h: (0, h, 0))
    prior_values = pl.BlockSpec((None, HEAD_SIZE, WINDOW), lambda h: (1, h, 0))
    body = functools.partial(attend_body, block=min(256, WINDOW), window=WINDOW)

    def early_body(*refs):
        body(*refs[:7], *refs[8:])

    return pl.pallas_call(
        early_body,
        out_shape=jax.ShapeDtypeStruct((features, tokens), jnp.bfloat16),
        grid=(heads,),
        in_specs=[here, prior_keys, prior_values, here, here, here, here]
        + [pl.BlockSpec(memory_space=pl.ANY)],
        out_specs=here,
        scratch_shapes=attend_scratch(),
        input_output_aliases={7: 0},
        cost_estimate=pl.CostEstimate(
            flops=5 * heads * HEAD_SIZE * WINDOW**2,
            bytes_accessed=14 * heads * HEAD_SIZE * WINDOW,
            transcendentals=heads * WINDOW**2,
        ),
        name="attend_early",
        compiler_params=pltpu.CompilerParams(vmem_limit_bytes=VMEM_GRANT),
    )(queries, prior, prior, keys, values, cache_keys, cache_values, late)


def anywhere(count):
    return [pl.BlockSpec(memory_space=pl.ANY)] * count


def half_rows(part, half):
    return pl.ds(pl.multiple_of(part * half, half), half)


def prepare_body(gate_ref, lift_ref, down_ref, own_ref, other_ref, w_ref, out_ref, sem):
    owned = gate_ref.shape[0]
    local = lax.axis_index("wide") % owned
    side = lax.axis_index("narrow") % 2
    half = own_ref.shape[1]
    copies = [
        pltpu.make_async_copy(source.at[local], w_ref.at[place], sem.at[0, place])
        for place, source in enumerate((down_ref, gate_ref, lift_ref))
    ]
    for copy in copies:
        copy.start()
    leaving = []
    copies[0].wait()
    out_ref[...] = w_ref[0].T
    for order, (place, source) in enumerate(((2, out_ref), (0, w_ref.at[1]), (1, w_ref.at[2]))):
        if order:
            copies[order].wait()
        for turn, (target, part) in enumerate(((own_ref, side), (other_ref, 1 - side))):
            leaving.append(
                pltpu.make_async_copy(
                    source.at[half_rows(part, half)], target.at[place], sem.at[1 + turn, place]
                )
            )
            leaving[-1].start()
    for copy in leaving:
        copy.wait()


def prepare(gate_fast, lift_fast, down_fast):
    _, hidden_rows, features = gate_fast.shape
    shape = (3, hidden_rows // 2, features)
    return pl.pallas_call(
        prepare_body,
        out_shape=(jax.ShapeDtypeStruct(shape, jnp.bfloat16),) * 2,
        in_specs=anywhere(3),
        out_specs=tuple(anywhere(2)),
        scratch_shapes=[
            pltpu.VMEM((3, hidden_rows, features), jnp.bfloat16),
            pltpu.VMEM((hidden_rows, features), jnp.bfloat16),
            pltpu.SemaphoreType.DMA((3, 3)),
        ],
        cost_estimate=pl.CostEstimate(
            flops=0, bytes_accessed=12 * hidden_rows * features, transcendentals=0
        ),
        name="prepare",
        compiler_params=pltpu.CompilerParams(vmem_limit_bytes=VMEM_GRANT),
    )(gate_fast, lift_fast, down_fast)


def stage_body(key_ref, value_ref, rate_ref, target_ref, *refs):
    end_refs, (held_ref, values_ref, made_ref, sem, sem_end) = refs[:-5], refs[-5:]
    features, tokens = key_ref.shape
    rows, window = end_refs[0].shape[1:]
    step = HEAD_SIZE
    last = slice(tokens - window, tokens)
    begin = pl.multiple_of(lax.axis_index("narrow") * tokens, tokens)
    rates = -rate_ref[pl.ds(lax.axis_index("wide"), 1), pl.ds(begin, tokens)]
    values = [
        pltpu.make_async_copy(
            value_ref.at[at : at + step], values_ref.at[at : at + step], sem.at[0, at // step]
        )
        for at in range(0, features, step)
    ]
    keys = [
        pltpu.make_async_copy(
            key_ref.at[part * rows : (part + 1) * rows, last], held_ref.at[part], sem_end.at[0, part]
        )
        for part in range(len(end_refs))
    ]
    for copy in values + keys:
        copy.start()
    leaving = []

    def leave(source, target, mark):
        leaving.append(pltpu.make_async_copy(source, target, mark))
        leaving[-1].start()

    for place, copy in enumerate(values):
        at = slice(place * step, (place + 1) * step)
        copy.wait()
        made_ref[at] = (values_ref[at].astype(jnp.float32) * rates).astype(jnp.bfloat16)
        leave(made_ref.at[at], target_ref.at[at], sem.at[1, place])
    for part, end_ref in enumerate(end_refs):
        leave(
            values_ref.at[part * rows : (part + 1) * rows, last], end_ref.at[1], sem_end.at[1, part]
        )
        keys[part].wait()
        leave(held_ref.at[part], end_ref.at[0], sem_end.at[2, part])
    for copy in leaving:
        copy.wait()


def stage(keys, values, rates, parts):
    features, tokens = keys.shape
    rows = features // parts
    return pl.pallas_call(
        stage_body,
        out_shape=(jax.ShapeDtypeStruct((features, tokens), jnp.bfloat16),)
        + (jax.ShapeDtypeStruct((2, rows, WINDOW), jnp.bfloat16),) * parts,
        in_specs=anywhere(2) + [pl.BlockSpec(memory_space=pltpu.VMEM)],
        out_specs=tuple(anywhere(1 + parts)),
        scratch_shapes=[
            pltpu.VMEM((parts, rows, WINDOW), jnp.bfloat16),
            pltpu.VMEM((features, tokens), jnp.bfloat16),
            pltpu.VMEM((features, tokens), jnp.bfloat16),
            pltpu.SemaphoreType.DMA((2, features // HEAD_SIZE)),
            pltpu.SemaphoreType.DMA((3, parts)),
        ],
        cost_estimate=pl.CostEstimate(
            flops=features * tokens,
            bytes_accessed=4 * features * tokens + 8 * features * WINDOW,
            transcendentals=0,
        ),
        name="stage",
        compiler_params=pltpu.CompilerParams(vmem_limit_bytes=VMEM_GRANT),
    )(keys, values, rates)


def sums_body(*refs, owned, block):
    sources = refs[:-15]
    (
        key_ref, target_ref, pair_key_ref, pair_target_ref,
        send_out, pack_out,
        send_ref, pack_ref, keys_ref, targets_ref, hidden_ref, back_ref, sem, sem_in, sem_out,
    ) = refs[-15:]
    _, tokens = key_ref.shape
    half = pack_ref.shape[1]
    count = tokens // block
    role = lax.axis_index("narrow") ^ (lax.axis_index("wide") // owned)

    def moved(keys, targets, index, slot):
        source = slice(index * block, (index + 1) * block)
        place = slice(slot * block, (slot + 1) * block)
        return (
            pltpu.make_async_copy(keys.at[:, source], keys_ref.at[:, place], sem_in.at[0, slot]),
            pltpu.make_async_copy(
                targets.at[:, source], targets_ref.at[:, place], sem_in.at[1, slot]
            ),
        )

    for place, source in enumerate(sources):

        @pl.when(role == place)
        def _(source=source):
            pltpu.make_async_copy(source, pack_ref, sem).start()

    arrivals = [moved(key_ref, target_ref, index, index) for index in range(count)]
    arrivals += [moved(pair_key_ref, pair_target_ref, index, count + index) for index in range(count)]
    for copies in arrivals:
        for copy in copies:
            copy.start()
    pltpu.make_async_copy(sources[0], pack_ref, sem).wait()
    leaving = [pltpu.make_async_copy(pack_ref, pack_out, sem_out.at[3])]
    leaving[0].start()
    gate_lift = jnp.concatenate([pack_ref[0] * jnp.bfloat16(0.5), pack_ref[1]], axis=0)
    down = pack_ref[2]

    def multiply(slot):
        for copy in arrivals[slot]:
            copy.wait()
        at = slice(slot * block, (slot + 1) * block)
        pre = jnp.dot(gate_lift, keys_ref[:, at], preferred_element_type=jnp.float32)
        back_hidden = jnp.dot(down, targets_ref[:, at], preferred_element_type=jnp.float32)
        return pre, back_hidden

    def combine(slot, pre, back_hidden):
        at = slice(slot * block, (slot + 1) * block)
        half_gate = pre[:half]
        pre_lift = pre[half:]
        twice = jnp.tanh(half_gate) + 1.0
        silu_gate = half_gate * twice
        hidden_ref[:, at] = (silu_gate * pre_lift).astype(jnp.bfloat16)
        slope = twice + silu_gate * (2.0 - twice)
        back_ref[:half, at] = (back_hidden * pre_lift * slope).astype(jnp.bfloat16)
        back_ref[half:, at] = (back_hidden * silu_gate).astype(jnp.bfloat16)

    for slot in range(2 * count):
        combine(slot, *multiply(slot))

    def leave(place, value):
        send_ref[place] = value.astype(jnp.bfloat16)
        leaving.append(
            pltpu.make_async_copy(send_ref.at[place], send_out.at[place], sem_out.at[place])
        )
        leaving[-1].start()

    contract = (((1,), (1,)), ((), ()))
    sums = lax.dot_general(
        back_ref[...], keys_ref[...], contract, preferred_element_type=jnp.float32
    )
    leave(0, sums[:half] * 0.5)
    leave(1, sums[half:])
    sums = lax.dot_general(
        hidden_ref[...], targets_ref[...], contract, preferred_element_type=jnp.float32
    )
    leave(2, sums)
    for copy in leaving:
        copy.wait()


def fast_sums(sources, keys, targets, pair_keys, pair_targets, owned):
    features, tokens = keys.shape
    shape = sources[0].shape
    half = shape[1]
    block = tokens
    return pl.pallas_call(
        functools.partial(sums_body, owned=owned, block=block),
        out_shape=(jax.ShapeDtypeStruct(shape, jnp.bfloat16),) * 2,
        in_specs=anywhere(len(sources) + 4),
        out_specs=tuple(anywhere(2)),
        scratch_shapes=[
            pltpu.VMEM(shape, jnp.bfloat16),
            pltpu.VMEM(shape, jnp.bfloat16),
            pltpu.VMEM((features, 2 * tokens), jnp.bfloat16),
            pltpu.VMEM((features, 2 * tokens), jnp.bfloat16),
            pltpu.VMEM((half, 2 * tokens), jnp.bfloat16),
            pltpu.VMEM((2 * half, 2 * tokens), jnp.bfloat16),
            pltpu.SemaphoreType.DMA(()),
            pltpu.SemaphoreType.DMA((2, 2 * tokens // block)),
            pltpu.SemaphoreType.DMA((4,)),
        ],
        cost_estimate=pl.CostEstimate(
            flops=24 * half * features * tokens,
            bytes_accessed=8 * features * tokens + 6 * 3 * half * features,
            transcendentals=2 * half * tokens,
        ),
        name="fast_sums",
        compiler_params=pltpu.CompilerParams(vmem_limit_bytes=VMEM_GRANT),
    )(*sources, keys, targets, pair_keys, pair_targets)


def recall_body(
    mine_ref, other_ref, far_ref, other_far_ref, pack_ref, pair_pack_ref, query_ref, out_ref,
    w_ref, near_sums_ref, far_sums_ref, held_ref, made_ref, sem,
):
    half = mine_ref.shape[1]
    hidden_rows, features = w_ref.shape[1:]
    nt = (((1,), (1,)), ((), ()))

    side = lax.axis_index("narrow") % 2

    def arriving(matrix):
        moves = (
            (mine_ref, near_sums_ref, side),
            (other_ref, near_sums_ref, 1 - side),
            (far_ref, far_sums_ref, side),
            (other_far_ref, far_sums_ref, 1 - side),
        )
        return [
            pltpu.make_async_copy(
                source.at[matrix],
                target.at[matrix, half_rows(part, half)],
                sem.at[place, matrix],
            )
            for place, (source, target, part) in enumerate(moves)
        ]

    sums = [arriving(matrix) for matrix in range(3)]
    weights = [
        pltpu.make_async_copy(source, w_ref.at[:, half_rows(part, half)], sem.at[4, place])
        for place, (source, part) in enumerate(((pack_ref, side), (pair_pack_ref, 1 - side)))
    ]
    queries = pltpu.make_async_copy(query_ref, held_ref, sem.at[5, 2])
    for copies in sums + [weights, [queries]]:
        for copy in copies:
            copy.start()
    rows = lax.broadcasted_iota(jnp.int32, (hidden_rows, features), 0)
    cols = lax.broadcasted_iota(jnp.int32, (hidden_rows, features), 1)
    diagonal = rows == cols
    rounded, gram, scale = [], [], []
    for matrix, copies in enumerate(sums):
        for copy in copies:
            copy.wait()
        summed = near_sums_ref[matrix].astype(jnp.float32) + far_sums_ref[matrix].astype(
            jnp.float32
        )
        x = summed.astype(jnp.bfloat16)
        product = lax.dot_general(x, x, nt, preferred_element_type=jnp.float32)
        trace = jnp.sum(jnp.where(diagonal, product, 0.0), axis=0, keepdims=True)
        scale.append(lax.rsqrt(jnp.sum(trace, axis=1, keepdims=True) + EPS))
        rounded.append(x)
        gram.append((product * (scale[-1] * scale[-1])).astype(jnp.bfloat16))
    current = rounded
    for sweep_index in range(NS_ITERS):
        if sweep_index:
            scale = [1.0] * 3
            gram = [
                lax.dot_general(x, x, nt, preferred_element_type=jnp.float32).astype(
                    jnp.bfloat16
                )
                for x in current
            ]
        lifted = [
            jnp.dot(g, x, preferred_element_type=jnp.float32).astype(jnp.bfloat16)
            for x, g in zip(current, gram)
        ]
        current = [
            (
                (COEF_A * r) * x.astype(jnp.float32)
                + (COEF_B * r) * y.astype(jnp.float32)
                + (COEF_C * r) * jnp.dot(g, y, preferred_element_type=jnp.float32)
            ).astype(jnp.bfloat16)
            for x, y, g, r in zip(current, lifted, gram, scale)
        ]
    for copy in weights:
        copy.wait()

    def fresh(i):
        axis = 0 if i == 2 else 1
        initial = w_ref[i].astype(jnp.float32)
        moved = initial - current[i].astype(jnp.float32)
        wanted = jnp.mean(jnp.square(initial), axis=axis, keepdims=True) + EPS
        present = jnp.mean(jnp.square(moved), axis=axis, keepdims=True) + EPS
        return (moved * (wanted * lax.rsqrt(wanted * present))).astype(jnp.bfloat16)

    queries.wait()
    tokens = held_ref.shape[1]
    block = tokens // 2
    spans = [slice(at, at + block) for at in range(0, tokens, block)]
    fresh_gate = fresh(0)
    gates = [
        jnp.dot(fresh_gate * jnp.bfloat16(0.5), held_ref[:, span], preferred_element_type=jnp.float32)
        for span in spans
    ]
    fresh_lift = fresh(1)
    lifts = [
        jnp.dot(fresh_lift, held_ref[:, span], preferred_element_type=jnp.float32) for span in spans
    ]
    fresh_down = fresh(2).T
    leaving = []
    for place, (span, gate, lift) in enumerate(zip(spans, gates, lifts)):
        hidden = (gate * (jnp.tanh(gate) + 1.0) * lift).astype(jnp.bfloat16)
        made_ref[:, span] = jnp.dot(
            fresh_down, hidden, preferred_element_type=jnp.float32
        ).astype(jnp.bfloat16)
        leaving.append(
            pltpu.make_async_copy(made_ref.at[:, span], out_ref.at[:, span], sem.at[5, place])
        )
        leaving[-1].start()
    for copy in leaving:
        copy.wait()


def fast_recall(sums, packs, queries):
    features, tokens = queries.shape
    half = packs[0].shape[1]
    hidden_rows = 2 * half
    return pl.pallas_call(
        recall_body,
        out_shape=jax.ShapeDtypeStruct((features, tokens), jnp.bfloat16),
        in_specs=anywhere(7),
        out_specs=pl.BlockSpec(memory_space=pl.ANY),
        scratch_shapes=[
            pltpu.VMEM((3, hidden_rows, features), jnp.bfloat16),
            pltpu.VMEM((3, hidden_rows, features), jnp.bfloat16),
            pltpu.VMEM((3, hidden_rows, features), jnp.bfloat16),
            pltpu.VMEM((features, tokens), jnp.bfloat16),
            pltpu.VMEM((features, tokens), jnp.bfloat16),
            pltpu.SemaphoreType.DMA((6, 3)),
        ],
        cost_estimate=pl.CostEstimate(
            flops=6 * hidden_rows * features * tokens + 18 * NS_ITERS * hidden_rows * features**2,
            bytes_accessed=4 * features * tokens + 12 * hidden_rows * features,
            transcendentals=hidden_rows * tokens,
        ),
        name="fast_recall",
        compiler_params=pltpu.CompilerParams(vmem_limit_bytes=VMEM_GRANT),
    )(*sums, *packs, queries)


def in_place(query_states, key_states, value_states, cache_keys, cache_values, gate_fast, *rest):
    features, tok_count = query_states.shape
    narrow_count = lax.axis_size("narrow")
    return (
        features == FD
        and gate_fast.shape[1:] == (FD, FD)
        and features % HEAD_SIZE == 0
        and tok_count % WINDOW == 0
        and tok_count >= 2 * WINDOW
        and narrow_count >= 4
        and narrow_count & (narrow_count - 1) == 0
    )


def in_place_plan(
    query_states,
    key_states,
    value_states,
    cache_keys,
    cache_values,
    gate_fast,
    lift_fast,
    down_fast,
    token_rates,
):
    wide_count = lax.axis_size("wide")
    narrow_count = lax.axis_size("narrow")
    owned = gate_fast.shape[0]

    def from_owner(value, step):
        pairs = []
        for wide in range(wide_count):
            start = wide * narrow_count
            owner = wide // owned
            pairs.append((start + owner, start + (owner ^ step)))
        return lax.ppermute(value, ("wide", "narrow"), pairs)

    own, other = prepare(gate_fast, lift_fast, down_fast)
    arrivals = {}
    for step in sorted(range(1, narrow_count), key=lambda step: step < 2):
        arrivals[step] = from_owner((own, other)[step % 2], step)
    pair_keys = swapped(key_states, "narrow", 0)
    parts = 2
    targets, *ends = stage(key_states, value_states, token_rates, parts)
    pair_targets = swapped(targets, "narrow", 0)
    attended = attend_late(query_states, key_states, value_states)
    sources = [own] + [arrivals[step] for step in range(1, narrow_count)]
    sources, attended, ends = lax.optimization_barrier((sources, attended, ends))
    prior = []
    for end in ends:
        prior.append(from_behind(end, "narrow", 1))
    near, pack = fast_sums(sources, key_states, targets, pair_keys, pair_targets, owned)
    distances = range(1, narrow_count.bit_length() - 1)
    for distance in distances:
        far = swapped(near, "narrow", distance)
        if distance != distances[-1]:
            near = stored(near.astype(jnp.float32) + far.astype(jnp.float32))
    pair_pack = swapped(pack, "narrow", 0)
    pair_near = swapped(near, "narrow", 0)
    pair_far = swapped(far, "narrow", 0)
    for part, before in enumerate(prior):
        attended = attend_early(
            query_states, key_states, value_states, before, cache_keys, cache_values, attended, part
        )
    recalled = fast_recall((near, pair_near, far, pair_far), (pack, pair_pack), query_states)
    return (attended, recalled)


def spread_plan(
    query_states,
    key_states,
    value_states,
    cache_keys,
    cache_values,
    gate_fast,
    lift_fast,
    down_fast,
    token_rates,
):
    features, tok_count = query_states.shape
    edge_cols = jnp.stack(
        [key_states[:, tok_count - WINDOW :], value_states[:, tok_count - WINDOW :]]
    )
    arrived = from_behind(edge_cols, "narrow", 1)
    leading = lax.axis_index("narrow") == 0
    prior_cols = jnp.where(leading, jnp.stack([cache_keys, cache_values]), arrived)
    ext_keys = jnp.concatenate([prior_cols[0], key_states], axis=1)
    ext_values = jnp.concatenate([prior_cols[1], value_states], axis=1)
    if features % HEAD_SIZE == 0:
        attended = attend_local(query_states, ext_keys, ext_values, 0)
    else:
        attended = attend_paired(query_states, ext_keys, ext_values)
    query_fast, key_fast, value_fast = (
        lax.all_to_all(
            lax.all_to_all(query_states, "wide", split_axis=1, concat_axis=0, tiled=True),
            "narrow",
            split_axis=0,
            concat_axis=1,
            tiled=True,
        ),
        lax.all_to_all(
            lax.all_to_all(key_states, "wide", split_axis=1, concat_axis=0, tiled=True),
            "narrow",
            split_axis=0,
            concat_axis=1,
            tiled=True,
        ),
        lax.all_to_all(
            lax.all_to_all(value_states, "wide", split_axis=1, concat_axis=0, tiled=True),
            "narrow",
            split_axis=0,
            concat_axis=1,
            tiled=True,
        ),
    )
    head_count = gate_fast.shape[0]
    wide_count = lax.axis_size("wide")
    narrow_count = lax.axis_size("narrow")
    piece_rows = tok_count // wide_count
    fast_tokens = query_fast.shape[1]
    rate_blocks = token_rates.reshape(token_rates.shape[0], narrow_count, wide_count, piece_rows)
    rates_here = lax.dynamic_slice(
        rate_blocks,
        (lax.axis_index("narrow") * head_count, 0, lax.axis_index("wide"), 0),
        (head_count, narrow_count, 1, piece_rows),
    ).reshape(head_count, fast_tokens)
    query_heads = query_fast.reshape(head_count, FD, fast_tokens)
    key_heads = key_fast.reshape(head_count, FD, fast_tokens)
    value_heads = value_fast.reshape(head_count, FD, fast_tokens)
    recall = fast_group(
        gate_fast, lift_fast, down_fast, query_heads, key_heads, value_heads, rates_here
    )
    recall = recall.reshape(head_count * FD, fast_tokens)
    recalled = lax.all_to_all(
        lax.all_to_all(recall, "narrow", split_axis=1, concat_axis=0, tiled=True),
        "wide",
        split_axis=0,
        concat_axis=1,
        tiled=True,
    )
    return (attended, recalled)


def per_device(*arrays):
    if in_place(*arrays):
        return in_place_plan(*arrays)
    return spread_plan(*arrays)


def solution(mesh):
    in_specs = (
        P("wide", "narrow"),
        P("wide", "narrow"),
        P("wide", "narrow"),
        P("wide", None),
        P("wide", None),
        P("narrow", None, None),
        P("narrow", None, None),
        P("narrow", None, None),
        P(),
    )
    out_specs = (P("wide", "narrow"), P("wide", "narrow"))
    return jax.shard_map(
        per_device, mesh=mesh, in_specs=in_specs, out_specs=out_specs, check_vma=False
    )
```

```python
import functools
import math

import jax
import jax.numpy as jnp
from jax import lax
from jax.experimental import pallas as pl
from jax.experimental.pallas import tpu as pltpu
from jax.sharding import PartitionSpec as P


FD = 512
HEAD_SIZE = 128
WINDOW = 1024
NS_ITERS = 2


EPS = 1e-06
COEF_A = 3.4445
COEF_B = -4.775
COEF_C = 2.0315
LOG2E = math.log2(math.e)
VMEM_GRANT = 67043328


def swapped(array, axis, distance):
    return lax.ppermute(array, axis, [(i, i ^ 1 << distance) for i in range(lax.axis_size(axis))])


def shortened(array):

    def short(part):
        return part.astype(jnp.bfloat16) if part.dtype == jnp.float32 else part

    return jax.tree.map(short, array)


def from_behind(value, axis, steps):
    count = lax.axis_size(axis)
    initial, last = (max(0, -steps), min(count, count - steps))
    return lax.ppermute(value, axis, [(source, source + steps) for source in range(initial, last)])


def stored(value):
    return lax.optimization_barrier(value.astype(jnp.bfloat16))


def attend_local(query_states, ext_keys, ext_values, key_start):
    features, tok_count = query_states.shape
    head_count = features // HEAD_SIZE
    block_rows = min(512, tok_count)
    block_count = tok_count // block_rows
    key_span = WINDOW + block_rows
    scaling = 1.0 / math.sqrt(HEAD_SIZE)
    rows_at = lax.broadcasted_iota(jnp.int32, (block_rows, key_span), 0)
    cols_at = lax.broadcasted_iota(jnp.int32, (block_rows, key_span), 1)
    visible = (cols_at > rows_at) & (cols_at <= rows_at + WINDOW)

    def one_block(block_index):
        offset = block_index * block_rows
        query_part = lax.dynamic_slice_in_dim(query_states, offset, block_rows, 1).reshape(
            head_count, HEAD_SIZE, block_rows
        )
        key_part = lax.dynamic_slice_in_dim(ext_keys, key_start + offset, key_span, 1).reshape(
            head_count, HEAD_SIZE, key_span
        )
        value_part = lax.dynamic_slice_in_dim(ext_values, key_start + offset, key_span, 1).reshape(
            head_count, HEAD_SIZE, key_span
        )
        scores = (
            jnp.einsum("hdq,hdk->hqk", query_part, key_part, preferred_element_type=jnp.float32)
            * scaling
        )
        scores = jnp.where(visible[None], scores, -jnp.inf)
        highest = jnp.max(scores, axis=2, keepdims=True)
        raised = jnp.exp(scores - highest)
        weights = (raised / jnp.sum(raised, axis=2, keepdims=True)).astype(jnp.bfloat16)
        blended = jnp.einsum(
            "hdk,hqk->hdq", value_part, weights, preferred_element_type=jnp.float32
        )
        return blended.astype(jnp.bfloat16).reshape(features, block_rows)

    blocks_out = lax.map(one_block, jnp.arange(block_count, dtype=jnp.int32))
    return jnp.transpose(blocks_out, (1, 0, 2)).reshape(features, tok_count)


def attend_paired(query_states, ext_keys, ext_values):
    features, tok_count = query_states.shape
    half_rows = tok_count // 2
    lower = lax.axis_index("wide") % 2 == 0
    query_send = jnp.where(lower, query_states[:, half_rows:], query_states[:, :half_rows])
    query_keep = jnp.where(lower, query_states[:, :half_rows], query_states[:, half_rows:])
    other_keys, other_values, other_queries = swapped((ext_keys, ext_values, query_send), "wide", 0)
    full_keys = jnp.where(
        lower,
        jnp.concatenate([ext_keys, other_keys], axis=0),
        jnp.concatenate([other_keys, ext_keys], axis=0),
    )
    full_values = jnp.where(
        lower,
        jnp.concatenate([ext_values, other_values], axis=0),
        jnp.concatenate([other_values, ext_values], axis=0),
    )
    full_queries = jnp.where(
        lower,
        jnp.concatenate([query_keep, other_queries], axis=0),
        jnp.concatenate([other_queries, query_keep], axis=0),
    )
    key_start = jnp.where(lower, 0, half_rows).astype(jnp.int32)
    head_out = attend_local(full_queries, full_keys, full_values, key_start)
    out_keep = jnp.where(lower, head_out[:features], head_out[features:])
    out_send = jnp.where(lower, head_out[features:], head_out[:features])
    out_other = swapped(shortened(out_send), "wide", 0).astype(out_send.dtype)
    return jnp.where(
        lower,
        jnp.concatenate([out_keep, out_other], axis=1),
        jnp.concatenate([out_other, out_keep], axis=1),
    )


def fast_terms(gate_weight, lift_weight, down_weight, key_heads, value_heads, rates_here):
    pre_gate = jnp.einsum(
        "hcf,hft->hct", gate_weight, key_heads, preferred_element_type=jnp.float32
    )
    pre_lift = jnp.einsum(
        "hcf,hft->hct", lift_weight, key_heads, preferred_element_type=jnp.float32
    )
    sigmoid_gate = jax.nn.sigmoid(pre_gate)
    silu_gate = pre_gate * sigmoid_gate
    hidden = (silu_gate * pre_lift).astype(jnp.bfloat16)
    target = (-(value_heads.astype(jnp.float32) * rates_here[:, None, :])).astype(jnp.bfloat16)
    grad_down = jnp.einsum("hft,hct->hfc", target, hidden, preferred_element_type=jnp.float32)
    back_hidden = jnp.einsum(
        "hfc,hft->hct", down_weight, target, preferred_element_type=jnp.float32
    )
    back_lift = (back_hidden * silu_gate).astype(jnp.bfloat16)
    back_gate = (
        back_hidden * pre_lift * sigmoid_gate * (1.0 + pre_gate * (1.0 - sigmoid_gate))
    ).astype(jnp.bfloat16)
    grad_gate = jnp.einsum("hct,hft->hcf", back_gate, key_heads, preferred_element_type=jnp.float32)
    grad_lift = jnp.einsum("hct,hft->hcf", back_lift, key_heads, preferred_element_type=jnp.float32)
    return (grad_gate, grad_lift, grad_down)


def scaled_start(rounded):
    widened = rounded.astype(jnp.float32)
    norm_val = jnp.sqrt(jnp.sum(jnp.square(widened), axis=(1, 2), keepdims=True) + EPS)
    return stored(widened / norm_val)


def starting(grad_gate, grad_lift, grad_down):
    sum_gate, sum_lift, sum_down = lax.psum((grad_gate, grad_lift, grad_down), "wide")
    return (
        scaled_start(stored(sum_gate)),
        scaled_start(stored(sum_lift)),
        scaled_start(stored(sum_down)),
    )


def orthogonal(current):
    for _ in range(NS_ITERS):
        gram_mat = jnp.einsum(
            "hrc,hrd->hcd", current, current, preferred_element_type=jnp.float32
        ).astype(jnp.bfloat16)
        lifted = stored(
            jnp.einsum("hrc,hcd->hrd", current, gram_mat, preferred_element_type=jnp.float32)
        )
        current = stored(
            COEF_A * current.astype(jnp.float32)
            + COEF_B * lifted.astype(jnp.float32)
            + COEF_C
            * jnp.einsum("hrc,hcd->hrd", lifted, gram_mat, preferred_element_type=jnp.float32)
        )
    return current


def refreshed(weight, ortho):
    initial = weight.astype(jnp.float32)
    moved_rows = initial - ortho.astype(jnp.float32)
    wanted = jnp.sqrt(jnp.mean(jnp.square(initial), axis=-1, keepdims=True) + EPS)
    present = jnp.sqrt(jnp.mean(jnp.square(moved_rows), axis=-1, keepdims=True) + EPS)
    return (moved_rows * (wanted / present)).astype(jnp.bfloat16)


def fast_group(
    gate_weight, lift_weight, down_weight, query_heads, key_heads, value_heads, rates_here
):
    grad_gate, grad_lift, grad_down = fast_terms(
        gate_weight, lift_weight, down_weight, key_heads, value_heads, rates_here
    )
    start_gate, start_lift, start_down = starting(grad_gate, grad_lift, grad_down)
    fresh_gate = refreshed(gate_weight, orthogonal(start_gate))
    fresh_lift = refreshed(lift_weight, orthogonal(start_lift))
    fresh_down = refreshed(down_weight, orthogonal(start_down))
    query_gate = jnp.einsum(
        "hcf,hft->hct", fresh_gate, query_heads, preferred_element_type=jnp.float32
    )
    query_lift = jnp.einsum(
        "hcf,hft->hct", fresh_lift, query_heads, preferred_element_type=jnp.float32
    )
    query_hidden = (jax.nn.silu(query_gate) * query_lift).astype(jnp.bfloat16)
    return jnp.einsum(
        "hfc,hct->hft", fresh_down, query_hidden, preferred_element_type=jnp.float32
    ).astype(jnp.bfloat16)


def attend_body(
    q_ref, kp_ref, vp_ref, kc_ref, vc_ref, o_ref, kt_ref, v_ref, *, block, window
):
    hd = q_ref.shape[0]
    scale = LOG2E / math.sqrt(hd)

    placed(kp_ref, vp_ref, kt_ref, v_ref, 0)
    placed(kc_ref, vc_ref, kt_ref, v_ref, window)
    v_ref[hd:, :] = jnp.ones((v_ref.shape[0] - hd, 2 * window), jnp.bfloat16)
    rows = lax.broadcasted_iota(jnp.int32, (block, block), 0)
    cols = lax.broadcasted_iota(jnp.int32, (block, block), 1)
    first = rows > cols
    inner = window // block

    def scores(b):
        q = q_ref[:, b * block : (b + 1) * block].astype(jnp.float32) * scale
        high = q.astype(jnp.bfloat16)
        low = (q - high.astype(jnp.float32)).astype(jnp.bfloat16)
        pair = jnp.concatenate([high, low], axis=0)
        parts = [
            jnp.dot(
                kt_ref[(b + j) * block : (b + j + 1) * block, :],
                pair,
                preferred_element_type=jnp.float32,
            )
            for j in range(inner + 1)
        ]
        return [jnp.where(first, parts[0], parts[inner])] + parts[1:inner]

    def blend(b, parts):
        top = functools.reduce(jnp.maximum, parts)
        top = jnp.max(top, axis=0, keepdims=True)
        raised = [jnp.exp2(part - top).astype(jnp.bfloat16) for part in parts]
        zero = jnp.zeros_like(raised[0])
        ends = jnp.where(first, raised[0], zero), jnp.where(first, zero, raised[0])
        weights = jnp.concatenate([ends[0]] + raised[1:] + [ends[1]], axis=0)
        span = v_ref[:, b * block : (b + inner + 1) * block]
        out = jnp.dot(span, weights, preferred_element_type=jnp.float32)
        o_ref[:, b * block : (b + 1) * block] = (out[:hd] * (1.0 / out[hd : hd + 1])).astype(
            jnp.bfloat16
        )

    ready = scores(0)
    for b in range(1, inner):
        following = scores(b)
        blend(b - 1, ready)
        ready = following
    blend(inner - 1, ready)


def attend_scratch():
    return [
        pltpu.VMEM((2 * WINDOW, 2 * HEAD_SIZE), jnp.bfloat16),
        pltpu.VMEM((HEAD_SIZE + 16, 2 * WINDOW), jnp.bfloat16),
    ]


def attend_late(queries, keys, values):
    features, tokens = queries.shape
    heads, chunks = features // HEAD_SIZE, tokens // WINDOW - 1
    here = pl.BlockSpec((HEAD_SIZE, WINDOW), lambda h, c: (h, c + 1))
    before = pl.BlockSpec((HEAD_SIZE, WINDOW), lambda h, c: (h, c))
    return pl.pallas_call(
        functools.partial(attend_body, block=min(256, WINDOW), window=WINDOW),
        out_shape=jax.ShapeDtypeStruct((features, tokens), jnp.bfloat16),
        grid=(heads, chunks),
        in_specs=[here, before, before, here, here],
        out_specs=here,
        scratch_shapes=attend_scratch(),
        cost_estimate=pl.CostEstimate(
            flops=5 * features * chunks * WINDOW**2,
            bytes_accessed=10 * features * chunks * WINDOW,
            transcendentals=heads * chunks * WINDOW**2,
        ),
        name="attend_late",
        compiler_params=pltpu.CompilerParams(vmem_limit_bytes=VMEM_GRANT),
    )(queries, keys, values, keys, values)


def two_term(q_ref, at, scale):
    q = q_ref[:, at].astype(jnp.float32) * scale
    high = q.astype(jnp.bfloat16)
    low = (q - high.astype(jnp.float32)).astype(jnp.bfloat16)
    return jnp.concatenate([high, low], axis=0)


def placed(k, v, kt_ref, v_ref, at):
    hd, width = k.shape
    turned = k[...].T
    kt_ref[at : at + width, :hd] = turned
    kt_ref[at : at + width, hd:] = turned
    v_ref[:hd, at : at + width] = v[...]


def early_body(
    q_ref, kp_ref, vp_ref, kc_ref, vc_ref, ck_ref, cv_ref, _, o_ref, part_ref, top_ref, mass_ref,
    kt_ref, v_ref, *, block,
):
    hd, window = q_ref.shape
    scale = LOG2E / math.sqrt(hd)
    near = kp_ref.shape[1]
    inner = window // block
    missing = (window - near) // block
    leading = lax.axis_index("narrow") == 0

    @pl.when(leading)
    def _():
        placed(ck_ref, cv_ref, kt_ref, v_ref, 0)

    @pl.when(jnp.logical_not(leading))
    def _():
        placed(kp_ref, vp_ref, kt_ref, v_ref, 0)

    placed(kc_ref, vc_ref, kt_ref, v_ref, near)
    v_ref[hd:, :] = jnp.ones((v_ref.shape[0] - hd, v_ref.shape[1]), jnp.bfloat16)
    rows = lax.broadcasted_iota(jnp.int32, (block, block), 0)
    cols = lax.broadcasted_iota(jnp.int32, (block, block), 1)
    first = rows > cols

    def chunk(j):
        return slice((j - missing) * block, (j - missing + 1) * block)

    def scores(b):
        pair = two_term(q_ref, slice(b * block, (b + 1) * block), scale)
        parts = [
            jnp.dot(kt_ref[chunk(j), :], pair, preferred_element_type=jnp.float32)
            for j in range(max(b, missing), b + inner + 1)
        ]
        if b >= missing:
            return [jnp.where(first, parts[0], parts[inner])] + parts[1:inner]
        return parts[:-1] + [jnp.where(first, -jnp.inf, parts[-1])]

    def blend(b, parts):
        top = functools.reduce(jnp.maximum, parts)
        top = jnp.max(top, axis=0, keepdims=True)
        raised = [jnp.exp2(part - top).astype(jnp.bfloat16) for part in parts]
        if b >= missing:
            zero = jnp.zeros_like(raised[0])
            ends = jnp.where(first, raised[0], zero), jnp.where(first, zero, raised[0])
            raised = [ends[0]] + raised[1:] + [ends[1]]
        span = v_ref[:, chunk(max(b, missing)).start : chunk(b + inner).stop]
        out = jnp.dot(span, jnp.concatenate(raised, axis=0), preferred_element_type=jnp.float32)
        if b >= missing:
            at = slice((b - missing) * block, (b - missing + 1) * block)
            o_ref[:, at] = (out[:hd] * (1.0 / out[hd : hd + 1])).astype(jnp.bfloat16)
        else:
            at = slice(b * block, (b + 1) * block)
            part_ref[:, at] = out[:hd]
            top_ref[:, at] = jnp.broadcast_to(top, (top_ref.shape[0], block))
            mass_ref[:, at] = jnp.broadcast_to(out[hd : hd + 1], (top_ref.shape[0], block))

    ready = scores(0)
    for b in range(1, inner):
        following = scores(b)
        blend(b - 1, ready)
        ready = following
    blend(inner - 1, ready)


def attend_early(queries, keys, values, prior, cache_keys, cache_values, late):
    features, tokens = queries.shape
    heads = features // HEAD_SIZE
    near = prior.shape[2]
    far = WINDOW - near
    here = pl.BlockSpec((HEAD_SIZE, WINDOW), lambda h: (h, 0))
    nearer = pl.BlockSpec((HEAD_SIZE, near), lambda h: (h, far // near))
    prior_keys = pl.BlockSpec((None, HEAD_SIZE, near), lambda h: (0, h, 0))
    prior_values = pl.BlockSpec((None, HEAD_SIZE, near), lambda h: (1, h, 0))
    rows = 8
    stats = jax.ShapeDtypeStruct((heads * rows, far), jnp.float32)
    stat = pl.BlockSpec((rows, far), lambda h: (h, 0))
    return pl.pallas_call(
        functools.partial(early_body, block=min(256, near)),
        out_shape=(
            jax.ShapeDtypeStruct((features, tokens), jnp.bfloat16),
            jax.ShapeDtypeStruct((features, far), jnp.float32),
            stats,
            stats,
        ),
        grid=(heads,),
        in_specs=[here, prior_keys, prior_values, here, here, nearer, nearer]
        + [pl.BlockSpec(memory_space=pl.ANY)],
        out_specs=(nearer, pl.BlockSpec((HEAD_SIZE, far), lambda h: (h, 0)), stat, stat),
        scratch_shapes=[
            pltpu.VMEM((near + WINDOW, 2 * HEAD_SIZE), jnp.bfloat16),
            pltpu.VMEM((HEAD_SIZE + 16, near + WINDOW), jnp.bfloat16),
        ],
        input_output_aliases={7: 0},
        cost_estimate=pl.CostEstimate(
            flops=5 * features * WINDOW**2,
            bytes_accessed=14 * features * WINDOW,
            transcendentals=heads * WINDOW**2,
        ),
        name="attend_early",
        compiler_params=pltpu.CompilerParams(vmem_limit_bytes=VMEM_GRANT),
    )(queries, prior, prior, keys, values, cache_keys, cache_values, late)


def last_body(
    q_ref, prior_ref, ck_ref, cv_ref, part_ref, top_ref, mass_ref, _, o_ref,
    held_q, held_k, held_v, held_part, held_top, held_mass, kt_ref, v_ref, made_ref, sem,
    *, block,
):
    features, far = part_ref.shape
    hd = HEAD_SIZE
    heads = features // hd
    scale = LOG2E / math.sqrt(hd)
    missing = far // block
    leading = lax.axis_index("narrow") == 0
    plain = [
        pltpu.make_async_copy(top_ref, held_top, sem.at[0, 0]),
        pltpu.make_async_copy(mass_ref, held_mass, sem.at[0, 1]),
    ]
    arriving = []
    for h in range(heads):
        at = slice(h * hd, (h + 1) * hd)
        keys = pltpu.make_async_copy(prior_ref.at[0, at], held_k.at[at], sem.at[1, h])
        values = pltpu.make_async_copy(prior_ref.at[1, at], held_v.at[at], sem.at[2, h])

        @pl.when(leading)
        def _(at=at, h=h):
            pltpu.make_async_copy(ck_ref.at[at, :far], held_k.at[at], sem.at[1, h]).start()
            pltpu.make_async_copy(cv_ref.at[at, :far], held_v.at[at], sem.at[2, h]).start()

        @pl.when(jnp.logical_not(leading))
        def _(keys=keys, values=values):
            keys.start()
            values.start()

        others = [
            pltpu.make_async_copy(q_ref.at[at, :far], held_q.at[at], sem.at[3, h]),
            pltpu.make_async_copy(part_ref.at[at], held_part.at[at], sem.at[4, h]),
        ]
        for copy in others + (plain if h == 0 else []):
            copy.start()
        arriving.append([keys, values] + others)
    rows = lax.broadcasted_iota(jnp.int32, (block, block), 0)
    cols = lax.broadcasted_iota(jnp.int32, (block, block), 1)
    first = rows > cols
    v_ref[:, hd:, :] = jnp.ones((heads, v_ref.shape[1] - hd, far), jnp.bfloat16)
    leaving = []
    for copy in plain:
        copy.wait()

    def scores(h, b):
        at = slice(h * hd, (h + 1) * hd)
        if b == 0:
            for copy in arriving[h]:
                copy.wait()
            placed(held_k.at[at], held_v.at[at], kt_ref.at[h], v_ref.at[h], 0)
        pair = two_term(held_q.at[at], slice(b * block, (b + 1) * block), scale)
        parts = [
            jnp.dot(
                kt_ref[h, j * block : (j + 1) * block, :], pair, preferred_element_type=jnp.float32
            )
            for j in range(b, missing)
        ]
        return [jnp.where(first, parts[0], -jnp.inf)] + parts[1:]

    def blend(h, b, parts):
        at = slice(h * hd, (h + 1) * hd)
        span = slice(b * block, (b + 1) * block)
        before = held_top[h * 8 : h * 8 + 1, span]
        top = functools.reduce(jnp.maximum, parts)
        top = jnp.maximum(jnp.max(top, axis=0, keepdims=True), before)
        kept = jnp.exp2(before - top)
        weights = jnp.concatenate(
            [jnp.exp2(part - top).astype(jnp.bfloat16) for part in parts], axis=0
        )
        out = jnp.dot(v_ref[h, :, b * block :], weights, preferred_element_type=jnp.float32)
        mass = held_mass[h * 8 : h * 8 + 1, span] * kept + out[hd : hd + 1]
        made_ref[at, span] = ((held_part[at, span] * kept + out[:hd]) * (1.0 / mass)).astype(
            jnp.bfloat16
        )
        if b == missing - 1:
            leaving.append(
                pltpu.make_async_copy(made_ref.at[at], o_ref.at[at, :far], sem.at[5, h])
            )
            leaving[-1].start()

    turns = [(h, b) for h in range(heads) for b in range(missing)]
    ready = scores(*turns[0])
    for turn, ahead in zip(turns, turns[1:]):
        following = scores(*ahead)
        blend(*turn, ready)
        ready = following
    blend(*turns[-1], ready)
    for copy in leaving:
        copy.wait()


def attend_last(queries, prior, cache_keys, cache_values, part, top, mass, early):
    features, tokens = queries.shape
    heads = features // HEAD_SIZE
    far = part.shape[1]
    pieces = pltpu.VMEM((features, far), jnp.bfloat16)
    return pl.pallas_call(
        functools.partial(last_body, block=min(256, far)),
        out_shape=jax.ShapeDtypeStruct((features, tokens), jnp.bfloat16),
        in_specs=[pl.BlockSpec(memory_space=pl.ANY)] * 8,
        out_specs=pl.BlockSpec(memory_space=pl.ANY),
        scratch_shapes=[
            pieces,
            pieces,
            pieces,
            pltpu.VMEM((features, far), jnp.float32),
            pltpu.VMEM(top.shape, jnp.float32),
            pltpu.VMEM(top.shape, jnp.float32),
            pltpu.VMEM((heads, far, 2 * HEAD_SIZE), jnp.bfloat16),
            pltpu.VMEM((heads, HEAD_SIZE + 16, far), jnp.bfloat16),
            pieces,
            pltpu.SemaphoreType.DMA((6, max(heads, 2))),
        ],
        input_output_aliases={7: 0},
        cost_estimate=pl.CostEstimate(
            flops=3 * features * far**2,
            bytes_accessed=14 * features * far,
            transcendentals=heads * far**2,
        ),
        name="attend_last",
        compiler_params=pltpu.CompilerParams(vmem_limit_bytes=VMEM_GRANT),
    )(queries, prior, cache_keys, cache_values, part, top, mass, early)


def anywhere(count):
    return [pl.BlockSpec(memory_space=pl.ANY)] * count


def half_rows(part, half):
    return pl.ds(pl.multiple_of(part * half, half), half)


def prepare_body(gate_ref, lift_ref, down_ref, own_ref, other_ref, w_ref, out_ref, sem):
    owned = gate_ref.shape[0]
    local = lax.axis_index("wide") % owned
    side = lax.axis_index("narrow") % 2
    half = own_ref.shape[1]
    copies = [
        pltpu.make_async_copy(source.at[local], w_ref.at[place], sem.at[0, place])
        for place, source in enumerate((down_ref, gate_ref, lift_ref))
    ]
    for copy in copies:
        copy.start()
    leaving = []
    copies[0].wait()
    out_ref[...] = w_ref[0].T
    for order, (place, source) in enumerate(((2, out_ref), (0, w_ref.at[1]), (1, w_ref.at[2]))):
        if order:
            copies[order].wait()
        for turn, (target, part) in enumerate(((own_ref, side), (other_ref, 1 - side))):
            leaving.append(
                pltpu.make_async_copy(
                    source.at[half_rows(part, half)], target.at[place], sem.at[1 + turn, place]
                )
            )
            leaving[-1].start()
    for copy in leaving:
        copy.wait()


def prepare(gate_fast, lift_fast, down_fast):
    _, hidden_rows, features = gate_fast.shape
    shape = (3, hidden_rows // 2, features)
    return pl.pallas_call(
        prepare_body,
        out_shape=(jax.ShapeDtypeStruct(shape, jnp.bfloat16),) * 2,
        in_specs=anywhere(3),
        out_specs=tuple(anywhere(2)),
        scratch_shapes=[
            pltpu.VMEM((3, hidden_rows, features), jnp.bfloat16),
            pltpu.VMEM((hidden_rows, features), jnp.bfloat16),
            pltpu.SemaphoreType.DMA((3, 3)),
        ],
        cost_estimate=pl.CostEstimate(
            flops=0, bytes_accessed=12 * hidden_rows * features, transcendentals=0
        ),
        name="prepare",
        compiler_params=pltpu.CompilerParams(vmem_limit_bytes=VMEM_GRANT),
    )(gate_fast, lift_fast, down_fast)


def stage_body(key_ref, value_ref, rate_ref, target_ref, *refs):
    end_refs, (held_ref, values_ref, made_ref, sem, sem_end) = refs[:-5], refs[-5:]
    features, tokens = key_ref.shape
    width = end_refs[0].shape[2]
    step = HEAD_SIZE
    lasts = [slice(tokens - (part + 1) * width, tokens - part * width) for part in range(len(end_refs))]
    begin = pl.multiple_of(lax.axis_index("narrow") * tokens, tokens)
    rates = -rate_ref[pl.ds(lax.axis_index("wide"), 1), pl.ds(begin, tokens)]
    values = [
        pltpu.make_async_copy(
            value_ref.at[at : at + step], values_ref.at[at : at + step], sem.at[0, at // step]
        )
        for at in range(0, features, step)
    ]
    keys = [
        pltpu.make_async_copy(
            key_ref.at[:, last], held_ref.at[part], sem_end.at[0, part]
        )
        for part, last in enumerate(lasts)
    ]
    for copy in values + keys:
        copy.start()
    leaving = []

    def leave(source, target, mark):
        leaving.append(pltpu.make_async_copy(source, target, mark))
        leaving[-1].start()

    for place, copy in enumerate(values):
        at = slice(place * step, (place + 1) * step)
        copy.wait()
        made_ref[at] = (values_ref[at].astype(jnp.float32) * rates).astype(jnp.bfloat16)
        leave(made_ref.at[at], target_ref.at[at], sem.at[1, place])
    for part, end_ref in enumerate(end_refs):
        leave(values_ref.at[:, lasts[part]], end_ref.at[1], sem_end.at[1, part])
        keys[part].wait()
        leave(held_ref.at[part], end_ref.at[0], sem_end.at[2, part])
    for copy in leaving:
        copy.wait()


def stage(keys, values, rates, parts):
    features, tokens = keys.shape
    width = WINDOW // parts
    return pl.pallas_call(
        stage_body,
        out_shape=(jax.ShapeDtypeStruct((features, tokens), jnp.bfloat16),)
        + (jax.ShapeDtypeStruct((2, features, width), jnp.bfloat16),) * parts,
        in_specs=anywhere(2) + [pl.BlockSpec(memory_space=pltpu.VMEM)],
        out_specs=tuple(anywhere(1 + parts)),
        scratch_shapes=[
            pltpu.VMEM((parts, features, width), jnp.bfloat16),
            pltpu.VMEM((features, tokens), jnp.bfloat16),
            pltpu.VMEM((features, tokens), jnp.bfloat16),
            pltpu.SemaphoreType.DMA((2, features // HEAD_SIZE)),
            pltpu.SemaphoreType.DMA((3, parts)),
        ],
        cost_estimate=pl.CostEstimate(
            flops=features * tokens,
            bytes_accessed=4 * features * tokens + 8 * features * WINDOW,
            transcendentals=0,
        ),
        name="stage",
        compiler_params=pltpu.CompilerParams(vmem_limit_bytes=VMEM_GRANT),
    )(keys, values, rates)


def sums_body(*refs, owned, block):
    sources = refs[:-15]
    (
        key_ref, target_ref, pair_key_ref, pair_target_ref,
        send_out, pack_out,
        send_ref, pack_ref, keys_ref, targets_ref, hidden_ref, back_ref, sem, sem_in, sem_out,
    ) = refs[-15:]
    _, tokens = key_ref.shape
    half = pack_ref.shape[1]
    count = tokens // block
    role = lax.axis_index("narrow") ^ (lax.axis_index("wide") // owned)

    def moved(keys, targets, index, slot):
        source = slice(index * block, (index + 1) * block)
        place = slice(slot * block, (slot + 1) * block)
        return (
            pltpu.make_async_copy(keys.at[:, source], keys_ref.at[:, place], sem_in.at[0, slot]),
            pltpu.make_async_copy(
                targets.at[:, source], targets_ref.at[:, place], sem_in.at[1, slot]
            ),
        )

    for place, source in enumerate(sources):

        @pl.when(role == place)
        def _(source=source):
            pltpu.make_async_copy(source, pack_ref, sem).start()

    arrivals = [moved(key_ref, target_ref, index, index) for index in range(count)]
    arrivals += [moved(pair_key_ref, pair_target_ref, index, count + index) for index in range(count)]
    for copies in arrivals:
        for copy in copies:
            copy.start()
    pltpu.make_async_copy(sources[0], pack_ref, sem).wait()
    leaving = [pltpu.make_async_copy(pack_ref, pack_out, sem_out.at[3])]
    leaving[0].start()
    gate_lift = jnp.concatenate([pack_ref[0] * jnp.bfloat16(0.5), pack_ref[1]], axis=0)
    down = pack_ref[2]

    def multiply(slot):
        for copy in arrivals[slot]:
            copy.wait()
        at = slice(slot * block, (slot + 1) * block)
        pre = jnp.dot(gate_lift, keys_ref[:, at], preferred_element_type=jnp.float32)
        back_hidden = jnp.dot(down, targets_ref[:, at], preferred_element_type=jnp.float32)
        return pre, back_hidden

    def combine(slot, pre, back_hidden):
        at = slice(slot * block, (slot + 1) * block)
        half_gate = pre[:half]
        pre_lift = pre[half:]
        twice = jnp.tanh(half_gate) + 1.0
        silu_gate = half_gate * twice
        hidden_ref[:, at] = (silu_gate * pre_lift).astype(jnp.bfloat16)
        slope = twice + silu_gate * (2.0 - twice)
        back_ref[:half, at] = (back_hidden * pre_lift * slope).astype(jnp.bfloat16)
        back_ref[half:, at] = (back_hidden * silu_gate).astype(jnp.bfloat16)

    for slot in range(2 * count):
        combine(slot, *multiply(slot))

    def leave(place, value):
        send_ref[place] = value.astype(jnp.bfloat16)
        leaving.append(
            pltpu.make_async_copy(send_ref.at[place], send_out.at[place], sem_out.at[place])
        )
        leaving[-1].start()

    contract = (((1,), (1,)), ((), ()))
    sums = lax.dot_general(
        back_ref[...], keys_ref[...], contract, preferred_element_type=jnp.float32
    )
    leave(0, sums[:half] * 0.5)
    leave(1, sums[half:])
    sums = lax.dot_general(
        hidden_ref[...], targets_ref[...], contract, preferred_element_type=jnp.float32
    )
    leave(2, sums)
    for copy in leaving:
        copy.wait()


def fast_sums(sources, keys, targets, pair_keys, pair_targets, owned):
    features, tokens = keys.shape
    shape = sources[0].shape
    half = shape[1]
    block = tokens
    return pl.pallas_call(
        functools.partial(sums_body, owned=owned, block=block),
        out_shape=(jax.ShapeDtypeStruct(shape, jnp.bfloat16),) * 2,
        in_specs=anywhere(len(sources) + 4),
        out_specs=tuple(anywhere(2)),
        scratch_shapes=[
            pltpu.VMEM(shape, jnp.bfloat16),
            pltpu.VMEM(shape, jnp.bfloat16),
            pltpu.VMEM((features, 2 * tokens), jnp.bfloat16),
            pltpu.VMEM((features, 2 * tokens), jnp.bfloat16),
            pltpu.VMEM((half, 2 * tokens), jnp.bfloat16),
            pltpu.VMEM((2 * half, 2 * tokens), jnp.bfloat16),
            pltpu.SemaphoreType.DMA(()),
            pltpu.SemaphoreType.DMA((2, 2 * tokens // block)),
            pltpu.SemaphoreType.DMA((4,)),
        ],
        cost_estimate=pl.CostEstimate(
            flops=24 * half * features * tokens,
            bytes_accessed=8 * features * tokens + 6 * 3 * half * features,
            transcendentals=2 * half * tokens,
        ),
        name="fast_sums",
        compiler_params=pltpu.CompilerParams(vmem_limit_bytes=VMEM_GRANT),
    )(*sources, keys, targets, pair_keys, pair_targets)


def recall_body(
    mine_ref, other_ref, far_ref, other_far_ref, pack_ref, pair_pack_ref, query_ref, out_ref,
    w_ref, near_sums_ref, far_sums_ref, held_ref, made_ref, sem,
):
    half = mine_ref.shape[1]
    hidden_rows, features = w_ref.shape[1:]
    nt = (((1,), (1,)), ((), ()))

    side = lax.axis_index("narrow") % 2

    def arriving(matrix):
        moves = (
            (mine_ref, near_sums_ref, side),
            (other_ref, near_sums_ref, 1 - side),
            (far_ref, far_sums_ref, side),
            (other_far_ref, far_sums_ref, 1 - side),
        )
        return [
            pltpu.make_async_copy(
                source.at[matrix],
                target.at[matrix, half_rows(part, half)],
                sem.at[place, matrix],
            )
            for place, (source, target, part) in enumerate(moves)
        ]

    sums = [arriving(matrix) for matrix in range(3)]
    weights = [
        pltpu.make_async_copy(source, w_ref.at[:, half_rows(part, half)], sem.at[4, place])
        for place, (source, part) in enumerate(((pack_ref, side), (pair_pack_ref, 1 - side)))
    ]
    queries = pltpu.make_async_copy(query_ref, held_ref, sem.at[5, 2])
    for copies in sums + [weights, [queries]]:
        for copy in copies:
            copy.start()
    rows = lax.broadcasted_iota(jnp.int32, (hidden_rows, features), 0)
    cols = lax.broadcasted_iota(jnp.int32, (hidden_rows, features), 1)
    diagonal = rows == cols
    rounded, gram, scale = [], [], []
    for matrix, copies in enumerate(sums):
        for copy in copies:
            copy.wait()
        summed = near_sums_ref[matrix].astype(jnp.float32) + far_sums_ref[matrix].astype(
            jnp.float32
        )
        x = summed.astype(jnp.bfloat16)
        product = lax.dot_general(x, x, nt, preferred_element_type=jnp.float32)
        trace = jnp.sum(jnp.where(diagonal, product, 0.0), axis=0, keepdims=True)
        scale.append(lax.rsqrt(jnp.sum(trace, axis=1, keepdims=True) + EPS))
        rounded.append(x)
        gram.append((product * (scale[-1] * scale[-1])).astype(jnp.bfloat16))
    current = rounded
    for sweep_index in range(NS_ITERS):
        if sweep_index:
            scale = [1.0] * 3
            gram = [
                lax.dot_general(x, x, nt, preferred_element_type=jnp.float32).astype(
                    jnp.bfloat16
                )
                for x in current
            ]
        lifted = [
            jnp.dot(g, x, preferred_element_type=jnp.float32).astype(jnp.bfloat16)
            for x, g in zip(current, gram)
        ]
        current = [
            (
                (COEF_A * r) * x.astype(jnp.float32)
                + (COEF_B * r) * y.astype(jnp.float32)
                + (COEF_C * r) * jnp.dot(g, y, preferred_element_type=jnp.float32)
            ).astype(jnp.bfloat16)
            for x, y, g, r in zip(current, lifted, gram, scale)
        ]
    for copy in weights:
        copy.wait()

    def fresh(i):
        axis = 0 if i == 2 else 1
        initial = w_ref[i].astype(jnp.float32)
        moved = initial - current[i].astype(jnp.float32)
        wanted = jnp.mean(jnp.square(initial), axis=axis, keepdims=True) + EPS
        present = jnp.mean(jnp.square(moved), axis=axis, keepdims=True) + EPS
        return (moved * (wanted * lax.rsqrt(wanted * present))).astype(jnp.bfloat16)

    queries.wait()
    tokens = held_ref.shape[1]
    block = tokens // 2
    spans = [slice(at, at + block) for at in range(0, tokens, block)]
    fresh_gate = fresh(0)
    gates = [
        jnp.dot(fresh_gate * jnp.bfloat16(0.5), held_ref[:, span], preferred_element_type=jnp.float32)
        for span in spans
    ]
    fresh_lift = fresh(1)
    lifts = [
        jnp.dot(fresh_lift, held_ref[:, span], preferred_element_type=jnp.float32) for span in spans
    ]
    fresh_down = fresh(2).T
    leaving = []
    for place, (span, gate, lift) in enumerate(zip(spans, gates, lifts)):
        hidden = (gate * (jnp.tanh(gate) + 1.0) * lift).astype(jnp.bfloat16)
        made_ref[:, span] = jnp.dot(
            fresh_down, hidden, preferred_element_type=jnp.float32
        ).astype(jnp.bfloat16)
        leaving.append(
            pltpu.make_async_copy(made_ref.at[:, span], out_ref.at[:, span], sem.at[5, place])
        )
        leaving[-1].start()
    for copy in leaving:
        copy.wait()


def fast_recall(sums, packs, queries):
    features, tokens = queries.shape
    half = packs[0].shape[1]
    hidden_rows = 2 * half
    return pl.pallas_call(
        recall_body,
        out_shape=jax.ShapeDtypeStruct((features, tokens), jnp.bfloat16),
        in_specs=anywhere(7),
        out_specs=pl.BlockSpec(memory_space=pl.ANY),
        scratch_shapes=[
            pltpu.VMEM((3, hidden_rows, features), jnp.bfloat16),
            pltpu.VMEM((3, hidden_rows, features), jnp.bfloat16),
            pltpu.VMEM((3, hidden_rows, features), jnp.bfloat16),
            pltpu.VMEM((features, tokens), jnp.bfloat16),
            pltpu.VMEM((features, tokens), jnp.bfloat16),
            pltpu.SemaphoreType.DMA((6, 3)),
        ],
        cost_estimate=pl.CostEstimate(
            flops=6 * hidden_rows * features * tokens + 18 * NS_ITERS * hidden_rows * features**2,
            bytes_accessed=4 * features * tokens + 12 * hidden_rows * features,
            transcendentals=hidden_rows * tokens,
        ),
        name="fast_recall",
        compiler_params=pltpu.CompilerParams(vmem_limit_bytes=VMEM_GRANT),
    )(*sums, *packs, queries)


def in_place(query_states, key_states, value_states, cache_keys, cache_values, gate_fast, *rest):
    features, tok_count = query_states.shape
    narrow_count = lax.axis_size("narrow")
    return (
        features == FD
        and gate_fast.shape[1:] == (FD, FD)
        and features % HEAD_SIZE == 0
        and tok_count % WINDOW == 0
        and tok_count >= 2 * WINDOW
        and narrow_count >= 4
        and narrow_count & (narrow_count - 1) == 0
    )


def in_place_plan(
    query_states,
    key_states,
    value_states,
    cache_keys,
    cache_values,
    gate_fast,
    lift_fast,
    down_fast,
    token_rates,
):
    wide_count = lax.axis_size("wide")
    narrow_count = lax.axis_size("narrow")
    owned = gate_fast.shape[0]

    def from_owner(value, step):
        pairs = []
        for wide in range(wide_count):
            start = wide * narrow_count
            owner = wide // owned
            pairs.append((start + owner, start + (owner ^ step)))
        return lax.ppermute(value, ("wide", "narrow"), pairs)

    own, other = prepare(gate_fast, lift_fast, down_fast)
    arrivals = {}
    for step in sorted(range(1, narrow_count), key=lambda step: step < 2):
        arrivals[step] = from_owner((own, other)[step % 2], step)
    pair_keys = swapped(key_states, "narrow", 0)
    parts = 2
    targets, *ends = stage(key_states, value_states, token_rates, parts)
    pair_targets = swapped(targets, "narrow", 0)
    attended = attend_late(query_states, key_states, value_states)
    sources = [own] + [arrivals[step] for step in range(1, narrow_count)]
    sources, attended, ends = lax.optimization_barrier((sources, attended, ends))
    prior = []
    for end in ends:
        prior.append(from_behind(end, "narrow", 1))
    near, pack = fast_sums(sources, key_states, targets, pair_keys, pair_targets, owned)
    distances = range(1, narrow_count.bit_length() - 1)
    for distance in distances:
        far = swapped(near, "narrow", distance)
        if distance != distances[-1]:
            near = stored(near.astype(jnp.float32) + far.astype(jnp.float32))
    pair_pack = swapped(pack, "narrow", 0)
    pair_near = swapped(near, "narrow", 0)
    pair_far = swapped(far, "narrow", 0)
    attended, *state = attend_early(
        query_states, key_states, value_states, prior[0], cache_keys, cache_values, attended
    )
    attended = attend_last(query_states, prior[1], cache_keys, cache_values, *state, attended)
    recalled = fast_recall((near, pair_near, far, pair_far), (pack, pair_pack), query_states)
    return (attended, recalled)


def spread_plan(
    query_states,
    key_states,
    value_states,
    cache_keys,
    cache_values,
    gate_fast,
    lift_fast,
    down_fast,
    token_rates,
):
    features, tok_count = query_states.shape
    edge_cols = jnp.stack(
        [key_states[:, tok_count - WINDOW :], value_states[:, tok_count - WINDOW :]]
    )
    arrived = from_behind(edge_cols, "narrow", 1)
    leading = lax.axis_index("narrow") == 0
    prior_cols = jnp.where(leading, jnp.stack([cache_keys, cache_values]), arrived)
    ext_keys = jnp.concatenate([prior_cols[0], key_states], axis=1)
    ext_values = jnp.concatenate([prior_cols[1], value_states], axis=1)
    if features % HEAD_SIZE == 0:
        attended = attend_local(query_states, ext_keys, ext_values, 0)
    else:
        attended = attend_paired(query_states, ext_keys, ext_values)
    query_fast, key_fast, value_fast = (
        lax.all_to_all(
            lax.all_to_all(query_states, "wide", split_axis=1, concat_axis=0, tiled=True),
            "narrow",
            split_axis=0,
            concat_axis=1,
            tiled=True,
        ),
        lax.all_to_all(
            lax.all_to_all(key_states, "wide", split_axis=1, concat_axis=0, tiled=True),
            "narrow",
            split_axis=0,
            concat_axis=1,
            tiled=True,
        ),
        lax.all_to_all(
            lax.all_to_all(value_states, "wide", split_axis=1, concat_axis=0, tiled=True),
            "narrow",
            split_axis=0,
            concat_axis=1,
            tiled=True,
        ),
    )
    head_count = gate_fast.shape[0]
    wide_count = lax.axis_size("wide")
    narrow_count = lax.axis_size("narrow")
    piece_rows = tok_count // wide_count
    fast_tokens = query_fast.shape[1]
    rate_blocks = token_rates.reshape(token_rates.shape[0], narrow_count, wide_count, piece_rows)
    rates_here = lax.dynamic_slice(
        rate_blocks,
        (lax.axis_index("narrow") * head_count, 0, lax.axis_index("wide"), 0),
        (head_count, narrow_count, 1, piece_rows),
    ).reshape(head_count, fast_tokens)
    query_heads = query_fast.reshape(head_count, FD, fast_tokens)
    key_heads = key_fast.reshape(head_count, FD, fast_tokens)
    value_heads = value_fast.reshape(head_count, FD, fast_tokens)
    recall = fast_group(
        gate_fast, lift_fast, down_fast, query_heads, key_heads, value_heads, rates_here
    )
    recall = recall.reshape(head_count * FD, fast_tokens)
    recalled = lax.all_to_all(
        lax.all_to_all(recall, "narrow", split_axis=1, concat_axis=0, tiled=True),
        "wide",
        split_axis=0,
        concat_axis=1,
        tiled=True,
    )
    return (attended, recalled)


def per_device(*arrays):
    if in_place(*arrays):
        return in_place_plan(*arrays)
    return spread_plan(*arrays)


def solution(mesh):
    in_specs = (
        P("wide", "narrow"),
        P("wide", "narrow"),
        P("wide", "narrow"),
        P("wide", None),
        P("wide", None),
        P("narrow", None, None),
        P("narrow", None, None),
        P("narrow", None, None),
        P(),
    )
    out_specs = (P("wide", "narrow"), P("wide", "narrow"))
    return jax.shard_map(
        per_device, mesh=mesh, in_specs=in_specs, out_specs=out_specs, check_vma=False
    )
```

```python
import functools
import math

import jax
import jax.numpy as jnp
from jax import lax
from jax.experimental import pallas as pl
from jax.experimental.pallas import tpu as pltpu
from jax.sharding import PartitionSpec as P


FD = 512
HEAD_SIZE = 128
WINDOW = 1024
NS_ITERS = 2


EPS = 1e-06
COEF_A = 3.4445
COEF_B = -4.775
COEF_C = 2.0315
LOG2E = math.log2(math.e)
VMEM_GRANT = 67043328


def swapped(array, axis, distance):
    return lax.ppermute(array, axis, [(i, i ^ 1 << distance) for i in range(lax.axis_size(axis))])


def shortened(array):

    def short(part):
        return part.astype(jnp.bfloat16) if part.dtype == jnp.float32 else part

    return jax.tree.map(short, array)


def from_behind(value, axis, steps):
    count = lax.axis_size(axis)
    initial, last = (max(0, -steps), min(count, count - steps))
    return lax.ppermute(value, axis, [(source, source + steps) for source in range(initial, last)])


def stored(value):
    return lax.optimization_barrier(value.astype(jnp.bfloat16))


def attend_local(query_states, ext_keys, ext_values, key_start):
    features, tok_count = query_states.shape
    head_count = features // HEAD_SIZE
    block_rows = min(512, tok_count)
    block_count = tok_count // block_rows
    key_span = WINDOW + block_rows
    scaling = 1.0 / math.sqrt(HEAD_SIZE)
    rows_at = lax.broadcasted_iota(jnp.int32, (block_rows, key_span), 0)
    cols_at = lax.broadcasted_iota(jnp.int32, (block_rows, key_span), 1)
    visible = (cols_at > rows_at) & (cols_at <= rows_at + WINDOW)

    def one_block(block_index):
        offset = block_index * block_rows
        query_part = lax.dynamic_slice_in_dim(query_states, offset, block_rows, 1).reshape(
            head_count, HEAD_SIZE, block_rows
        )
        key_part = lax.dynamic_slice_in_dim(ext_keys, key_start + offset, key_span, 1).reshape(
            head_count, HEAD_SIZE, key_span
        )
        value_part = lax.dynamic_slice_in_dim(ext_values, key_start + offset, key_span, 1).reshape(
            head_count, HEAD_SIZE, key_span
        )
        scores = (
            jnp.einsum("hdq,hdk->hqk", query_part, key_part, preferred_element_type=jnp.float32)
            * scaling
        )
        scores = jnp.where(visible[None], scores, -jnp.inf)
        highest = jnp.max(scores, axis=2, keepdims=True)
        raised = jnp.exp(scores - highest)
        weights = (raised / jnp.sum(raised, axis=2, keepdims=True)).astype(jnp.bfloat16)
        blended = jnp.einsum(
            "hdk,hqk->hdq", value_part, weights, preferred_element_type=jnp.float32
        )
        return blended.astype(jnp.bfloat16).reshape(features, block_rows)

    blocks_out = lax.map(one_block, jnp.arange(block_count, dtype=jnp.int32))
    return jnp.transpose(blocks_out, (1, 0, 2)).reshape(features, tok_count)


def attend_paired(query_states, ext_keys, ext_values):
    features, tok_count = query_states.shape
    half_rows = tok_count // 2
    lower = lax.axis_index("wide") % 2 == 0
    query_send = jnp.where(lower, query_states[:, half_rows:], query_states[:, :half_rows])
    query_keep = jnp.where(lower, query_states[:, :half_rows], query_states[:, half_rows:])
    other_keys, other_values, other_queries = swapped((ext_keys, ext_values, query_send), "wide", 0)
    full_keys = jnp.where(
        lower,
        jnp.concatenate([ext_keys, other_keys], axis=0),
        jnp.concatenate([other_keys, ext_keys], axis=0),
    )
    full_values = jnp.where(
        lower,
        jnp.concatenate([ext_values, other_values], axis=0),
        jnp.concatenate([other_values, ext_values], axis=0),
    )
    full_queries = jnp.where(
        lower,
        jnp.concatenate([query_keep, other_queries], axis=0),
        jnp.concatenate([other_queries, query_keep], axis=0),
    )
    key_start = jnp.where(lower, 0, half_rows).astype(jnp.int32)
    head_out = attend_local(full_queries, full_keys, full_values, key_start)
    out_keep = jnp.where(lower, head_out[:features], head_out[features:])
    out_send = jnp.where(lower, head_out[features:], head_out[:features])
    out_other = swapped(shortened(out_send), "wide", 0).astype(out_send.dtype)
    return jnp.where(
        lower,
        jnp.concatenate([out_keep, out_other], axis=1),
        jnp.concatenate([out_other, out_keep], axis=1),
    )


def fast_terms(gate_weight, lift_weight, down_weight, key_heads, value_heads, rates_here):
    pre_gate = jnp.einsum(
        "hcf,hft->hct", gate_weight, key_heads, preferred_element_type=jnp.float32
    )
    pre_lift = jnp.einsum(
        "hcf,hft->hct", lift_weight, key_heads, preferred_element_type=jnp.float32
    )
    sigmoid_gate = jax.nn.sigmoid(pre_gate)
    silu_gate = pre_gate * sigmoid_gate
    hidden = (silu_gate * pre_lift).astype(jnp.bfloat16)
    target = (-(value_heads.astype(jnp.float32) * rates_here[:, None, :])).astype(jnp.bfloat16)
    grad_down = jnp.einsum("hft,hct->hfc", target, hidden, preferred_element_type=jnp.float32)
    back_hidden = jnp.einsum(
        "hfc,hft->hct", down_weight, target, preferred_element_type=jnp.float32
    )
    back_lift = (back_hidden * silu_gate).astype(jnp.bfloat16)
    back_gate = (
        back_hidden * pre_lift * sigmoid_gate * (1.0 + pre_gate * (1.0 - sigmoid_gate))
    ).astype(jnp.bfloat16)
    grad_gate = jnp.einsum("hct,hft->hcf", back_gate, key_heads, preferred_element_type=jnp.float32)
    grad_lift = jnp.einsum("hct,hft->hcf", back_lift, key_heads, preferred_element_type=jnp.float32)
    return (grad_gate, grad_lift, grad_down)


def scaled_start(rounded):
    widened = rounded.astype(jnp.float32)
    norm_val = jnp.sqrt(jnp.sum(jnp.square(widened), axis=(1, 2), keepdims=True) + EPS)
    return stored(widened / norm_val)


def starting(grad_gate, grad_lift, grad_down):
    sum_gate, sum_lift, sum_down = lax.psum((grad_gate, grad_lift, grad_down), "wide")
    return (
        scaled_start(stored(sum_gate)),
        scaled_start(stored(sum_lift)),
        scaled_start(stored(sum_down)),
    )


def orthogonal(current):
    for _ in range(NS_ITERS):
        gram_mat = jnp.einsum(
            "hrc,hrd->hcd", current, current, preferred_element_type=jnp.float32
        ).astype(jnp.bfloat16)
        lifted = stored(
            jnp.einsum("hrc,hcd->hrd", current, gram_mat, preferred_element_type=jnp.float32)
        )
        current = stored(
            COEF_A * current.astype(jnp.float32)
            + COEF_B * lifted.astype(jnp.float32)
            + COEF_C
            * jnp.einsum("hrc,hcd->hrd", lifted, gram_mat, preferred_element_type=jnp.float32)
        )
    return current


def refreshed(weight, ortho):
    initial = weight.astype(jnp.float32)
    moved_rows = initial - ortho.astype(jnp.float32)
    wanted = jnp.sqrt(jnp.mean(jnp.square(initial), axis=-1, keepdims=True) + EPS)
    present = jnp.sqrt(jnp.mean(jnp.square(moved_rows), axis=-1, keepdims=True) + EPS)
    return (moved_rows * (wanted / present)).astype(jnp.bfloat16)


def fast_group(
    gate_weight, lift_weight, down_weight, query_heads, key_heads, value_heads, rates_here
):
    grad_gate, grad_lift, grad_down = fast_terms(
        gate_weight, lift_weight, down_weight, key_heads, value_heads, rates_here
    )
    start_gate, start_lift, start_down = starting(grad_gate, grad_lift, grad_down)
    fresh_gate = refreshed(gate_weight, orthogonal(start_gate))
    fresh_lift = refreshed(lift_weight, orthogonal(start_lift))
    fresh_down = refreshed(down_weight, orthogonal(start_down))
    query_gate = jnp.einsum(
        "hcf,hft->hct", fresh_gate, query_heads, preferred_element_type=jnp.float32
    )
    query_lift = jnp.einsum(
        "hcf,hft->hct", fresh_lift, query_heads, preferred_element_type=jnp.float32
    )
    query_hidden = (jax.nn.silu(query_gate) * query_lift).astype(jnp.bfloat16)
    return jnp.einsum(
        "hfc,hct->hft", fresh_down, query_hidden, preferred_element_type=jnp.float32
    ).astype(jnp.bfloat16)


def attend_body(
    q_ref, kp_ref, vp_ref, kc_ref, vc_ref, o_ref, kt_ref, v_ref, *, block, window
):
    hd = q_ref.shape[0]
    scale = LOG2E / math.sqrt(hd)

    placed(kp_ref, vp_ref, kt_ref, v_ref, 0)
    placed(kc_ref, vc_ref, kt_ref, v_ref, window)
    v_ref[hd:, :] = jnp.ones((v_ref.shape[0] - hd, 2 * window), jnp.bfloat16)
    rows = lax.broadcasted_iota(jnp.int32, (block, block), 0)
    cols = lax.broadcasted_iota(jnp.int32, (block, block), 1)
    first = rows > cols
    inner = window // block

    def scores(b):
        q = q_ref[:, b * block : (b + 1) * block].astype(jnp.float32) * scale
        high = q.astype(jnp.bfloat16)
        low = (q - high.astype(jnp.float32)).astype(jnp.bfloat16)
        pair = jnp.concatenate([high, low], axis=0)
        parts = [
            jnp.dot(
                kt_ref[(b + j) * block : (b + j + 1) * block, :],
                pair,
                preferred_element_type=jnp.float32,
            )
            for j in range(inner + 1)
        ]
        return [jnp.where(first, parts[0], parts[inner])] + parts[1:inner]

    def blend(b, parts):
        top = functools.reduce(jnp.maximum, parts)
        top = jnp.max(top, axis=0, keepdims=True)
        raised = [jnp.exp2(part - top).astype(jnp.bfloat16) for part in parts]
        zero = jnp.zeros_like(raised[0])
        ends = jnp.where(first, raised[0], zero), jnp.where(first, zero, raised[0])
        weights = jnp.concatenate([ends[0]] + raised[1:] + [ends[1]], axis=0)
        span = v_ref[:, b * block : (b + inner + 1) * block]
        out = jnp.dot(span, weights, preferred_element_type=jnp.float32)
        o_ref[:, b * block : (b + 1) * block] = (out[:hd] * (1.0 / out[hd : hd + 1])).astype(
            jnp.bfloat16
        )

    ready = scores(0)
    for b in range(1, inner):
        following = scores(b)
        blend(b - 1, ready)
        ready = following
    blend(inner - 1, ready)


def attend_scratch():
    return [
        pltpu.VMEM((2 * WINDOW, 2 * HEAD_SIZE), jnp.bfloat16),
        pltpu.VMEM((HEAD_SIZE + 16, 2 * WINDOW), jnp.bfloat16),
    ]


def attend_late(queries, keys, values):
    features, tokens = queries.shape
    heads, chunks = features // HEAD_SIZE, tokens // WINDOW - 1
    here = pl.BlockSpec((HEAD_SIZE, WINDOW), lambda h, c: (h, c + 1))
    before = pl.BlockSpec((HEAD_SIZE, WINDOW), lambda h, c: (h, c))
    return pl.pallas_call(
        functools.partial(attend_body, block=min(256, WINDOW), window=WINDOW),
        out_shape=jax.ShapeDtypeStruct((features, tokens), jnp.bfloat16),
        grid=(heads, chunks),
        in_specs=[here, before, before, here, here],
        out_specs=here,
        scratch_shapes=attend_scratch(),
        cost_estimate=pl.CostEstimate(
            flops=5 * features * chunks * WINDOW**2,
            bytes_accessed=10 * features * chunks * WINDOW,
            transcendentals=heads * chunks * WINDOW**2,
        ),
        name="attend_late",
        compiler_params=pltpu.CompilerParams(vmem_limit_bytes=VMEM_GRANT),
    )(queries, keys, values, keys, values)


def two_term(q_ref, at, scale):
    q = q_ref[:, at].astype(jnp.float32) * scale
    high = q.astype(jnp.bfloat16)
    low = (q - high.astype(jnp.float32)).astype(jnp.bfloat16)
    return jnp.concatenate([high, low], axis=0)


def placed(k, v, kt_ref, v_ref, at):
    hd, width = k.shape
    turned = k[...].T
    kt_ref[at : at + width, :hd] = turned
    kt_ref[at : at + width, hd:] = turned
    v_ref[:hd, at : at + width] = v[...]


def early_body(
    q_ref, kp_ref, vp_ref, kc_ref, vc_ref, ck_ref, cv_ref, _, o_ref, part_ref, top_ref, mass_ref,
    kt_ref, v_ref, *, block,
):
    hd, window = q_ref.shape
    scale = LOG2E / math.sqrt(hd)
    near = kp_ref.shape[1]
    inner = window // block
    missing = (window - near) // block
    leading = lax.axis_index("narrow") == 0

    @pl.when(leading)
    def _():
        placed(ck_ref, cv_ref, kt_ref, v_ref, 0)

    @pl.when(jnp.logical_not(leading))
    def _():
        placed(kp_ref, vp_ref, kt_ref, v_ref, 0)

    placed(kc_ref, vc_ref, kt_ref, v_ref, near)
    v_ref[hd:, :] = jnp.ones((v_ref.shape[0] - hd, v_ref.shape[1]), jnp.bfloat16)
    rows = lax.broadcasted_iota(jnp.int32, (block, block), 0)
    cols = lax.broadcasted_iota(jnp.int32, (block, block), 1)
    first = rows > cols

    def chunk(j):
        return slice((j - missing) * block, (j - missing + 1) * block)

    def scores(b):
        pair = two_term(q_ref, slice(b * block, (b + 1) * block), scale)
        parts = [
            jnp.dot(kt_ref[chunk(j), :], pair, preferred_element_type=jnp.float32)
            for j in range(max(b, missing), b + inner + 1)
        ]
        if b >= missing:
            return [jnp.where(first, parts[0], parts[inner])] + parts[1:inner]
        return parts[:-1] + [jnp.where(first, -jnp.inf, parts[-1])]

    def blend(b, parts):
        top = functools.reduce(jnp.maximum, parts)
        top = jnp.max(top, axis=0, keepdims=True)
        raised = [jnp.exp2(part - top).astype(jnp.bfloat16) for part in parts]
        if b >= missing:
            zero = jnp.zeros_like(raised[0])
            ends = jnp.where(first, raised[0], zero), jnp.where(first, zero, raised[0])
            raised = [ends[0]] + raised[1:] + [ends[1]]
        span = v_ref[:, chunk(max(b, missing)).start : chunk(b + inner).stop]
        out = jnp.dot(span, jnp.concatenate(raised, axis=0), preferred_element_type=jnp.float32)
        if b >= missing:
            at = slice((b - missing) * block, (b - missing + 1) * block)
            o_ref[:, at] = (out[:hd] * (1.0 / out[hd : hd + 1])).astype(jnp.bfloat16)
        else:
            at = slice(b * block, (b + 1) * block)
            part_ref[:, at] = out[:hd]
            top_ref[:, at] = jnp.broadcast_to(top, (top_ref.shape[0], block))
            mass_ref[:, at] = jnp.broadcast_to(out[hd : hd + 1], (top_ref.shape[0], block))

    ready = scores(0)
    for b in range(1, inner):
        following = scores(b)
        blend(b - 1, ready)
        ready = following
    blend(inner - 1, ready)


def attend_early(queries, keys, values, prior, cache_keys, cache_values, late):
    features, tokens = queries.shape
    heads = features // HEAD_SIZE
    near = prior.shape[2]
    far = WINDOW - near
    here = pl.BlockSpec((HEAD_SIZE, WINDOW), lambda h: (h, 0))
    nearer = pl.BlockSpec((HEAD_SIZE, near), lambda h: (h, far // near))
    prior_keys = pl.BlockSpec((None, HEAD_SIZE, near), lambda h: (0, h, 0))
    prior_values = pl.BlockSpec((None, HEAD_SIZE, near), lambda h: (1, h, 0))
    rows = 8
    stats = jax.ShapeDtypeStruct((heads * rows, far), jnp.float32)
    stat = pl.BlockSpec((rows, far), lambda h: (h, 0))
    return pl.pallas_call(
        functools.partial(early_body, block=min(256, near)),
        out_shape=(
            jax.ShapeDtypeStruct((features, tokens), jnp.bfloat16),
            jax.ShapeDtypeStruct((features, far), jnp.float32),
            stats,
            stats,
        ),
        grid=(heads,),
        in_specs=[here, prior_keys, prior_values, here, here, nearer, nearer]
        + [pl.BlockSpec(memory_space=pl.ANY)],
        out_specs=(nearer, pl.BlockSpec((HEAD_SIZE, far), lambda h: (h, 0)), stat, stat),
        scratch_shapes=[
            pltpu.VMEM((near + WINDOW, 2 * HEAD_SIZE), jnp.bfloat16),
            pltpu.VMEM((HEAD_SIZE + 16, near + WINDOW), jnp.bfloat16),
        ],
        input_output_aliases={7: 0},
        cost_estimate=pl.CostEstimate(
            flops=5 * features * WINDOW**2,
            bytes_accessed=14 * features * WINDOW,
            transcendentals=heads * WINDOW**2,
        ),
        name="attend_early",
        compiler_params=pltpu.CompilerParams(vmem_limit_bytes=VMEM_GRANT),
    )(queries, prior, prior, keys, values, cache_keys, cache_values, late)


def last_body(
    q_ref, prior_ref, ck_ref, cv_ref, part_ref, top_ref, mass_ref, _, o_ref,
    held_q, held_k, held_v, held_part, held_top, held_mass, kt_ref, v_ref, made_ref, sem,
    *, block,
):
    features, far = part_ref.shape
    hd = HEAD_SIZE
    heads = features // hd
    scale = LOG2E / math.sqrt(hd)
    missing = far // block
    leading = lax.axis_index("narrow") == 0
    plain = [
        pltpu.make_async_copy(top_ref, held_top, sem.at[0, 0]),
        pltpu.make_async_copy(mass_ref, held_mass, sem.at[0, 1]),
    ]
    arriving = []
    for h in range(heads):
        at = slice(h * hd, (h + 1) * hd)
        keys = pltpu.make_async_copy(prior_ref.at[0, at], held_k.at[at], sem.at[1, h])
        values = pltpu.make_async_copy(prior_ref.at[1, at], held_v.at[at], sem.at[2, h])

        @pl.when(leading)
        def _(at=at, h=h):
            pltpu.make_async_copy(ck_ref.at[at, :far], held_k.at[at], sem.at[1, h]).start()
            pltpu.make_async_copy(cv_ref.at[at, :far], held_v.at[at], sem.at[2, h]).start()

        @pl.when(jnp.logical_not(leading))
        def _(keys=keys, values=values):
            keys.start()
            values.start()

        others = [
            pltpu.make_async_copy(q_ref.at[at, :far], held_q.at[at], sem.at[3, h]),
            pltpu.make_async_copy(part_ref.at[at], held_part.at[at], sem.at[4, h]),
        ]
        for copy in others + (plain if h == 0 else []):
            copy.start()
        arriving.append([keys, values] + others)
    rows = lax.broadcasted_iota(jnp.int32, (block, block), 0)
    cols = lax.broadcasted_iota(jnp.int32, (block, block), 1)
    first = rows > cols
    v_ref[:, hd:, :] = jnp.ones((heads, v_ref.shape[1] - hd, far), jnp.bfloat16)
    leaving = []
    for copy in plain:
        copy.wait()

    def scores(h, b):
        at = slice(h * hd, (h + 1) * hd)
        if b == 0:
            for copy in arriving[h]:
                copy.wait()
            placed(held_k.at[at], held_v.at[at], kt_ref.at[h], v_ref.at[h], 0)
        pair = two_term(held_q.at[at], slice(b * block, (b + 1) * block), scale)
        parts = [
            jnp.dot(
                kt_ref[h, j * block : (j + 1) * block, :], pair, preferred_element_type=jnp.float32
            )
            for j in range(b, missing)
        ]
        return [jnp.where(first, parts[0], -jnp.inf)] + parts[1:]

    def blend(h, b, parts):
        at = slice(h * hd, (h + 1) * hd)
        span = slice(b * block, (b + 1) * block)
        before = held_top[h * 8 : h * 8 + 1, span]
        top = functools.reduce(jnp.maximum, parts)
        top = jnp.maximum(jnp.max(top, axis=0, keepdims=True), before)
        kept = jnp.exp2(before - top)
        weights = jnp.concatenate(
            [jnp.exp2(part - top).astype(jnp.bfloat16) for part in parts], axis=0
        )
        out = jnp.dot(v_ref[h, :, b * block :], weights, preferred_element_type=jnp.float32)
        mass = held_mass[h * 8 : h * 8 + 1, span] * kept + out[hd : hd + 1]
        made_ref[at, span] = ((held_part[at, span] * kept + out[:hd]) * (1.0 / mass)).astype(
            jnp.bfloat16
        )
        if b == missing - 1:
            leaving.append(
                pltpu.make_async_copy(made_ref.at[at], o_ref.at[at, :far], sem.at[5, h])
            )
            leaving[-1].start()

    turns = [(h, b) for h in range(heads) for b in range(missing)]
    ready = scores(*turns[0])
    for turn, ahead in zip(turns, turns[1:]):
        following = scores(*ahead)
        blend(*turn, ready)
        ready = following
    blend(*turns[-1], ready)
    for copy in leaving:
        copy.wait()


def attend_last(queries, prior, cache_keys, cache_values, part, top, mass, early):
    features, tokens = queries.shape
    heads = features // HEAD_SIZE
    far = part.shape[1]
    pieces = pltpu.VMEM((features, far), jnp.bfloat16)
    return pl.pallas_call(
        functools.partial(last_body, block=min(256, far)),
        out_shape=jax.ShapeDtypeStruct((features, tokens), jnp.bfloat16),
        in_specs=[pl.BlockSpec(memory_space=pl.ANY)] * 8,
        out_specs=pl.BlockSpec(memory_space=pl.ANY),
        scratch_shapes=[
            pieces,
            pieces,
            pieces,
            pltpu.VMEM((features, far), jnp.float32),
            pltpu.VMEM(top.shape, jnp.float32),
            pltpu.VMEM(top.shape, jnp.float32),
            pltpu.VMEM((heads, far, 2 * HEAD_SIZE), jnp.bfloat16),
            pltpu.VMEM((heads, HEAD_SIZE + 16, far), jnp.bfloat16),
            pieces,
            pltpu.SemaphoreType.DMA((6, max(heads, 2))),
        ],
        input_output_aliases={7: 0},
        cost_estimate=pl.CostEstimate(
            flops=3 * features * far**2,
            bytes_accessed=14 * features * far,
            transcendentals=heads * far**2,
        ),
        name="attend_last",
        compiler_params=pltpu.CompilerParams(vmem_limit_bytes=VMEM_GRANT),
    )(queries, prior, cache_keys, cache_values, part, top, mass, early)


def anywhere(count):
    return [pl.BlockSpec(memory_space=pl.ANY)] * count


def half_rows(part, half):
    return pl.ds(pl.multiple_of(part * half, half), half)


def prepare_body(gate_ref, lift_ref, down_ref, own_ref, other_ref, w_ref, out_ref, sem):
    owned = gate_ref.shape[0]
    local = lax.axis_index("wide") % owned
    side = lax.axis_index("narrow") % 2
    half = own_ref.shape[1]
    copies = [
        pltpu.make_async_copy(source.at[local], w_ref.at[place], sem.at[0, place])
        for place, source in enumerate((down_ref, gate_ref, lift_ref))
    ]
    for copy in copies:
        copy.start()
    leaving = []
    copies[0].wait()
    out_ref[...] = w_ref[0].T
    for order, (place, source) in enumerate(((2, out_ref), (0, w_ref.at[1]), (1, w_ref.at[2]))):
        if order:
            copies[order].wait()
        for turn, (target, part) in enumerate(((own_ref, side), (other_ref, 1 - side))):
            leaving.append(
                pltpu.make_async_copy(
                    source.at[half_rows(part, half)], target.at[place], sem.at[1 + turn, place]
                )
            )
            leaving[-1].start()
    for copy in leaving:
        copy.wait()


def prepare(gate_fast, lift_fast, down_fast):
    _, hidden_rows, features = gate_fast.shape
    shape = (3, hidden_rows // 2, features)
    return pl.pallas_call(
        prepare_body,
        out_shape=(jax.ShapeDtypeStruct(shape, jnp.bfloat16),) * 2,
        in_specs=anywhere(3),
        out_specs=tuple(anywhere(2)),
        scratch_shapes=[
            pltpu.VMEM((3, hidden_rows, features), jnp.bfloat16),
            pltpu.VMEM((hidden_rows, features), jnp.bfloat16),
            pltpu.SemaphoreType.DMA((3, 3)),
        ],
        cost_estimate=pl.CostEstimate(
            flops=0, bytes_accessed=12 * hidden_rows * features, transcendentals=0
        ),
        name="prepare",
        compiler_params=pltpu.CompilerParams(vmem_limit_bytes=VMEM_GRANT),
    )(gate_fast, lift_fast, down_fast)


def stage_body(key_ref, value_ref, rate_ref, target_ref, *refs):
    end_refs, (held_ref, values_ref, made_ref, sem, sem_end) = refs[:-5], refs[-5:]
    features, tokens = key_ref.shape
    width = end_refs[0].shape[2]
    step = HEAD_SIZE
    lasts = [slice(tokens - (part + 1) * width, tokens - part * width) for part in range(len(end_refs))]
    begin = pl.multiple_of(lax.axis_index("narrow") * tokens, tokens)
    rates = -rate_ref[pl.ds(lax.axis_index("wide"), 1), pl.ds(begin, tokens)]
    values = [
        pltpu.make_async_copy(
            value_ref.at[at : at + step], values_ref.at[at : at + step], sem.at[0, at // step]
        )
        for at in range(0, features, step)
    ]
    keys = [
        pltpu.make_async_copy(
            key_ref.at[:, last], held_ref.at[part], sem_end.at[0, part]
        )
        for part, last in enumerate(lasts)
    ]
    for copy in values + keys:
        copy.start()
    leaving = []

    def leave(source, target, mark):
        leaving.append(pltpu.make_async_copy(source, target, mark))
        leaving[-1].start()

    for place, copy in enumerate(values):
        at = slice(place * step, (place + 1) * step)
        copy.wait()
        made_ref[at] = (values_ref[at].astype(jnp.float32) * rates).astype(jnp.bfloat16)
        leave(made_ref.at[at], target_ref.at[at], sem.at[1, place])
    for part, end_ref in enumerate(end_refs):
        leave(values_ref.at[:, lasts[part]], end_ref.at[1], sem_end.at[1, part])
        keys[part].wait()
        leave(held_ref.at[part], end_ref.at[0], sem_end.at[2, part])
    for copy in leaving:
        copy.wait()


def stage(keys, values, rates, parts):
    features, tokens = keys.shape
    width = WINDOW // parts
    return pl.pallas_call(
        stage_body,
        out_shape=(jax.ShapeDtypeStruct((features, tokens), jnp.bfloat16),)
        + (jax.ShapeDtypeStruct((2, features, width), jnp.bfloat16),) * parts,
        in_specs=anywhere(2) + [pl.BlockSpec(memory_space=pltpu.VMEM)],
        out_specs=tuple(anywhere(1 + parts)),
        scratch_shapes=[
            pltpu.VMEM((parts, features, width), jnp.bfloat16),
            pltpu.VMEM((features, tokens), jnp.bfloat16),
            pltpu.VMEM((features, tokens), jnp.bfloat16),
            pltpu.SemaphoreType.DMA((2, features // HEAD_SIZE)),
            pltpu.SemaphoreType.DMA((3, parts)),
        ],
        cost_estimate=pl.CostEstimate(
            flops=features * tokens,
            bytes_accessed=4 * features * tokens + 8 * features * WINDOW,
            transcendentals=0,
        ),
        name="stage",
        compiler_params=pltpu.CompilerParams(vmem_limit_bytes=VMEM_GRANT),
    )(keys, values, rates)


def sums_body(*refs, owned, cuts):
    sources = refs[:-15]
    (
        key_ref, target_ref, pair_key_ref, pair_target_ref,
        send_out, pack_out,
        send_ref, pack_ref, keys_ref, targets_ref, hidden_ref, back_ref, sem, sem_in, sem_out,
    ) = refs[-15:]
    _, tokens = key_ref.shape
    half = pack_ref.shape[1]
    role = lax.axis_index("narrow") ^ (lax.axis_index("wide") // owned)

    for place, source in enumerate(sources):

        @pl.when(role == place)
        def _(source=source):
            pltpu.make_async_copy(source, pack_ref, sem).start()

    spans = [(key_ref, target_ref, 0, begin, end) for begin, end in zip(cuts, cuts[1:])]
    spans.append((pair_key_ref, pair_target_ref, tokens, 0, tokens))
    arrivals = []
    for slot, (keys, targets, base, begin, end) in enumerate(spans):
        source, place = slice(begin, end), slice(base + begin, base + end)
        copies = (
            pltpu.make_async_copy(keys.at[:, source], keys_ref.at[:, place], sem_in.at[0, slot]),
            pltpu.make_async_copy(
                targets.at[:, source], targets_ref.at[:, place], sem_in.at[1, slot]
            ),
        )
        for copy in copies:
            copy.start()
        arrivals.append((place, *copies))
    pltpu.make_async_copy(sources[0], pack_ref, sem).wait()
    leaving = [pltpu.make_async_copy(pack_ref, pack_out, sem_out.at[3])]
    leaving[0].start()
    gate_lift = jnp.concatenate([pack_ref[0] * jnp.bfloat16(0.5), pack_ref[1]], axis=0)
    down = pack_ref[2]

    for at, keys, targets in arrivals:
        keys.wait()
        pre = jnp.dot(gate_lift, keys_ref[:, at], preferred_element_type=jnp.float32)
        targets.wait()
        back_hidden = jnp.dot(down, targets_ref[:, at], preferred_element_type=jnp.float32)
        half_gate = pre[:half]
        pre_lift = pre[half:]
        twice = jnp.tanh(half_gate) + 1.0
        silu_gate = half_gate * twice
        hidden_ref[:, at] = (silu_gate * pre_lift).astype(jnp.bfloat16)
        slope = twice + silu_gate * (2.0 - twice)
        back_ref[:half, at] = (back_hidden * pre_lift * slope).astype(jnp.bfloat16)
        back_ref[half:, at] = (back_hidden * silu_gate).astype(jnp.bfloat16)

    def leave(place, value):
        send_ref[place] = value.astype(jnp.bfloat16)
        leaving.append(
            pltpu.make_async_copy(send_ref.at[place], send_out.at[place], sem_out.at[place])
        )
        leaving[-1].start()

    contract = (((1,), (1,)), ((), ()))
    sums = lax.dot_general(
        back_ref[...], keys_ref[...], contract, preferred_element_type=jnp.float32
    )
    leave(0, sums[:half] * 0.5)
    leave(1, sums[half:])
    sums = lax.dot_general(
        hidden_ref[...], targets_ref[...], contract, preferred_element_type=jnp.float32
    )
    leave(2, sums)
    for copy in leaving:
        copy.wait()


def fast_sums(sources, keys, targets, pair_keys, pair_targets, owned):
    features, tokens = keys.shape
    shape = sources[0].shape
    half = shape[1]
    cuts = (0, tokens)
    return pl.pallas_call(
        functools.partial(sums_body, owned=owned, cuts=cuts),
        out_shape=(jax.ShapeDtypeStruct(shape, jnp.bfloat16),) * 2,
        in_specs=anywhere(len(sources) + 4),
        out_specs=tuple(anywhere(2)),
        scratch_shapes=[
            pltpu.VMEM(shape, jnp.bfloat16),
            pltpu.VMEM(shape, jnp.bfloat16),
            pltpu.VMEM((features, 2 * tokens), jnp.bfloat16),
            pltpu.VMEM((features, 2 * tokens), jnp.bfloat16),
            pltpu.VMEM((half, 2 * tokens), jnp.bfloat16),
            pltpu.VMEM((2 * half, 2 * tokens), jnp.bfloat16),
            pltpu.SemaphoreType.DMA(()),
            pltpu.SemaphoreType.DMA((2, len(cuts))),
            pltpu.SemaphoreType.DMA((4,)),
        ],
        cost_estimate=pl.CostEstimate(
            flops=24 * half * features * tokens,
            bytes_accessed=8 * features * tokens + 6 * 3 * half * features,
            transcendentals=2 * half * tokens,
        ),
        name="fast_sums",
        compiler_params=pltpu.CompilerParams(vmem_limit_bytes=VMEM_GRANT),
    )(*sources, keys, targets, pair_keys, pair_targets)


def recall_body(
    mine_ref, other_ref, far_ref, other_far_ref, pack_ref, pair_pack_ref, query_ref, out_ref,
    w_ref, near_sums_ref, far_sums_ref, held_ref, made_ref, sem,
):
    half = mine_ref.shape[1]
    hidden_rows, features = w_ref.shape[1:]
    nt = (((1,), (1,)), ((), ()))

    side = lax.axis_index("narrow") % 2

    def arriving(matrix):
        moves = (
            (mine_ref, near_sums_ref, side),
            (other_ref, near_sums_ref, 1 - side),
            (far_ref, far_sums_ref, side),
            (other_far_ref, far_sums_ref, 1 - side),
        )
        return [
            pltpu.make_async_copy(
                source.at[matrix],
                target.at[matrix, half_rows(part, half)],
                sem.at[place, matrix],
            )
            for place, (source, target, part) in enumerate(moves)
        ]

    sums = [arriving(matrix) for matrix in range(3)]
    weights = [
        pltpu.make_async_copy(source, w_ref.at[:, half_rows(part, half)], sem.at[4, place])
        for place, (source, part) in enumerate(((pack_ref, side), (pair_pack_ref, 1 - side)))
    ]
    queries = pltpu.make_async_copy(query_ref, held_ref, sem.at[5, 2])
    for copies in sums + [weights, [queries]]:
        for copy in copies:
            copy.start()
    rows = lax.broadcasted_iota(jnp.int32, (hidden_rows, features), 0)
    cols = lax.broadcasted_iota(jnp.int32, (hidden_rows, features), 1)
    diagonal = rows == cols
    rounded, gram, scale = [], [], []
    for matrix, copies in enumerate(sums):
        for copy in copies:
            copy.wait()
        summed = near_sums_ref[matrix].astype(jnp.float32) + far_sums_ref[matrix].astype(
            jnp.float32
        )
        x = summed.astype(jnp.bfloat16)
        product = lax.dot_general(x, x, nt, preferred_element_type=jnp.float32)
        trace = jnp.sum(jnp.where(diagonal, product, 0.0), axis=0, keepdims=True)
        scale.append(lax.rsqrt(jnp.sum(trace, axis=1, keepdims=True) + EPS))
        rounded.append(x)
        gram.append((product * (scale[-1] * scale[-1])).astype(jnp.bfloat16))
    current = rounded
    for sweep_index in range(NS_ITERS):
        if sweep_index:
            scale = [1.0] * 3
            gram = [
                lax.dot_general(x, x, nt, preferred_element_type=jnp.float32).astype(
                    jnp.bfloat16
                )
                for x in current
            ]
        lifted = [
            jnp.dot(g, x, preferred_element_type=jnp.float32).astype(jnp.bfloat16)
            for x, g in zip(current, gram)
        ]
        current = [
            (
                (COEF_A * r) * x.astype(jnp.float32)
                + (COEF_B * r) * y.astype(jnp.float32)
                + (COEF_C * r) * jnp.dot(g, y, preferred_element_type=jnp.float32)
            ).astype(jnp.bfloat16)
            for x, y, g, r in zip(current, lifted, gram, scale)
        ]
    for copy in weights:
        copy.wait()

    def fresh(i):
        axis = 0 if i == 2 else 1
        initial = w_ref[i].astype(jnp.float32)
        moved = initial - current[i].astype(jnp.float32)
        wanted = jnp.mean(jnp.square(initial), axis=axis, keepdims=True) + EPS
        present = jnp.mean(jnp.square(moved), axis=axis, keepdims=True) + EPS
        return (moved * (wanted * lax.rsqrt(wanted * present))).astype(jnp.bfloat16)

    queries.wait()
    tokens = held_ref.shape[1]
    block = tokens // 2
    spans = [slice(at, at + block) for at in range(0, tokens, block)]
    fresh_gate = fresh(0)
    gates = [
        jnp.dot(fresh_gate * jnp.bfloat16(0.5), held_ref[:, span], preferred_element_type=jnp.float32)
        for span in spans
    ]
    fresh_lift = fresh(1)
    lifts = [
        jnp.dot(fresh_lift, held_ref[:, span], preferred_element_type=jnp.float32) for span in spans
    ]
    fresh_down = fresh(2).T
    leaving = []
    for place, (span, gate, lift) in enumerate(zip(spans, gates, lifts)):
        hidden = (gate * (jnp.tanh(gate) + 1.0) * lift).astype(jnp.bfloat16)
        made_ref[:, span] = jnp.dot(
            fresh_down, hidden, preferred_element_type=jnp.float32
        ).astype(jnp.bfloat16)
        leaving.append(
            pltpu.make_async_copy(made_ref.at[:, span], out_ref.at[:, span], sem.at[5, place])
        )
        leaving[-1].start()
    for copy in leaving:
        copy.wait()


def fast_recall(sums, packs, queries):
    features, tokens = queries.shape
    half = packs[0].shape[1]
    hidden_rows = 2 * half
    return pl.pallas_call(
        recall_body,
        out_shape=jax.ShapeDtypeStruct((features, tokens), jnp.bfloat16),
        in_specs=anywhere(7),
        out_specs=pl.BlockSpec(memory_space=pl.ANY),
        scratch_shapes=[
            pltpu.VMEM((3, hidden_rows, features), jnp.bfloat16),
            pltpu.VMEM((3, hidden_rows, features), jnp.bfloat16),
            pltpu.VMEM((3, hidden_rows, features), jnp.bfloat16),
            pltpu.VMEM((features, tokens), jnp.bfloat16),
            pltpu.VMEM((features, tokens), jnp.bfloat16),
            pltpu.SemaphoreType.DMA((6, 3)),
        ],
        cost_estimate=pl.CostEstimate(
            flops=6 * hidden_rows * features * tokens + 18 * NS_ITERS * hidden_rows * features**2,
            bytes_accessed=4 * features * tokens + 12 * hidden_rows * features,
            transcendentals=hidden_rows * tokens,
        ),
        name="fast_recall",
        compiler_params=pltpu.CompilerParams(vmem_limit_bytes=VMEM_GRANT),
    )(*sums, *packs, queries)


def in_place(query_states, key_states, value_states, cache_keys, cache_values, gate_fast, *rest):
    features, tok_count = query_states.shape
    narrow_count = lax.axis_size("narrow")
    return (
        features == FD
        and gate_fast.shape[1:] == (FD, FD)
        and features % HEAD_SIZE == 0
        and tok_count % WINDOW == 0
        and tok_count >= 2 * WINDOW
        and narrow_count >= 4
        and narrow_count & (narrow_count - 1) == 0
    )


def in_place_plan(
    query_states,
    key_states,
    value_states,
    cache_keys,
    cache_values,
    gate_fast,
    lift_fast,
    down_fast,
    token_rates,
):
    wide_count = lax.axis_size("wide")
    narrow_count = lax.axis_size("narrow")
    owned = gate_fast.shape[0]

    def from_owner(value, step):
        pairs = []
        for wide in range(wide_count):
            start = wide * narrow_count
            owner = wide // owned
            pairs.append((start + owner, start + (owner ^ step)))
        return lax.ppermute(value, ("wide", "narrow"), pairs)

    own, other = prepare(gate_fast, lift_fast, down_fast)
    arrivals = {}
    for step in sorted(range(1, narrow_count), key=lambda step: step < 2):
        arrivals[step] = from_owner((own, other)[step % 2], step)
    pair_keys = swapped(key_states, "narrow", 0)
    parts = 2
    targets, *ends = stage(key_states, value_states, token_rates, parts)
    pair_targets = swapped(targets, "narrow", 0)
    attended = attend_late(query_states, key_states, value_states)
    sources = [own] + [arrivals[step] for step in range(1, narrow_count)]
    attended, ends = lax.optimization_barrier((attended, ends))
    sources, attended = lax.optimization_barrier((sources, attended))
    prior = []
    for end in ends:
        prior.append(from_behind(end, "narrow", 1))
    near, pack = fast_sums(sources, key_states, targets, pair_keys, pair_targets, owned)
    distances = range(1, narrow_count.bit_length() - 1)
    for distance in distances:
        far = swapped(near, "narrow", distance)
        if distance != distances[-1]:
            near = stored(near.astype(jnp.float32) + far.astype(jnp.float32))
    pair_pack = swapped(pack, "narrow", 0)
    pair_near = swapped(near, "narrow", 0)
    pair_far = swapped(far, "narrow", 0)
    attended, *state = attend_early(
        query_states, key_states, value_states, prior[0], cache_keys, cache_values, attended
    )
    attended = attend_last(query_states, prior[1], cache_keys, cache_values, *state, attended)
    recalled = fast_recall((near, pair_near, far, pair_far), (pack, pair_pack), query_states)
    return (attended, recalled)


def spread_plan(
    query_states,
    key_states,
    value_states,
    cache_keys,
    cache_values,
    gate_fast,
    lift_fast,
    down_fast,
    token_rates,
):
    features, tok_count = query_states.shape
    edge_cols = jnp.stack(
        [key_states[:, tok_count - WINDOW :], value_states[:, tok_count - WINDOW :]]
    )
    arrived = from_behind(edge_cols, "narrow", 1)
    leading = lax.axis_index("narrow") == 0
    prior_cols = jnp.where(leading, jnp.stack([cache_keys, cache_values]), arrived)
    ext_keys = jnp.concatenate([prior_cols[0], key_states], axis=1)
    ext_values = jnp.concatenate([prior_cols[1], value_states], axis=1)
    if features % HEAD_SIZE == 0:
        attended = attend_local(query_states, ext_keys, ext_values, 0)
    else:
        attended = attend_paired(query_states, ext_keys, ext_values)
    query_fast, key_fast, value_fast = (
        lax.all_to_all(
            lax.all_to_all(query_states, "wide", split_axis=1, concat_axis=0, tiled=True),
            "narrow",
            split_axis=0,
            concat_axis=1,
            tiled=True,
        ),
        lax.all_to_all(
            lax.all_to_all(key_states, "wide", split_axis=1, concat_axis=0, tiled=True),
            "narrow",
            split_axis=0,
            concat_axis=1,
            tiled=True,
        ),
        lax.all_to_all(
            lax.all_to_all(value_states, "wide", split_axis=1, concat_axis=0, tiled=True),
            "narrow",
            split_axis=0,
            concat_axis=1,
            tiled=True,
        ),
    )
    head_count = gate_fast.shape[0]
    wide_count = lax.axis_size("wide")
    narrow_count = lax.axis_size("narrow")
    piece_rows = tok_count // wide_count
    fast_tokens = query_fast.shape[1]
    rate_blocks = token_rates.reshape(token_rates.shape[0], narrow_count, wide_count, piece_rows)
    rates_here = lax.dynamic_slice(
        rate_blocks,
        (lax.axis_index("narrow") * head_count, 0, lax.axis_index("wide"), 0),
        (head_count, narrow_count, 1, piece_rows),
    ).reshape(head_count, fast_tokens)
    query_heads = query_fast.reshape(head_count, FD, fast_tokens)
    key_heads = key_fast.reshape(head_count, FD, fast_tokens)
    value_heads = value_fast.reshape(head_count, FD, fast_tokens)
    recall = fast_group(
        gate_fast, lift_fast, down_fast, query_heads, key_heads, value_heads, rates_here
    )
    recall = recall.reshape(head_count * FD, fast_tokens)
    recalled = lax.all_to_all(
        lax.all_to_all(recall, "narrow", split_axis=1, concat_axis=0, tiled=True),
        "wide",
        split_axis=0,
        concat_axis=1,
        tiled=True,
    )
    return (attended, recalled)


def per_device(*arrays):
    if in_place(*arrays):
        return in_place_plan(*arrays)
    return spread_plan(*arrays)


def solution(mesh):
    in_specs = (
        P("wide", "narrow"),
        P("wide", "narrow"),
        P("wide", "narrow"),
        P("wide", None),
        P("wide", None),
        P("narrow", None, None),
        P("narrow", None, None),
        P("narrow", None, None),
        P(),
    )
    out_specs = (P("wide", "narrow"), P("wide", "narrow"))
    return jax.shard_map(
        per_device, mesh=mesh, in_specs=in_specs, out_specs=out_specs, check_vma=False
    )
```

```python
import functools
import math

import jax
import jax.numpy as jnp
from jax import lax
from jax.experimental import pallas as pl
from jax.experimental.pallas import tpu as pltpu
from jax.sharding import PartitionSpec as P


FD = 512
HEAD_SIZE = 128
WINDOW = 1024
NS_ITERS = 2


EPS = 1e-06
COEF_A = 3.4445
COEF_B = -4.775
COEF_C = 2.0315
LOG2E = math.log2(math.e)
VMEM_GRANT = 67043328


def swapped(array, axis, distance):
    return lax.ppermute(array, axis, [(i, i ^ 1 << distance) for i in range(lax.axis_size(axis))])


def shortened(array):

    def short(part):
        return part.astype(jnp.bfloat16) if part.dtype == jnp.float32 else part

    return jax.tree.map(short, array)


def from_behind(value, axis, steps):
    count = lax.axis_size(axis)
    initial, last = (max(0, -steps), min(count, count - steps))
    return lax.ppermute(value, axis, [(source, source + steps) for source in range(initial, last)])


def stored(value):
    return lax.optimization_barrier(value.astype(jnp.bfloat16))


def attend_local(query_states, ext_keys, ext_values, key_start):
    features, tok_count = query_states.shape
    head_count = features // HEAD_SIZE
    block_rows = min(512, tok_count)
    block_count = tok_count // block_rows
    key_span = WINDOW + block_rows
    scaling = 1.0 / math.sqrt(HEAD_SIZE)
    rows_at = lax.broadcasted_iota(jnp.int32, (block_rows, key_span), 0)
    cols_at = lax.broadcasted_iota(jnp.int32, (block_rows, key_span), 1)
    visible = (cols_at > rows_at) & (cols_at <= rows_at + WINDOW)

    def one_block(block_index):
        offset = block_index * block_rows
        query_part = lax.dynamic_slice_in_dim(query_states, offset, block_rows, 1).reshape(
            head_count, HEAD_SIZE, block_rows
        )
        key_part = lax.dynamic_slice_in_dim(ext_keys, key_start + offset, key_span, 1).reshape(
            head_count, HEAD_SIZE, key_span
        )
        value_part = lax.dynamic_slice_in_dim(ext_values, key_start + offset, key_span, 1).reshape(
            head_count, HEAD_SIZE, key_span
        )
        scores = (
            jnp.einsum("hdq,hdk->hqk", query_part, key_part, preferred_element_type=jnp.float32)
            * scaling
        )
        scores = jnp.where(visible[None], scores, -jnp.inf)
        highest = jnp.max(scores, axis=2, keepdims=True)
        raised = jnp.exp(scores - highest)
        weights = (raised / jnp.sum(raised, axis=2, keepdims=True)).astype(jnp.bfloat16)
        blended = jnp.einsum(
            "hdk,hqk->hdq", value_part, weights, preferred_element_type=jnp.float32
        )
        return blended.astype(jnp.bfloat16).reshape(features, block_rows)

    blocks_out = lax.map(one_block, jnp.arange(block_count, dtype=jnp.int32))
    return jnp.transpose(blocks_out, (1, 0, 2)).reshape(features, tok_count)


def attend_paired(query_states, ext_keys, ext_values):
    features, tok_count = query_states.shape
    half_rows = tok_count // 2
    lower = lax.axis_index("wide") % 2 == 0
    query_send = jnp.where(lower, query_states[:, half_rows:], query_states[:, :half_rows])
    query_keep = jnp.where(lower, query_states[:, :half_rows], query_states[:, half_rows:])
    other_keys, other_values, other_queries = swapped((ext_keys, ext_values, query_send), "wide", 0)
    full_keys = jnp.where(
        lower,
        jnp.concatenate([ext_keys, other_keys], axis=0),
        jnp.concatenate([other_keys, ext_keys], axis=0),
    )
    full_values = jnp.where(
        lower,
        jnp.concatenate([ext_values, other_values], axis=0),
        jnp.concatenate([other_values, ext_values], axis=0),
    )
    full_queries = jnp.where(
        lower,
        jnp.concatenate([query_keep, other_queries], axis=0),
        jnp.concatenate([other_queries, query_keep], axis=0),
    )
    key_start = jnp.where(lower, 0, half_rows).astype(jnp.int32)
    head_out = attend_local(full_queries, full_keys, full_values, key_start)
    out_keep = jnp.where(lower, head_out[:features], head_out[features:])
    out_send = jnp.where(lower, head_out[features:], head_out[:features])
    out_other = swapped(shortened(out_send), "wide", 0).astype(out_send.dtype)
    return jnp.where(
        lower,
        jnp.concatenate([out_keep, out_other], axis=1),
        jnp.concatenate([out_other, out_keep], axis=1),
    )


def fast_terms(gate_weight, lift_weight, down_weight, key_heads, value_heads, rates_here):
    pre_gate = jnp.einsum(
        "hcf,hft->hct", gate_weight, key_heads, preferred_element_type=jnp.float32
    )
    pre_lift = jnp.einsum(
        "hcf,hft->hct", lift_weight, key_heads, preferred_element_type=jnp.float32
    )
    sigmoid_gate = jax.nn.sigmoid(pre_gate)
    silu_gate = pre_gate * sigmoid_gate
    hidden = (silu_gate * pre_lift).astype(jnp.bfloat16)
    target = (-(value_heads.astype(jnp.float32) * rates_here[:, None, :])).astype(jnp.bfloat16)
    grad_down = jnp.einsum("hft,hct->hfc", target, hidden, preferred_element_type=jnp.float32)
    back_hidden = jnp.einsum(
        "hfc,hft->hct", down_weight, target, preferred_element_type=jnp.float32
    )
    back_lift = (back_hidden * silu_gate).astype(jnp.bfloat16)
    back_gate = (
        back_hidden * pre_lift * sigmoid_gate * (1.0 + pre_gate * (1.0 - sigmoid_gate))
    ).astype(jnp.bfloat16)
    grad_gate = jnp.einsum("hct,hft->hcf", back_gate, key_heads, preferred_element_type=jnp.float32)
    grad_lift = jnp.einsum("hct,hft->hcf", back_lift, key_heads, preferred_element_type=jnp.float32)
    return (grad_gate, grad_lift, grad_down)


def scaled_start(rounded):
    widened = rounded.astype(jnp.float32)
    norm_val = jnp.sqrt(jnp.sum(jnp.square(widened), axis=(1, 2), keepdims=True) + EPS)
    return stored(widened / norm_val)


def starting(grad_gate, grad_lift, grad_down):
    sum_gate, sum_lift, sum_down = lax.psum((grad_gate, grad_lift, grad_down), "wide")
    return (
        scaled_start(stored(sum_gate)),
        scaled_start(stored(sum_lift)),
        scaled_start(stored(sum_down)),
    )


def orthogonal(current):
    for _ in range(NS_ITERS):
        gram_mat = jnp.einsum(
            "hrc,hrd->hcd", current, current, preferred_element_type=jnp.float32
        ).astype(jnp.bfloat16)
        lifted = stored(
            jnp.einsum("hrc,hcd->hrd", current, gram_mat, preferred_element_type=jnp.float32)
        )
        current = stored(
            COEF_A * current.astype(jnp.float32)
            + COEF_B * lifted.astype(jnp.float32)
            + COEF_C
            * jnp.einsum("hrc,hcd->hrd", lifted, gram_mat, preferred_element_type=jnp.float32)
        )
    return current


def refreshed(weight, ortho):
    initial = weight.astype(jnp.float32)
    moved_rows = initial - ortho.astype(jnp.float32)
    wanted = jnp.sqrt(jnp.mean(jnp.square(initial), axis=-1, keepdims=True) + EPS)
    present = jnp.sqrt(jnp.mean(jnp.square(moved_rows), axis=-1, keepdims=True) + EPS)
    return (moved_rows * (wanted / present)).astype(jnp.bfloat16)


def fast_group(
    gate_weight, lift_weight, down_weight, query_heads, key_heads, value_heads, rates_here
):
    grad_gate, grad_lift, grad_down = fast_terms(
        gate_weight, lift_weight, down_weight, key_heads, value_heads, rates_here
    )
    start_gate, start_lift, start_down = starting(grad_gate, grad_lift, grad_down)
    fresh_gate = refreshed(gate_weight, orthogonal(start_gate))
    fresh_lift = refreshed(lift_weight, orthogonal(start_lift))
    fresh_down = refreshed(down_weight, orthogonal(start_down))
    query_gate = jnp.einsum(
        "hcf,hft->hct", fresh_gate, query_heads, preferred_element_type=jnp.float32
    )
    query_lift = jnp.einsum(
        "hcf,hft->hct", fresh_lift, query_heads, preferred_element_type=jnp.float32
    )
    query_hidden = (jax.nn.silu(query_gate) * query_lift).astype(jnp.bfloat16)
    return jnp.einsum(
        "hfc,hct->hft", fresh_down, query_hidden, preferred_element_type=jnp.float32
    ).astype(jnp.bfloat16)


def attend_body(
    q_ref, kp_ref, vp_ref, kc_ref, vc_ref, o_ref, kt_ref, v_ref, *, block, window
):
    hd = q_ref.shape[0]
    scale = LOG2E / math.sqrt(hd)

    placed(kp_ref, vp_ref, kt_ref, v_ref, 0)
    placed(kc_ref, vc_ref, kt_ref, v_ref, window)
    v_ref[hd:, :] = jnp.ones((v_ref.shape[0] - hd, 2 * window), jnp.bfloat16)
    rows = lax.broadcasted_iota(jnp.int32, (block, block), 0)
    cols = lax.broadcasted_iota(jnp.int32, (block, block), 1)
    first = rows > cols
    inner = window // block

    def scores(b):
        q = q_ref[:, b * block : (b + 1) * block].astype(jnp.float32) * scale
        high = q.astype(jnp.bfloat16)
        low = (q - high.astype(jnp.float32)).astype(jnp.bfloat16)
        pair = jnp.concatenate([high, low], axis=0)
        parts = [
            jnp.dot(
                kt_ref[(b + j) * block : (b + j + 1) * block, :],
                pair,
                preferred_element_type=jnp.float32,
            )
            for j in range(inner + 1)
        ]
        return [jnp.where(first, parts[0], parts[inner])] + parts[1:inner]

    def blend(b, parts):
        top = functools.reduce(jnp.maximum, parts)
        top = jnp.max(top, axis=0, keepdims=True)
        raised = [jnp.exp2(part - top).astype(jnp.bfloat16) for part in parts]
        zero = jnp.zeros_like(raised[0])
        ends = jnp.where(first, raised[0], zero), jnp.where(first, zero, raised[0])
        weights = jnp.concatenate([ends[0]] + raised[1:] + [ends[1]], axis=0)
        span = v_ref[:, b * block : (b + inner + 1) * block]
        out = jnp.dot(span, weights, preferred_element_type=jnp.float32)
        o_ref[:, b * block : (b + 1) * block] = (out[:hd] * (1.0 / out[hd : hd + 1])).astype(
            jnp.bfloat16
        )

    ready = scores(0)
    for b in range(1, inner):
        following = scores(b)
        blend(b - 1, ready)
        ready = following
    blend(inner - 1, ready)


def attend_scratch():
    return [
        pltpu.VMEM((2 * WINDOW, 2 * HEAD_SIZE), jnp.bfloat16),
        pltpu.VMEM((HEAD_SIZE + 16, 2 * WINDOW), jnp.bfloat16),
    ]


def attend_late(queries, keys, values):
    features, tokens = queries.shape
    heads, chunks = features // HEAD_SIZE, tokens // WINDOW - 1
    here = pl.BlockSpec((HEAD_SIZE, WINDOW), lambda h, c: (h, c + 1))
    before = pl.BlockSpec((HEAD_SIZE, WINDOW), lambda h, c: (h, c))
    return pl.pallas_call(
        functools.partial(attend_body, block=min(256, WINDOW), window=WINDOW),
        out_shape=jax.ShapeDtypeStruct((features, tokens), jnp.bfloat16),
        grid=(heads, chunks),
        in_specs=[here, before, before, here, here],
        out_specs=here,
        scratch_shapes=attend_scratch(),
        cost_estimate=pl.CostEstimate(
            flops=5 * features * chunks * WINDOW**2,
            bytes_accessed=10 * features * chunks * WINDOW,
            transcendentals=heads * chunks * WINDOW**2,
        ),
        name="attend_late",
        compiler_params=pltpu.CompilerParams(vmem_limit_bytes=VMEM_GRANT),
    )(queries, keys, values, keys, values)


def two_term(q_ref, at, scale):
    q = q_ref[:, at].astype(jnp.float32) * scale
    high = q.astype(jnp.bfloat16)
    low = (q - high.astype(jnp.float32)).astype(jnp.bfloat16)
    return jnp.concatenate([high, low], axis=0)


def placed(k, v, kt_ref, v_ref, at):
    hd, width = k.shape
    turned = k[...].T
    kt_ref[at : at + width, :hd] = turned
    kt_ref[at : at + width, hd:] = turned
    v_ref[:hd, at : at + width] = v[...]


def early_body(
    q_ref, kp_ref, vp_ref, kc_ref, vc_ref, ck_ref, cv_ref, _, o_ref, part_ref, top_ref, mass_ref,
    kt_ref, v_ref, *, block,
):
    hd, window = q_ref.shape
    scale = LOG2E / math.sqrt(hd)
    near = kp_ref.shape[1]
    inner = window // block
    missing = (window - near) // block
    leading = lax.axis_index("narrow") == 0

    @pl.when(leading)
    def _():
        placed(ck_ref.at[:, window - near :], cv_ref.at[:, window - near :], kt_ref, v_ref, 0)

    @pl.when(jnp.logical_not(leading))
    def _():
        placed(kp_ref, vp_ref, kt_ref, v_ref, 0)

    placed(kc_ref, vc_ref, kt_ref, v_ref, near)
    v_ref[hd:, :] = jnp.ones((v_ref.shape[0] - hd, v_ref.shape[1]), jnp.bfloat16)
    rows = lax.broadcasted_iota(jnp.int32, (block, block), 0)
    cols = lax.broadcasted_iota(jnp.int32, (block, block), 1)
    first = rows > cols

    def chunk(j):
        return slice((j - missing) * block, (j - missing + 1) * block)

    def scores(b):
        pair = two_term(q_ref, slice(b * block, (b + 1) * block), scale)
        parts = [
            jnp.dot(kt_ref[chunk(j), :], pair, preferred_element_type=jnp.float32)
            for j in range(max(b, missing), b + inner + 1)
        ]
        if b >= missing:
            return [jnp.where(first, parts[0], parts[inner])] + parts[1:inner]
        return parts[:-1] + [jnp.where(first, -jnp.inf, parts[-1])]

    def blend(b, parts):
        top = functools.reduce(jnp.maximum, parts)
        top = jnp.max(top, axis=0, keepdims=True)
        raised = [jnp.exp2(part - top).astype(jnp.bfloat16) for part in parts]
        if b >= missing:
            zero = jnp.zeros_like(raised[0])
            ends = jnp.where(first, raised[0], zero), jnp.where(first, zero, raised[0])
            raised = [ends[0]] + raised[1:] + [ends[1]]
        span = v_ref[:, chunk(max(b, missing)).start : chunk(b + inner).stop]
        out = jnp.dot(span, jnp.concatenate(raised, axis=0), preferred_element_type=jnp.float32)
        if b >= missing:
            at = slice(b * block, (b + 1) * block)
            o_ref[:, at] = (out[:hd] * (1.0 / out[hd : hd + 1])).astype(jnp.bfloat16)
        else:
            at = slice(b * block, (b + 1) * block)
            part_ref[:, at] = out[:hd]
            top_ref[:, at] = jnp.broadcast_to(top, (top_ref.shape[0], block))
            mass_ref[:, at] = jnp.broadcast_to(out[hd : hd + 1], (top_ref.shape[0], block))

    ready = scores(0)
    for b in range(1, inner):
        following = scores(b)
        blend(b - 1, ready)
        ready = following
    blend(inner - 1, ready)


def attend_early(queries, keys, values, prior, cache_keys, cache_values, late):
    features, tokens = queries.shape
    heads = features // HEAD_SIZE
    near = prior.shape[2]
    far = WINDOW - near
    here = pl.BlockSpec((HEAD_SIZE, WINDOW), lambda h: (h, 0))
    prior_keys = pl.BlockSpec((None, HEAD_SIZE, near), lambda h: (0, h, 0))
    prior_values = pl.BlockSpec((None, HEAD_SIZE, near), lambda h: (1, h, 0))
    rows = 8
    stats = jax.ShapeDtypeStruct((heads * rows, far), jnp.float32)
    stat = pl.BlockSpec((rows, far), lambda h: (h, 0))
    return pl.pallas_call(
        functools.partial(early_body, block=min(256, far)),
        out_shape=(
            jax.ShapeDtypeStruct((features, tokens), jnp.bfloat16),
            jax.ShapeDtypeStruct((features, far), jnp.float32),
            stats,
            stats,
        ),
        grid=(heads,),
        in_specs=[here, prior_keys, prior_values, here, here, here, here]
        + [pl.BlockSpec(memory_space=pl.ANY)],
        out_specs=(here, pl.BlockSpec((HEAD_SIZE, far), lambda h: (h, 0)), stat, stat),
        scratch_shapes=[
            pltpu.VMEM((near + WINDOW, 2 * HEAD_SIZE), jnp.bfloat16),
            pltpu.VMEM((HEAD_SIZE + 16, near + WINDOW), jnp.bfloat16),
        ],
        input_output_aliases={7: 0},
        cost_estimate=pl.CostEstimate(
            flops=5 * features * WINDOW**2,
            bytes_accessed=14 * features * WINDOW,
            transcendentals=heads * WINDOW**2,
        ),
        name="attend_early",
        compiler_params=pltpu.CompilerParams(vmem_limit_bytes=VMEM_GRANT),
    )(queries, prior, prior, keys, values, cache_keys, cache_values, late)


def last_body(
    q_ref, prior_ref, ck_ref, cv_ref, part_ref, top_ref, mass_ref, _, o_ref,
    held_q, held_k, held_v, held_part, held_top, held_mass, kt_ref, v_ref, made_ref, sem,
    *, block,
):
    features, far = part_ref.shape
    hd = HEAD_SIZE
    heads = features // hd
    scale = LOG2E / math.sqrt(hd)
    missing = far // block
    leading = lax.axis_index("narrow") == 0
    plain = [
        pltpu.make_async_copy(top_ref, held_top, sem.at[0, 0]),
        pltpu.make_async_copy(mass_ref, held_mass, sem.at[0, 1]),
    ]
    arriving = []
    for h in range(heads):
        at = slice(h * hd, (h + 1) * hd)
        keys = pltpu.make_async_copy(prior_ref.at[0, at], held_k.at[at], sem.at[1, h])
        values = pltpu.make_async_copy(prior_ref.at[1, at], held_v.at[at], sem.at[2, h])

        @pl.when(leading)
        def _(at=at, h=h):
            pltpu.make_async_copy(ck_ref.at[at, :far], held_k.at[at], sem.at[1, h]).start()
            pltpu.make_async_copy(cv_ref.at[at, :far], held_v.at[at], sem.at[2, h]).start()

        @pl.when(jnp.logical_not(leading))
        def _(keys=keys, values=values):
            keys.start()
            values.start()

        others = [
            pltpu.make_async_copy(q_ref.at[at, :far], held_q.at[at], sem.at[3, h]),
            pltpu.make_async_copy(part_ref.at[at], held_part.at[at], sem.at[4, h]),
        ]
        for copy in others + (plain if h == 0 else []):
            copy.start()
        arriving.append([keys, values] + others)
    rows = lax.broadcasted_iota(jnp.int32, (block, block), 0)
    cols = lax.broadcasted_iota(jnp.int32, (block, block), 1)
    first = rows > cols
    v_ref[:, hd:, :] = jnp.ones((heads, v_ref.shape[1] - hd, far), jnp.bfloat16)
    leaving = []
    for copy in plain:
        copy.wait()

    def scores(h, b):
        at = slice(h * hd, (h + 1) * hd)
        if b == 0:
            for copy in arriving[h]:
                copy.wait()
            placed(held_k.at[at], held_v.at[at], kt_ref.at[h], v_ref.at[h], 0)
        pair = two_term(held_q.at[at], slice(b * block, (b + 1) * block), scale)
        parts = [
            jnp.dot(
                kt_ref[h, j * block : (j + 1) * block, :], pair, preferred_element_type=jnp.float32
            )
            for j in range(b, missing)
        ]
        return [jnp.where(first, parts[0], -jnp.inf)] + parts[1:]

    def blend(h, b, parts):
        at = slice(h * hd, (h + 1) * hd)
        span = slice(b * block, (b + 1) * block)
        before = held_top[h * 8 : h * 8 + 1, span]
        top = functools.reduce(jnp.maximum, parts)
        top = jnp.maximum(jnp.max(top, axis=0, keepdims=True), before)
        kept = jnp.exp2(before - top)
        weights = jnp.concatenate(
            [jnp.exp2(part - top).astype(jnp.bfloat16) for part in parts], axis=0
        )
        out = jnp.dot(v_ref[h, :, b * block :], weights, preferred_element_type=jnp.float32)
        mass = held_mass[h * 8 : h * 8 + 1, span] * kept + out[hd : hd + 1]
        made_ref[at, span] = ((held_part[at, span] * kept + out[:hd]) * (1.0 / mass)).astype(
            jnp.bfloat16
        )
        if b == missing - 1:
            leaving.append(
                pltpu.make_async_copy(made_ref.at[at], o_ref.at[at, :far], sem.at[5, h])
            )
            leaving[-1].start()

    turns = [(h, b) for h in range(heads) for b in range(missing)]
    ready = scores(*turns[0])
    for turn, ahead in zip(turns, turns[1:]):
        following = scores(*ahead)
        blend(*turn, ready)
        ready = following
    blend(*turns[-1], ready)
    for copy in leaving:
        copy.wait()


def attend_last(queries, prior, cache_keys, cache_values, part, top, mass, early):
    features, tokens = queries.shape
    heads = features // HEAD_SIZE
    far = part.shape[1]
    pieces = pltpu.VMEM((features, far), jnp.bfloat16)
    return pl.pallas_call(
        functools.partial(last_body, block=min(256, far)),
        out_shape=jax.ShapeDtypeStruct((features, tokens), jnp.bfloat16),
        in_specs=[pl.BlockSpec(memory_space=pl.ANY)] * 8,
        out_specs=pl.BlockSpec(memory_space=pl.ANY),
        scratch_shapes=[
            pieces,
            pieces,
            pieces,
            pltpu.VMEM((features, far), jnp.float32),
            pltpu.VMEM(top.shape, jnp.float32),
            pltpu.VMEM(top.shape, jnp.float32),
            pltpu.VMEM((heads, far, 2 * HEAD_SIZE), jnp.bfloat16),
            pltpu.VMEM((heads, HEAD_SIZE + 16, far), jnp.bfloat16),
            pieces,
            pltpu.SemaphoreType.DMA((6, max(heads, 2))),
        ],
        input_output_aliases={7: 0},
        cost_estimate=pl.CostEstimate(
            flops=3 * features * far**2,
            bytes_accessed=14 * features * far,
            transcendentals=heads * far**2,
        ),
        name="attend_last",
        compiler_params=pltpu.CompilerParams(vmem_limit_bytes=VMEM_GRANT),
    )(queries, prior, cache_keys, cache_values, part, top, mass, early)


def anywhere(count):
    return [pl.BlockSpec(memory_space=pl.ANY)] * count


def half_rows(part, half):
    return pl.ds(pl.multiple_of(part * half, half), half)


def prepare_body(gate_ref, lift_ref, down_ref, own_ref, other_ref, w_ref, out_ref, sem):
    owned = gate_ref.shape[0]
    local = lax.axis_index("wide") % owned
    side = lax.axis_index("narrow") % 2
    half = own_ref.shape[1]
    copies = [
        pltpu.make_async_copy(source.at[local], w_ref.at[place], sem.at[0, place])
        for place, source in enumerate((down_ref, gate_ref, lift_ref))
    ]
    for copy in copies:
        copy.start()
    leaving = []
    copies[0].wait()
    out_ref[...] = w_ref[0].T
    for order, (place, source) in enumerate(((2, out_ref), (0, w_ref.at[1]), (1, w_ref.at[2]))):
        if order:
            copies[order].wait()
        for turn, (target, part) in enumerate(((own_ref, side), (other_ref, 1 - side))):
            leaving.append(
                pltpu.make_async_copy(
                    source.at[half_rows(part, half)], target.at[place], sem.at[1 + turn, place]
                )
            )
            leaving[-1].start()
    for copy in leaving:
        copy.wait()


def prepare(gate_fast, lift_fast, down_fast):
    _, hidden_rows, features = gate_fast.shape
    shape = (3, hidden_rows // 2, features)
    return pl.pallas_call(
        prepare_body,
        out_shape=(jax.ShapeDtypeStruct(shape, jnp.bfloat16),) * 2,
        in_specs=anywhere(3),
        out_specs=tuple(anywhere(2)),
        scratch_shapes=[
            pltpu.VMEM((3, hidden_rows, features), jnp.bfloat16),
            pltpu.VMEM((hidden_rows, features), jnp.bfloat16),
            pltpu.SemaphoreType.DMA((3, 3)),
        ],
        cost_estimate=pl.CostEstimate(
            flops=0, bytes_accessed=12 * hidden_rows * features, transcendentals=0
        ),
        name="prepare",
        compiler_params=pltpu.CompilerParams(vmem_limit_bytes=VMEM_GRANT),
    )(gate_fast, lift_fast, down_fast)


def stage_body(key_ref, value_ref, rate_ref, target_ref, *refs):
    end_refs, (held_ref, values_ref, made_ref, sem, sem_end) = refs[:-5], refs[-5:]
    features, tokens = key_ref.shape
    step = HEAD_SIZE
    lasts, stop = [], tokens
    for end_ref in end_refs:
        lasts.append(slice(stop - end_ref.shape[2], stop))
        stop -= end_ref.shape[2]
    begin = pl.multiple_of(lax.axis_index("narrow") * tokens, tokens)
    rates = -rate_ref[pl.ds(lax.axis_index("wide"), 1), pl.ds(begin, tokens)]
    values = [
        pltpu.make_async_copy(
            value_ref.at[at : at + step], values_ref.at[at : at + step], sem.at[0, at // step]
        )
        for at in range(0, features, step)
    ]
    keys = [
        pltpu.make_async_copy(
            key_ref.at[:, last], held_ref.at[:, last.start - stop : last.stop - stop], sem_end.at[0, part]
        )
        for part, last in enumerate(lasts)
    ]
    for copy in values + keys:
        copy.start()
    leaving = []

    def leave(source, target, mark):
        leaving.append(pltpu.make_async_copy(source, target, mark))
        leaving[-1].start()

    for place, copy in enumerate(values):
        at = slice(place * step, (place + 1) * step)
        copy.wait()
        made_ref[at] = (values_ref[at].astype(jnp.float32) * rates).astype(jnp.bfloat16)
        leave(made_ref.at[at], target_ref.at[at], sem.at[1, place])
    for part, end_ref in enumerate(end_refs):
        leave(values_ref.at[:, lasts[part]], end_ref.at[1], sem_end.at[1, part])
        keys[part].wait()
        last = lasts[part]
        leave(
            held_ref.at[:, last.start - stop : last.stop - stop], end_ref.at[0], sem_end.at[2, part]
        )
    for copy in leaving:
        copy.wait()


def stage(keys, values, rates, widths):
    features, tokens = keys.shape
    parts = len(widths)
    return pl.pallas_call(
        stage_body,
        out_shape=(jax.ShapeDtypeStruct((features, tokens), jnp.bfloat16),)
        + tuple(jax.ShapeDtypeStruct((2, features, width), jnp.bfloat16) for width in widths),
        in_specs=anywhere(2) + [pl.BlockSpec(memory_space=pltpu.VMEM)],
        out_specs=tuple(anywhere(1 + parts)),
        scratch_shapes=[
            pltpu.VMEM((features, sum(widths)), jnp.bfloat16),
            pltpu.VMEM((features, tokens), jnp.bfloat16),
            pltpu.VMEM((features, tokens), jnp.bfloat16),
            pltpu.SemaphoreType.DMA((2, features // HEAD_SIZE)),
            pltpu.SemaphoreType.DMA((3, parts)),
        ],
        cost_estimate=pl.CostEstimate(
            flops=features * tokens,
            bytes_accessed=4 * features * tokens + 8 * features * WINDOW,
            transcendentals=0,
        ),
        name="stage",
        compiler_params=pltpu.CompilerParams(vmem_limit_bytes=VMEM_GRANT),
    )(keys, values, rates)


def sums_body(*refs, owned, cuts):
    sources = refs[:-15]
    (
        key_ref, target_ref, pair_key_ref, pair_target_ref,
        send_out, pack_out,
        send_ref, pack_ref, keys_ref, targets_ref, hidden_ref, back_ref, sem, sem_in, sem_out,
    ) = refs[-15:]
    _, tokens = key_ref.shape
    half = pack_ref.shape[1]
    role = lax.axis_index("narrow") ^ (lax.axis_index("wide") // owned)

    for place, source in enumerate(sources):

        @pl.when(role == place)
        def _(source=source):
            pltpu.make_async_copy(source, pack_ref, sem).start()

    spans = [(key_ref, target_ref, 0, begin, end) for begin, end in zip(cuts, cuts[1:])]
    spans.append((pair_key_ref, pair_target_ref, tokens, 0, tokens))
    arrivals = []
    for slot, (keys, targets, base, begin, end) in enumerate(spans):
        source, place = slice(begin, end), slice(base + begin, base + end)
        copies = (
            pltpu.make_async_copy(keys.at[:, source], keys_ref.at[:, place], sem_in.at[0, slot]),
            pltpu.make_async_copy(
                targets.at[:, source], targets_ref.at[:, place], sem_in.at[1, slot]
            ),
        )
        for copy in copies:
            copy.start()
        arrivals.append((place, *copies))
    pltpu.make_async_copy(sources[0], pack_ref, sem).wait()
    leaving = [pltpu.make_async_copy(pack_ref, pack_out, sem_out.at[3])]
    leaving[0].start()
    gate_lift = jnp.concatenate([pack_ref[0] * jnp.bfloat16(0.5), pack_ref[1]], axis=0)
    down = pack_ref[2]

    for at, keys, targets in arrivals:
        keys.wait()
        pre = jnp.dot(gate_lift, keys_ref[:, at], preferred_element_type=jnp.float32)
        targets.wait()
        back_hidden = jnp.dot(down, targets_ref[:, at], preferred_element_type=jnp.float32)
        half_gate = pre[:half]
        pre_lift = pre[half:]
        twice = jnp.tanh(half_gate) + 1.0
        silu_gate = half_gate * twice
        hidden_ref[:, at] = (silu_gate * pre_lift).astype(jnp.bfloat16)
        slope = twice + silu_gate * (2.0 - twice)
        back_ref[:half, at] = (back_hidden * pre_lift * slope).astype(jnp.bfloat16)
        back_ref[half:, at] = (back_hidden * silu_gate).astype(jnp.bfloat16)

    def leave(place, value):
        send_ref[place] = value.astype(jnp.bfloat16)
        leaving.append(
            pltpu.make_async_copy(send_ref.at[place], send_out.at[place], sem_out.at[place])
        )
        leaving[-1].start()

    contract = (((1,), (1,)), ((), ()))
    sums = lax.dot_general(
        back_ref[...], keys_ref[...], contract, preferred_element_type=jnp.float32
    )
    leave(0, sums[:half] * 0.5)
    leave(1, sums[half:])
    sums = lax.dot_general(
        hidden_ref[...], targets_ref[...], contract, preferred_element_type=jnp.float32
    )
    leave(2, sums)
    for copy in leaving:
        copy.wait()


def fast_sums(sources, keys, targets, pair_keys, pair_targets, owned):
    features, tokens = keys.shape
    shape = sources[0].shape
    half = shape[1]
    cuts = (0, tokens)
    return pl.pallas_call(
        functools.partial(sums_body, owned=owned, cuts=cuts),
        out_shape=(jax.ShapeDtypeStruct(shape, jnp.bfloat16),) * 2,
        in_specs=anywhere(len(sources) + 4),
        out_specs=tuple(anywhere(2)),
        scratch_shapes=[
            pltpu.VMEM(shape, jnp.bfloat16),
            pltpu.VMEM(shape, jnp.bfloat16),
            pltpu.VMEM((features, 2 * tokens), jnp.bfloat16),
            pltpu.VMEM((features, 2 * tokens), jnp.bfloat16),
            pltpu.VMEM((half, 2 * tokens), jnp.bfloat16),
            pltpu.VMEM((2 * half, 2 * tokens), jnp.bfloat16),
            pltpu.SemaphoreType.DMA(()),
            pltpu.SemaphoreType.DMA((2, len(cuts))),
            pltpu.SemaphoreType.DMA((4,)),
        ],
        cost_estimate=pl.CostEstimate(
            flops=24 * half * features * tokens,
            bytes_accessed=8 * features * tokens + 6 * 3 * half * features,
            transcendentals=2 * half * tokens,
        ),
        name="fast_sums",
        compiler_params=pltpu.CompilerParams(vmem_limit_bytes=VMEM_GRANT),
    )(*sources, keys, targets, pair_keys, pair_targets)


def recall_body(
    mine_ref, other_ref, far_ref, other_far_ref, pack_ref, pair_pack_ref, query_ref, out_ref,
    w_ref, near_sums_ref, far_sums_ref, held_ref, made_ref, sem,
):
    half = mine_ref.shape[1]
    hidden_rows, features = w_ref.shape[1:]
    nt = (((1,), (1,)), ((), ()))

    side = lax.axis_index("narrow") % 2

    def arriving(matrix):
        moves = (
            (mine_ref, near_sums_ref, side),
            (other_ref, near_sums_ref, 1 - side),
            (far_ref, far_sums_ref, side),
            (other_far_ref, far_sums_ref, 1 - side),
        )
        return [
            pltpu.make_async_copy(
                source.at[matrix],
                target.at[matrix, half_rows(part, half)],
                sem.at[place, matrix],
            )
            for place, (source, target, part) in enumerate(moves)
        ]

    sums = [arriving(matrix) for matrix in range(3)]
    weights = [
        pltpu.make_async_copy(source, w_ref.at[:, half_rows(part, half)], sem.at[4, place])
        for place, (source, part) in enumerate(((pack_ref, side), (pair_pack_ref, 1 - side)))
    ]
    queries = pltpu.make_async_copy(query_ref, held_ref, sem.at[5, 2])
    for copies in sums + [weights, [queries]]:
        for copy in copies:
            copy.start()
    rows = lax.broadcasted_iota(jnp.int32, (hidden_rows, features), 0)
    cols = lax.broadcasted_iota(jnp.int32, (hidden_rows, features), 1)
    diagonal = rows == cols
    rounded, gram, scale = [], [], []
    for matrix, copies in enumerate(sums):
        for copy in copies:
            copy.wait()
        summed = near_sums_ref[matrix].astype(jnp.float32) + far_sums_ref[matrix].astype(
            jnp.float32
        )
        x = summed.astype(jnp.bfloat16)
        product = lax.dot_general(x, x, nt, preferred_element_type=jnp.float32)
        trace = jnp.sum(jnp.where(diagonal, product, 0.0), axis=0, keepdims=True)
        scale.append(lax.rsqrt(jnp.sum(trace, axis=1, keepdims=True) + EPS))
        rounded.append(x)
        gram.append((product * (scale[-1] * scale[-1])).astype(jnp.bfloat16))
    current = rounded
    for sweep_index in range(NS_ITERS):
        if sweep_index:
            scale = [1.0] * 3
            gram = [
                lax.dot_general(x, x, nt, preferred_element_type=jnp.float32).astype(
                    jnp.bfloat16
                )
                for x in current
            ]
        lifted = [
            jnp.dot(g, x, preferred_element_type=jnp.float32).astype(jnp.bfloat16)
            for x, g in zip(current, gram)
        ]
        current = [
            (
                (COEF_A * r) * x.astype(jnp.float32)
                + (COEF_B * r) * y.astype(jnp.float32)
                + (COEF_C * r) * jnp.dot(g, y, preferred_element_type=jnp.float32)
            ).astype(jnp.bfloat16)
            for x, y, g, r in zip(current, lifted, gram, scale)
        ]
    for copy in weights:
        copy.wait()

    def fresh(i):
        axis = 0 if i == 2 else 1
        initial = w_ref[i].astype(jnp.float32)
        moved = initial - current[i].astype(jnp.float32)
        wanted = jnp.mean(jnp.square(initial), axis=axis, keepdims=True) + EPS
        present = jnp.mean(jnp.square(moved), axis=axis, keepdims=True) + EPS
        return (moved * (wanted * lax.rsqrt(wanted * present))).astype(jnp.bfloat16)

    queries.wait()
    tokens = held_ref.shape[1]
    block = tokens // 2
    spans = [slice(at, at + block) for at in range(0, tokens, block)]
    fresh_gate = fresh(0)
    gates = [
        jnp.dot(fresh_gate * jnp.bfloat16(0.5), held_ref[:, span], preferred_element_type=jnp.float32)
        for span in spans
    ]
    fresh_lift = fresh(1)
    lifts = [
        jnp.dot(fresh_lift, held_ref[:, span], preferred_element_type=jnp.float32) for span in spans
    ]
    fresh_down = fresh(2).T
    leaving = []
    for place, (span, gate, lift) in enumerate(zip(spans, gates, lifts)):
        hidden = (gate * (jnp.tanh(gate) + 1.0) * lift).astype(jnp.bfloat16)
        made_ref[:, span] = jnp.dot(
            fresh_down, hidden, preferred_element_type=jnp.float32
        ).astype(jnp.bfloat16)
        leaving.append(
            pltpu.make_async_copy(made_ref.at[:, span], out_ref.at[:, span], sem.at[5, place])
        )
        leaving[-1].start()
    for copy in leaving:
        copy.wait()


def fast_recall(sums, packs, queries):
    features, tokens = queries.shape
    half = packs[0].shape[1]
    hidden_rows = 2 * half
    return pl.pallas_call(
        recall_body,
        out_shape=jax.ShapeDtypeStruct((features, tokens), jnp.bfloat16),
        in_specs=anywhere(7),
        out_specs=pl.BlockSpec(memory_space=pl.ANY),
        scratch_shapes=[
            pltpu.VMEM((3, hidden_rows, features), jnp.bfloat16),
            pltpu.VMEM((3, hidden_rows, features), jnp.bfloat16),
            pltpu.VMEM((3, hidden_rows, features), jnp.bfloat16),
            pltpu.VMEM((features, tokens), jnp.bfloat16),
            pltpu.VMEM((features, tokens), jnp.bfloat16),
            pltpu.SemaphoreType.DMA((6, 3)),
        ],
        cost_estimate=pl.CostEstimate(
            flops=6 * hidden_rows * features * tokens + 18 * NS_ITERS * hidden_rows * features**2,
            bytes_accessed=4 * features * tokens + 12 * hidden_rows * features,
            transcendentals=hidden_rows * tokens,
        ),
        name="fast_recall",
        compiler_params=pltpu.CompilerParams(vmem_limit_bytes=VMEM_GRANT),
    )(*sums, *packs, queries)


def in_place(query_states, key_states, value_states, cache_keys, cache_values, gate_fast, *rest):
    features, tok_count = query_states.shape
    narrow_count = lax.axis_size("narrow")
    return (
        features == FD
        and gate_fast.shape[1:] == (FD, FD)
        and features % HEAD_SIZE == 0
        and tok_count % WINDOW == 0
        and tok_count >= 2 * WINDOW
        and narrow_count >= 4
        and narrow_count & (narrow_count - 1) == 0
    )


def in_place_plan(
    query_states,
    key_states,
    value_states,
    cache_keys,
    cache_values,
    gate_fast,
    lift_fast,
    down_fast,
    token_rates,
):
    wide_count = lax.axis_size("wide")
    narrow_count = lax.axis_size("narrow")
    owned = gate_fast.shape[0]

    def from_owner(value, step):
        pairs = []
        for wide in range(wide_count):
            start = wide * narrow_count
            owner = wide // owned
            pairs.append((start + owner, start + (owner ^ step)))
        return lax.ppermute(value, ("wide", "narrow"), pairs)

    own, other = prepare(gate_fast, lift_fast, down_fast)
    arrivals = {}
    for step in sorted(range(1, narrow_count), key=lambda step: step < 2):
        if step == 1:
            arrivals[step] = swapped(other, "narrow", 0)
        else:
            arrivals[step] = from_owner((own, other)[step % 2], step)
    pair_keys = swapped(key_states, "narrow", 0)
    widths = (WINDOW - WINDOW // 4, WINDOW // 4)
    targets, *ends = stage(key_states, value_states, token_rates, widths)
    pair_targets = swapped(targets, "narrow", 0)
    attended = attend_late(query_states, key_states, value_states)
    sources = [own] + [arrivals[step] for step in range(1, narrow_count)]
    attended, ends = lax.optimization_barrier((attended, ends))
    sources, attended = lax.optimization_barrier((sources, attended))
    prior = []
    for end in ends:
        prior.append(from_behind(end, "narrow", 1))
    near, pack = fast_sums(sources, key_states, targets, pair_keys, pair_targets, owned)
    distances = range(1, narrow_count.bit_length() - 1)
    for distance in distances:
        far = swapped(near, "narrow", distance)
        if distance != distances[-1]:
            near = stored(near.astype(jnp.float32) + far.astype(jnp.float32))
    pair_pack = swapped(pack, "narrow", 0)
    pair_near = swapped(near, "narrow", 0)
    pair_far = swapped(far, "narrow", 0)
    attended, *state = attend_early(
        query_states, key_states, value_states, prior[0], cache_keys, cache_values, attended
    )
    attended = attend_last(query_states, prior[1], cache_keys, cache_values, *state, attended)
    recalled = fast_recall((near, pair_near, far, pair_far), (pack, pair_pack), query_states)
    return (attended, recalled)


def spread_plan(
    query_states,
    key_states,
    value_states,
    cache_keys,
    cache_values,
    gate_fast,
    lift_fast,
    down_fast,
    token_rates,
):
    features, tok_count = query_states.shape
    edge_cols = jnp.stack(
        [key_states[:, tok_count - WINDOW :], value_states[:, tok_count - WINDOW :]]
    )
    arrived = from_behind(edge_cols, "narrow", 1)
    leading = lax.axis_index("narrow") == 0
    prior_cols = jnp.where(leading, jnp.stack([cache_keys, cache_values]), arrived)
    ext_keys = jnp.concatenate([prior_cols[0], key_states], axis=1)
    ext_values = jnp.concatenate([prior_cols[1], value_states], axis=1)
    if features % HEAD_SIZE == 0:
        attended = attend_local(query_states, ext_keys, ext_values, 0)
    else:
        attended = attend_paired(query_states, ext_keys, ext_values)
    query_fast, key_fast, value_fast = (
        lax.all_to_all(
            lax.all_to_all(query_states, "wide", split_axis=1, concat_axis=0, tiled=True),
            "narrow",
            split_axis=0,
            concat_axis=1,
            tiled=True,
        ),
        lax.all_to_all(
            lax.all_to_all(key_states, "wide", split_axis=1, concat_axis=0, tiled=True),
            "narrow",
            split_axis=0,
            concat_axis=1,
            tiled=True,
        ),
        lax.all_to_all(
            lax.all_to_all(value_states, "wide", split_axis=1, concat_axis=0, tiled=True),
            "narrow",
            split_axis=0,
            concat_axis=1,
            tiled=True,
        ),
    )
    head_count = gate_fast.shape[0]
    wide_count = lax.axis_size("wide")
    narrow_count = lax.axis_size("narrow")
    piece_rows = tok_count // wide_count
    fast_tokens = query_fast.shape[1]
    rate_blocks = token_rates.reshape(token_rates.shape[0], narrow_count, wide_count, piece_rows)
    rates_here = lax.dynamic_slice(
        rate_blocks,
        (lax.axis_index("narrow") * head_count, 0, lax.axis_index("wide"), 0),
        (head_count, narrow_count, 1, piece_rows),
    ).reshape(head_count, fast_tokens)
    query_heads = query_fast.reshape(head_count, FD, fast_tokens)
    key_heads = key_fast.reshape(head_count, FD, fast_tokens)
    value_heads = value_fast.reshape(head_count, FD, fast_tokens)
    recall = fast_group(
        gate_fast, lift_fast, down_fast, query_heads, key_heads, value_heads, rates_here
    )
    recall = recall.reshape(head_count * FD, fast_tokens)
    recalled = lax.all_to_all(
        lax.all_to_all(recall, "narrow", split_axis=1, concat_axis=0, tiled=True),
        "wide",
        split_axis=0,
        concat_axis=1,
        tiled=True,
    )
    return (attended, recalled)


def per_device(*arrays):
    if in_place(*arrays):
        return in_place_plan(*arrays)
    return spread_plan(*arrays)


def solution(mesh):
    in_specs = (
        P("wide", "narrow"),
        P("wide", "narrow"),
        P("wide", "narrow"),
        P("wide", None),
        P("wide", None),
        P("narrow", None, None),
        P("narrow", None, None),
        P("narrow", None, None),
        P(),
    )
    out_specs = (P("wide", "narrow"), P("wide", "narrow"))
    return jax.shard_map(
        per_device, mesh=mesh, in_specs=in_specs, out_specs=out_specs, check_vma=False
    )
```

```python
import functools
import math

import jax
import jax.numpy as jnp
from jax import lax
from jax.experimental import pallas as pl
from jax.experimental.pallas import tpu as pltpu
from jax.sharding import PartitionSpec as P


FD = 512
HEAD_SIZE = 128
WINDOW = 1024
NS_ITERS = 2


EPS = 1e-06
COEF_A = 3.4445
COEF_B = -4.775
COEF_C = 2.0315
LOG2E = math.log2(math.e)
VMEM_GRANT = 67043328


def swapped(array, axis, distance):
    return lax.ppermute(array, axis, [(i, i ^ 1 << distance) for i in range(lax.axis_size(axis))])


def shortened(array):

    def short(part):
        return part.astype(jnp.bfloat16) if part.dtype == jnp.float32 else part

    return jax.tree.map(short, array)


def from_behind(value, axis, steps):
    count = lax.axis_size(axis)
    initial, last = (max(0, -steps), min(count, count - steps))
    return lax.ppermute(value, axis, [(source, source + steps) for source in range(initial, last)])


def stored(value):
    return lax.optimization_barrier(value.astype(jnp.bfloat16))


def attend_local(query_states, ext_keys, ext_values, key_start):
    features, tok_count = query_states.shape
    head_count = features // HEAD_SIZE
    block_rows = min(512, tok_count)
    block_count = tok_count // block_rows
    key_span = WINDOW + block_rows
    scaling = 1.0 / math.sqrt(HEAD_SIZE)
    rows_at = lax.broadcasted_iota(jnp.int32, (block_rows, key_span), 0)
    cols_at = lax.broadcasted_iota(jnp.int32, (block_rows, key_span), 1)
    visible = (cols_at > rows_at) & (cols_at <= rows_at + WINDOW)

    def one_block(block_index):
        offset = block_index * block_rows
        query_part = lax.dynamic_slice_in_dim(query_states, offset, block_rows, 1).reshape(
            head_count, HEAD_SIZE, block_rows
        )
        key_part = lax.dynamic_slice_in_dim(ext_keys, key_start + offset, key_span, 1).reshape(
            head_count, HEAD_SIZE, key_span
        )
        value_part = lax.dynamic_slice_in_dim(ext_values, key_start + offset, key_span, 1).reshape(
            head_count, HEAD_SIZE, key_span
        )
        scores = (
            jnp.einsum("hdq,hdk->hqk", query_part, key_part, preferred_element_type=jnp.float32)
            * scaling
        )
        scores = jnp.where(visible[None], scores, -jnp.inf)
        highest = jnp.max(scores, axis=2, keepdims=True)
        raised = jnp.exp(scores - highest)
        weights = (raised / jnp.sum(raised, axis=2, keepdims=True)).astype(jnp.bfloat16)
        blended = jnp.einsum(
            "hdk,hqk->hdq", value_part, weights, preferred_element_type=jnp.float32
        )
        return blended.astype(jnp.bfloat16).reshape(features, block_rows)

    blocks_out = lax.map(one_block, jnp.arange(block_count, dtype=jnp.int32))
    return jnp.transpose(blocks_out, (1, 0, 2)).reshape(features, tok_count)


def attend_paired(query_states, ext_keys, ext_values):
    features, tok_count = query_states.shape
    half_rows = tok_count // 2
    lower = lax.axis_index("wide") % 2 == 0
    query_send = jnp.where(lower, query_states[:, half_rows:], query_states[:, :half_rows])
    query_keep = jnp.where(lower, query_states[:, :half_rows], query_states[:, half_rows:])
    other_keys, other_values, other_queries = swapped((ext_keys, ext_values, query_send), "wide", 0)
    full_keys = jnp.where(
        lower,
        jnp.concatenate([ext_keys, other_keys], axis=0),
        jnp.concatenate([other_keys, ext_keys], axis=0),
    )
    full_values = jnp.where(
        lower,
        jnp.concatenate([ext_values, other_values], axis=0),
        jnp.concatenate([other_values, ext_values], axis=0),
    )
    full_queries = jnp.where(
        lower,
        jnp.concatenate([query_keep, other_queries], axis=0),
        jnp.concatenate([other_queries, query_keep], axis=0),
    )
    key_start = jnp.where(lower, 0, half_rows).astype(jnp.int32)
    head_out = attend_local(full_queries, full_keys, full_values, key_start)
    out_keep = jnp.where(lower, head_out[:features], head_out[features:])
    out_send = jnp.where(lower, head_out[features:], head_out[:features])
    out_other = swapped(shortened(out_send), "wide", 0).astype(out_send.dtype)
    return jnp.where(
        lower,
        jnp.concatenate([out_keep, out_other], axis=1),
        jnp.concatenate([out_other, out_keep], axis=1),
    )


def fast_terms(gate_weight, lift_weight, down_weight, key_heads, value_heads, rates_here):
    pre_gate = jnp.einsum(
        "hcf,hft->hct", gate_weight, key_heads, preferred_element_type=jnp.float32
    )
    pre_lift = jnp.einsum(
        "hcf,hft->hct", lift_weight, key_heads, preferred_element_type=jnp.float32
    )
    sigmoid_gate = jax.nn.sigmoid(pre_gate)
    silu_gate = pre_gate * sigmoid_gate
    hidden = (silu_gate * pre_lift).astype(jnp.bfloat16)
    target = (-(value_heads.astype(jnp.float32) * rates_here[:, None, :])).astype(jnp.bfloat16)
    grad_down = jnp.einsum("hft,hct->hfc", target, hidden, preferred_element_type=jnp.float32)
    back_hidden = jnp.einsum(
        "hfc,hft->hct", down_weight, target, preferred_element_type=jnp.float32
    )
    back_lift = (back_hidden * silu_gate).astype(jnp.bfloat16)
    back_gate = (
        back_hidden * pre_lift * sigmoid_gate * (1.0 + pre_gate * (1.0 - sigmoid_gate))
    ).astype(jnp.bfloat16)
    grad_gate = jnp.einsum("hct,hft->hcf", back_gate, key_heads, preferred_element_type=jnp.float32)
    grad_lift = jnp.einsum("hct,hft->hcf", back_lift, key_heads, preferred_element_type=jnp.float32)
    return (grad_gate, grad_lift, grad_down)


def scaled_start(rounded):
    widened = rounded.astype(jnp.float32)
    norm_val = jnp.sqrt(jnp.sum(jnp.square(widened), axis=(1, 2), keepdims=True) + EPS)
    return stored(widened / norm_val)


def starting(grad_gate, grad_lift, grad_down):
    sum_gate, sum_lift, sum_down = lax.psum((grad_gate, grad_lift, grad_down), "wide")
    return (
        scaled_start(stored(sum_gate)),
        scaled_start(stored(sum_lift)),
        scaled_start(stored(sum_down)),
    )


def orthogonal(current):
    for _ in range(NS_ITERS):
        gram_mat = jnp.einsum(
            "hrc,hrd->hcd", current, current, preferred_element_type=jnp.float32
        ).astype(jnp.bfloat16)
        lifted = stored(
            jnp.einsum("hrc,hcd->hrd", current, gram_mat, preferred_element_type=jnp.float32)
        )
        current = stored(
            COEF_A * current.astype(jnp.float32)
            + COEF_B * lifted.astype(jnp.float32)
            + COEF_C
            * jnp.einsum("hrc,hcd->hrd", lifted, gram_mat, preferred_element_type=jnp.float32)
        )
    return current


def refreshed(weight, ortho):
    initial = weight.astype(jnp.float32)
    moved_rows = initial - ortho.astype(jnp.float32)
    wanted = jnp.sqrt(jnp.mean(jnp.square(initial), axis=-1, keepdims=True) + EPS)
    present = jnp.sqrt(jnp.mean(jnp.square(moved_rows), axis=-1, keepdims=True) + EPS)
    return (moved_rows * (wanted / present)).astype(jnp.bfloat16)


def fast_group(
    gate_weight, lift_weight, down_weight, query_heads, key_heads, value_heads, rates_here
):
    grad_gate, grad_lift, grad_down = fast_terms(
        gate_weight, lift_weight, down_weight, key_heads, value_heads, rates_here
    )
    start_gate, start_lift, start_down = starting(grad_gate, grad_lift, grad_down)
    fresh_gate = refreshed(gate_weight, orthogonal(start_gate))
    fresh_lift = refreshed(lift_weight, orthogonal(start_lift))
    fresh_down = refreshed(down_weight, orthogonal(start_down))
    query_gate = jnp.einsum(
        "hcf,hft->hct", fresh_gate, query_heads, preferred_element_type=jnp.float32
    )
    query_lift = jnp.einsum(
        "hcf,hft->hct", fresh_lift, query_heads, preferred_element_type=jnp.float32
    )
    query_hidden = (jax.nn.silu(query_gate) * query_lift).astype(jnp.bfloat16)
    return jnp.einsum(
        "hfc,hct->hft", fresh_down, query_hidden, preferred_element_type=jnp.float32
    ).astype(jnp.bfloat16)


def attend_body(
    q_ref, kp_ref, vp_ref, kc_ref, vc_ref, o_ref, kt_ref, v_ref, *, block, window
):
    hd = q_ref.shape[0]
    scale = LOG2E / math.sqrt(hd)

    placed(kp_ref, vp_ref, kt_ref, v_ref, 0)
    placed(kc_ref, vc_ref, kt_ref, v_ref, window)
    v_ref[hd:, :] = jnp.ones((v_ref.shape[0] - hd, 2 * window), jnp.bfloat16)
    rows = lax.broadcasted_iota(jnp.int32, (block, block), 0)
    cols = lax.broadcasted_iota(jnp.int32, (block, block), 1)
    first = rows > cols
    inner = window // block

    def scores(b):
        q = q_ref[:, b * block : (b + 1) * block].astype(jnp.float32) * scale
        high = q.astype(jnp.bfloat16)
        low = (q - high.astype(jnp.float32)).astype(jnp.bfloat16)
        pair = jnp.concatenate([high, low], axis=0)
        parts = [
            jnp.dot(
                kt_ref[(b + j) * block : (b + j + 1) * block, :],
                pair,
                preferred_element_type=jnp.float32,
            )
            for j in range(inner + 1)
        ]
        return [jnp.where(first, parts[0], parts[inner])] + parts[1:inner]

    def blend(b, parts):
        top = functools.reduce(jnp.maximum, parts)
        top = jnp.max(top, axis=0, keepdims=True)
        raised = [jnp.exp2(part - top).astype(jnp.bfloat16) for part in parts]
        zero = jnp.zeros_like(raised[0])
        ends = jnp.where(first, raised[0], zero), jnp.where(first, zero, raised[0])
        weights = jnp.concatenate([ends[0]] + raised[1:] + [ends[1]], axis=0)
        span = v_ref[:, b * block : (b + inner + 1) * block]
        out = jnp.dot(span, weights, preferred_element_type=jnp.float32)
        o_ref[:, b * block : (b + 1) * block] = (out[:hd] * (1.0 / out[hd : hd + 1])).astype(
            jnp.bfloat16
        )

    ready = scores(0)
    for b in range(1, inner):
        following = scores(b)
        blend(b - 1, ready)
        ready = following
    blend(inner - 1, ready)


def attend_scratch():
    return [
        pltpu.VMEM((2 * WINDOW, 2 * HEAD_SIZE), jnp.bfloat16),
        pltpu.VMEM((HEAD_SIZE + 16, 2 * WINDOW), jnp.bfloat16),
    ]


def attend_late(queries, keys, values):
    features, tokens = queries.shape
    heads, chunks = features // HEAD_SIZE, tokens // WINDOW - 1
    here = pl.BlockSpec((HEAD_SIZE, WINDOW), lambda h, c: (h, c + 1))
    before = pl.BlockSpec((HEAD_SIZE, WINDOW), lambda h, c: (h, c))
    return pl.pallas_call(
        functools.partial(attend_body, block=min(256, WINDOW), window=WINDOW),
        out_shape=jax.ShapeDtypeStruct((features, tokens), jnp.bfloat16),
        grid=(heads, chunks),
        in_specs=[here, before, before, here, here],
        out_specs=here,
        scratch_shapes=attend_scratch(),
        cost_estimate=pl.CostEstimate(
            flops=5 * features * chunks * WINDOW**2,
            bytes_accessed=10 * features * chunks * WINDOW,
            transcendentals=heads * chunks * WINDOW**2,
        ),
        name="attend_late",
        compiler_params=pltpu.CompilerParams(vmem_limit_bytes=VMEM_GRANT),
    )(queries, keys, values, keys, values)


def two_term(q_ref, at, scale):
    q = q_ref[:, at].astype(jnp.float32) * scale
    high = q.astype(jnp.bfloat16)
    low = (q - high.astype(jnp.float32)).astype(jnp.bfloat16)
    return jnp.concatenate([high, low], axis=0)


def placed(k, v, kt_ref, v_ref, at):
    hd, width = k.shape
    turned = k[...].T
    kt_ref[at : at + width, :hd] = turned
    kt_ref[at : at + width, hd:] = turned
    v_ref[:hd, at : at + width] = v[...]


def early_body(
    q_ref, kp_ref, vp_ref, kc_ref, vc_ref, ck_ref, cv_ref, _, o_ref, part_ref, top_ref, mass_ref,
    kt_ref, v_ref, *, block,
):
    hd, window = q_ref.shape
    scale = LOG2E / math.sqrt(hd)
    near = kp_ref.shape[1]
    inner = window // block
    missing = (window - near) // block
    leading = lax.axis_index("narrow") == 0

    @pl.when(leading)
    def _():
        placed(ck_ref, cv_ref, kt_ref, v_ref, 0)

    @pl.when(jnp.logical_not(leading))
    def _():
        placed(kp_ref, vp_ref, kt_ref, v_ref, 0)

    placed(kc_ref, vc_ref, kt_ref, v_ref, near)
    v_ref[hd:, :] = jnp.ones((v_ref.shape[0] - hd, v_ref.shape[1]), jnp.bfloat16)
    rows = lax.broadcasted_iota(jnp.int32, (block, block), 0)
    cols = lax.broadcasted_iota(jnp.int32, (block, block), 1)
    first = rows > cols

    def chunk(j):
        return slice((j - missing) * block, (j - missing + 1) * block)

    def scores(b):
        pair = two_term(q_ref, slice(b * block, (b + 1) * block), scale)
        parts = [
            jnp.dot(kt_ref[chunk(j), :], pair, preferred_element_type=jnp.float32)
            for j in range(max(b, missing), b + inner + 1)
        ]
        if b >= missing:
            return [jnp.where(first, parts[0], parts[inner])] + parts[1:inner]
        return parts[:-1] + [jnp.where(first, -jnp.inf, parts[-1])]

    def blend(b, parts):
        top = functools.reduce(jnp.maximum, parts)
        top = jnp.max(top, axis=0, keepdims=True)
        raised = [jnp.exp2(part - top).astype(jnp.bfloat16) for part in parts]
        if b >= missing:
            zero = jnp.zeros_like(raised[0])
            ends = jnp.where(first, raised[0], zero), jnp.where(first, zero, raised[0])
            raised = [ends[0]] + raised[1:] + [ends[1]]
        span = v_ref[:, chunk(max(b, missing)).start : chunk(b + inner).stop]
        out = jnp.dot(span, jnp.concatenate(raised, axis=0), preferred_element_type=jnp.float32)
        if b >= missing:
            at = slice((b - missing) * block, (b - missing + 1) * block)
            o_ref[:, at] = (out[:hd] * (1.0 / out[hd : hd + 1])).astype(jnp.bfloat16)
        else:
            at = slice(b * block, (b + 1) * block)
            part_ref[:, at] = out[:hd]
            top_ref[:, at] = jnp.broadcast_to(top, (top_ref.shape[0], block))
            mass_ref[:, at] = jnp.broadcast_to(out[hd : hd + 1], (top_ref.shape[0], block))

    ready = scores(0)
    for b in range(1, inner):
        following = scores(b)
        blend(b - 1, ready)
        ready = following
    blend(inner - 1, ready)


def attend_early(queries, keys, values, prior, cache_keys, cache_values, late):
    features, tokens = queries.shape
    heads = features // HEAD_SIZE
    near = prior.shape[2]
    far = WINDOW - near
    here = pl.BlockSpec((HEAD_SIZE, WINDOW), lambda h: (h, 0))
    nearer = pl.BlockSpec((HEAD_SIZE, near), lambda h: (h, far // near))
    prior_keys = pl.BlockSpec((None, HEAD_SIZE, near), lambda h: (0, h, 0))
    prior_values = pl.BlockSpec((None, HEAD_SIZE, near), lambda h: (1, h, 0))
    rows = 8
    stats = jax.ShapeDtypeStruct((heads * rows, far), jnp.float32)
    stat = pl.BlockSpec((rows, far), lambda h: (h, 0))
    return pl.pallas_call(
        functools.partial(early_body, block=min(256, near)),
        out_shape=(
            jax.ShapeDtypeStruct((features, tokens), jnp.bfloat16),
            jax.ShapeDtypeStruct((features, far), jnp.float32),
            stats,
            stats,
        ),
        grid=(heads,),
        in_specs=[here, prior_keys, prior_values, here, here, nearer, nearer]
        + [pl.BlockSpec(memory_space=pl.ANY)],
        out_specs=(nearer, pl.BlockSpec((HEAD_SIZE, far), lambda h: (h, 0)), stat, stat),
        scratch_shapes=[
            pltpu.VMEM((near + WINDOW, 2 * HEAD_SIZE), jnp.bfloat16),
            pltpu.VMEM((HEAD_SIZE + 16, near + WINDOW), jnp.bfloat16),
        ],
        input_output_aliases={7: 0},
        cost_estimate=pl.CostEstimate(
            flops=5 * features * WINDOW**2,
            bytes_accessed=14 * features * WINDOW,
            transcendentals=heads * WINDOW**2,
        ),
        name="attend_early",
        compiler_params=pltpu.CompilerParams(vmem_limit_bytes=VMEM_GRANT),
    )(queries, prior, prior, keys, values, cache_keys, cache_values, late)


def last_body(
    q_ref, prior_ref, ck_ref, cv_ref, part_ref, top_ref, mass_ref, _, o_ref,
    held_q, held_k, held_v, held_part, held_top, held_mass, kt_ref, v_ref, made_ref, sem,
    *, block,
):
    features, far = part_ref.shape
    hd = HEAD_SIZE
    heads = features // hd
    scale = LOG2E / math.sqrt(hd)
    missing = far // block
    leading = lax.axis_index("narrow") == 0
    plain = [
        pltpu.make_async_copy(top_ref, held_top, sem.at[0, 0]),
        pltpu.make_async_copy(mass_ref, held_mass, sem.at[0, 1]),
    ]
    arriving = []
    for h in range(heads):
        at = slice(h * hd, (h + 1) * hd)
        keys = pltpu.make_async_copy(prior_ref.at[0, at], held_k.at[at], sem.at[1, h])
        values = pltpu.make_async_copy(prior_ref.at[1, at], held_v.at[at], sem.at[2, h])

        @pl.when(leading)
        def _(at=at, h=h):
            pltpu.make_async_copy(ck_ref.at[at, :far], held_k.at[at], sem.at[1, h]).start()
            pltpu.make_async_copy(cv_ref.at[at, :far], held_v.at[at], sem.at[2, h]).start()

        @pl.when(jnp.logical_not(leading))
        def _(keys=keys, values=values):
            keys.start()
            values.start()

        others = [
            pltpu.make_async_copy(q_ref.at[at, :far], held_q.at[at], sem.at[3, h]),
            pltpu.make_async_copy(part_ref.at[at], held_part.at[at], sem.at[4, h]),
        ]
        for copy in others + (plain if h == 0 else []):
            copy.start()
        arriving.append([keys, values] + others)
    rows = lax.broadcasted_iota(jnp.int32, (block, block), 0)
    cols = lax.broadcasted_iota(jnp.int32, (block, block), 1)
    first = rows > cols
    v_ref[:, hd:, :] = jnp.ones((heads, v_ref.shape[1] - hd, far), jnp.bfloat16)
    leaving = []
    for copy in plain:
        copy.wait()

    def scores(h, b):
        at = slice(h * hd, (h + 1) * hd)
        if b == 0:
            for copy in arriving[h]:
                copy.wait()
            placed(held_k.at[at], held_v.at[at], kt_ref.at[h], v_ref.at[h], 0)
        pair = two_term(held_q.at[at], slice(b * block, (b + 1) * block), scale)
        parts = [
            jnp.dot(
                kt_ref[h, j * block : (j + 1) * block, :], pair, preferred_element_type=jnp.float32
            )
            for j in range(b, missing)
        ]
        return [jnp.where(first, parts[0], -jnp.inf)] + parts[1:]

    def blend(h, b, parts):
        at = slice(h * hd, (h + 1) * hd)
        span = slice(b * block, (b + 1) * block)
        before = held_top[h * 8 : h * 8 + 1, span]
        top = functools.reduce(jnp.maximum, parts)
        top = jnp.maximum(jnp.max(top, axis=0, keepdims=True), before)
        kept = jnp.exp2(before - top)
        weights = jnp.concatenate(
            [jnp.exp2(part - top).astype(jnp.bfloat16) for part in parts], axis=0
        )
        out = jnp.dot(v_ref[h, :, b * block :], weights, preferred_element_type=jnp.float32)
        mass = held_mass[h * 8 : h * 8 + 1, span] * kept + out[hd : hd + 1]
        made_ref[at, span] = ((held_part[at, span] * kept + out[:hd]) * (1.0 / mass)).astype(
            jnp.bfloat16
        )
        if b == missing - 1:
            leaving.append(
                pltpu.make_async_copy(made_ref.at[at], o_ref.at[at, :far], sem.at[5, h])
            )
            leaving[-1].start()

    turns = [(h, b) for h in range(heads) for b in range(missing)]
    ready = scores(*turns[0])
    for turn, ahead in zip(turns, turns[1:]):
        following = scores(*ahead)
        blend(*turn, ready)
        ready = following
    blend(*turns[-1], ready)
    for copy in leaving:
        copy.wait()


def attend_last(queries, prior, cache_keys, cache_values, part, top, mass, early):
    features, tokens = queries.shape
    heads = features // HEAD_SIZE
    far = part.shape[1]
    pieces = pltpu.VMEM((features, far), jnp.bfloat16)
    return pl.pallas_call(
        functools.partial(last_body, block=min(512, far)),
        out_shape=jax.ShapeDtypeStruct((features, tokens), jnp.bfloat16),
        in_specs=[pl.BlockSpec(memory_space=pl.ANY)] * 8,
        out_specs=pl.BlockSpec(memory_space=pl.ANY),
        scratch_shapes=[
            pieces,
            pieces,
            pieces,
            pltpu.VMEM((features, far), jnp.float32),
            pltpu.VMEM(top.shape, jnp.float32),
            pltpu.VMEM(top.shape, jnp.float32),
            pltpu.VMEM((heads, far, 2 * HEAD_SIZE), jnp.bfloat16),
            pltpu.VMEM((heads, HEAD_SIZE + 16, far), jnp.bfloat16),
            pieces,
            pltpu.SemaphoreType.DMA((6, max(heads, 2))),
        ],
        input_output_aliases={7: 0},
        cost_estimate=pl.CostEstimate(
            flops=3 * features * far**2,
            bytes_accessed=14 * features * far,
            transcendentals=heads * far**2,
        ),
        name="attend_last",
        compiler_params=pltpu.CompilerParams(vmem_limit_bytes=VMEM_GRANT),
    )(queries, prior, cache_keys, cache_values, part, top, mass, early)


def anywhere(count):
    return [pl.BlockSpec(memory_space=pl.ANY)] * count


def half_rows(part, half):
    return pl.ds(pl.multiple_of(part * half, half), half)


def prepare_body(gate_ref, lift_ref, down_ref, own_ref, other_ref, w_ref, out_ref, sem):
    owned = gate_ref.shape[0]
    local = lax.axis_index("wide") % owned
    side = lax.axis_index("narrow") % 2
    half = own_ref.shape[1]
    copies = [
        pltpu.make_async_copy(source.at[local], w_ref.at[place], sem.at[0, place])
        for place, source in enumerate((down_ref, gate_ref, lift_ref))
    ]
    for copy in copies:
        copy.start()
    leaving = []
    copies[0].wait()
    out_ref[...] = w_ref[0].T
    for order, (place, source) in enumerate(((2, out_ref), (0, w_ref.at[1]), (1, w_ref.at[2]))):
        if order:
            copies[order].wait()
        for turn, (target, part) in enumerate(((own_ref, side), (other_ref, 1 - side))):
            leaving.append(
                pltpu.make_async_copy(
                    source.at[half_rows(part, half)], target.at[place], sem.at[1 + turn, place]
                )
            )
            leaving[-1].start()
    for copy in leaving:
        copy.wait()


def prepare(gate_fast, lift_fast, down_fast):
    _, hidden_rows, features = gate_fast.shape
    shape = (3, hidden_rows // 2, features)
    return pl.pallas_call(
        prepare_body,
        out_shape=(jax.ShapeDtypeStruct(shape, jnp.bfloat16),) * 2,
        in_specs=anywhere(3),
        out_specs=tuple(anywhere(2)),
        scratch_shapes=[
            pltpu.VMEM((3, hidden_rows, features), jnp.bfloat16),
            pltpu.VMEM((hidden_rows, features), jnp.bfloat16),
            pltpu.SemaphoreType.DMA((3, 3)),
        ],
        cost_estimate=pl.CostEstimate(
            flops=0, bytes_accessed=12 * hidden_rows * features, transcendentals=0
        ),
        name="prepare",
        compiler_params=pltpu.CompilerParams(vmem_limit_bytes=VMEM_GRANT),
    )(gate_fast, lift_fast, down_fast)


def stage_body(key_ref, value_ref, rate_ref, target_ref, *refs):
    end_refs, (held_ref, values_ref, made_ref, sem, sem_end) = refs[:-5], refs[-5:]
    features, tokens = key_ref.shape
    width = end_refs[0].shape[2]
    step = HEAD_SIZE
    lasts = [slice(tokens - (part + 1) * width, tokens - part * width) for part in range(len(end_refs))]
    begin = pl.multiple_of(lax.axis_index("narrow") * tokens, tokens)
    rates = -rate_ref[pl.ds(lax.axis_index("wide"), 1), pl.ds(begin, tokens)]
    values = [
        pltpu.make_async_copy(
            value_ref.at[at : at + step], values_ref.at[at : at + step], sem.at[0, at // step]
        )
        for at in range(0, features, step)
    ]
    keys = [
        pltpu.make_async_copy(
            key_ref.at[:, last], held_ref.at[part], sem_end.at[0, part]
        )
        for part, last in enumerate(lasts)
    ]
    for copy in values + keys:
        copy.start()
    leaving = []

    def leave(source, target, mark):
        leaving.append(pltpu.make_async_copy(source, target, mark))
        leaving[-1].start()

    for place, copy in enumerate(values):
        at = slice(place * step, (place + 1) * step)
        copy.wait()
        made_ref[at] = (values_ref[at].astype(jnp.float32) * rates).astype(jnp.bfloat16)
        leave(made_ref.at[at], target_ref.at[at], sem.at[1, place])
    for part, end_ref in enumerate(end_refs):
        leave(values_ref.at[:, lasts[part]], end_ref.at[1], sem_end.at[1, part])
        keys[part].wait()
        leave(held_ref.at[part], end_ref.at[0], sem_end.at[2, part])
    for copy in leaving:
        copy.wait()


def stage(keys, values, rates, parts):
    features, tokens = keys.shape
    width = WINDOW // parts
    return pl.pallas_call(
        stage_body,
        out_shape=(jax.ShapeDtypeStruct((features, tokens), jnp.bfloat16),)
        + (jax.ShapeDtypeStruct((2, features, width), jnp.bfloat16),) * parts,
        in_specs=anywhere(2) + [pl.BlockSpec(memory_space=pltpu.VMEM)],
        out_specs=tuple(anywhere(1 + parts)),
        scratch_shapes=[
            pltpu.VMEM((parts, features, width), jnp.bfloat16),
            pltpu.VMEM((features, tokens), jnp.bfloat16),
            pltpu.VMEM((features, tokens), jnp.bfloat16),
            pltpu.SemaphoreType.DMA((2, features // HEAD_SIZE)),
            pltpu.SemaphoreType.DMA((3, parts)),
        ],
        cost_estimate=pl.CostEstimate(
            flops=features * tokens,
            bytes_accessed=4 * features * tokens + 8 * features * WINDOW,
            transcendentals=0,
        ),
        name="stage",
        compiler_params=pltpu.CompilerParams(vmem_limit_bytes=VMEM_GRANT),
    )(keys, values, rates)


def sums_body(*refs, owned, cuts):
    sources = refs[:-15]
    (
        key_ref, target_ref, pair_key_ref, pair_target_ref,
        send_out, pack_out,
        send_ref, pack_ref, keys_ref, targets_ref, hidden_ref, back_ref, sem, sem_in, sem_out,
    ) = refs[-15:]
    _, tokens = key_ref.shape
    half = pack_ref.shape[1]
    role = lax.axis_index("narrow") ^ (lax.axis_index("wide") // owned)

    for place, source in enumerate(sources):

        @pl.when(role == place)
        def _(source=source):
            pltpu.make_async_copy(source, pack_ref, sem).start()

    spans = [(key_ref, target_ref, 0, begin, end) for begin, end in zip(cuts, cuts[1:])]
    spans.append((pair_key_ref, pair_target_ref, tokens, 0, tokens))
    arrivals = []
    for slot, (keys, targets, base, begin, end) in enumerate(spans):
        source, place = slice(begin, end), slice(base + begin, base + end)
        copies = (
            pltpu.make_async_copy(keys.at[:, source], keys_ref.at[:, place], sem_in.at[0, slot]),
            pltpu.make_async_copy(
                targets.at[:, source], targets_ref.at[:, place], sem_in.at[1, slot]
            ),
        )
        for copy in copies:
            copy.start()
        arrivals.append((place, *copies))
    pltpu.make_async_copy(sources[0], pack_ref, sem).wait()
    leaving = [pltpu.make_async_copy(pack_ref, pack_out, sem_out.at[3])]
    leaving[0].start()
    gate_lift = jnp.concatenate([pack_ref[0] * jnp.bfloat16(0.5), pack_ref[1]], axis=0)
    down = pack_ref[2]

    for at, keys, targets in arrivals:
        keys.wait()
        pre = jnp.dot(gate_lift, keys_ref[:, at], preferred_element_type=jnp.float32)
        targets.wait()
        back_hidden = jnp.dot(down, targets_ref[:, at], preferred_element_type=jnp.float32)
        half_gate = pre[:half]
        pre_lift = pre[half:]
        twice = jnp.tanh(half_gate) + 1.0
        silu_gate = half_gate * twice
        hidden_ref[:, at] = (silu_gate * pre_lift).astype(jnp.bfloat16)
        slope = twice + silu_gate * (2.0 - twice)
        back_ref[:half, at] = (back_hidden * pre_lift * slope).astype(jnp.bfloat16)
        back_ref[half:, at] = (back_hidden * silu_gate).astype(jnp.bfloat16)

    def leave(place, value):
        send_ref[place] = value.astype(jnp.bfloat16)
        leaving.append(
            pltpu.make_async_copy(send_ref.at[place], send_out.at[place], sem_out.at[place])
        )
        leaving[-1].start()

    contract = (((1,), (1,)), ((), ()))
    sums = lax.dot_general(
        back_ref[...], keys_ref[...], contract, preferred_element_type=jnp.float32
    )
    leave(0, sums[:half] * 0.5)
    leave(1, sums[half:])
    sums = lax.dot_general(
        hidden_ref[...], targets_ref[...], contract, preferred_element_type=jnp.float32
    )
    leave(2, sums)
    for copy in leaving:
        copy.wait()


def fast_sums(sources, keys, targets, pair_keys, pair_targets, owned):
    features, tokens = keys.shape
    shape = sources[0].shape
    half = shape[1]
    cuts = (0, tokens)
    return pl.pallas_call(
        functools.partial(sums_body, owned=owned, cuts=cuts),
        out_shape=(jax.ShapeDtypeStruct(shape, jnp.bfloat16),) * 2,
        in_specs=anywhere(len(sources) + 4),
        out_specs=tuple(anywhere(2)),
        scratch_shapes=[
            pltpu.VMEM(shape, jnp.bfloat16),
            pltpu.VMEM(shape, jnp.bfloat16),
            pltpu.VMEM((features, 2 * tokens), jnp.bfloat16),
            pltpu.VMEM((features, 2 * tokens), jnp.bfloat16),
            pltpu.VMEM((half, 2 * tokens), jnp.bfloat16),
            pltpu.VMEM((2 * half, 2 * tokens), jnp.bfloat16),
            pltpu.SemaphoreType.DMA(()),
            pltpu.SemaphoreType.DMA((2, len(cuts))),
            pltpu.SemaphoreType.DMA((4,)),
        ],
        cost_estimate=pl.CostEstimate(
            flops=24 * half * features * tokens,
            bytes_accessed=8 * features * tokens + 6 * 3 * half * features,
            transcendentals=2 * half * tokens,
        ),
        name="fast_sums",
        compiler_params=pltpu.CompilerParams(vmem_limit_bytes=VMEM_GRANT),
    )(*sources, keys, targets, pair_keys, pair_targets)


def recall_body(
    mine_ref, other_ref, far_ref, other_far_ref, pack_ref, pair_pack_ref, query_ref, out_ref,
    w_ref, near_sums_ref, far_sums_ref, held_ref, made_ref, sem,
):
    half = mine_ref.shape[1]
    hidden_rows, features = w_ref.shape[1:]
    nt = (((1,), (1,)), ((), ()))

    side = lax.axis_index("narrow") % 2

    def arriving(matrix):
        moves = (
            (mine_ref, near_sums_ref, side),
            (other_ref, near_sums_ref, 1 - side),
            (far_ref, far_sums_ref, side),
            (other_far_ref, far_sums_ref, 1 - side),
        )
        return [
            pltpu.make_async_copy(
                source.at[matrix],
                target.at[matrix, half_rows(part, half)],
                sem.at[place, matrix],
            )
            for place, (source, target, part) in enumerate(moves)
        ]

    sums = [arriving(matrix) for matrix in range(3)]
    weights = [
        pltpu.make_async_copy(source, w_ref.at[:, half_rows(part, half)], sem.at[4, place])
        for place, (source, part) in enumerate(((pack_ref, side), (pair_pack_ref, 1 - side)))
    ]
    queries = pltpu.make_async_copy(query_ref, held_ref, sem.at[5, 2])
    for copies in sums + [weights, [queries]]:
        for copy in copies:
            copy.start()
    rows = lax.broadcasted_iota(jnp.int32, (hidden_rows, features), 0)
    cols = lax.broadcasted_iota(jnp.int32, (hidden_rows, features), 1)
    diagonal = rows == cols
    rounded, gram, scale = [], [], []
    for matrix, copies in enumerate(sums):
        for copy in copies:
            copy.wait()
        summed = near_sums_ref[matrix].astype(jnp.float32) + far_sums_ref[matrix].astype(
            jnp.float32
        )
        x = summed.astype(jnp.bfloat16)
        product = lax.dot_general(x, x, nt, preferred_element_type=jnp.float32)
        trace = jnp.sum(jnp.where(diagonal, product, 0.0), axis=0, keepdims=True)
        scale.append(lax.rsqrt(jnp.sum(trace, axis=1, keepdims=True) + EPS))
        rounded.append(x)
        gram.append((product * (scale[-1] * scale[-1])).astype(jnp.bfloat16))
    current = rounded
    for sweep_index in range(NS_ITERS):
        if sweep_index:
            scale = [1.0] * 3
            gram = [
                lax.dot_general(x, x, nt, preferred_element_type=jnp.float32).astype(
                    jnp.bfloat16
                )
                for x in current
            ]
        lifted = [
            jnp.dot(g, x, preferred_element_type=jnp.float32).astype(jnp.bfloat16)
            for x, g in zip(current, gram)
        ]
        current = [
            (
                (COEF_A * r) * x.astype(jnp.float32)
                + (COEF_B * r) * y.astype(jnp.float32)
                + (COEF_C * r) * jnp.dot(g, y, preferred_element_type=jnp.float32)
            ).astype(jnp.bfloat16)
            for x, y, g, r in zip(current, lifted, gram, scale)
        ]
    for copy in weights:
        copy.wait()

    def fresh(i):
        axis = 0 if i == 2 else 1
        initial = w_ref[i].astype(jnp.float32)
        moved = initial - current[i].astype(jnp.float32)
        wanted = jnp.mean(jnp.square(initial), axis=axis, keepdims=True) + EPS
        present = jnp.mean(jnp.square(moved), axis=axis, keepdims=True) + EPS
        return (moved * (wanted * lax.rsqrt(wanted * present))).astype(jnp.bfloat16)

    queries.wait()
    tokens = held_ref.shape[1]
    block = tokens // 2
    spans = [slice(at, at + block) for at in range(0, tokens, block)]
    fresh_gate = fresh(0)
    gates = [
        jnp.dot(fresh_gate * jnp.bfloat16(0.5), held_ref[:, span], preferred_element_type=jnp.float32)
        for span in spans
    ]
    fresh_lift = fresh(1)
    lifts = [
        jnp.dot(fresh_lift, held_ref[:, span], preferred_element_type=jnp.float32) for span in spans
    ]
    fresh_down = fresh(2).T
    leaving = []
    for place, (span, gate, lift) in enumerate(zip(spans, gates, lifts)):
        hidden = (gate * (jnp.tanh(gate) + 1.0) * lift).astype(jnp.bfloat16)
        made_ref[:, span] = jnp.dot(
            fresh_down, hidden, preferred_element_type=jnp.float32
        ).astype(jnp.bfloat16)
        leaving.append(
            pltpu.make_async_copy(made_ref.at[:, span], out_ref.at[:, span], sem.at[5, place])
        )
        leaving[-1].start()
    for copy in leaving:
        copy.wait()


def fast_recall(sums, packs, queries):
    features, tokens = queries.shape
    half = packs[0].shape[1]
    hidden_rows = 2 * half
    return pl.pallas_call(
        recall_body,
        out_shape=jax.ShapeDtypeStruct((features, tokens), jnp.bfloat16),
        in_specs=anywhere(7),
        out_specs=pl.BlockSpec(memory_space=pl.ANY),
        scratch_shapes=[
            pltpu.VMEM((3, hidden_rows, features), jnp.bfloat16),
            pltpu.VMEM((3, hidden_rows, features), jnp.bfloat16),
            pltpu.VMEM((3, hidden_rows, features), jnp.bfloat16),
            pltpu.VMEM((features, tokens), jnp.bfloat16),
            pltpu.VMEM((features, tokens), jnp.bfloat16),
            pltpu.SemaphoreType.DMA((6, 3)),
        ],
        cost_estimate=pl.CostEstimate(
            flops=6 * hidden_rows * features * tokens + 18 * NS_ITERS * hidden_rows * features**2,
            bytes_accessed=4 * features * tokens + 12 * hidden_rows * features,
            transcendentals=hidden_rows * tokens,
        ),
        name="fast_recall",
        compiler_params=pltpu.CompilerParams(vmem_limit_bytes=VMEM_GRANT),
    )(*sums, *packs, queries)


def in_place(query_states, key_states, value_states, cache_keys, cache_values, gate_fast, *rest):
    features, tok_count = query_states.shape
    narrow_count = lax.axis_size("narrow")
    return (
        features == FD
        and gate_fast.shape[1:] == (FD, FD)
        and features % HEAD_SIZE == 0
        and tok_count % WINDOW == 0
        and tok_count >= 2 * WINDOW
        and narrow_count >= 4
        and narrow_count & (narrow_count - 1) == 0
    )


def in_place_plan(
    query_states,
    key_states,
    value_states,
    cache_keys,
    cache_values,
    gate_fast,
    lift_fast,
    down_fast,
    token_rates,
):
    wide_count = lax.axis_size("wide")
    narrow_count = lax.axis_size("narrow")
    owned = gate_fast.shape[0]

    def from_owner(value, step):
        pairs = []
        for wide in range(wide_count):
            start = wide * narrow_count
            owner = wide // owned
            pairs.append((start + owner, start + (owner ^ step)))
        return lax.ppermute(value, ("wide", "narrow"), pairs)

    own, other = prepare(gate_fast, lift_fast, down_fast)
    arrivals = {}
    for step in sorted(range(1, narrow_count), key=lambda step: step < 2):
        if step == 1:
            arrivals[step] = swapped(other, "narrow", 0)
        else:
            arrivals[step] = from_owner((own, other)[step % 2], step)
    pair_keys = swapped(key_states, "narrow", 0)
    parts = 2
    targets, *ends = stage(key_states, value_states, token_rates, parts)
    pair_targets = swapped(targets, "narrow", 0)
    attended = attend_late(query_states, key_states, value_states)
    sources = [own] + [arrivals[step] for step in range(1, narrow_count)]
    attended, ends = lax.optimization_barrier((attended, ends))
    sources, attended = lax.optimization_barrier((sources, attended))
    prior = []
    for end in ends:
        prior.append(from_behind(end, "narrow", 1))
    near, pack = fast_sums(sources, key_states, targets, pair_keys, pair_targets, owned)
    distances = range(1, narrow_count.bit_length() - 1)
    for distance in distances:
        far = swapped(near, "narrow", distance)
        if distance != distances[-1]:
            near = stored(near.astype(jnp.float32) + far.astype(jnp.float32))
    pair_pack = swapped(pack, "narrow", 0)
    pair_near = swapped(near, "narrow", 0)
    pair_far = swapped(far, "narrow", 0)
    attended, *state = attend_early(
        query_states, key_states, value_states, prior[0], cache_keys, cache_values, attended
    )
    attended = attend_last(query_states, prior[1], cache_keys, cache_values, *state, attended)
    recalled = fast_recall((near, pair_near, far, pair_far), (pack, pair_pack), query_states)
    return (attended, recalled)


def spread_plan(
    query_states,
    key_states,
    value_states,
    cache_keys,
    cache_values,
    gate_fast,
    lift_fast,
    down_fast,
    token_rates,
):
    features, tok_count = query_states.shape
    edge_cols = jnp.stack(
        [key_states[:, tok_count - WINDOW :], value_states[:, tok_count - WINDOW :]]
    )
    arrived = from_behind(edge_cols, "narrow", 1)
    leading = lax.axis_index("narrow") == 0
    prior_cols = jnp.where(leading, jnp.stack([cache_keys, cache_values]), arrived)
    ext_keys = jnp.concatenate([prior_cols[0], key_states], axis=1)
    ext_values = jnp.concatenate([prior_cols[1], value_states], axis=1)
    if features % HEAD_SIZE == 0:
        attended = attend_local(query_states, ext_keys, ext_values, 0)
    else:
        attended = attend_paired(query_states, ext_keys, ext_values)
    query_fast, key_fast, value_fast = (
        lax.all_to_all(
            lax.all_to_all(query_states, "wide", split_axis=1, concat_axis=0, tiled=True),
            "narrow",
            split_axis=0,
            concat_axis=1,
            tiled=True,
        ),
        lax.all_to_all(
            lax.all_to_all(key_states, "wide", split_axis=1, concat_axis=0, tiled=True),
            "narrow",
            split_axis=0,
            concat_axis=1,
            tiled=True,
        ),
        lax.all_to_all(
            lax.all_to_all(value_states, "wide", split_axis=1, concat_axis=0, tiled=True),
            "narrow",
            split_axis=0,
            concat_axis=1,
            tiled=True,
        ),
    )
    head_count = gate_fast.shape[0]
    wide_count = lax.axis_size("wide")
    narrow_count = lax.axis_size("narrow")
    piece_rows = tok_count // wide_count
    fast_tokens = query_fast.shape[1]
    rate_blocks = token_rates.reshape(token_rates.shape[0], narrow_count, wide_count, piece_rows)
    rates_here = lax.dynamic_slice(
        rate_blocks,
        (lax.axis_index("narrow") * head_count, 0, lax.axis_index("wide"), 0),
        (head_count, narrow_count, 1, piece_rows),
    ).reshape(head_count, fast_tokens)
    query_heads = query_fast.reshape(head_count, FD, fast_tokens)
    key_heads = key_fast.reshape(head_count, FD, fast_tokens)
    value_heads = value_fast.reshape(head_count, FD, fast_tokens)
    recall = fast_group(
        gate_fast, lift_fast, down_fast, query_heads, key_heads, value_heads, rates_here
    )
    recall = recall.reshape(head_count * FD, fast_tokens)
    recalled = lax.all_to_all(
        lax.all_to_all(recall, "narrow", split_axis=1, concat_axis=0, tiled=True),
        "wide",
        split_axis=0,
        concat_axis=1,
        tiled=True,
    )
    return (attended, recalled)


def per_device(*arrays):
    if in_place(*arrays):
        return in_place_plan(*arrays)
    return spread_plan(*arrays)


def solution(mesh):
    in_specs = (
        P("wide", "narrow"),
        P("wide", "narrow"),
        P("wide", "narrow"),
        P("wide", None),
        P("wide", None),
        P("narrow", None, None),
        P("narrow", None, None),
        P("narrow", None, None),
        P(),
    )
    out_specs = (P("wide", "narrow"), P("wide", "narrow"))
    return jax.shard_map(
        per_device, mesh=mesh, in_specs=in_specs, out_specs=out_specs, check_vma=False
    )
```

```python
import functools
import math

import jax
import jax.numpy as jnp
from jax import lax
from jax.experimental import pallas as pl
from jax.experimental.pallas import tpu as pltpu
from jax.sharding import PartitionSpec as P


FD = 512
HEAD_SIZE = 128
WINDOW = 1024
NS_ITERS = 2


EPS = 1e-06
COEF_A = 3.4445
COEF_B = -4.775
COEF_C = 2.0315
LOG2E = math.log2(math.e)
VMEM_GRANT = 67043328


def swapped(array, axis, distance):
    return lax.ppermute(array, axis, [(i, i ^ 1 << distance) for i in range(lax.axis_size(axis))])


def shortened(array):

    def short(part):
        return part.astype(jnp.bfloat16) if part.dtype == jnp.float32 else part

    return jax.tree.map(short, array)


def from_behind(value, axis, steps):
    count = lax.axis_size(axis)
    initial, last = (max(0, -steps), min(count, count - steps))
    return lax.ppermute(value, axis, [(source, source + steps) for source in range(initial, last)])


def stored(value):
    return lax.optimization_barrier(value.astype(jnp.bfloat16))


def attend_local(query_states, ext_keys, ext_values, key_start):
    features, tok_count = query_states.shape
    head_count = features // HEAD_SIZE
    block_rows = min(512, tok_count)
    block_count = tok_count // block_rows
    key_span = WINDOW + block_rows
    scaling = 1.0 / math.sqrt(HEAD_SIZE)
    rows_at = lax.broadcasted_iota(jnp.int32, (block_rows, key_span), 0)
    cols_at = lax.broadcasted_iota(jnp.int32, (block_rows, key_span), 1)
    visible = (cols_at > rows_at) & (cols_at <= rows_at + WINDOW)

    def one_block(block_index):
        offset = block_index * block_rows
        query_part = lax.dynamic_slice_in_dim(query_states, offset, block_rows, 1).reshape(
            head_count, HEAD_SIZE, block_rows
        )
        key_part = lax.dynamic_slice_in_dim(ext_keys, key_start + offset, key_span, 1).reshape(
            head_count, HEAD_SIZE, key_span
        )
        value_part = lax.dynamic_slice_in_dim(ext_values, key_start + offset, key_span, 1).reshape(
            head_count, HEAD_SIZE, key_span
        )
        scores = (
            jnp.einsum("hdq,hdk->hqk", query_part, key_part, preferred_element_type=jnp.float32)
            * scaling
        )
        scores = jnp.where(visible[None], scores, -jnp.inf)
        highest = jnp.max(scores, axis=2, keepdims=True)
        raised = jnp.exp(scores - highest)
        weights = (raised / jnp.sum(raised, axis=2, keepdims=True)).astype(jnp.bfloat16)
        blended = jnp.einsum(
            "hdk,hqk->hdq", value_part, weights, preferred_element_type=jnp.float32
        )
        return blended.astype(jnp.bfloat16).reshape(features, block_rows)

    blocks_out = lax.map(one_block, jnp.arange(block_count, dtype=jnp.int32))
    return jnp.transpose(blocks_out, (1, 0, 2)).reshape(features, tok_count)


def attend_paired(query_states, ext_keys, ext_values):
    features, tok_count = query_states.shape
    half_rows = tok_count // 2
    lower = lax.axis_index("wide") % 2 == 0
    query_send = jnp.where(lower, query_states[:, half_rows:], query_states[:, :half_rows])
    query_keep = jnp.where(lower, query_states[:, :half_rows], query_states[:, half_rows:])
    other_keys, other_values, other_queries = swapped((ext_keys, ext_values, query_send), "wide", 0)
    full_keys = jnp.where(
        lower,
        jnp.concatenate([ext_keys, other_keys], axis=0),
        jnp.concatenate([other_keys, ext_keys], axis=0),
    )
    full_values = jnp.where(
        lower,
        jnp.concatenate([ext_values, other_values], axis=0),
        jnp.concatenate([other_values, ext_values], axis=0),
    )
    full_queries = jnp.where(
        lower,
        jnp.concatenate([query_keep, other_queries], axis=0),
        jnp.concatenate([other_queries, query_keep], axis=0),
    )
    key_start = jnp.where(lower, 0, half_rows).astype(jnp.int32)
    head_out = attend_local(full_queries, full_keys, full_values, key_start)
    out_keep = jnp.where(lower, head_out[:features], head_out[features:])
    out_send = jnp.where(lower, head_out[features:], head_out[:features])
    out_other = swapped(shortened(out_send), "wide", 0).astype(out_send.dtype)
    return jnp.where(
        lower,
        jnp.concatenate([out_keep, out_other], axis=1),
        jnp.concatenate([out_other, out_keep], axis=1),
    )


def fast_terms(gate_weight, lift_weight, down_weight, key_heads, value_heads, rates_here):
    pre_gate = jnp.einsum(
        "hcf,hft->hct", gate_weight, key_heads, preferred_element_type=jnp.float32
    )
    pre_lift = jnp.einsum(
        "hcf,hft->hct", lift_weight, key_heads, preferred_element_type=jnp.float32
    )
    sigmoid_gate = jax.nn.sigmoid(pre_gate)
    silu_gate = pre_gate * sigmoid_gate
    hidden = (silu_gate * pre_lift).astype(jnp.bfloat16)
    target = (-(value_heads.astype(jnp.float32) * rates_here[:, None, :])).astype(jnp.bfloat16)
    grad_down = jnp.einsum("hft,hct->hfc", target, hidden, preferred_element_type=jnp.float32)
    back_hidden = jnp.einsum(
        "hfc,hft->hct", down_weight, target, preferred_element_type=jnp.float32
    )
    back_lift = (back_hidden * silu_gate).astype(jnp.bfloat16)
    back_gate = (
        back_hidden * pre_lift * sigmoid_gate * (1.0 + pre_gate * (1.0 - sigmoid_gate))
    ).astype(jnp.bfloat16)
    grad_gate = jnp.einsum("hct,hft->hcf", back_gate, key_heads, preferred_element_type=jnp.float32)
    grad_lift = jnp.einsum("hct,hft->hcf", back_lift, key_heads, preferred_element_type=jnp.float32)
    return (grad_gate, grad_lift, grad_down)


def scaled_start(rounded):
    widened = rounded.astype(jnp.float32)
    norm_val = jnp.sqrt(jnp.sum(jnp.square(widened), axis=(1, 2), keepdims=True) + EPS)
    return stored(widened / norm_val)


def starting(grad_gate, grad_lift, grad_down):
    sum_gate, sum_lift, sum_down = lax.psum((grad_gate, grad_lift, grad_down), "wide")
    return (
        scaled_start(stored(sum_gate)),
        scaled_start(stored(sum_lift)),
        scaled_start(stored(sum_down)),
    )


def orthogonal(current):
    for _ in range(NS_ITERS):
        gram_mat = jnp.einsum(
            "hrc,hrd->hcd", current, current, preferred_element_type=jnp.float32
        ).astype(jnp.bfloat16)
        lifted = stored(
            jnp.einsum("hrc,hcd->hrd", current, gram_mat, preferred_element_type=jnp.float32)
        )
        current = stored(
            COEF_A * current.astype(jnp.float32)
            + COEF_B * lifted.astype(jnp.float32)
            + COEF_C
            * jnp.einsum("hrc,hcd->hrd", lifted, gram_mat, preferred_element_type=jnp.float32)
        )
    return current


def refreshed(weight, ortho):
    initial = weight.astype(jnp.float32)
    moved_rows = initial - ortho.astype(jnp.float32)
    wanted = jnp.sqrt(jnp.mean(jnp.square(initial), axis=-1, keepdims=True) + EPS)
    present = jnp.sqrt(jnp.mean(jnp.square(moved_rows), axis=-1, keepdims=True) + EPS)
    return (moved_rows * (wanted / present)).astype(jnp.bfloat16)


def fast_group(
    gate_weight, lift_weight, down_weight, query_heads, key_heads, value_heads, rates_here
):
    grad_gate, grad_lift, grad_down = fast_terms(
        gate_weight, lift_weight, down_weight, key_heads, value_heads, rates_here
    )
    start_gate, start_lift, start_down = starting(grad_gate, grad_lift, grad_down)
    fresh_gate = refreshed(gate_weight, orthogonal(start_gate))
    fresh_lift = refreshed(lift_weight, orthogonal(start_lift))
    fresh_down = refreshed(down_weight, orthogonal(start_down))
    query_gate = jnp.einsum(
        "hcf,hft->hct", fresh_gate, query_heads, preferred_element_type=jnp.float32
    )
    query_lift = jnp.einsum(
        "hcf,hft->hct", fresh_lift, query_heads, preferred_element_type=jnp.float32
    )
    query_hidden = (jax.nn.silu(query_gate) * query_lift).astype(jnp.bfloat16)
    return jnp.einsum(
        "hfc,hct->hft", fresh_down, query_hidden, preferred_element_type=jnp.float32
    ).astype(jnp.bfloat16)


def attend_body(
    q_ref, kp_ref, vp_ref, kc_ref, vc_ref, o_ref, kt_ref, v_ref, *, block, window
):
    hd = q_ref.shape[0]
    scale = LOG2E / math.sqrt(hd)

    placed(kp_ref, vp_ref, kt_ref, v_ref, 0)
    placed(kc_ref, vc_ref, kt_ref, v_ref, window)
    v_ref[hd:, :] = jnp.ones((v_ref.shape[0] - hd, 2 * window), jnp.bfloat16)
    rows = lax.broadcasted_iota(jnp.int32, (block, block), 0)
    cols = lax.broadcasted_iota(jnp.int32, (block, block), 1)
    first = rows > cols
    inner = window // block

    def scores(b):
        q = q_ref[:, b * block : (b + 1) * block].astype(jnp.float32) * scale
        high = q.astype(jnp.bfloat16)
        low = (q - high.astype(jnp.float32)).astype(jnp.bfloat16)
        pair = jnp.concatenate([high, low], axis=0)
        parts = [
            jnp.dot(
                kt_ref[(b + j) * block : (b + j + 1) * block, :],
                pair,
                preferred_element_type=jnp.float32,
            )
            for j in range(inner + 1)
        ]
        return [jnp.where(first, parts[0], parts[inner])] + parts[1:inner]

    def blend(b, parts):
        top = functools.reduce(jnp.maximum, parts)
        top = jnp.max(top, axis=0, keepdims=True)
        raised = [jnp.exp2(part - top).astype(jnp.bfloat16) for part in parts]
        zero = jnp.zeros_like(raised[0])
        ends = jnp.where(first, raised[0], zero), jnp.where(first, zero, raised[0])
        weights = jnp.concatenate([ends[0]] + raised[1:] + [ends[1]], axis=0)
        span = v_ref[:, b * block : (b + inner + 1) * block]
        out = jnp.dot(span, weights, preferred_element_type=jnp.float32)
        o_ref[:, b * block : (b + 1) * block] = (out[:hd] * (1.0 / out[hd : hd + 1])).astype(
            jnp.bfloat16
        )

    ready = scores(0)
    for b in range(1, inner):
        following = scores(b)
        blend(b - 1, ready)
        ready = following
    blend(inner - 1, ready)


def attend_scratch():
    return [
        pltpu.VMEM((2 * WINDOW, 2 * HEAD_SIZE), jnp.bfloat16),
        pltpu.VMEM((HEAD_SIZE + 16, 2 * WINDOW), jnp.bfloat16),
    ]


def attend_late(queries, keys, values):
    features, tokens = queries.shape
    heads, chunks = features // HEAD_SIZE, tokens // WINDOW - 1
    here = pl.BlockSpec((HEAD_SIZE, WINDOW), lambda h, c: (h, c + 1))
    before = pl.BlockSpec((HEAD_SIZE, WINDOW), lambda h, c: (h, c))
    return pl.pallas_call(
        functools.partial(attend_body, block=min(256, WINDOW), window=WINDOW),
        out_shape=jax.ShapeDtypeStruct((features, tokens), jnp.bfloat16),
        grid=(heads, chunks),
        in_specs=[here, before, before, here, here],
        out_specs=here,
        scratch_shapes=attend_scratch(),
        cost_estimate=pl.CostEstimate(
            flops=5 * features * chunks * WINDOW**2,
            bytes_accessed=10 * features * chunks * WINDOW,
            transcendentals=heads * chunks * WINDOW**2,
        ),
        name="attend_late",
        compiler_params=pltpu.CompilerParams(vmem_limit_bytes=VMEM_GRANT),
    )(queries, keys, values, keys, values)


def two_term(q_ref, at, scale):
    q = q_ref[:, at].astype(jnp.float32) * scale
    high = q.astype(jnp.bfloat16)
    low = (q - high.astype(jnp.float32)).astype(jnp.bfloat16)
    return jnp.concatenate([high, low], axis=0)


def placed(k, v, kt_ref, v_ref, at):
    hd, width = k.shape
    turned = k[...].T
    kt_ref[at : at + width, :hd] = turned
    kt_ref[at : at + width, hd:] = turned
    v_ref[:hd, at : at + width] = v[...]


def early_body(
    q_ref, kp_ref, vp_ref, kc_ref, vc_ref, ck_ref, cv_ref, _, o_ref, part_ref, top_ref, mass_ref,
    kt_ref, v_ref, *, block,
):
    hd, window = q_ref.shape
    scale = LOG2E / math.sqrt(hd)
    near = kp_ref.shape[1]
    inner = window // block
    missing = (window - near) // block
    leading = lax.axis_index("narrow") == 0

    @pl.when(leading)
    def _():
        placed(ck_ref, cv_ref, kt_ref, v_ref, 0)

    @pl.when(jnp.logical_not(leading))
    def _():
        placed(kp_ref, vp_ref, kt_ref, v_ref, 0)

    placed(kc_ref, vc_ref, kt_ref, v_ref, near)
    v_ref[hd:, :] = jnp.ones((v_ref.shape[0] - hd, v_ref.shape[1]), jnp.bfloat16)
    rows = lax.broadcasted_iota(jnp.int32, (block, block), 0)
    cols = lax.broadcasted_iota(jnp.int32, (block, block), 1)
    first = rows > cols

    def chunk(j):
        return slice((j - missing) * block, (j - missing + 1) * block)

    def scores(b):
        pair = two_term(q_ref, slice(b * block, (b + 1) * block), scale)
        parts = [
            jnp.dot(kt_ref[chunk(j), :], pair, preferred_element_type=jnp.float32)
            for j in range(max(b, missing), b + inner + 1)
        ]
        if b >= missing:
            return [jnp.where(first, parts[0], parts[inner])] + parts[1:inner]
        return parts[:-1] + [jnp.where(first, -jnp.inf, parts[-1])]

    def blend(b, parts):
        top = functools.reduce(jnp.maximum, parts)
        top = jnp.max(top, axis=0, keepdims=True)
        raised = [jnp.exp2(part - top).astype(jnp.bfloat16) for part in parts]
        if b >= missing:
            zero = jnp.zeros_like(raised[0])
            ends = jnp.where(first, raised[0], zero), jnp.where(first, zero, raised[0])
            raised = [ends[0]] + raised[1:] + [ends[1]]
        span = v_ref[:, chunk(max(b, missing)).start : chunk(b + inner).stop]
        out = jnp.dot(span, jnp.concatenate(raised, axis=0), preferred_element_type=jnp.float32)
        if b >= missing:
            at = slice((b - missing) * block, (b - missing + 1) * block)
            o_ref[:, at] = (out[:hd] * (1.0 / out[hd : hd + 1])).astype(jnp.bfloat16)
        else:
            at = slice(b * block, (b + 1) * block)
            part_ref[:, at] = out[:hd]
            top_ref[:, at] = jnp.broadcast_to(top, (top_ref.shape[0], block))
            mass_ref[:, at] = jnp.broadcast_to(out[hd : hd + 1], (top_ref.shape[0], block))

    ready = scores(0)
    for b in range(1, inner):
        following = scores(b)
        blend(b - 1, ready)
        ready = following
    blend(inner - 1, ready)


def attend_early(queries, keys, values, prior, cache_keys, cache_values, late):
    features, tokens = queries.shape
    heads = features // HEAD_SIZE
    near = prior.shape[2]
    far = WINDOW - near
    here = pl.BlockSpec((HEAD_SIZE, WINDOW), lambda h: (h, 0))
    nearer = pl.BlockSpec((HEAD_SIZE, near), lambda h: (h, far // near))
    prior_keys = pl.BlockSpec((None, HEAD_SIZE, near), lambda h: (0, h, 0))
    prior_values = pl.BlockSpec((None, HEAD_SIZE, near), lambda h: (1, h, 0))
    rows = 8
    stats = jax.ShapeDtypeStruct((heads * rows, far), jnp.float32)
    stat = pl.BlockSpec((rows, far), lambda h: (h, 0))
    return pl.pallas_call(
        functools.partial(early_body, block=min(256, near)),
        out_shape=(
            jax.ShapeDtypeStruct((features, tokens), jnp.bfloat16),
            jax.ShapeDtypeStruct((features, far), jnp.float32),
            stats,
            stats,
        ),
        grid=(heads,),
        in_specs=[here, prior_keys, prior_values, here, here, nearer, nearer]
        + [pl.BlockSpec(memory_space=pl.ANY)],
        out_specs=(nearer, pl.BlockSpec((HEAD_SIZE, far), lambda h: (h, 0)), stat, stat),
        scratch_shapes=[
            pltpu.VMEM((near + WINDOW, 2 * HEAD_SIZE), jnp.bfloat16),
            pltpu.VMEM((HEAD_SIZE + 16, near + WINDOW), jnp.bfloat16),
        ],
        input_output_aliases={7: 0},
        cost_estimate=pl.CostEstimate(
            flops=5 * features * WINDOW**2,
            bytes_accessed=14 * features * WINDOW,
            transcendentals=heads * WINDOW**2,
        ),
        name="attend_early",
        compiler_params=pltpu.CompilerParams(vmem_limit_bytes=VMEM_GRANT),
    )(queries, prior, prior, keys, values, cache_keys, cache_values, late)


def last_body(
    q_ref, prior_ref, ck_ref, cv_ref, part_ref, top_ref, mass_ref, _, o_ref,
    held_q, held_k, held_v, held_part, held_top, held_mass, kt_ref, v_ref, made_ref, sem,
    *, block,
):
    features, far = part_ref.shape
    hd = HEAD_SIZE
    heads = features // hd
    scale = LOG2E / math.sqrt(hd)
    missing = far // block
    leading = lax.axis_index("narrow") == 0
    plain = [
        pltpu.make_async_copy(top_ref, held_top, sem.at[0, 0]),
        pltpu.make_async_copy(mass_ref, held_mass, sem.at[0, 1]),
    ]
    arriving = []
    for h in range(heads):
        at = slice(h * hd, (h + 1) * hd)
        keys = pltpu.make_async_copy(prior_ref.at[0, at], held_k.at[at], sem.at[1, h])
        values = pltpu.make_async_copy(prior_ref.at[1, at], held_v.at[at], sem.at[2, h])

        @pl.when(leading)
        def _(at=at, h=h):
            pltpu.make_async_copy(ck_ref.at[at, :far], held_k.at[at], sem.at[1, h]).start()
            pltpu.make_async_copy(cv_ref.at[at, :far], held_v.at[at], sem.at[2, h]).start()

        @pl.when(jnp.logical_not(leading))
        def _(keys=keys, values=values):
            keys.start()
            values.start()

        others = [
            pltpu.make_async_copy(q_ref.at[at, :far], held_q.at[at], sem.at[3, h]),
            pltpu.make_async_copy(part_ref.at[at], held_part.at[at], sem.at[4, h]),
        ]
        for copy in others + (plain if h == 0 else []):
            copy.start()
        arriving.append([keys, values] + others)
    rows = lax.broadcasted_iota(jnp.int32, (block, block), 0)
    cols = lax.broadcasted_iota(jnp.int32, (block, block), 1)
    first = rows > cols
    v_ref[:, hd:, :] = jnp.ones((heads, v_ref.shape[1] - hd, far), jnp.bfloat16)
    leaving = []
    for copy in plain:
        copy.wait()

    def scores(h, b):
        at = slice(h * hd, (h + 1) * hd)
        if b == 0:
            for copy in arriving[h]:
                copy.wait()
            placed(held_k.at[at], held_v.at[at], kt_ref.at[h], v_ref.at[h], 0)
        pair = two_term(held_q.at[at], slice(b * block, (b + 1) * block), scale)
        parts = [
            jnp.dot(
                kt_ref[h, j * block : (j + 1) * block, :], pair, preferred_element_type=jnp.float32
            )
            for j in range(b, missing)
        ]
        return [jnp.where(first, parts[0], -jnp.inf)] + parts[1:]

    def blend(h, b, parts):
        at = slice(h * hd, (h + 1) * hd)
        span = slice(b * block, (b + 1) * block)
        before = held_top[h * 8 : h * 8 + 1, span]
        top = functools.reduce(jnp.maximum, parts)
        top = jnp.maximum(jnp.max(top, axis=0, keepdims=True), before)
        kept = jnp.exp2(before - top)
        weights = jnp.concatenate(
            [jnp.exp2(part - top).astype(jnp.bfloat16) for part in parts], axis=0
        )
        out = jnp.dot(v_ref[h, :, b * block :], weights, preferred_element_type=jnp.float32)
        mass = held_mass[h * 8 : h * 8 + 1, span] * kept + out[hd : hd + 1]
        made_ref[at, span] = ((held_part[at, span] * kept + out[:hd]) * (1.0 / mass)).astype(
            jnp.bfloat16
        )
        if b == missing - 1:
            leaving.append(
                pltpu.make_async_copy(made_ref.at[at], o_ref.at[at, :far], sem.at[5, h])
            )
            leaving[-1].start()

    turns = [(h, b) for h in range(heads) for b in range(missing)]
    ready = scores(*turns[0])
    for turn, ahead in zip(turns, turns[1:]):
        following = scores(*ahead)
        blend(*turn, ready)
        ready = following
    blend(*turns[-1], ready)
    for copy in leaving:
        copy.wait()


def attend_last(queries, prior, cache_keys, cache_values, part, top, mass, early):
    features, tokens = queries.shape
    heads = features // HEAD_SIZE
    far = part.shape[1]
    pieces = pltpu.VMEM((features, far), jnp.bfloat16)
    return pl.pallas_call(
        functools.partial(last_body, block=min(512, far)),
        out_shape=jax.ShapeDtypeStruct((features, tokens), jnp.bfloat16),
        in_specs=[pl.BlockSpec(memory_space=pl.ANY)] * 8,
        out_specs=pl.BlockSpec(memory_space=pl.ANY),
        scratch_shapes=[
            pieces,
            pieces,
            pieces,
            pltpu.VMEM((features, far), jnp.float32),
            pltpu.VMEM(top.shape, jnp.float32),
            pltpu.VMEM(top.shape, jnp.float32),
            pltpu.VMEM((heads, far, 2 * HEAD_SIZE), jnp.bfloat16),
            pltpu.VMEM((heads, HEAD_SIZE + 16, far), jnp.bfloat16),
            pieces,
            pltpu.SemaphoreType.DMA((6, max(heads, 2))),
        ],
        input_output_aliases={7: 0},
        cost_estimate=pl.CostEstimate(
            flops=3 * features * far**2,
            bytes_accessed=14 * features * far,
            transcendentals=heads * far**2,
        ),
        name="attend_last",
        compiler_params=pltpu.CompilerParams(vmem_limit_bytes=VMEM_GRANT),
    )(queries, prior, cache_keys, cache_values, part, top, mass, early)


def anywhere(count):
    return [pl.BlockSpec(memory_space=pl.ANY)] * count


def half_rows(part, half):
    return pl.ds(pl.multiple_of(part * half, half), half)


def prepare_body(gate_ref, lift_ref, down_ref, own_ref, other_ref, w_ref, out_ref, sem):
    owned = gate_ref.shape[0]
    local = lax.axis_index("wide") % owned
    side = lax.axis_index("narrow") % 2
    half = own_ref.shape[1]
    copies = [
        pltpu.make_async_copy(source.at[local], w_ref.at[place], sem.at[0, place])
        for place, source in enumerate((down_ref, gate_ref, lift_ref))
    ]
    for copy in copies:
        copy.start()
    leaving = []
    copies[0].wait()
    out_ref[...] = w_ref[0].T
    for order, (place, source) in enumerate(((2, out_ref), (0, w_ref.at[1]), (1, w_ref.at[2]))):
        if order:
            copies[order].wait()
        for turn, (target, part) in enumerate(((own_ref, side), (other_ref, 1 - side))):
            leaving.append(
                pltpu.make_async_copy(
                    source.at[half_rows(part, half)], target.at[place], sem.at[1 + turn, place]
                )
            )
            leaving[-1].start()
    for copy in leaving:
        copy.wait()


def prepare(gate_fast, lift_fast, down_fast):
    _, hidden_rows, features = gate_fast.shape
    shape = (3, hidden_rows // 2, features)
    return pl.pallas_call(
        prepare_body,
        out_shape=(jax.ShapeDtypeStruct(shape, jnp.bfloat16),) * 2,
        in_specs=anywhere(3),
        out_specs=tuple(anywhere(2)),
        scratch_shapes=[
            pltpu.VMEM((3, hidden_rows, features), jnp.bfloat16),
            pltpu.VMEM((hidden_rows, features), jnp.bfloat16),
            pltpu.SemaphoreType.DMA((3, 3)),
        ],
        cost_estimate=pl.CostEstimate(
            flops=0, bytes_accessed=12 * hidden_rows * features, transcendentals=0
        ),
        name="prepare",
        compiler_params=pltpu.CompilerParams(vmem_limit_bytes=VMEM_GRANT),
    )(gate_fast, lift_fast, down_fast)


def stage_body(key_ref, value_ref, rate_ref, target_ref, *refs):
    end_refs, (held_ref, values_ref, made_ref, rates_ref, sem, sem_end) = refs[:-6], refs[-6:]
    features, tokens = key_ref.shape
    width = end_refs[0].shape[2]
    step = HEAD_SIZE
    lasts = [slice(tokens - (part + 1) * width, tokens - part * width) for part in range(len(end_refs))]
    begin = pl.multiple_of(lax.axis_index("narrow") * tokens, tokens)
    rates = pltpu.make_async_copy(rate_ref.at[:, pl.ds(begin, tokens)], rates_ref, sem_end.at[0, len(end_refs)])
    rates.start()
    values = [
        pltpu.make_async_copy(
            value_ref.at[at : at + step], values_ref.at[at : at + step], sem.at[0, at // step]
        )
        for at in range(0, features, step)
    ]
    keys = [
        pltpu.make_async_copy(
            key_ref.at[:, last], held_ref.at[part], sem_end.at[0, part]
        )
        for part, last in enumerate(lasts)
    ]
    for copy in values + keys:
        copy.start()
    leaving = []

    def leave(source, target, mark):
        leaving.append(pltpu.make_async_copy(source, target, mark))
        leaving[-1].start()

    rates.wait()
    rates = -rates_ref[pl.ds(lax.axis_index("wide"), 1), :]
    for place, copy in enumerate(values):
        at = slice(place * step, (place + 1) * step)
        copy.wait()
        made_ref[at] = (values_ref[at].astype(jnp.float32) * rates).astype(jnp.bfloat16)
        leave(made_ref.at[at], target_ref.at[at], sem.at[1, place])
    for part, end_ref in enumerate(end_refs):
        leave(values_ref.at[:, lasts[part]], end_ref.at[1], sem_end.at[1, part])
        keys[part].wait()
        leave(held_ref.at[part], end_ref.at[0], sem_end.at[2, part])
    for copy in leaving:
        copy.wait()


def stage(keys, values, rates, parts):
    features, tokens = keys.shape
    width = WINDOW // parts
    return pl.pallas_call(
        stage_body,
        out_shape=(jax.ShapeDtypeStruct((features, tokens), jnp.bfloat16),)
        + (jax.ShapeDtypeStruct((2, features, width), jnp.bfloat16),) * parts,
        in_specs=anywhere(3),
        out_specs=tuple(anywhere(1 + parts)),
        scratch_shapes=[
            pltpu.VMEM((parts, features, width), jnp.bfloat16),
            pltpu.VMEM((features, tokens), jnp.bfloat16),
            pltpu.VMEM((features, tokens), jnp.bfloat16),
            pltpu.VMEM((rates.shape[0], tokens), jnp.float32),
            pltpu.SemaphoreType.DMA((2, features // HEAD_SIZE)),
            pltpu.SemaphoreType.DMA((3, parts + 1)),
        ],
        cost_estimate=pl.CostEstimate(
            flops=features * tokens,
            bytes_accessed=4 * features * tokens + 8 * features * WINDOW,
            transcendentals=0,
        ),
        name="stage",
        compiler_params=pltpu.CompilerParams(vmem_limit_bytes=VMEM_GRANT),
    )(keys, values, rates)


def sums_body(*refs, owned, cuts):
    sources = refs[:-15]
    (
        key_ref, target_ref, pair_key_ref, pair_target_ref,
        send_out, pack_out,
        send_ref, pack_ref, keys_ref, targets_ref, hidden_ref, back_ref, sem, sem_in, sem_out,
    ) = refs[-15:]
    _, tokens = key_ref.shape
    half = pack_ref.shape[1]
    role = lax.axis_index("narrow") ^ (lax.axis_index("wide") // owned)

    for place, source in enumerate(sources):

        @pl.when(role == place)
        def _(source=source):
            pltpu.make_async_copy(source, pack_ref, sem).start()

    spans = [(key_ref, target_ref, 0, begin, end) for begin, end in zip(cuts, cuts[1:])]
    spans.append((pair_key_ref, pair_target_ref, tokens, 0, tokens))
    arrivals = []
    for slot, (keys, targets, base, begin, end) in enumerate(spans):
        source, place = slice(begin, end), slice(base + begin, base + end)
        copies = (
            pltpu.make_async_copy(keys.at[:, source], keys_ref.at[:, place], sem_in.at[0, slot]),
            pltpu.make_async_copy(
                targets.at[:, source], targets_ref.at[:, place], sem_in.at[1, slot]
            ),
        )
        for copy in copies:
            copy.start()
        arrivals.append((place, *copies))
    pltpu.make_async_copy(sources[0], pack_ref, sem).wait()
    leaving = [pltpu.make_async_copy(pack_ref, pack_out, sem_out.at[3])]
    leaving[0].start()
    gate_lift = jnp.concatenate([pack_ref[0] * jnp.bfloat16(0.5), pack_ref[1]], axis=0)
    down = pack_ref[2]

    for at, keys, targets in arrivals:
        keys.wait()
        pre = jnp.dot(gate_lift, keys_ref[:, at], preferred_element_type=jnp.float32)
        targets.wait()
        back_hidden = jnp.dot(down, targets_ref[:, at], preferred_element_type=jnp.float32)
        half_gate = pre[:half]
        pre_lift = pre[half:]
        twice = jnp.tanh(half_gate) + 1.0
        silu_gate = half_gate * twice
        hidden_ref[:, at] = (silu_gate * pre_lift).astype(jnp.bfloat16)
        slope = twice + silu_gate * (2.0 - twice)
        back_ref[:half, at] = (back_hidden * pre_lift * slope).astype(jnp.bfloat16)
        back_ref[half:, at] = (back_hidden * silu_gate).astype(jnp.bfloat16)

    def leave(place, value):
        send_ref[place] = value.astype(jnp.bfloat16)
        leaving.append(
            pltpu.make_async_copy(send_ref.at[place], send_out.at[place], sem_out.at[place])
        )
        leaving[-1].start()

    contract = (((1,), (1,)), ((), ()))
    sums = lax.dot_general(
        back_ref[...], keys_ref[...], contract, preferred_element_type=jnp.float32
    )
    leave(0, sums[:half] * 0.5)
    leave(1, sums[half:])
    sums = lax.dot_general(
        hidden_ref[...], targets_ref[...], contract, preferred_element_type=jnp.float32
    )
    leave(2, sums)
    for copy in leaving:
        copy.wait()


def fast_sums(sources, keys, targets, pair_keys, pair_targets, owned):
    features, tokens = keys.shape
    shape = sources[0].shape
    half = shape[1]
    cuts = (0, tokens)
    return pl.pallas_call(
        functools.partial(sums_body, owned=owned, cuts=cuts),
        out_shape=(jax.ShapeDtypeStruct(shape, jnp.bfloat16),) * 2,
        in_specs=anywhere(len(sources) + 4),
        out_specs=tuple(anywhere(2)),
        scratch_shapes=[
            pltpu.VMEM(shape, jnp.bfloat16),
            pltpu.VMEM(shape, jnp.bfloat16),
            pltpu.VMEM((features, 2 * tokens), jnp.bfloat16),
            pltpu.VMEM((features, 2 * tokens), jnp.bfloat16),
            pltpu.VMEM((half, 2 * tokens), jnp.bfloat16),
            pltpu.VMEM((2 * half, 2 * tokens), jnp.bfloat16),
            pltpu.SemaphoreType.DMA(()),
            pltpu.SemaphoreType.DMA((2, len(cuts))),
            pltpu.SemaphoreType.DMA((4,)),
        ],
        cost_estimate=pl.CostEstimate(
            flops=24 * half * features * tokens,
            bytes_accessed=8 * features * tokens + 6 * 3 * half * features,
            transcendentals=2 * half * tokens,
        ),
        name="fast_sums",
        compiler_params=pltpu.CompilerParams(vmem_limit_bytes=VMEM_GRANT),
    )(*sources, keys, targets, pair_keys, pair_targets)


def recall_body(
    mine_ref, other_ref, far_ref, other_far_ref, pack_ref, pair_pack_ref, query_ref, out_ref,
    w_ref, near_sums_ref, far_sums_ref, held_ref, made_ref, sem,
):
    half = mine_ref.shape[1]
    hidden_rows, features = w_ref.shape[1:]
    nt = (((1,), (1,)), ((), ()))

    side = lax.axis_index("narrow") % 2

    def arriving(matrix):
        moves = (
            (mine_ref, near_sums_ref, side),
            (other_ref, near_sums_ref, 1 - side),
            (far_ref, far_sums_ref, side),
            (other_far_ref, far_sums_ref, 1 - side),
        )
        return [
            pltpu.make_async_copy(
                source.at[matrix],
                target.at[matrix, half_rows(part, half)],
                sem.at[place, matrix],
            )
            for place, (source, target, part) in enumerate(moves)
        ]

    sums = [arriving(matrix) for matrix in range(3)]
    weights = [
        pltpu.make_async_copy(source, w_ref.at[:, half_rows(part, half)], sem.at[4, place])
        for place, (source, part) in enumerate(((pack_ref, side), (pair_pack_ref, 1 - side)))
    ]
    queries = pltpu.make_async_copy(query_ref, held_ref, sem.at[5, 2])
    for copies in sums + [weights, [queries]]:
        for copy in copies:
            copy.start()
    rows = lax.broadcasted_iota(jnp.int32, (hidden_rows, features), 0)
    cols = lax.broadcasted_iota(jnp.int32, (hidden_rows, features), 1)
    diagonal = rows == cols
    rounded, gram, scale = [], [], []
    for matrix, copies in enumerate(sums):
        for copy in copies:
            copy.wait()
        summed = near_sums_ref[matrix].astype(jnp.float32) + far_sums_ref[matrix].astype(
            jnp.float32
        )
        x = summed.astype(jnp.bfloat16)
        product = lax.dot_general(x, x, nt, preferred_element_type=jnp.float32)
        trace = jnp.sum(jnp.where(diagonal, product, 0.0), axis=0, keepdims=True)
        scale.append(lax.rsqrt(jnp.sum(trace, axis=1, keepdims=True) + EPS))
        rounded.append(x)
        gram.append((product * (scale[-1] * scale[-1])).astype(jnp.bfloat16))
    current = rounded
    for sweep_index in range(NS_ITERS):
        if sweep_index:
            scale = [1.0] * 3
            gram = [
                lax.dot_general(x, x, nt, preferred_element_type=jnp.float32).astype(
                    jnp.bfloat16
                )
                for x in current
            ]
        lifted = [
            jnp.dot(g, x, preferred_element_type=jnp.float32).astype(jnp.bfloat16)
            for x, g in zip(current, gram)
        ]
        current = [
            (
                (COEF_A * r) * x.astype(jnp.float32)
                + (COEF_B * r) * y.astype(jnp.float32)
                + (COEF_C * r) * jnp.dot(g, y, preferred_element_type=jnp.float32)
            ).astype(jnp.bfloat16)
            for x, y, g, r in zip(current, lifted, gram, scale)
        ]
    for copy in weights:
        copy.wait()

    def fresh(i):
        axis = 0 if i == 2 else 1
        initial = w_ref[i].astype(jnp.float32)
        moved = initial - current[i].astype(jnp.float32)
        wanted = jnp.mean(jnp.square(initial), axis=axis, keepdims=True) + EPS
        present = jnp.mean(jnp.square(moved), axis=axis, keepdims=True) + EPS
        return (moved * (wanted * lax.rsqrt(wanted * present))).astype(jnp.bfloat16)

    queries.wait()
    tokens = held_ref.shape[1]
    block = tokens // 2
    spans = [slice(at, at + block) for at in range(0, tokens, block)]
    fresh_gate = fresh(0)
    gates = [
        jnp.dot(fresh_gate * jnp.bfloat16(0.5), held_ref[:, span], preferred_element_type=jnp.float32)
        for span in spans
    ]
    fresh_lift = fresh(1)
    lifts = [
        jnp.dot(fresh_lift, held_ref[:, span], preferred_element_type=jnp.float32) for span in spans
    ]
    fresh_down = fresh(2).T
    leaving = []
    for place, (span, gate, lift) in enumerate(zip(spans, gates, lifts)):
        hidden = (gate * (jnp.tanh(gate) + 1.0) * lift).astype(jnp.bfloat16)
        made_ref[:, span] = jnp.dot(
            fresh_down, hidden, preferred_element_type=jnp.float32
        ).astype(jnp.bfloat16)
        leaving.append(
            pltpu.make_async_copy(made_ref.at[:, span], out_ref.at[:, span], sem.at[5, place])
        )
        leaving[-1].start()
    for copy in leaving:
        copy.wait()


def fast_recall(sums, packs, queries):
    features, tokens = queries.shape
    half = packs[0].shape[1]
    hidden_rows = 2 * half
    return pl.pallas_call(
        recall_body,
        out_shape=jax.ShapeDtypeStruct((features, tokens), jnp.bfloat16),
        in_specs=anywhere(7),
        out_specs=pl.BlockSpec(memory_space=pl.ANY),
        scratch_shapes=[
            pltpu.VMEM((3, hidden_rows, features), jnp.bfloat16),
            pltpu.VMEM((3, hidden_rows, features), jnp.bfloat16),
            pltpu.VMEM((3, hidden_rows, features), jnp.bfloat16),
            pltpu.VMEM((features, tokens), jnp.bfloat16),
            pltpu.VMEM((features, tokens), jnp.bfloat16),
            pltpu.SemaphoreType.DMA((6, 3)),
        ],
        cost_estimate=pl.CostEstimate(
            flops=6 * hidden_rows * features * tokens + 18 * NS_ITERS * hidden_rows * features**2,
            bytes_accessed=4 * features * tokens + 12 * hidden_rows * features,
            transcendentals=hidden_rows * tokens,
        ),
        name="fast_recall",
        compiler_params=pltpu.CompilerParams(vmem_limit_bytes=VMEM_GRANT),
    )(*sums, *packs, queries)


def in_place(query_states, key_states, value_states, cache_keys, cache_values, gate_fast, *rest):
    features, tok_count = query_states.shape
    narrow_count = lax.axis_size("narrow")
    return (
        features == FD
        and gate_fast.shape[1:] == (FD, FD)
        and features % HEAD_SIZE == 0
        and tok_count % WINDOW == 0
        and tok_count >= 2 * WINDOW
        and narrow_count >= 4
        and narrow_count & (narrow_count - 1) == 0
    )


def in_place_plan(
    query_states,
    key_states,
    value_states,
    cache_keys,
    cache_values,
    gate_fast,
    lift_fast,
    down_fast,
    token_rates,
):
    wide_count = lax.axis_size("wide")
    narrow_count = lax.axis_size("narrow")
    owned = gate_fast.shape[0]

    def from_owner(value, step):
        pairs = []
        for wide in range(wide_count):
            start = wide * narrow_count
            owner = wide // owned
            pairs.append((start + owner, start + (owner ^ step)))
        return lax.ppermute(value, ("wide", "narrow"), pairs)

    own, other = prepare(gate_fast, lift_fast, down_fast)
    arrivals = {}
    for step in sorted(range(1, narrow_count), key=lambda step: step < 2):
        if step == 1:
            arrivals[step] = swapped(other, "narrow", 0)
        else:
            arrivals[step] = from_owner((own, other)[step % 2], step)
    pair_keys = swapped(key_states, "narrow", 0)
    parts = 2
    targets, *ends = stage(key_states, value_states, token_rates, parts)
    pair_targets = swapped(targets, "narrow", 0)
    attended = attend_late(query_states, key_states, value_states)
    sources = [own] + [arrivals[step] for step in range(1, narrow_count)]
    attended, ends = lax.optimization_barrier((attended, ends))
    sources, attended = lax.optimization_barrier((sources, attended))
    prior = []
    for end in ends:
        prior.append(from_behind(end, "narrow", 1))
    near, pack = fast_sums(sources, key_states, targets, pair_keys, pair_targets, owned)
    distances = range(1, narrow_count.bit_length() - 1)
    for distance in distances:
        far = swapped(near, "narrow", distance)
        if distance != distances[-1]:
            near = stored(near.astype(jnp.float32) + far.astype(jnp.float32))
    pair_pack = swapped(pack, "narrow", 0)
    pair_near = swapped(near, "narrow", 0)
    pair_far = swapped(far, "narrow", 0)
    attended, *state = attend_early(
        query_states, key_states, value_states, prior[0], cache_keys, cache_values, attended
    )
    attended = attend_last(query_states, prior[1], cache_keys, cache_values, *state, attended)
    recalled = fast_recall((near, pair_near, far, pair_far), (pack, pair_pack), query_states)
    return (attended, recalled)


def spread_plan(
    query_states,
    key_states,
    value_states,
    cache_keys,
    cache_values,
    gate_fast,
    lift_fast,
    down_fast,
    token_rates,
):
    features, tok_count = query_states.shape
    edge_cols = jnp.stack(
        [key_states[:, tok_count - WINDOW :], value_states[:, tok_count - WINDOW :]]
    )
    arrived = from_behind(edge_cols, "narrow", 1)
    leading = lax.axis_index("narrow") == 0
    prior_cols = jnp.where(leading, jnp.stack([cache_keys, cache_values]), arrived)
    ext_keys = jnp.concatenate([prior_cols[0], key_states], axis=1)
    ext_values = jnp.concatenate([prior_cols[1], value_states], axis=1)
    if features % HEAD_SIZE == 0:
        attended = attend_local(query_states, ext_keys, ext_values, 0)
    else:
        attended = attend_paired(query_states, ext_keys, ext_values)
    query_fast, key_fast, value_fast = (
        lax.all_to_all(
            lax.all_to_all(query_states, "wide", split_axis=1, concat_axis=0, tiled=True),
            "narrow",
            split_axis=0,
            concat_axis=1,
            tiled=True,
        ),
        lax.all_to_all(
            lax.all_to_all(key_states, "wide", split_axis=1, concat_axis=0, tiled=True),
            "narrow",
            split_axis=0,
            concat_axis=1,
            tiled=True,
        ),
        lax.all_to_all(
            lax.all_to_all(value_states, "wide", split_axis=1, concat_axis=0, tiled=True),
            "narrow",
            split_axis=0,
            concat_axis=1,
            tiled=True,
        ),
    )
    head_count = gate_fast.shape[0]
    wide_count = lax.axis_size("wide")
    narrow_count = lax.axis_size("narrow")
    piece_rows = tok_count // wide_count
    fast_tokens = query_fast.shape[1]
    rate_blocks = token_rates.reshape(token_rates.shape[0], narrow_count, wide_count, piece_rows)
    rates_here = lax.dynamic_slice(
        rate_blocks,
        (lax.axis_index("narrow") * head_count, 0, lax.axis_index("wide"), 0),
        (head_count, narrow_count, 1, piece_rows),
    ).reshape(head_count, fast_tokens)
    query_heads = query_fast.reshape(head_count, FD, fast_tokens)
    key_heads = key_fast.reshape(head_count, FD, fast_tokens)
    value_heads = value_fast.reshape(head_count, FD, fast_tokens)
    recall = fast_group(
        gate_fast, lift_fast, down_fast, query_heads, key_heads, value_heads, rates_here
    )
    recall = recall.reshape(head_count * FD, fast_tokens)
    recalled = lax.all_to_all(
        lax.all_to_all(recall, "narrow", split_axis=1, concat_axis=0, tiled=True),
        "wide",
        split_axis=0,
        concat_axis=1,
        tiled=True,
    )
    return (attended, recalled)


def per_device(*arrays):
    if in_place(*arrays):
        return in_place_plan(*arrays)
    return spread_plan(*arrays)


def solution(mesh):
    in_specs = (
        P("wide", "narrow"),
        P("wide", "narrow"),
        P("wide", "narrow"),
        P("wide", None),
        P("wide", None),
        P("narrow", None, None),
        P("narrow", None, None),
        P("narrow", None, None),
        P(),
    )
    out_specs = (P("wide", "narrow"), P("wide", "narrow"))
    return jax.shard_map(
        per_device, mesh=mesh, in_specs=in_specs, out_specs=out_specs, check_vma=False
    )
```
